32 devices in a mesh: batch: 8 (over z, y), group: 4 (over x, core).
Axes of the slice: x: 2, y: 2, z: 4, core: 2. Of those that a mesh axis runs over, the one named last changes fastest.
Arguments:
- inputs: bfloat16 [16, 32, 32, 768], P('batch', 'group'), may hold values from -6 to 6
- segments: int32 [16, 1024], P('batch'), may hold values from 0 to 3, never falling along the last dimension, each value on 1 to 384 neighbouring positions
- class_labels: int32 [16], P('batch'), may hold values from 0 to 999
- time_steps: int32 [16], P('batch'), may hold values from 0 to 999
- class_table: bfloat16 [1000, 768], replicated, may hold values from -6 to 6
- time_table: bfloat16 [1000, 768], replicated, may hold values from -6 to 6
- modulation_weight: bfloat16 [768, 4608], replicated, may hold values from -0.21875 to 0.21875
- project_weight: bfloat16 [768, 2304], replicated, may hold values from -0.21875 to 0.21875
- output_weight: bfloat16 [768, 768], replicated, may hold values from -0.875 to 0.875
- kernel_attention: bfloat16 [9, 768], replicated, may hold values from -2 to 2
- up_weight: bfloat16 [768, 3072], replicated, may hold values from -0.21875 to 0.21875
- kernel_feed: bfloat16 [9, 3072], replicated, may hold values from -2 to 2
- down_weight: bfloat16 [3072, 768], replicated, may hold values from -0.109375 to 0.109375
- cotangent: bfloat16 [16, 32, 32, 768], P('batch', 'group'), may hold values from -6 to 6
Outputs:
- result: bfloat16 [16, 32, 32, 768], P('batch', 'group')
- inputs_gradient: bfloat16 [16, 32, 32, 768], P('batch', 'group')
- class_table_gradient: float32 [1000, 768], P(None, 'batch')
- time_table_gradient: float32 [1000, 768], P(None, 'batch')
- modulation_weight_gradient: float32 [768, 4608], P('batch')
- project_weight_gradient: float32 [768, 2304], P('batch')
- output_weight_gradient: float32 [768, 768], P('batch')
- kernel_attention_gradient: float32 [9, 768], P(None, 'batch')
- up_weight_gradient: float32 [768, 3072], P('batch')
- kernel_feed_gradient: float32 [9, 3072], P(None, 'batch')
- down_weight_gradient: float32 [3072, 768], P('batch')
The draws below stay inside these ranges and needn't reach their ends.
All inputs are finite; a program needn't handle non-finite values.
Results may differ from the reference program's by a relative error of at most 0.023.
The reference program's roundings to bfloat16 on the way count: a program that leaves them out, or rounds other values in their place, can miss the bound.
Values may be sent and summed in bfloat16 or wider, within the bound.
A program may use at most 192 MiB of HBM per device.

```python
import math
import jax
import jax.numpy as jnp
import numpy as np
from jax import lax

D = 768
HEADS = 12
FF = 3072
CLASSES = 1000
STEPS = 1000
SIDE = 32
CANVASES = 16
SEG_MOST = 384


def with_ends(drawn, rng, least, largest):
    longest = drawn.shape.index(max(drawn.shape))
    spots = []
    for shift in (0, 1):
        where = [jax.random.randint(jax.random.fold_in(rng, axis), (), 0, length) for axis, length in enumerate(drawn.shape)]
        where[longest] = (where[longest] + shift) % drawn.shape[longest]
        spots.append(tuple(where))
    return drawn.at[spots[0]].set(least).at[spots[1]].set(largest)


def shard_levels(key, dims, shards, smallest, largest):
    loudness = 1.0
    for dim, shards_of in shards:
        draws = jax.random.uniform(jax.random.fold_in(jax.random.fold_in(key, 6), dim), (shards_of,), jnp.float32, smallest / len(shards), largest / len(shards))
        loudness = loudness * jnp.repeat(jnp.exp(draws), dims[dim] // shards_of).reshape((-1,) + (1,) * (len(dims) - 1 - dim))
    return loudness


def profile(count, total, most, lean):
    loads = [(1 << 20) // math.isqrt(standing ** lean) + 1 for standing in range(2, count + 1)]
    spare, counts = total - most - (count - 1), [1] * (count - 1)
    while spare > 0:
        movable = [i for i in range(count - 1) if counts[i] < most]
        pool, remaining = sum([loads[i] for i in movable]), spare
        for i in movable:
            addition = min(most - counts[i], max(1, remaining * loads[i] // pool), spare)
            counts[i] = counts[i] + addition
            spare = spare - addition
    return np.array([most] + counts)


def ragged_sizes(stream_key, amount, total, reach, skew):
    if amount == 2:
        one = jax.random.randint(stream_key, (), max(1, total - reach), min(reach, total - 1) + 1)
        return jnp.stack([one, total - one])
    tallies = jnp.asarray(profile(amount, total, reach, skew), jnp.int32)
    couples = (amount - 1) // 2
    donor, taker = tallies[1:1 + 2 * couples:2], tallies[2:2 + 2 * couples:2]
    slack = jnp.minimum(donor - 1, reach - taker)
    moved = jax.random.randint(jax.random.fold_in(stream_key, 1), (couples,), 0, 1 << 20) % (slack + 1)
    tallies = tallies.at[1:1 + 2 * couples:2].set(donor - moved).at[2:2 + 2 * couples:2].set(taker + moved)
    return tallies[jax.random.permutation(jax.random.fold_in(stream_key, 2), amount)]


def normal_values(stream_key, extent, scale, most, split=(), dtype=jnp.bfloat16):
    factor_of = shard_levels(stream_key, extent, split, -0.22, 0.18) if split else 1.0
    array = jax.random.normal(stream_key, extent, jnp.float32) * scale * factor_of
    return jnp.minimum(jnp.maximum(array, -most), most).astype(dtype)


def setup_inputs(seed: int = 0) -> dict:
    streams_of = jax.random.split(jax.random.key(seed), 15)
    return {
        "inputs": normal_values(streams_of[0], (CANVASES, SIDE, SIDE, D), 1.0, 6.0, ((0, 8), (1, 4))),
        "segments": jax.vmap(lambda own: jnp.searchsorted(jnp.cumsum(ragged_sizes(own, 4, SIDE * SIDE, SEG_MOST, 0)), jnp.arange(SIDE * SIDE), side="right"))(jax.random.split(streams_of[1], CANVASES)).reshape((CANVASES, SIDE * SIDE)).astype(jnp.int32),
        "class_labels": with_ends(jax.random.randint(streams_of[2], (CANVASES,), 0, CLASSES), jax.random.fold_in(streams_of[2], 1), 0, CLASSES - 1).astype(jnp.int32),
        "time_steps": with_ends(jax.random.randint(streams_of[3], (CANVASES,), 0, STEPS), jax.random.fold_in(streams_of[3], 1), 0, STEPS - 1).astype(jnp.int32),
        "class_table": normal_values(streams_of[4], (CLASSES, D), 1.0, 6.0),
        "time_table": normal_values(streams_of[5], (STEPS, D), 1.0, 6.0),
        "modulation_weight": normal_values(streams_of[6], (D, 6 * D), D ** -0.5, 0.21875),
        "project_weight": normal_values(streams_of[7], (D, 3 * D), D ** -0.5, 0.21875),
        "output_weight": normal_values(streams_of[8], (D, D), (D // 16) ** -0.5, 0.875),
        "kernel_attention": normal_values(streams_of[9], (9, D), 0.33, 2.0),
        "up_weight": normal_values(streams_of[10], (D, FF), D ** -0.5, 0.21875),
        "kernel_feed": normal_values(streams_of[11], (9, FF), 0.33, 2.0),
        "down_weight": normal_values(streams_of[12], (FF, D), FF ** -0.5, 0.109375),
        "cotangent": normal_values(streams_of[13], (CANVASES, SIDE, SIDE, D), 1.0, 6.0, ((0, 8), (1, 4))),
    }


highest = lax.Precision.HIGHEST

@jax.custom_vjp
def low(v):
    return lax.optimization_barrier(v.astype(jnp.bfloat16)).astype(jnp.float32)

@jax.custom_vjp
def low_back(v):
    return v

def low_keep(v):
    return (low(v), None)

def low_pass(kept, grad):
    return (grad,)

def back_keep(v):
    return (v, None)

def back_low(kept, grad):
    return (low(grad),)
low.defvjp(low_keep, low_pass)
low_back.defvjp(back_keep, back_low)

def layer_norm(values):
    center = values - lax.optimization_barrier(jnp.mean(values, axis=-1, keepdims=True))
    second = lax.optimization_barrier(jnp.mean(center * center, axis=-1, keepdims=True))
    return center * lax.rsqrt(second + 1e-06)

def modulate(values, shift, scale):
    return layer_norm(values) * (1.0 + scale) + shift

def depthwise(values, kernel):
    padded = jnp.pad(values, ((0, 0), (1, 1), (1, 1), (0, 0)))
    height = values.shape[1]
    across = values.shape[2]
    total = jnp.zeros_like(values)
    for offset in range(9):
        down = offset // 3
        right = offset % 3
        total = total + kernel[offset] * padded[:, down:down + height, right:right + across, :]
    return total

def unshuffle(values):
    count = values.shape[0]
    half = values.shape[1] // 2
    channels = values.shape[3]
    parted = values.reshape(count, half, 2, half, 2, channels)
    return parted.transpose(0, 2, 4, 1, 3, 5).reshape(count, 4, half * half, channels)

def reshuffle(values, side):
    count = values.shape[0]
    half = side // 2
    channels = values.shape[3]
    parted = values.reshape(count, 2, 2, half, half, channels)
    return parted.transpose(0, 3, 1, 4, 2, 5).reshape(count, side, side, channels)

def forward(inputs, weights_all, segments, class_labels, time_steps):
    class_table, time_table, modulation_weight, project_weight, output_weight, kernel_attention, up_weight, kernel_feed, down_weight = weights_all
    count = inputs.shape[0]
    side = inputs.shape[1]
    width = inputs.shape[3]
    head_size = width // HEADS
    cond = class_table[class_labels] + time_table[time_steps]
    cond_low = low(jax.nn.silu(cond))
    modulation = jnp.dot(cond_low, modulation_weight, precision=highest)
    parts = [modulation[:, index * width:(index + 1) * width][:, None, None, :] for index in range(6)]
    attention_in = low(modulate(inputs, parts[0], parts[1]))
    mixed = low_back(low(depthwise(attention_in, kernel_attention)))
    grouped = unshuffle(mixed)
    length = grouped.shape[2]
    projected = jnp.dot(grouped, project_weight, precision=highest).reshape(count, 4, length, 3, HEADS, head_size)
    queries = low_back(low(projected[:, :, :, 0]))
    keys = low_back(low(projected[:, :, :, 1]))
    values = low_back(low(projected[:, :, :, 2]))
    scores = low_back(jnp.einsum('cglhe,cgmhe->cghlm', queries, keys, precision=highest) * head_size ** (-0.5))
    labels = unshuffle(segments.reshape(count, side, side, 1))[..., 0]
    allowed = labels[:, :, None, :, None] == labels[:, :, None, None, :]
    masked = jnp.where(allowed, scores, -1e+30)
    top = lax.optimization_barrier(jnp.max(masked, axis=-1, keepdims=True))
    powers = jnp.exp(masked - top)
    weights = low(powers / lax.optimization_barrier(jnp.sum(powers, axis=-1, keepdims=True)))
    attended = jnp.einsum('cghlm,cgmhe->cglhe', weights, values, precision=highest)
    attended = low_back(low(attended.reshape(count, 4, length, width)))
    branch = low_back(low(jnp.dot(attended, output_weight, precision=highest)))
    middle = inputs + parts[2] * reshuffle(branch, side)
    feed_in = low(modulate(middle, parts[3], parts[4]))
    hidden = low_back(low(jnp.dot(feed_in, up_weight, precision=highest)))
    spread = low_back(depthwise(hidden, kernel_feed))
    activated = low(jax.nn.gelu(spread, approximate=False))
    branch_two = low_back(jnp.dot(activated, down_weight, precision=highest))
    return middle + parts[5] * branch_two

def reference(inputs, segments, class_labels, time_steps, class_table, time_table, modulation_weight, project_weight, output_weight, kernel_attention, up_weight, kernel_feed, down_weight, cotangent):
    weights_all = tuple((item.astype(jnp.float32) for item in (class_table, time_table, modulation_weight, project_weight, output_weight, kernel_attention, up_weight, kernel_feed, down_weight)))
    block = 4
    rounds = CANVASES // block
    side = inputs.shape[1]
    width = inputs.shape[3]
    stacked = (inputs.reshape(rounds, block, side, side, width), cotangent.reshape(rounds, block, side, side, width), segments.reshape(rounds, block, side * side), class_labels.reshape(rounds, block), time_steps.reshape(rounds, block))

    def one_block(totals, sliced):
        canvas_in, canvas_grad, labels, classes, timesteps = sliced

        def closed(values, params_in):
            return forward(values, params_in, labels, classes, timesteps)
        output, pullback = jax.vjp(closed, canvas_in.astype(jnp.float32), weights_all)
        input_grad, weight_grads = pullback(canvas_grad.astype(jnp.float32))
        summed = tuple((total + extra for total, extra in zip(totals, weight_grads)))
        return (summed, (output.astype(jnp.bfloat16), input_grad.astype(jnp.bfloat16)))
    initial = tuple((jnp.zeros_like(item) for item in weights_all))
    totals, outputs_all = lax.scan(one_block, initial, stacked)
    outputs, input_grads = outputs_all
    return (outputs.reshape(inputs.shape), input_grads.reshape(inputs.shape), totals[0], totals[1], totals[2], totals[3], totals[4], totals[5], totals[6], totals[7], totals[8])
```

```python
from functools import partial

import jax
import jax.numpy as jnp
from jax import lax
from jax.experimental import pallas as pl
from jax.experimental.pallas import tpu as pltpu
from jax.sharding import PartitionSpec as P

HEADS = 12


highest = lax.Precision.HIGHEST


def padded_2(block, sides, width):
    for axis, dim in sides:
        count = lax.axis_size(axis)
        forward = [(i, i + 1) for i in range(count - 1)]
        backward = [(target, source) for source, target in forward]
        low = lax.ppermute(
            lax.slice_in_dim(block, block.shape[dim] - width, None, axis=dim), axis, forward
        )
        high = lax.ppermute(lax.slice_in_dim(block, 0, width, axis=dim), axis, backward)
        block = jnp.concatenate([low, block, high], axis=dim)
    return block


def layer_norm(values):
    center = values - jnp.mean(values, axis=-1, keepdims=True)
    second = jnp.mean(center * center, axis=-1, keepdims=True)
    return center * lax.rsqrt(second + 1e-06)


def modulate(values, shift, scale):
    return layer_norm(values) * (1.0 + scale) + shift


def pad_columns(values):
    return jnp.pad(values, ((0, 0), (0, 0), (1, 1), (0, 0)))


def depthwise(padded, kernel, height, across):
    total = jnp.zeros((padded.shape[0], height, across, padded.shape[3]), jnp.float32)
    for offset in range(9):
        down = offset // 3
        right = offset % 3
        total = (
            total
            + kernel[offset].astype(jnp.float32)
            * padded[:, down : down + height, right : right + across, :]
        )
    return total


def depthwise_back(padded, kernel, height, across):
    total = jnp.zeros((padded.shape[0], height, across, padded.shape[3]), jnp.float32)
    for offset in range(9):
        down = offset // 3
        right = offset % 3
        total = (
            total
            + kernel[offset].astype(jnp.float32)
            * padded[:, 2 - down : 2 - down + height, 2 - right : 2 - right + across, :]
        )
    return total


def kernel_terms(padded, upstream, height, across):
    rows_all = []
    for offset in range(9):
        down = offset // 3
        right = offset % 3
        rows_all.append(
            jnp.sum(
                padded[:, down : down + height, right : right + across, :] * upstream,
                axis=(0, 1, 2),
            )
        )
    return jnp.stack(rows_all)


def to_groups(values):
    count, height, across, channels = values.shape
    parted = values.reshape(count, height // 2, 2, across // 2, 2, channels)
    return parted.transpose(0, 2, 4, 1, 3, 5).reshape(count, 4, height // 2, across // 2, channels)


def finish_groups(received):
    count = received.shape[0]
    rows_half = received.shape[2]
    half = received.shape[3]
    channels = received.shape[4]
    parted = received.reshape(count, 2, 2, rows_half, half, channels)
    return parted.transpose(0, 3, 1, 4, 2, 5).reshape(count, 2 * rows_half, 2 * half, channels)


def attend_block(queries, keys, values, labels, score_scale):
    allowed = labels[:, :, None] == labels[:, None, :]
    scores = (
        jnp.einsum("blhe,bmhe->bhlm", queries, keys, preferred_element_type=jnp.float32)
        * score_scale
    )
    masked = jnp.where(allowed[:, None], scores, -1e30)
    top = jnp.max(masked, axis=-1, keepdims=True)
    total = jnp.sum(jnp.exp(masked - top), axis=-1, keepdims=True)
    logsum = top + jnp.log(total)
    weights = jnp.exp(masked - logsum).astype(jnp.bfloat16)
    attended = jnp.einsum("bhlm,bmhe->blhe", weights, values, preferred_element_type=jnp.float32)
    return (attended.astype(jnp.bfloat16), logsum)


def attend_back(queries, keys, values, labels, logsum, upstream, score_scale):
    allowed = labels[:, :, None] == labels[:, None, :]
    scores = (
        jnp.einsum("blhe,bmhe->bhlm", queries, keys, preferred_element_type=jnp.float32)
        * score_scale
    )
    masked = jnp.where(allowed[:, None], scores, -1e30)
    weights = jnp.exp(masked - logsum)
    weights_low = weights.astype(jnp.bfloat16)
    weights_grad = jnp.einsum(
        "blhe,bmhe->bhlm", upstream, values, preferred_element_type=jnp.float32
    )
    inner = jnp.sum(weights * weights_grad, axis=-1, keepdims=True)
    scores_grad = (weights * (weights_grad - inner)).astype(jnp.bfloat16)
    query_grad = (
        jnp.einsum("bhlm,bmhe->blhe", scores_grad, keys, preferred_element_type=jnp.float32)
        * score_scale
    )
    key_grad = (
        jnp.einsum("bhlm,blhe->bmhe", scores_grad, queries, preferred_element_type=jnp.float32)
        * score_scale
    )
    value_grad = jnp.einsum(
        "bhlm,blhe->bmhe", weights_low, upstream, preferred_element_type=jnp.float32
    )
    return jnp.stack([query_grad, key_grad, value_grad], axis=2).astype(jnp.bfloat16)


MESH = pl.DeviceIdType.MESH
CHUNK = 384


def reduce_kernel(
    nb, units, proj, outw, up, down, mg,
    o_proj, o_out, o_up, o_down, o_mg,
    s0, r1, r2x, r2y, r3, r4, fin, mg_own, mg_r1, mg_r2, mg_all,
    load_sem, s1, q1, s2, q2, s3, q3, s4, q4, s5, q5, s6, q6, out_sem,
    mg_send, mg_recv, mz_send, mz_recv, mg_io,
):
    nz = nb // 2
    chunks = len(units)
    b = lax.axis_index("batch")
    g = lax.axis_index("group")
    cb, xb = lax.rem(g, 2), g // 2
    yb, zb = lax.rem(b, 2), b // 2
    core = (b, g + 1 - 2 * cb)
    side = (b, g + 2 - 4 * xb)
    across = (b + 1 - 2 * yb, g)
    others = [lax.rem(zb + d, nz) for d in range(nz)]
    far = [(2 * z + yb, g) for z in others]
    arrays = {"proj": proj, "out": outw, "up": up, "down": down}
    results = {"proj": o_proj, "out": o_out, "up": o_up, "down": o_down}

    def window(name, part, column, ref, lead):
        if name == "down":
            return ref.at[(*lead, part, slice(None), pl.ds(column, CHUNK))]
        return ref.at[(*lead, slice(None), pl.ds(column, CHUNK))]

    def remote(src, dst, send, recv, target):
        return pltpu.make_async_remote_copy(
            src_ref=src, dst_ref=dst, send_sem=send, recv_sem=recv, device_id=target,
            device_id_type=MESH,
        )

    def load(k, q):
        name, part, column = units[k][q]
        source = window(name, part, column, arrays[name], (slice(None), slice(None)))
        return pltpu.make_async_copy(source, s0.at[k, q % 2, q // 2], load_sem.at[k, q])

    def store(k, q):
        name, part, column = units[k][q]
        target = window(name, part, column, results[name], ())
        return pltpu.make_async_copy(fin.at[k, q % 2, q // 2], target, out_sem.at[k, q])

    def copy_1(k):
        return remote(s0.at[k, 1 - cb], r1.at[k], s1.at[k], q1.at[k], core)

    def copy_2(k):
        if k % 2 == 0:
            return remote(s0.at[k, cb, 1 - xb], r2x.at[k // 2], s2.at[k], q2.at[k], side)
        return remote(
            s0.at[k, cb, :, :, 1 - yb], r2y.at[k // 2], s2.at[k], q2.at[k], across
        )

    def copy_3(k):
        if k % 2 == 0:
            return remote(s0.at[k, cb, xb, :, 1 - yb], r3.at[k], s3.at[k], q3.at[k], across)
        return remote(s0.at[k, cb, 1 - xb, :, yb], r3.at[k], s3.at[k], q3.at[k], side)

    def copy_4(k, d):
        return remote(
            s0.at[k, cb, xb, others[d], yb], r4.at[k, d - 1], s4.at[k, d - 1], q4.at[k, d - 1],
            far[d],
        )

    def copy_5(k, mine):
        place = xb if mine else 1 - xb
        return remote(fin.at[k, cb, place], fin.at[k, cb, place], s5.at[k], q5.at[k], side)

    def copy_6(k, mine):
        place = cb if mine else 1 - cb
        return remote(fin.at[k, place], fin.at[k, place], s6.at[k], q6.at[k], core)

    def add_1(k):
        copy_1(k).wait_recv()

        def step(i, carry):
            x, z, y = i // (2 * nz), lax.rem(i // 2, nz), lax.rem(i, 2)
            s0[k, cb, x, z, y] = s0[k, cb, x, z, y] + r1[k, x, z, y]
            return carry

        lax.fori_loop(0, 4 * nz, step, 0)
        copy_2(k).start()

    def add_2(k):
        copy_2(k).wait_recv()

        def step(i, carry):
            if k % 2 == 0:
                z, y = i // 2, lax.rem(i, 2)
                s0[k, cb, xb, z, y] = s0[k, cb, xb, z, y] + r2x[k // 2, z, y]
            else:
                x, z = i // nz, lax.rem(i, nz)
                s0[k, cb, x, z, yb] = s0[k, cb, x, z, yb] + r2y[k // 2, x, z]
            return carry

        lax.fori_loop(0, 2 * nz, step, 0)
        copy_3(k).start()

    def add_3(k):
        copy_3(k).wait_recv()

        def step(z, carry):
            s0[k, cb, xb, z, yb] = s0[k, cb, xb, z, yb] + r3[k, z]
            return carry

        lax.fori_loop(0, nz, step, 0)
        for d in range(1, nz):
            copy_4(k, d).start()

    def add_4(k):
        total = s0[k, cb, xb, zb, yb].astype(jnp.float32)
        for d in range(1, nz):
            copy_4(k, d).wait_recv()
            total = total + r4[k, d - 1].astype(jnp.float32)
        fin[k, cb, xb] = total.astype(jnp.bfloat16)
        copy_5(k, True).start()

    def pass_5(k):
        copy_5(k, False).wait_recv()
        copy_6(k, True).start()

    def pass_6(k):
        copy_6(k, False).wait_recv()
        for q in range(4):
            store(k, q).start()

    for k in range(chunks):
        for q in range(4):
            load(k, q).start()
    mg_load = pltpu.make_async_copy(mg, mg_own, mg_io)
    mg_load.start()

    barrier = pltpu.get_barrier_semaphore()
    partners = [core, side, across, *far[1:]]
    for partner in partners:
        pl.semaphore_signal(barrier, inc=1, device_id=partner, device_id_type=MESH)
    pl.semaphore_wait(barrier, len(partners))

    mg_load.wait()
    small_1 = remote(mg_own, mg_r1, mg_send.at[0], mg_recv.at[0], core)
    small_1.start()
    for k in range(chunks):
        for q in range(4):
            load(k, q).wait()
        copy_1(k).start()

    small_1.wait()
    mg_own[...] = mg_own[...] + mg_r1[...]
    small_2 = remote(mg_own, mg_r2, mg_send.at[1], mg_recv.at[1], side)
    small_2.start()
    add_1(0)
    small_2.wait()
    mg_all[zb, yb] = mg_own[...] + mg_r2[...]
    small_3 = remote(mg_all.at[zb, yb], mg_all.at[zb, yb], mg_send.at[2], mg_recv.at[2], across)
    small_3.start()
    stages = [add_1, add_2, add_3, add_4, pass_5, pass_6]
    for t in range(1, chunks + len(stages) - 1):
        for index, stage in enumerate(stages):
            if 0 <= t - index < chunks:
                stage(t - index)
        if t == 1:
            small_3.wait_send()
            remote(
                mg_all.at[zb, 1 - yb], mg_all.at[zb, 1 - yb], mg_send.at[2], mg_recv.at[2], across
            ).wait_recv()
            for d in range(1, nz):
                remote(
                    mg_all.at[zb], mg_all.at[zb], mz_send.at[d - 1], mz_recv.at[d - 1], far[d]
                ).start()
    for d in range(1, nz):
        back = lax.rem(zb + nz - d, nz)
        remote(
            mg_all.at[back], mg_all.at[back], mz_send.at[d - 1], mz_recv.at[d - 1], far[d]
        ).wait()
    mg_store = pltpu.make_async_copy(mg_all, o_mg, mg_io)
    mg_store.start()
    mg_store.wait()
    for k in range(chunks):
        copy_1(k).wait_send()
        copy_2(k).wait_send()
        copy_3(k).wait_send()
        for d in range(1, nz):
            copy_4(k, d).wait_send()
        copy_5(k, True).wait_send()
        copy_6(k, True).wait_send()
        for q in range(4):
            store(k, q).wait()


def reduce_all(proj, outw, up, down, mg):
    nb = lax.axis_size("batch")
    nz = nb // 2
    rows = proj.shape[0] // nb
    parts = down.shape[0] // (nb * rows)
    spans = [("proj", 0, proj.shape[1]), ("out", 0, outw.shape[1]), ("up", 0, up.shape[1])]
    spans = spans + [("down", part, down.shape[1]) for part in range(parts)]
    flat = [
        (name, part, column) for name, part, size in spans for column in range(0, size, CHUNK)
    ]
    chunks = len(flat) // 4
    units = [[flat[q * chunks + k] for q in range(4)] for k in range(chunks)]
    bf = jnp.bfloat16
    dma = pltpu.SemaphoreType.DMA
    many = max(nz - 1, 1)
    scratch = [
        pltpu.VMEM((chunks, 2, 2, nz, 2, rows, CHUNK), bf),
        pltpu.VMEM((chunks, 2, nz, 2, rows, CHUNK), bf),
        pltpu.VMEM(((chunks + 1) // 2, nz, 2, rows, CHUNK), bf),
        pltpu.VMEM(((chunks + 1) // 2, 2, nz, rows, CHUNK), bf),
        pltpu.VMEM((chunks, nz, rows, CHUNK), bf),
        pltpu.VMEM((chunks, many, rows, CHUNK), bf),
        pltpu.VMEM((chunks, 2, 2, rows, CHUNK), bf),
        pltpu.VMEM(mg.shape, jnp.float32),
        pltpu.VMEM(mg.shape, jnp.float32),
        pltpu.VMEM(mg.shape, jnp.float32),
        pltpu.VMEM((nz, 2, *mg.shape), jnp.float32),
        dma((chunks, 4)),
        *[dma((chunks,)) for _ in range(6)],
        dma((chunks, many)),
        dma((chunks, many)),
        *[dma((chunks,)) for _ in range(4)],
        dma((chunks, 4)),
        dma((3,)),
        dma((3,)),
        dma((many,)),
        dma((many,)),
        dma,
    ]
    any_space = pl.BlockSpec(memory_space=pl.ANY)
    shape = jax.ShapeDtypeStruct
    results = pl.pallas_call(
        partial(reduce_kernel, nb, units),
        out_shape=(
            shape((rows, proj.shape[1]), bf),
            shape((rows, outw.shape[1]), bf),
            shape((rows, up.shape[1]), bf),
            shape((parts, rows, down.shape[1]), bf),
            shape((nz, 2, *mg.shape), jnp.float32),
        ),
        in_specs=[any_space] * 5,
        out_specs=[any_space] * 5,
        scratch_shapes=scratch,
        compiler_params=pltpu.CompilerParams(
            collective_id=0, has_side_effects=True, vmem_limit_bytes=60 << 20
        ),
        name="reduce_grads",
    )(
        proj.reshape(nz, 2, rows, proj.shape[1]),
        outw.reshape(nz, 2, rows, outw.shape[1]),
        up.reshape(nz, 2, rows, up.shape[1]),
        down.reshape(nz, 2, parts, rows, down.shape[1]),
        mg,
    )
    return results


def body(
    inputs,
    segments,
    class_labels,
    time_steps,
    class_table,
    time_table,
    modulation_weight,
    project_weight,
    output_weight,
    kernel_attention,
    up_weight,
    kernel_feed,
    down_weight,
    cotangent,
):
    count, height, across, width = inputs.shape
    place = lax.axis_index("group")
    head_size = width // HEADS
    score_scale = head_size ** (-0.5)
    half = across // 2
    length = half * half
    blocks = count // 2
    class_hot = (class_labels[:, None] == jnp.arange(class_table.shape[0])[None, :]).astype(
        jnp.bfloat16
    )
    time_hot = (time_steps[:, None] == jnp.arange(time_table.shape[0])[None, :]).astype(
        jnp.bfloat16
    )
    cond = jnp.dot(class_hot, class_table, preferred_element_type=jnp.float32) + jnp.dot(
        time_hot, time_table, preferred_element_type=jnp.float32
    )
    cond_act, silu_back = jax.vjp(jax.nn.silu, cond)
    cond_low = cond_act.astype(jnp.bfloat16)
    modulation = jnp.dot(cond_low, modulation_weight, preferred_element_type=jnp.float32)
    pieces = [
        modulation[:, index * width : (index + 1) * width][:, None, None, :] for index in range(6)
    ]
    shift_one, scale_one, gate_one, shift_two, scale_two, gate_two = pieces
    values_in = inputs.astype(jnp.float32)
    attention_in = modulate(values_in, shift_one, scale_one).astype(jnp.bfloat16)
    padded_in = pad_columns(padded_2(attention_in, (("group", 1),), 1)).astype(jnp.float32)
    mixed = depthwise(padded_in, kernel_attention, height, across).astype(jnp.bfloat16)
    grouped = lax.all_to_all(to_groups(mixed), "group", split_axis=1, concat_axis=1, tiled=True)
    tokens = grouped.reshape(count, length, width)
    projected = jnp.dot(tokens, project_weight, preferred_element_type=jnp.float32).astype(
        jnp.bfloat16
    )
    split = projected.reshape(blocks, 2, length, 3, HEADS, head_size)
    queries = split[:, :, :, 0]
    keys = split[:, :, :, 1]
    values = split[:, :, :, 2]
    label_grid = (
        segments.reshape(count, half, 2, half, 2).transpose(0, 2, 4, 1, 3).reshape(count, 4, length)
    )
    labels = lax.dynamic_index_in_dim(label_grid, place, axis=1, keepdims=False).reshape(
        blocks, 2, length
    )

    def forward_block(items):
        return attend_block(items[0], items[1], items[2], items[3], score_scale)

    attended, logsum = lax.map(forward_block, (queries, keys, values, labels))
    attended_flat = attended.reshape(count, length, width)
    branch = jnp.dot(attended_flat, output_weight, preferred_element_type=jnp.float32).astype(
        jnp.bfloat16
    )
    returned = finish_groups(
        lax.all_to_all(
            branch.reshape(count, 4, height // 2, half, width),
            "group",
            split_axis=1,
            concat_axis=1,
            tiled=True,
        )
    )
    returned_wide = returned.astype(jnp.float32)
    middle = values_in + gate_one * returned_wide
    feed_in = modulate(middle, shift_two, scale_two).astype(jnp.bfloat16)
    hidden = jnp.dot(feed_in, up_weight, preferred_element_type=jnp.float32).astype(jnp.bfloat16)
    padded_hidden = pad_columns(padded_2(hidden, (("group", 1),), 1)).astype(jnp.float32)
    spread = depthwise(padded_hidden, kernel_feed, height, across)
    activated, gelu_back = jax.vjp(partial(jax.nn.gelu, approximate=False), spread)
    activated_low = activated.astype(jnp.bfloat16)
    branch_two = jnp.dot(activated_low, down_weight, preferred_element_type=jnp.float32)
    result = (middle + gate_two * branch_two).astype(jnp.bfloat16)
    upstream = cotangent.astype(jnp.float32)
    gate_two_grad = jnp.sum(upstream * branch_two, axis=(1, 2))
    branch_two_grad = (gate_two * upstream).astype(jnp.bfloat16)
    down_grad = jnp.einsum(
        "crsf,crsd->fd", activated_low, branch_two_grad, preferred_element_type=jnp.float32
    )
    activated_grad = jnp.einsum(
        "crsd,fd->crsf", branch_two_grad, down_weight, preferred_element_type=jnp.float32
    )
    spread_grad = gelu_back(activated_grad)[0].astype(jnp.bfloat16)
    padded_spread = pad_columns(padded_2(spread_grad, (("group", 1),), 1)).astype(jnp.float32)
    feed_kernel_grad = kernel_terms(padded_hidden, spread_grad.astype(jnp.float32), height, across)
    hidden_grad = depthwise_back(padded_spread, kernel_feed, height, across).astype(jnp.bfloat16)
    up_grad = jnp.einsum("crsd,crsf->df", feed_in, hidden_grad, preferred_element_type=jnp.float32)
    feed_in_grad = jnp.einsum(
        "crsf,df->crsd", hidden_grad, up_weight, preferred_element_type=jnp.float32
    )
    second_back = jax.vjp(modulate, middle, shift_two, scale_two)[1]
    middle_term, shift_two_grad, scale_two_grad = second_back(feed_in_grad)
    middle_grad = upstream + middle_term
    gate_one_grad = jnp.sum(middle_grad * returned_wide, axis=(1, 2))
    returned_grad = (gate_one * middle_grad).astype(jnp.bfloat16)
    branch_grad = lax.all_to_all(
        to_groups(returned_grad), "group", split_axis=1, concat_axis=1, tiled=True
    ).reshape(count, length, width)
    output_grad = jnp.einsum(
        "cld,cle->de", attended_flat, branch_grad, preferred_element_type=jnp.float32
    )
    attended_grad = jnp.einsum(
        "cle,de->cld", branch_grad, output_weight, preferred_element_type=jnp.float32
    ).astype(jnp.bfloat16)

    def backward_block(items):
        return attend_back(items[0], items[1], items[2], items[3], items[4], items[5], score_scale)

    projected_grad = lax.map(
        backward_block,
        (
            queries,
            keys,
            values,
            labels,
            logsum,
            attended_grad.reshape(blocks, 2, length, HEADS, head_size),
        ),
    )
    projected_grad = projected_grad.reshape(count, length, 3 * width)
    project_grad = jnp.einsum(
        "cld,cle->de", tokens, projected_grad, preferred_element_type=jnp.float32
    )
    tokens_grad = jnp.einsum(
        "cle,de->cld", projected_grad, project_weight, preferred_element_type=jnp.float32
    ).astype(jnp.bfloat16)
    mixed_grad = finish_groups(
        lax.all_to_all(
            tokens_grad.reshape(count, 4, height // 2, half, width),
            "group",
            split_axis=1,
            concat_axis=1,
            tiled=True,
        )
    )
    padded_mixed = pad_columns(padded_2(mixed_grad, (("group", 1),), 1)).astype(jnp.float32)
    attention_kernel_grad = kernel_terms(padded_in, mixed_grad.astype(jnp.float32), height, across)
    attention_in_grad = depthwise_back(padded_mixed, kernel_attention, height, across)
    first_back = jax.vjp(modulate, values_in, shift_one, scale_one)[1]
    input_term, shift_one_grad, scale_one_grad = first_back(attention_in_grad)
    inputs_gradient = (middle_grad + input_term).astype(jnp.bfloat16)
    modulation_grad = jnp.concatenate(
        [
            shift_one_grad.reshape(count, width),
            scale_one_grad.reshape(count, width),
            gate_one_grad,
            shift_two_grad.reshape(count, width),
            scale_two_grad.reshape(count, width),
            gate_two_grad,
        ],
        axis=1,
    )
    nb = lax.axis_size("batch")
    members = lax.axis_size("group")
    place_b = lax.axis_index("batch")
    named = jnp.stack([class_labels, time_steps], axis=1).astype(jnp.float32)
    row = jnp.concatenate([modulation_grad, jnp.pad(named, ((0, 0), (0, 510)))], axis=1)
    bf = jnp.bfloat16
    project_total, output_total, up_total, down_total, gathered = reduce_all(
        project_grad.astype(bf), output_grad.astype(bf), up_grad.astype(bf), down_grad.astype(bf),
        row.reshape(8, row.size // 8),
    )
    project_total = project_total.astype(jnp.float32)
    output_total = output_total.astype(jnp.float32)
    up_total = up_total.astype(jnp.float32)
    down_total = down_total.reshape(-1, width).astype(jnp.float32)
    gathered = gathered.reshape(nb * count, row.shape[1])
    every_grad = gathered[:, : 6 * width]
    every_name = (gathered[:, 6 * width : 6 * width + 2] / members).astype(jnp.int32)
    own = width // nb
    class_all = (every_name[:, :1] == jnp.arange(class_table.shape[0])[None, :]).astype(bf)
    time_all = (every_name[:, 1:] == jnp.arange(time_table.shape[0])[None, :]).astype(bf)
    class_part = lax.dynamic_slice_in_dim(class_table, place_b * own, own, axis=1)
    time_part = lax.dynamic_slice_in_dim(time_table, place_b * own, own, axis=1)
    cond_all = jnp.dot(class_all, class_part, preferred_element_type=jnp.float32) + jnp.dot(
        time_all, time_part, preferred_element_type=jnp.float32
    )
    act_all, silu_all = jax.vjp(jax.nn.silu, cond_all)
    low_all = act_all.astype(bf)
    modulation_part = lax.dynamic_slice_in_dim(modulation_weight, place_b * own, own, axis=0)
    cond_act_grad = jnp.dot(every_grad, modulation_part.astype(jnp.float32).T, precision=highest)
    cond_grad = silu_all(cond_act_grad)[0]
    modulation_total = jnp.dot(low_all.astype(jnp.float32).T, every_grad, precision=highest)
    class_total = jnp.dot(class_all.astype(jnp.float32).T, cond_grad, precision=highest)
    time_total = jnp.dot(time_all.astype(jnp.float32).T, cond_grad, precision=highest)
    kernel_share = (
        lax.psum(attention_kernel_grad, ("batch", "group")),
        lax.psum(feed_kernel_grad, ("batch", "group")),
    )
    attention_kernel_total = lax.dynamic_slice_in_dim(kernel_share[0], place_b * own, own, axis=1)
    wide = feed_kernel_grad.shape[1] // nb
    feed_kernel_total = lax.dynamic_slice_in_dim(kernel_share[1], place_b * wide, wide, axis=1)
    return (
        result,
        inputs_gradient,
        class_total,
        time_total,
        modulation_total,
        project_total,
        output_total,
        attention_kernel_total,
        up_total,
        feed_kernel_total,
        down_total,
    )


def solution(mesh):
    in_specs = (
        P("batch", "group", None, None),
        P("batch", None),
        P("batch"),
        P("batch"),
        P(),
        P(),
        P(),
        P(),
        P(),
        P(),
        P(),
        P(),
        P(),
        P("batch", "group", None, None),
    )
    out_specs = (
        P("batch", "group", None, None),
        P("batch", "group", None, None),
        P(None, "batch"),
        P(None, "batch"),
        P("batch", None),
        P("batch", None),
        P("batch", None),
        P(None, "batch"),
        P("batch", None),
        P(None, "batch"),
        P("batch", None),
    )
    return jax.shard_map(body, mesh=mesh, in_specs=in_specs, out_specs=out_specs, check_vma=False)
```

```python
from functools import partial

import jax
import jax.numpy as jnp
from jax import lax
from jax.experimental import pallas as pl
from jax.experimental.pallas import tpu as pltpu
from jax.sharding import PartitionSpec as P

HEADS = 12
MESH = pl.DeviceIdType.MESH
LANES = 128
CHUNK = 384
TILE = 512
f32 = jnp.float32
bf16 = jnp.bfloat16
highest = lax.Precision.HIGHEST


def dot_nn(a, b):
    return lax.dot_general(a, b, (((1,), (0,)), ((), ())), preferred_element_type=f32)


def dot_nt(a, b):
    return lax.dot_general(a, b, (((1,), (1,)), ((), ())), preferred_element_type=f32)


def dot_tn(a, b):
    return lax.dot_general(a, b, (((0,), (0,)), ((), ())), preferred_element_type=f32)


def remote(src, dst, send, recv, target):
    return pltpu.make_async_remote_copy(
        src_ref=src, dst_ref=dst, send_sem=send, recv_sem=recv, device_id=target,
        device_id_type=MESH,
    )


def meet(partners):
    barrier = pltpu.get_barrier_semaphore()
    for partner in partners:
        pl.semaphore_signal(barrier, inc=1, device_id=partner, device_id_type=MESH)
    pl.semaphore_wait(barrier, len(partners))


def normalize(values):
    center = values - jnp.mean(values, axis=-1, keepdims=True)
    second = jnp.mean(center * center, axis=-1, keepdims=True)
    scale = lax.rsqrt(second + 1e-06)
    return center * scale, scale


def normalize_back(grad, normal, scale):
    return scale * (
        grad
        - jnp.mean(grad, axis=-1, keepdims=True)
        - normal * jnp.mean(grad * normal, axis=-1, keepdims=True)
    )


def column_shifts(row):
    across = row.shape[0]
    column = lax.broadcasted_iota(jnp.int32, row.shape, 0)
    before = jnp.where(column == 0, 0.0, pltpu.roll(row, 1, 0))
    after = jnp.where(column == across - 1, 0.0, pltpu.roll(row, across - 1, 0))
    return before, after


def fold(values):
    rows, width = values.shape
    return jnp.sum(values.reshape(rows // 8, 8, width), axis=0)


def permutation(inverse):
    n = 512
    to = lax.broadcasted_iota(jnp.int32, (n, n), 1 if inverse else 0)
    source = lax.broadcasted_iota(jnp.int32, (n, n), 0 if inverse else 1)
    wanted = lax.shift_left(lax.shift_right_logical(to & 255, 4), 5) + 2 * (to & 15) + (
        lax.shift_right_logical(to, 8)
    )
    return jnp.where(source == wanted, 1.0, 0.0).astype(bf16)


def mask_bias(row, column):
    return jnp.where(row == column, 0.0, -1e30)


def front_kernel(
    x_in, cot_in, mod, kern, wqkv_in, wo_in, lab_row, lab_col,
    o_x, o_cot, o_ret, o_tok, o_proj, o_att, o_lse,
    xf, wqkv, wo, shifts, mixed, rows_m, perm, bias, tok, proj, att, lse, brm,
    load_sem, x_send, x_recv, c_send, c_recv, ex_send, ex_recv, own_sem, out_sem,
):
    b = lax.axis_index("batch")
    g = lax.axis_index("group")
    c, p = lax.rem(g, 2), g // 2
    core, side, corner = (b, g + 1 - 2 * c), (b, g + 2 - 4 * p), (b, 3 - g)
    inner = jnp.logical_or(g == 1, g == 2)
    width = xf.shape[-1]
    across = xf.shape[1]

    def spread_out(src, dst, send, recv, waiting):
        main = c * 8 + p * 2
        other_main = remote(
            src.at[1 - p], dst.at[pl.ds(main, 8)], send.at[0], recv.at[c], (b, 2 - p)
        )
        edge = 6 * (2 - g)
        edge_to = 16 * (g - 1)
        other_edge = remote(
            src.at[1 - p, pl.ds(edge, 2)], dst.at[pl.ds(edge_to, 2)], send.at[1], recv.at[2], side
        )
        own_main = remote(src.at[p], dst.at[pl.ds(main, 8)], send.at[2], recv.at[c], core)
        own_edge = pltpu.make_async_copy(
            src.at[p, pl.ds(edge, 2)], dst.at[pl.ds(edge_to, 2)], recv.at[2]
        )
        stay_main = pltpu.make_async_copy(src.at[p], dst.at[pl.ds(main, 8)], recv.at[c])
        if waiting:
            other_main.wait_send()

            @pl.when(inner)
            def _():
                other_edge.wait_send()
                own_main.wait_send()

        else:
            other_main.start()

            @pl.when(inner)
            def _():
                other_edge.start()
                own_main.start()
                own_edge.start()

            @pl.when(jnp.logical_not(inner))
            def _():
                stay_main.start()

    def arrived(dst, recv):
        for j in range(2):
            place = dst.at[pl.ds(8 * j + 2 * c, 8)]
            pltpu.make_async_copy(place, place, recv.at[j]).wait()
        place = dst.at[pl.ds(16 * (1 - c), 2)]
        pltpu.make_async_copy(place, place, recv.at[2]).wait()

    loads = [
        pltpu.make_async_copy(wqkv_in, wqkv, load_sem.at[0]),
        pltpu.make_async_copy(wo_in, wo, load_sem.at[1]),
    ]
    for load in loads:
        load.start()
    meet([core, side, corner])
    spread_out(x_in, xf, x_send, x_recv, False)
    perm[0] = permutation(False)
    perm[1] = permutation(True)
    for half in range(2):
        bias[half] = mask_bias(lab_row[half], lab_col[half])
    arrived(xf, x_recv)
    spread_out(cot_in, o_cot, c_send, c_recv, False)
    x_out = pltpu.make_async_copy(xf, o_x, out_sem.at[0])
    x_out.start()

    shift = mod[0:1, :]
    scale = 1.0 + mod[1:2, :]

    def first(i, carry):
        normal, _ = normalize(xf[c + i].astype(f32))
        value = (normal * scale + shift).astype(bf16).astype(f32)
        before, after = column_shifts(value)
        shifts[0, 1 - c + i] = before
        shifts[1, 1 - c + i] = value
        shifts[2, 1 - c + i] = after
        return carry

    lax.fori_loop(0, 17, first, 0)
    for s in range(3):
        shifts[s, 17 * c] = jnp.zeros((across, width), f32)

    def conv(step, parity):
        o = 2 * step + parity
        for lane in range(0, width, LANES):
            cut = slice(lane, lane + LANES)
            total = jnp.zeros((across, LANES), f32)
            for r in range(3):
                for s in range(3):
                    tap = kern[3 * r + s : 3 * r + s + 1, cut].astype(f32)
                    total = total + tap * shifts[s, o + r, :, cut]
            mixed[step, parity, :, cut] = total.astype(bf16)

    def conv_away(step, carry):
        conv(step, 1 - c)
        return carry

    def conv_own(step, carry):
        conv(step, c)
        return carry

    lax.fori_loop(0, 8, conv_away, 0)
    mixed_away = remote(
        mixed.at[:, 1 - c], rows_m.at[pl.ds(8 * c, 8)], ex_send.at[0], ex_recv.at[0], core
    )
    mixed_away.start()
    lax.fori_loop(0, 8, conv_own, 0)
    mixed_own = pltpu.make_async_copy(mixed.at[:, c], rows_m.at[pl.ds(8 * c, 8)], own_sem.at[0])
    mixed_own.start()
    mixed_own.wait()
    mixed_away.wait()
    flat = rows_m[...].reshape(16 * across, width)
    tok[...] = dot_nn(perm[0], flat).astype(bf16)
    tok_out = pltpu.make_async_copy(tok, o_tok, out_sem.at[1])
    tok_out.start()
    loads[0].wait()
    for part in range(3):
        cut = slice(part * width, (part + 1) * width)
        proj[:, cut] = dot_nn(tok[...], wqkv[:, cut]).astype(bf16)
    proj_out = pltpu.make_async_copy(proj, o_proj, out_sem.at[2])
    proj_out.start()

    pairs = width // LANES
    size = tok.shape[0] // 2
    low_lane = lax.broadcasted_iota(jnp.int32, (size, LANES), 1) < LANES // 2
    lane_id = lax.broadcasted_iota(jnp.int32, (size, LANES), 1)
    zero = jnp.zeros((), bf16)

    def attend(index, carry):
        half, pair = index // pairs, lax.rem(index, pairs)
        rows = pl.ds(pl.multiple_of(half * size, size), size)

        def part(n):
            return proj[rows, pl.ds(pl.multiple_of(n * width + pair * LANES, LANES), LANES)]

        q, k, v = part(0) * jnp.asarray(0.125, bf16), part(1), part(2)
        total = jnp.zeros((size, LANES), f32)
        sums = lse[half]
        for h in range(2):
            mine = low_lane if h == 0 else jnp.logical_not(low_lane)
            scores = dot_nt(q, jnp.where(mine, k, zero)) + bias[half]
            top = jnp.max(scores, axis=-1, keepdims=True)
            powers = jnp.exp(scores - top)
            mass = jnp.sum(powers, axis=-1, keepdims=True)
            weights = (powers * (1.0 / mass)).astype(bf16)
            total = total + dot_nn(weights, jnp.where(mine, v, zero))
            sums = jnp.where(lane_id == 2 * pair + h, top + jnp.log(mass), sums)
        lse[half] = sums
        att[rows, pl.ds(pl.multiple_of(pair * LANES, LANES), LANES)] = total.astype(bf16)
        return carry

    lse[...] = jnp.zeros(lse.shape, f32)
    lax.fori_loop(0, 2 * pairs, attend, 0)
    att_out = pltpu.make_async_copy(att, o_att, out_sem.at[3])
    att_out.start()
    lse_out = pltpu.make_async_copy(lse, o_lse, out_sem.at[4])
    lse_out.start()
    loads[1].wait()
    branch = dot_nn(att[...], wo[...]).astype(bf16)
    brm[...] = dot_nn(perm[1], branch).astype(bf16).reshape(16, across, width)
    ret_away = remote(
        brm.at[pl.ds(7 * (1 - c), 9)], o_ret.at[:, c], ex_send.at[1], ex_recv.at[1], core
    )
    ret_away.start()
    ret_own = pltpu.make_async_copy(brm.at[pl.ds(7 * c, 9)], o_ret.at[:, c], own_sem.at[1])
    ret_own.start()
    for out in (x_out, tok_out, proj_out, att_out, lse_out, ret_own):
        out.wait()
    ret_away.wait()
    spread_out(x_in, xf, x_send, x_recv, True)
    spread_out(cot_in, o_cot, c_send, c_recv, True)
    arrived(o_cot, c_recv)


def front(inputs, cotangent, mod, kern, wqkv, wo, lab_row, lab_col):
    across, width = inputs.shape[2], inputs.shape[3]
    tokens = 16 * across
    any_space = pl.BlockSpec(memory_space=pl.ANY)
    vmem = pl.BlockSpec(memory_space=pltpu.VMEM)
    shape = jax.ShapeDtypeStruct
    dma = pltpu.SemaphoreType.DMA
    return pl.pallas_call(
        front_kernel,
        out_shape=(
            shape((18, across, width), bf16),
            shape((18, across, width), bf16),
            shape((9, 2, across, width), bf16),
            shape((tokens, width), bf16),
            shape((tokens, 3 * width), bf16),
            shape((tokens, width), bf16),
            shape((2, tokens // 2, LANES), f32),
        ),
        in_specs=[any_space, any_space, vmem, vmem, any_space, any_space, vmem, vmem],
        out_specs=[any_space] * 7,
        scratch_shapes=[
            pltpu.VMEM((18, across, width), bf16),
            pltpu.VMEM(wqkv.shape, bf16),
            pltpu.VMEM(wo.shape, bf16),
            pltpu.VMEM((3, 18, across, width), f32),
            pltpu.VMEM((8, 2, across, width), bf16),
            pltpu.VMEM((16, across, width), bf16),
            pltpu.VMEM((2, tokens, tokens), bf16),
            pltpu.VMEM((2, tokens // 2, tokens // 2), f32),
            pltpu.VMEM((tokens, width), bf16),
            pltpu.VMEM((tokens, 3 * width), bf16),
            pltpu.VMEM((tokens, width), bf16),
            pltpu.VMEM((2, tokens // 2, LANES), f32),
            pltpu.VMEM((16, across, width), bf16),
            dma((2,)), dma((3,)), dma((3,)), dma((3,)), dma((3,)), dma((2,)), dma((2,)),
            dma((2,)), dma((5,)),
        ],
        compiler_params=pltpu.CompilerParams(
            collective_id=1, has_side_effects=True, vmem_limit_bytes=60 << 20
        ),
        name="front",
    )(inputs, cotangent, mod, kern, wqkv, wo, lab_row, lab_col)


def gelu_parts(x):
    size = jnp.abs(x)
    t = 1.0 / (1.0 + (0.3275911 * 0.7071067811865476) * size)
    bell = jnp.exp(-0.5 * x * x)
    series = t * (
        0.254829592
        + t * (-0.284496736 + t * (1.421413741 + t * (-1.453152027 + t * 1.061405429)))
    )
    tail = 0.5 * series * bell
    mass = jnp.where(x >= 0, 1.0 - tail, tail)
    return x * mass, mass + x * bell * 0.3989422804014327


def feed_kernel(
    x_in, ret_in, cot_in, mod, up, kern, down,
    o_up, o_down, o_kern, o_res, o_mid, o_rg, o_small,
    feed_in, feed_t, btg, out_acc, back_acc, hid, hs, gs, act, slope, hg,
):
    j = pl.program_id(0)
    c = lax.rem(lax.axis_index("group"), 2)
    across = 32
    width = feed_in.shape[1]
    tile = up.shape[1]
    frame_rows = feed_in.shape[0] // across
    own = pl.ds(pl.multiple_of(2 * c * across, 64), 16 * across)

    def middle_of(row):
        place = pl.ds(pl.multiple_of(row * across, across), across)
        returned = ret_in[place, :].astype(f32)
        return x_in[place, :].astype(f32) + mod[2:3, :] * returned, returned

    @pl.when(j == 0)
    def _():
        def prepare(row, carry):
            place = pl.ds(pl.multiple_of(row * across, across), across)
            normal, _ = normalize(middle_of(row)[0])
            feed_in[place, :] = (normal * (1.0 + mod[4:5, :]) + mod[3:4, :]).astype(bf16)
            btg[place, :] = (mod[5:6, :] * cot_in[place, :].astype(f32)).astype(bf16)
            return carry

        lax.fori_loop(0, frame_rows, prepare, 0)
        feed_t[...] = feed_in[own, :].T
        out_acc[...] = jnp.zeros(out_acc.shape, f32)
        back_acc[...] = jnp.zeros(back_acc.shape, f32)
        for s in range(3):
            hs[s, 18 * c] = jnp.zeros((across, tile), f32)
            gs[s, 17 * c] = jnp.zeros((across, tile), f32)

    hid[...] = dot_nn(feed_in[...], up[...]).astype(bf16)

    def lay_hidden(row, carry):
        value = hid[pl.ds(pl.multiple_of(row * across, across), across), :].astype(f32)
        before, after = column_shifts(value)
        hs[0, 1 - c + row] = before
        hs[1, 1 - c + row] = value
        hs[2, 1 - c + row] = after
        return carry

    lax.fori_loop(0, frame_rows, lay_hidden, 0)

    for lane in range(0, tile, LANES):
        cut = slice(lane, lane + LANES)
        taps = [kern[n : n + 1, cut].astype(f32) for n in range(9)]

        def forward(row, carry):
            total = jnp.zeros((across, LANES), f32)
            for r in range(3):
                for s in range(3):
                    total = total + taps[3 * r + s] * hs[s, row + r, :, cut]
            place = pl.ds(pl.multiple_of(row * across, across), across)
            value, steep = gelu_parts(total)
            act[place, cut] = value.astype(bf16)
            slope[place, cut] = steep
            return carry

        lax.fori_loop(0, 17, forward, 0)

    inside = pl.ds(pl.multiple_of(c * across, across), 16 * across)
    around = pl.ds(pl.multiple_of(c * across, across), 17 * across)
    own_act = act[inside, :]
    out_acc[...] += dot_nn(own_act, down[...])
    o_down[...] = dot_tn(own_act, btg[own, :]).astype(bf16)
    slope[...] = slope[...] * dot_nt(btg[around, :], down[...])

    def lay_grad(row, carry):
        value = slope[pl.ds(pl.multiple_of(row * across, across), across), :]
        value = value.astype(bf16).astype(f32)
        before, after = column_shifts(value)
        gs[0, 1 - c + row] = after
        gs[1, 1 - c + row] = value
        gs[2, 1 - c + row] = before
        return carry

    lax.fori_loop(0, 17, lay_grad, 0)

    for lane in range(0, tile, LANES):
        cut = slice(lane, lane + LANES)
        taps = [kern[n : n + 1, cut].astype(f32) for n in range(9)]

        def backward(row, sums):
            total = jnp.zeros((across, LANES), f32)
            value = hs[1, row + c + 1, :, cut]
            later = []
            for r in range(3):
                for s in range(3):
                    grad = gs[s, row + 2 - r, :, cut]
                    total = total + taps[3 * r + s] * grad
                    later.append(sums[3 * r + s] + fold(value * grad))
            hg[pl.ds(pl.multiple_of(row * across, across), across), cut] = total.astype(bf16)
            return tuple(later)

        sums = lax.fori_loop(
            0, 16, backward, tuple(jnp.zeros((8, LANES), f32) for _ in range(9))
        )
        for n in range(9):
            o_kern[n : n + 1, cut] = jnp.sum(sums[n], axis=0, keepdims=True)

    o_kern[9:16, :] = jnp.zeros((7, tile), f32)
    o_up[...] = dot_nn(feed_t[...], hg[...]).astype(bf16)
    back_acc[...] += dot_nt(hg[...], up[...])

    @pl.when(j == pl.num_programs(0) - 1)
    def _():
        def finish(row, sums):
            frame = row + 2 * c
            place = pl.ds(pl.multiple_of(row * across, across), across)
            at = pl.ds(pl.multiple_of(frame * across, across), across)
            middle, returned = middle_of(frame)
            cot = cot_in[at, :].astype(f32)
            branch = out_acc[place, :]
            o_res[place, :] = (middle + mod[5:6, :] * branch).astype(bf16)
            normal, scale = normalize(middle)
            grad = back_acc[place, :]
            mid = cot + normalize_back(grad * (1.0 + mod[4:5, :]), normal, scale)
            o_mid[place, :] = mid
            o_rg[place, :] = (mod[2:3, :] * mid).astype(bf16)
            terms = (mid * returned, grad, grad * normal, cot * branch)
            return tuple(total + fold(term) for total, term in zip(sums, terms))

        sums = lax.fori_loop(
            0, 16, finish, tuple(jnp.zeros((8, width), f32) for _ in range(4))
        )
        o_small[...] = jnp.zeros((8, width), f32)
        for n in range(4):
            o_small[n + 2 : n + 3, :] = jnp.sum(sums[n], axis=0, keepdims=True)


def feed(x_frame, returned, cot_frame, mod, up, kern, down):
    width, units = up.shape
    frame = x_frame.shape[0]
    across = frame // 18
    tokens = 16 * across
    shape = jax.ShapeDtypeStruct
    tile = min(TILE, units)

    def still(*size):
        return pl.BlockSpec(size, lambda j: (0, 0), pipeline_mode=pl.Buffered(1))

    columns = pl.BlockSpec((width, tile), lambda j: (0, j))
    rows = pl.BlockSpec((tile, width), lambda j: (j, 0))
    work = 6 * 2 * tokens * width * units
    return pl.pallas_call(
        feed_kernel,
        grid=(units // tile,),
        out_shape=(
            shape((width, units), bf16),
            shape((units, width), bf16),
            shape((16, units), f32),
            shape((tokens, width), bf16),
            shape((tokens, width), f32),
            shape((tokens, width), bf16),
            shape((8, width), f32),
        ),
        in_specs=[
            still(frame, width), still(frame, width), still(frame, width), still(8, width),
            columns, pl.BlockSpec((9, tile), lambda j: (0, j)), rows,
        ],
        out_specs=[
            columns, rows, pl.BlockSpec((16, tile), lambda j: (0, j)),
            still(tokens, width), still(tokens, width), still(tokens, width), still(8, width),
        ],
        scratch_shapes=[
            pltpu.VMEM((frame, width), bf16),
            pltpu.VMEM((width, tokens), bf16),
            pltpu.VMEM((frame, width), bf16),
            pltpu.VMEM((tokens, width), f32),
            pltpu.VMEM((tokens, width), f32),
            pltpu.VMEM((frame, tile), bf16),
            pltpu.VMEM((3, 19, across, tile), f32),
            pltpu.VMEM((3, 18, across, tile), f32),
            pltpu.VMEM((17 * across, tile), bf16),
            pltpu.VMEM((17 * across, tile), f32),
            pltpu.VMEM((tokens, tile), bf16),
        ],
        compiler_params=pltpu.CompilerParams(
            dimension_semantics=("arbitrary",), vmem_limit_bytes=60 << 20
        ),
        cost_estimate=pl.CostEstimate(
            flops=work, bytes_accessed=8 * width * units, transcendentals=tokens * units
        ),
        name="feed",
    )(x_frame, returned, cot_frame, mod, up, kern, down)


def back_kernel(
    mid_in, rg_in, tok_in, proj_in, att_in, lse, x_in, mod, small, kern, wqkv_in, wo_in,
    lab_row, lab_col, res_in,
    o_wqkv, o_wo, o_res, o_ig, o_kern, o_small,
    mid, tok, proj, att, xf, wqkv, wo, rows_m, perm, bias, grad, datt, dproj, wgrad, wgrad_o,
    brm, frame, gs, value, agrad, ig,
    load_sem, r_send, r_recv, i_send, i_recv, ex_send, ex_recv, own_sem, out_sem,
):
    b = lax.axis_index("batch")
    g = lax.axis_index("group")
    c, p = lax.rem(g, 2), g // 2
    core, side, corner = (b, g + 1 - 2 * c), (b, g + 2 - 4 * p), (b, 3 - g)
    inner = jnp.logical_or(g == 1, g == 2)
    across, width = xf.shape[1], xf.shape[2]
    pairs = width // LANES
    tokens = tok.shape[0]
    size = tokens // 2

    def send_home(src, dst, send, recv, waiting):
        moves = [
            remote(
                src.at[pl.ds(8 * n, 8)], dst.at[p], send.at[n], recv.at[p], (b, 2 * c + n)
            )
            for n in range(2)
        ]
        away = remote(
            src.at[pl.ds(8 * (1 - c), 8)], dst.at[p], send.at[0], recv.at[p], core
        )
        stay = pltpu.make_async_copy(src.at[pl.ds(8 * c, 8)], dst.at[p], recv.at[p])

        @pl.when(inner)
        def _():
            for move in moves:
                if waiting:
                    move.wait_send()
                else:
                    move.start()

        @pl.when(jnp.logical_not(inner))
        def _():
            if waiting:
                away.wait_send()
            else:
                away.start()
                stay.start()

    def home(dst, recv):
        for n in range(2):
            pltpu.make_async_copy(dst.at[n], dst.at[n], recv.at[n]).wait()

    pieces = [
        (wo_in, wo), (att_in, att), (proj_in, proj), (tok_in, tok), (wqkv_in, wqkv), (x_in, xf),
        (mid_in, mid),
    ]
    loads = [
        pltpu.make_async_copy(src, dst, load_sem.at[n]) for n, (src, dst) in enumerate(pieces)
    ]
    for load in loads:
        load.start()
    meet([core, side, corner])
    grad_away = remote(
        rg_in.at[:, 1 - c], rows_m.at[pl.ds(8 * c, 8)], ex_send.at[0], ex_recv.at[0], core
    )
    grad_away.start()
    grad_own = pltpu.make_async_copy(rg_in.at[:, c], rows_m.at[pl.ds(8 * c, 8)], own_sem.at[0])
    grad_own.start()
    send_home(res_in, o_res, r_send, r_recv, False)
    perm[0] = permutation(False)
    perm[1] = permutation(True)
    for half in range(2):
        bias[half] = mask_bias(lab_row[half], lab_col[half])
    grad_own.wait()
    grad_away.wait()
    grad[...] = dot_nn(perm[0], rows_m[...].reshape(tokens, width)).astype(bf16)
    loads[0].wait()
    loads[1].wait()
    datt[...] = dot_nt(grad[...], wo[...]).astype(bf16)
    wgrad_o[...] = dot_tn(att[...], grad[...]).astype(bf16)
    wo_out = pltpu.make_async_copy(wgrad_o, o_wo, out_sem.at[0])
    wo_out.start()
    loads[2].wait()

    low_lane = lax.broadcasted_iota(jnp.int32, (size, LANES), 1) < LANES // 2
    lane_id = lax.broadcasted_iota(jnp.int32, (size, LANES), 1)
    zero = jnp.zeros((), bf16)

    def attend(index, carry):
        half, pair = index // pairs, lax.rem(index, pairs)
        rows = pl.ds(pl.multiple_of(half * size, size), size)

        def cut(n):
            return pl.ds(pl.multiple_of(n * width + pair * LANES, LANES), LANES)

        q = proj[rows, cut(0)] * jnp.asarray(0.125, bf16)
        k, v, up = proj[rows, cut(1)], proj[rows, cut(2)], datt[rows, cut(0)]
        sums = lse[half]
        dq = jnp.zeros((size, LANES), f32)
        dk = jnp.zeros((size, LANES), f32)
        dv = jnp.zeros((size, LANES), f32)
        for h in range(2):
            mine = low_lane if h == 0 else jnp.logical_not(low_lane)
            key = jnp.where(mine, k, zero)
            scores = dot_nt(q, key) + bias[half]
            mass = jnp.sum(
                jnp.where(lane_id == 2 * pair + h, sums, 0.0), axis=-1, keepdims=True
            )
            weights = jnp.exp(scores - mass)
            pull = dot_nt(up, jnp.where(mine, v, zero))
            mean = jnp.sum(weights * pull, axis=-1, keepdims=True)
            spare = (weights * (pull - mean)).astype(bf16)
            dq = dq + dot_nn(spare, key)
            dk = dk + dot_tn(spare, jnp.where(mine, q, zero))
            dv = dv + dot_tn(weights.astype(bf16), jnp.where(mine, up, zero))
        dproj[rows, cut(0)] = (dq * 0.125).astype(bf16)
        dproj[rows, cut(1)] = dk.astype(bf16)
        dproj[rows, cut(2)] = dv.astype(bf16)
        return carry

    lax.fori_loop(0, 2 * pairs, attend, 0)
    loads[4].wait()
    back = dot_nt(dproj[...], wqkv[...]).astype(bf16)
    brm[...] = dot_nn(perm[1], back).astype(bf16).reshape(16, across, width)
    mixed_away = remote(
        brm.at[pl.ds(7 * (1 - c), 9)], frame.at[:, c], ex_send.at[1], ex_recv.at[1], core
    )
    mixed_away.start()
    mixed_own = pltpu.make_async_copy(brm.at[pl.ds(7 * c, 9)], frame.at[:, c], own_sem.at[1])
    mixed_own.start()
    loads[3].wait()
    for part in range(3):
        span = slice(part * width, (part + 1) * width)
        wgrad[:, span] = dot_tn(tok[...], dproj[:, span]).astype(bf16)
    wqkv_out = pltpu.make_async_copy(wgrad, o_wqkv, out_sem.at[1])
    wqkv_out.start()
    loads[5].wait()
    loads[6].wait()

    shift = mod[0:1, :]
    scale_in = 1.0 + mod[1:2, :]

    def again(row, carry):
        normal, _ = normalize(xf[2 * c + row].astype(f32))
        value[row] = (normal * scale_in + shift).astype(bf16).astype(f32)
        return carry

    lax.fori_loop(0, 16, again, 0)
    mixed_own.wait()
    mixed_away.wait()

    def lay(row, carry):
        at = c + row
        line = frame[at // 2, lax.rem(at, 2)].astype(f32)
        before, after = column_shifts(line)
        gs[0, 1 - c + row] = after
        gs[1, 1 - c + row] = line
        gs[2, 1 - c + row] = before
        return carry

    lax.fori_loop(0, 17, lay, 0)
    for s in range(3):
        gs[s, 17 * c] = jnp.zeros((across, width), f32)

    for lane in range(0, width, LANES):
        span = slice(lane, lane + LANES)
        taps = [kern[n : n + 1, span].astype(f32) for n in range(9)]

        def backward(row, sums):
            total = jnp.zeros((across, LANES), f32)
            own = value[row, :, span]
            later = []
            for r in range(3):
                for s in range(3):
                    line = gs[s, row + 2 - r, :, span]
                    total = total + taps[3 * r + s] * line
                    later.append(sums[3 * r + s] + fold(own * line))
            agrad[row, :, span] = total
            return tuple(later)

        sums = lax.fori_loop(
            0, 16, backward, tuple(jnp.zeros((8, LANES), f32) for _ in range(9))
        )
        for n in range(9):
            o_kern[n : n + 1, span] = jnp.sum(sums[n], axis=0, keepdims=True)
    o_kern[9:16, :] = jnp.zeros((7, width), f32)

    def finish(row, sums):
        normal, scale = normalize(xf[2 * c + row].astype(f32))
        line = agrad[row]
        place = pl.ds(pl.multiple_of(row * across, across), across)
        total = mid[place, :] + normalize_back(line * scale_in, normal, scale)
        ig[row] = total.astype(bf16)
        return (sums[0] + fold(line), sums[1] + fold(line * normal))

    sums = lax.fori_loop(0, 16, finish, tuple(jnp.zeros((8, width), f32) for _ in range(2)))
    send_home(ig, o_ig, i_send, i_recv, False)
    o_small[...] = small[...]
    for n in range(2):
        o_small[n : n + 1, :] = jnp.sum(sums[n], axis=0, keepdims=True)
    o_small[6:7, :] = mod[6:7, :]
    wo_out.wait()
    wqkv_out.wait()
    send_home(res_in, o_res, r_send, r_recv, True)
    send_home(ig, o_ig, i_send, i_recv, True)
    home(o_res, r_recv)
    home(o_ig, i_recv)


def back(mid, rg, tok, proj, att, lse, x_frame, mod, small, kern, wqkv, wo, lab_row, lab_col, res):
    across, width = x_frame.shape[1], x_frame.shape[2]
    tokens = 16 * across
    any_space = pl.BlockSpec(memory_space=pl.ANY)
    vmem = pl.BlockSpec(memory_space=pltpu.VMEM)
    shape = jax.ShapeDtypeStruct
    dma = pltpu.SemaphoreType.DMA
    return pl.pallas_call(
        back_kernel,
        out_shape=(
            shape((width, 3 * width), bf16),
            shape((width, width), bf16),
            shape((2, 8, across, width), bf16),
            shape((2, 8, across, width), bf16),
            shape((16, width), f32),
            shape((8, width), f32),
        ),
        in_specs=[any_space] * 5 + [vmem, any_space, vmem, vmem, vmem, any_space, any_space,
                                    vmem, vmem, any_space],
        out_specs=[any_space] * 4 + [vmem, vmem],
        scratch_shapes=[
            pltpu.VMEM((tokens, width), f32),
            pltpu.VMEM((tokens, width), bf16),
            pltpu.VMEM((tokens, 3 * width), bf16),
            pltpu.VMEM((tokens, width), bf16),
            pltpu.VMEM((18, across, width), bf16),
            pltpu.VMEM(wqkv.shape, bf16),
            pltpu.VMEM(wo.shape, bf16),
            pltpu.VMEM((16, across, width), bf16),
            pltpu.VMEM((2, tokens, tokens), bf16),
            pltpu.VMEM((2, tokens // 2, tokens // 2), f32),
            pltpu.VMEM((tokens, width), bf16),
            pltpu.VMEM((tokens, width), bf16),
            pltpu.VMEM((tokens, 3 * width), bf16),
            pltpu.VMEM((width, 3 * width), bf16),
            pltpu.VMEM((width, width), bf16),
            pltpu.VMEM((16, across, width), bf16),
            pltpu.VMEM((9, 2, across, width), bf16),
            pltpu.VMEM((3, 18, across, width), f32),
            pltpu.VMEM((16, across, width), f32),
            pltpu.VMEM((16, across, width), f32),
            pltpu.VMEM((16, across, width), bf16),
            dma((7,)), dma((2,)), dma((2,)), dma((2,)), dma((2,)), dma((2,)), dma((2,)),
            dma((2,)), dma((2,)),
        ],
        compiler_params=pltpu.CompilerParams(
            collective_id=2, has_side_effects=True, vmem_limit_bytes=62 << 20
        ),
        name="back",
    )(mid, rg, tok, proj, att, lse, x_frame, mod, small, kern, wqkv, wo, lab_row, lab_col, res)


def reduce_kernel(
    nb, units, proj, outw, up, down, mg, kern_one, kern_two,
    o_proj, o_out, o_up, o_down, o_mg, o_one, o_two,
    s0, r1, r2x, r2y, r3, r4, fin, mg_r1, mg_all, kk, kr, kz,
    load_sem, s1, q1, s2, q2, s3, q3, s4, q4, s5, q5, s6, q6, out_sem,
    mg_send, mg_recv, mz_send, mz_recv, mg_io, k_send, k_recv, kz_send, kz_recv,
):
    nz = nb // 2
    chunks = len(units)
    b = lax.axis_index("batch")
    g = lax.axis_index("group")
    cb, xb = lax.rem(g, 2), g // 2
    yb, zb = lax.rem(b, 2), b // 2
    core = (b, g + 1 - 2 * cb)
    side = (b, g + 2 - 4 * xb)
    across = (b + 1 - 2 * yb, g)
    others = [lax.rem(zb + d, nz) for d in range(nz)]
    far = [(2 * z + yb, g) for z in others]
    arrays = {"proj": proj, "out": outw, "up": up, "down": down}
    results = {"proj": o_proj, "out": o_out, "up": o_up, "down": o_down}

    def window(name, part, column, ref, lead):
        if name == "down":
            return ref.at[(*lead, part, slice(None), pl.ds(column, CHUNK))]
        return ref.at[(*lead, slice(None), pl.ds(column, CHUNK))]

    def load(k, q):
        name, part, column = units[k][q]
        source = window(name, part, column, arrays[name], (slice(None), slice(None)))
        return pltpu.make_async_copy(source, s0.at[k, q % 2, q // 2], load_sem.at[k, q])

    def store(k, q):
        name, part, column = units[k][q]
        target = window(name, part, column, results[name], ())
        return pltpu.make_async_copy(fin.at[k, q % 2, q // 2], target, out_sem.at[k, q])

    def copy_1(k):
        return remote(s0.at[k, 1 - cb], r1.at[k], s1.at[k], q1.at[k], core)

    def copy_2(k):
        if k % 2 == 0:
            return remote(s0.at[k, cb, 1 - xb], r2x.at[k // 2], s2.at[k], q2.at[k], side)
        return remote(
            s0.at[k, cb, :, :, 1 - yb], r2y.at[k // 2], s2.at[k], q2.at[k], across
        )

    def copy_3(k):
        if k % 2 == 0:
            return remote(s0.at[k, cb, xb, :, 1 - yb], r3.at[k], s3.at[k], q3.at[k], across)
        return remote(s0.at[k, cb, 1 - xb, :, yb], r3.at[k], s3.at[k], q3.at[k], side)

    def copy_4(k, d):
        return remote(
            s0.at[k, cb, xb, others[d], yb], r4.at[k, d - 1], s4.at[k, d - 1], q4.at[k, d - 1],
            far[d],
        )

    def copy_5(k, mine):
        place = xb if mine else 1 - xb
        return remote(fin.at[k, cb, place], fin.at[k, cb, place], s5.at[k], q5.at[k], side)

    def copy_6(k, mine):
        place = cb if mine else 1 - cb
        return remote(fin.at[k, place], fin.at[k, place], s6.at[k], q6.at[k], core)

    def add_1(k):
        copy_1(k).wait_recv()

        def step(i, carry):
            x, z, y = i // (2 * nz), lax.rem(i // 2, nz), lax.rem(i, 2)
            s0[k, cb, x, z, y] = s0[k, cb, x, z, y] + r1[k, x, z, y]
            return carry

        lax.fori_loop(0, 4 * nz, step, 0)
        copy_2(k).start()

    def add_2(k):
        copy_2(k).wait_recv()

        def step(i, carry):
            if k % 2 == 0:
                z, y = i // 2, lax.rem(i, 2)
                s0[k, cb, xb, z, y] = s0[k, cb, xb, z, y] + r2x[k // 2, z, y]
            else:
                x, z = i // nz, lax.rem(i, nz)
                s0[k, cb, x, z, yb] = s0[k, cb, x, z, yb] + r2y[k // 2, x, z]
            return carry

        lax.fori_loop(0, 2 * nz, step, 0)
        copy_3(k).start()

    def add_3(k):
        copy_3(k).wait_recv()

        def step(z, carry):
            s0[k, cb, xb, z, yb] = s0[k, cb, xb, z, yb] + r3[k, z]
            return carry

        lax.fori_loop(0, nz, step, 0)
        for d in range(1, nz):
            copy_4(k, d).start()

    def add_4(k):
        total = s0[k, cb, xb, zb, yb].astype(f32)
        for d in range(1, nz):
            copy_4(k, d).wait_recv()
            total = total + r4[k, d - 1].astype(f32)
        fin[k, cb, xb] = total.astype(bf16)
        copy_5(k, True).start()

    def pass_5(k):
        copy_5(k, False).wait_recv()
        copy_6(k, True).start()

    def pass_6(k):
        copy_6(k, False).wait_recv()
        for q in range(4):
            store(k, q).start()

    for k in range(chunks):
        for q in range(4):
            load(k, q).start()

    meet([core, side, across, *far[1:]])
    split = kern_one.shape[1]
    kk[0, :, :split] = kern_one[...].astype(bf16)
    kk[0, :, split:] = kern_two[...].astype(bf16)
    here = (zb, yb, xb)
    peers = [core, side, across]

    def small_copy(stage):
        if stage == 0:
            return remote(mg, mg_r1, mg_send.at[0], mg_recv.at[0], core)
        place = mg_all.at[here] if stage == 1 else mg_all.at[zb, yb]
        return remote(place, place, mg_send.at[stage], mg_recv.at[stage], peers[stage])

    def small_come(stage):
        place = mg_all.at[zb, yb, 1 - xb] if stage == 1 else mg_all.at[zb, 1 - yb]
        remote(place, place, mg_send.at[stage], mg_recv.at[stage], peers[stage]).wait_recv()

    def small_far(d, z):
        return remote(mg_all.at[z], mg_all.at[z], mz_send.at[d - 1], mz_recv.at[d - 1], far[d])

    def kern_copy(stage):
        return remote(kk.at[stage], kr.at[stage], k_send.at[stage], k_recv.at[stage], peers[stage])

    def kern_far(d):
        return remote(kk.at[3], kz.at[d - 1], kz_send.at[d - 1], kz_recv.at[d - 1], far[d])

    def kern_add(stage):
        kern_copy(stage).wait_recv()
        kk[stage + 1] = (kk[stage].astype(f32) + kr[stage].astype(f32)).astype(bf16)

    def small_steps(t):
        if t == 1:
            small_copy(0).wait_recv()
            mg_all[here] = mg[...] + mg_r1[...]
            small_copy(1).start()
            kern_add(0)
            kern_copy(1).start()
        if t == 2:
            small_come(1)
            small_copy(2).start()
            kern_add(1)
            kern_copy(2).start()
        if t == 3:
            small_come(2)
            for d in range(1, nz):
                small_far(d, zb).start()
            kern_add(2)
            for d in range(1, nz):
                kern_far(d).start()

    small_copy(0).start()
    kern_copy(0).start()
    for k in range(chunks):
        for q in range(4):
            load(k, q).wait()
        copy_1(k).start()
    stages = [add_1, add_2, add_3, add_4, pass_5, pass_6]
    for t in range(chunks + len(stages) - 1):
        for index, stage in enumerate(stages):
            if 0 <= t - index < chunks:
                stage(t - index)
        small_steps(t)
    for d in range(1, nz):
        small_far(d, lax.rem(zb + nz - d, nz)).wait_recv()
        small_far(d, zb).wait_send()
    mg_store = pltpu.make_async_copy(mg_all, o_mg, mg_io)
    mg_store.start()
    total = kk[3].astype(f32)
    for d in range(1, nz):
        kern_far(d).wait()
        total = total + kz[d - 1].astype(f32)
    o_one[...] = total[:, :split]
    o_two[...] = total[:, split:]
    for stage in range(3):
        small_copy(stage).wait_send()
        kern_copy(stage).wait_send()
    mg_store.wait()
    for k in range(chunks):
        copy_1(k).wait_send()
        copy_2(k).wait_send()
        copy_3(k).wait_send()
        for d in range(1, nz):
            copy_4(k, d).wait_send()
        copy_5(k, True).wait_send()
        copy_6(k, True).wait_send()
        for q in range(4):
            store(k, q).wait()


def reduce_all(proj, outw, up, down, mg, kern_one, kern_two):
    nb = lax.axis_size("batch")
    nz = nb // 2
    rows = proj.shape[0] // nb
    parts = down.shape[0] // (nb * rows)
    spans = [("proj", 0, proj.shape[1]), ("out", 0, outw.shape[1]), ("up", 0, up.shape[1])]
    spans = spans + [("down", part, down.shape[1]) for part in range(parts)]
    flat = [
        (name, part, column) for name, part, size in spans for column in range(0, size, CHUNK)
    ]
    chunks = len(flat) // 4
    units = [[flat[q * chunks + k] for q in range(4)] for k in range(chunks)]
    bf = bf16
    extra = kern_one.shape[1] + kern_two.shape[1]
    dma = pltpu.SemaphoreType.DMA
    many = max(nz - 1, 1)
    scratch = [
        pltpu.VMEM((chunks, 2, 2, nz, 2, rows, CHUNK), bf),
        pltpu.VMEM((chunks, 2, nz, 2, rows, CHUNK), bf),
        pltpu.VMEM(((chunks + 1) // 2, nz, 2, rows, CHUNK), bf),
        pltpu.VMEM(((chunks + 1) // 2, 2, nz, rows, CHUNK), bf),
        pltpu.VMEM((chunks, nz, rows, CHUNK), bf),
        pltpu.VMEM((chunks, many, rows, CHUNK), bf),
        pltpu.VMEM((chunks, 2, 2, rows, CHUNK), bf),
        pltpu.VMEM(mg.shape, f32),
        pltpu.VMEM((nz, 2, 2, *mg.shape), f32),
        pltpu.VMEM((4, 16, extra), bf),
        pltpu.VMEM((3, 16, extra), bf),
        pltpu.VMEM((many, 16, extra), bf),
        dma((chunks, 4)),
        *[dma((chunks,)) for _ in range(6)],
        dma((chunks, many)),
        dma((chunks, many)),
        *[dma((chunks,)) for _ in range(4)],
        dma((chunks, 4)),
        dma((3,)),
        dma((3,)),
        dma((many,)),
        dma((many,)),
        dma,
        dma((3,)),
        dma((3,)),
        dma((many,)),
        dma((many,)),
    ]
    any_space = pl.BlockSpec(memory_space=pl.ANY)
    vmem = pl.BlockSpec(memory_space=pltpu.VMEM)
    shape = jax.ShapeDtypeStruct
    results = pl.pallas_call(
        partial(reduce_kernel, nb, units),
        out_shape=(
            shape((rows, proj.shape[1]), bf),
            shape((rows, outw.shape[1]), bf),
            shape((rows, up.shape[1]), bf),
            shape((parts, rows, down.shape[1]), bf),
            shape((nz, 2, 2, *mg.shape), f32),
            shape(kern_one.shape, f32),
            shape(kern_two.shape, f32),
        ),
        in_specs=[any_space] * 4 + [vmem] * 3,
        out_specs=[any_space] * 5 + [vmem] * 2,
        scratch_shapes=scratch,
        compiler_params=pltpu.CompilerParams(
            collective_id=0, has_side_effects=True, vmem_limit_bytes=60 << 20
        ),
        name="reduce_grads",
    )(
        proj.reshape(nz, 2, rows, proj.shape[1]),
        outw.reshape(nz, 2, rows, outw.shape[1]),
        up.reshape(nz, 2, rows, up.shape[1]),
        down.reshape(nz, 2, parts, rows, down.shape[1]),
        mg, kern_one, kern_two,
    )
    return results


def body(
    inputs,
    segments,
    class_labels,
    time_steps,
    class_table,
    time_table,
    modulation_weight,
    project_weight,
    output_weight,
    kernel_attention,
    up_weight,
    kernel_feed,
    down_weight,
    cotangent,
):
    count, height, across, width = inputs.shape
    nb = lax.axis_size("batch")
    place_b = lax.axis_index("batch")
    group = lax.axis_index("group")
    canvas, core = group // 2, lax.rem(group, 2)
    half = across // 2

    label = lax.dynamic_index_in_dim(class_labels, canvas, 0, keepdims=False)
    moment = lax.dynamic_index_in_dim(time_steps, canvas, 0, keepdims=False)
    cond = lax.dynamic_slice_in_dim(class_table, label, 1, axis=0).astype(
        f32
    ) + lax.dynamic_slice_in_dim(time_table, moment, 1, axis=0).astype(f32)
    cond_low = jax.nn.silu(cond).astype(bf16)
    modulation = jnp.dot(cond_low, modulation_weight, preferred_element_type=f32)
    named = jnp.stack([label, moment]).astype(f32)
    mod = jnp.concatenate(
        [modulation.reshape(6, width), jnp.pad(named, (0, width - 2))[None], jnp.zeros((1, width), f32)]
    )
    grid = lax.dynamic_index_in_dim(segments, canvas, 0, keepdims=False)
    grid = grid.reshape(half, 2, half, 2).transpose(1, 3, 0, 2).reshape(2, 2, half * half)
    labels = lax.dynamic_index_in_dim(grid, core, 0, keepdims=False)
    lab_row, lab_col = labels[:, None, :], labels[:, :, None]

    x_frame, cot_frame, returned, tok, proj, att, lse = front(
        inputs, cotangent, mod, kernel_attention, project_weight, output_weight, lab_row, lab_col
    )
    flat = (18 * across, width)
    up_grad, down_grad, feed_kernel_grad, res, mid, rg, small = feed(
        x_frame.reshape(flat), returned.reshape(flat), cot_frame.reshape(flat), mod, up_weight,
        kernel_feed, down_weight,
    )
    project_grad, output_grad, result, inputs_gradient, attention_kernel_grad, small = back(
        mid, rg.reshape(8, 2, across, width), tok, proj, att, lse, x_frame, mod, small,
        kernel_attention, project_weight, output_weight, lab_row, lab_col,
        res.reshape(16, across, width),
    )
    (
        project_total, output_total, up_total, down_total, gathered, kernel_one, kernel_two
    ) = reduce_all(
        project_grad, output_grad, up_grad, down_grad, small, attention_kernel_grad,
        feed_kernel_grad,
    )
    project_total = project_total.astype(f32)
    output_total = output_total.astype(f32)
    up_total = up_total.astype(f32)
    down_total = down_total.reshape(-1, width).astype(f32)
    gathered = gathered.reshape(nb * count, 8, width)
    every_grad = gathered[:, :6].reshape(nb * count, 6 * width)
    every_name = (gathered[:, 6, :2] * 0.5).astype(jnp.int32)
    own = width // nb
    class_all = (every_name[:, :1] == jnp.arange(class_table.shape[0])[None, :]).astype(bf16)
    time_all = (every_name[:, 1:] == jnp.arange(time_table.shape[0])[None, :]).astype(bf16)
    class_part = lax.dynamic_slice_in_dim(class_table, place_b * own, own, axis=1)
    time_part = lax.dynamic_slice_in_dim(time_table, place_b * own, own, axis=1)
    cond_all = jnp.dot(class_all, class_part, preferred_element_type=f32) + jnp.dot(
        time_all, time_part, preferred_element_type=f32
    )
    act_all, silu_all = jax.vjp(jax.nn.silu, cond_all)
    low_all = act_all.astype(bf16)
    modulation_part = lax.dynamic_slice_in_dim(modulation_weight, place_b * own, own, axis=0)
    cond_act_grad = jnp.dot(every_grad, modulation_part.astype(f32).T, precision=highest)
    cond_grad = silu_all(cond_act_grad)[0]
    modulation_total = jnp.dot(low_all.astype(f32).T, every_grad, precision=highest)
    class_total = jnp.dot(class_all.astype(f32).T, cond_grad, precision=highest)
    time_total = jnp.dot(time_all.astype(f32).T, cond_grad, precision=highest)
    wide = feed_kernel_grad.shape[1] // nb
    attention_kernel_total = lax.dynamic_slice(kernel_one, (0, place_b * own), (9, own)).astype(f32)
    feed_kernel_total = lax.dynamic_slice(kernel_two, (0, place_b * wide), (9, wide)).astype(f32)
    return (
        result,
        inputs_gradient,
        class_total,
        time_total,
        modulation_total,
        project_total,
        output_total,
        attention_kernel_total,
        up_total,
        feed_kernel_total,
        down_total,
    )


def solution(mesh):
    in_specs = (
        P("batch", "group", None, None),
        P("batch", None),
        P("batch"),
        P("batch"),
        P(),
        P(),
        P(),
        P(),
        P(),
        P(),
        P(),
        P(),
        P(),
        P("batch", "group", None, None),
    )
    out_specs = (
        P("batch", "group", None, None),
        P("batch", "group", None, None),
        P(None, "batch"),
        P(None, "batch"),
        P("batch", None),
        P("batch", None),
        P("batch", None),
        P(None, "batch"),
        P("batch", None),
        P(None, "batch"),
        P("batch", None),
    )
    return jax.shard_map(body, mesh=mesh, in_specs=in_specs, out_specs=out_specs, check_vma=False)
```

```python
from functools import partial

import jax
import jax.numpy as jnp
from jax import lax
from jax.experimental import pallas as pl
from jax.experimental.pallas import tpu as pltpu
from jax.sharding import PartitionSpec as P

HEADS = 12
MESH = pl.DeviceIdType.MESH
LANES = 128
f32 = jnp.float32
bf16 = jnp.bfloat16
highest = lax.Precision.HIGHEST


def dot_nn(a, b):
    return lax.dot_general(a, b, (((1,), (0,)), ((), ())), preferred_element_type=f32)


def dot_nt(a, b):
    return lax.dot_general(a, b, (((1,), (1,)), ((), ())), preferred_element_type=f32)


def dot_tn(a, b):
    return lax.dot_general(a, b, (((0,), (0,)), ((), ())), preferred_element_type=f32)


def remote(src, dst, send, recv, target):
    return pltpu.make_async_remote_copy(
        src_ref=src, dst_ref=dst, send_sem=send, recv_sem=recv, device_id=target,
        device_id_type=MESH,
    )


def meet(partners):
    barrier = pltpu.get_barrier_semaphore()
    for partner in partners:
        pl.semaphore_signal(barrier, inc=1, device_id=partner, device_id_type=MESH)
    pl.semaphore_wait(barrier, len(partners))


def normalize(values):
    center = values - jnp.mean(values, axis=-1, keepdims=True)
    second = jnp.mean(center * center, axis=-1, keepdims=True)
    scale = lax.rsqrt(second + 1e-06)
    return center * scale, scale


def normalize_back(grad, normal, scale):
    return scale * (
        grad
        - jnp.mean(grad, axis=-1, keepdims=True)
        - normal * jnp.mean(grad * normal, axis=-1, keepdims=True)
    )


def column_shifts(row):
    across = row.shape[0]
    column = lax.broadcasted_iota(jnp.int32, row.shape, 0)
    before = jnp.where(column == 0, 0.0, pltpu.roll(row, 1, 0))
    after = jnp.where(column == across - 1, 0.0, pltpu.roll(row, across - 1, 0))
    return before, after


def fold(values):
    rows, width = values.shape
    return jnp.sum(values.reshape(rows // 8, 8, width), axis=0)


def permutation(inverse):
    n = 512
    to = lax.broadcasted_iota(jnp.int32, (n, n), 1 if inverse else 0)
    source = lax.broadcasted_iota(jnp.int32, (n, n), 0 if inverse else 1)
    wanted = lax.shift_left(lax.shift_right_logical(to & 255, 4), 5) + 2 * (to & 15) + (
        lax.shift_right_logical(to, 8)
    )
    return jnp.where(source == wanted, 1.0, 0.0).astype(bf16)


def front_kernel(
    x_in, cot_in, names, moments, segments, kern, class_in, time_in, wmod_in, wqkv_in, wo_in,
    o_x, o_cot, o_ret, o_tok, o_proj, o_att, o_lse, o_bias, mod,
    xf, table, wmod, wqkv, wo, shifts, mixed, rows_m, perm, bias, tok, proj, att, lse, brm,
    load_sem, x_send, x_recv, c_send, c_recv, ex_send, ex_recv, own_sem, out_sem,
):
    b = lax.axis_index("batch")
    g = lax.axis_index("group")
    c, p = lax.rem(g, 2), g // 2
    core, side, corner = (b, g + 1 - 2 * c), (b, g + 2 - 4 * p), (b, 3 - g)
    inner = jnp.logical_or(g == 1, g == 2)
    width = xf.shape[-1]
    across = xf.shape[1]

    def spread_out(src, dst, send, recv, waiting):
        main = c * 8 + p * 2
        other_main = remote(
            src.at[1 - p], dst.at[pl.ds(main, 8)], send.at[0], recv.at[c], (b, 2 - p)
        )
        edge = 6 * (2 - g)
        edge_to = 16 * (g - 1)
        other_edge = remote(
            src.at[1 - p, pl.ds(edge, 2)], dst.at[pl.ds(edge_to, 2)], send.at[1], recv.at[2], side
        )
        own_main = remote(src.at[p], dst.at[pl.ds(main, 8)], send.at[2], recv.at[c], core)
        own_edge = pltpu.make_async_copy(
            src.at[p, pl.ds(edge, 2)], dst.at[pl.ds(edge_to, 2)], recv.at[2]
        )
        stay_main = pltpu.make_async_copy(src.at[p], dst.at[pl.ds(main, 8)], recv.at[c])
        if waiting:
            other_main.wait_send()

            @pl.when(inner)
            def _():
                other_edge.wait_send()
                own_main.wait_send()

        else:
            other_main.start()

            @pl.when(inner)
            def _():
                other_edge.start()
                own_main.start()
                own_edge.start()

            @pl.when(jnp.logical_not(inner))
            def _():
                stay_main.start()

    def arrived(dst, recv):
        for j in range(2):
            place = dst.at[pl.ds(8 * j + 2 * c, 8)]
            pltpu.make_async_copy(place, place, recv.at[j]).wait()
        place = dst.at[pl.ds(16 * (1 - c), 2)]
        pltpu.make_async_copy(place, place, recv.at[2]).wait()

    pieces = [
        (wqkv_in, wqkv), (wo_in, wo), (class_in, table.at[0]), (time_in, table.at[1]),
        (wmod_in, wmod),
    ]
    loads = [
        pltpu.make_async_copy(src, dst, load_sem.at[n]) for n, (src, dst) in enumerate(pieces)
    ]
    for n in (2, 3, 4, 0, 1):
        loads[n].start()
    meet([core, side, corner])
    spread_out(x_in, xf, x_send, x_recv, False)
    perm[0] = permutation(False)
    perm[1] = permutation(True)
    n = tok.shape[0]
    wide = segments.shape[1]
    to = lax.broadcasted_iota(jnp.int32, (n, wide), 0)
    source = lax.broadcasted_iota(jnp.int32, (n, wide), 1)
    wanted = lax.shift_left(2 * lax.shift_right_logical(to & 255, 4) + c, 5) + 2 * (to & 15) + (
        lax.shift_right_logical(to, 8)
    )
    chosen = source == wanted
    one_line = jnp.where(p == 0, segments[0:1, :], segments[1:2, :]).astype(f32)
    lines = jnp.broadcast_to(one_line, (8, wide)).astype(bf16)
    lab_row = dot_nt(lines, jnp.where(chosen, 1.0, 0.0).astype(bf16))
    lab_col = jnp.sum(jnp.where(chosen, one_line, 0.0), axis=-1, keepdims=True)
    for half in range(2):
        cut = slice(half * (n // 2), (half + 1) * (n // 2))
        bias[half] = jnp.where(lab_row[0:1, cut] == lab_col[cut], 0.0, -1e30)
    bias_out = pltpu.make_async_copy(bias, o_bias, out_sem.at[5])
    bias_out.start()
    name = jnp.where(p == 0, names[0], names[1])
    moment = jnp.where(p == 0, moments[0], moments[1])
    loads[2].wait()
    loads[3].wait()
    rows_all = lax.broadcasted_iota(jnp.int32, (8, table.shape[1]), 1)
    cond = dot_nn(jnp.where(rows_all == name, 1.0, 0.0).astype(bf16), table[0]) + dot_nn(
        jnp.where(rows_all == moment, 1.0, 0.0).astype(bf16), table[1]
    )
    cond_low = (cond / (1.0 + jnp.exp(-cond))).astype(bf16)
    loads[4].wait()
    for part in range(6):
        cut = slice(part * width, (part + 1) * width)
        mod[part : part + 1, :] = dot_nn(cond_low, wmod[:, cut])[0:1, :]
    lane_of = lax.broadcasted_iota(jnp.int32, (1, width), 1)
    mod[6:7, :] = jnp.where(
        lane_of == 0, name.astype(f32), jnp.where(lane_of == 1, moment.astype(f32), 0.0)
    )
    mod[7:8, :] = cond[0:1, :]
    arrived(xf, x_recv)
    spread_out(cot_in, o_cot, c_send, c_recv, False)
    x_out = pltpu.make_async_copy(xf, o_x, out_sem.at[0])
    x_out.start()

    shift = mod[0:1, :]
    scale = 1.0 + mod[1:2, :]

    def first(i, carry):
        normal, _ = normalize(xf[c + i].astype(f32))
        value = (normal * scale + shift).astype(bf16).astype(f32)
        before, after = column_shifts(value)
        shifts[0, 1 - c + i] = before
        shifts[1, 1 - c + i] = value
        shifts[2, 1 - c + i] = after
        return carry

    lax.fori_loop(0, 17, first, 0)
    for s in range(3):
        shifts[s, 17 * c] = jnp.zeros((across, width), f32)

    def conv(step, parity):
        o = 2 * step + parity
        for lane in range(0, width, LANES):
            cut = slice(lane, lane + LANES)
            total = jnp.zeros((across, LANES), f32)
            for r in range(3):
                for s in range(3):
                    tap = kern[3 * r + s : 3 * r + s + 1, cut].astype(f32)
                    total = total + tap * shifts[s, o + r, :, cut]
            mixed[step, parity, :, cut] = total.astype(bf16)

    def conv_away(step, carry):
        conv(step, 1 - c)
        return carry

    def conv_own(step, carry):
        conv(step, c)
        return carry

    lax.fori_loop(0, 8, conv_away, 0)
    mixed_away = remote(
        mixed.at[:, 1 - c], rows_m.at[pl.ds(8 * c, 8)], ex_send.at[0], ex_recv.at[0], core
    )
    mixed_away.start()
    lax.fori_loop(0, 8, conv_own, 0)
    mixed_own = pltpu.make_async_copy(mixed.at[:, c], rows_m.at[pl.ds(8 * c, 8)], own_sem.at[0])
    mixed_own.start()
    mixed_own.wait()
    mixed_away.wait()
    flat = rows_m[...].reshape(16 * across, width)
    tok[...] = dot_nn(perm[0], flat).astype(bf16)
    tok_out = pltpu.make_async_copy(tok, o_tok, out_sem.at[1])
    tok_out.start()
    loads[0].wait()
    for part in range(3):
        cut = slice(part * width, (part + 1) * width)
        proj[:, cut] = dot_nn(tok[...], wqkv[:, cut]).astype(bf16)
    proj_out = pltpu.make_async_copy(proj, o_proj, out_sem.at[2])
    proj_out.start()

    pairs = width // LANES
    size = tok.shape[0] // 2
    low_lane = lax.broadcasted_iota(jnp.int32, (size, LANES), 1) < LANES // 2
    lane_id = lax.broadcasted_iota(jnp.int32, (size, LANES), 1)
    zero = jnp.zeros((), bf16)

    def attend(index, carry):
        half, pair = index // pairs, lax.rem(index, pairs)
        rows = pl.ds(pl.multiple_of(half * size, size), size)

        def part(n):
            return proj[rows, pl.ds(pl.multiple_of(n * width + pair * LANES, LANES), LANES)]

        q, k, v = part(0) * jnp.asarray(0.125, bf16), part(1), part(2)
        total = jnp.zeros((size, LANES), f32)
        sums = lse[half]
        for h in range(2):
            mine = low_lane if h == 0 else jnp.logical_not(low_lane)
            scores = dot_nt(q, jnp.where(mine, k, zero)) + bias[half]
            top = jnp.max(scores, axis=-1, keepdims=True)
            powers = jnp.exp(scores - top)
            mass = jnp.sum(powers, axis=-1, keepdims=True)
            weights = (powers * (1.0 / mass)).astype(bf16)
            total = total + dot_nn(weights, jnp.where(mine, v, zero))
            sums = jnp.where(lane_id == 2 * pair + h, top + jnp.log(mass), sums)
        lse[half] = sums
        att[rows, pl.ds(pl.multiple_of(pair * LANES, LANES), LANES)] = total.astype(bf16)
        return carry

    lse[...] = jnp.zeros(lse.shape, f32)
    lax.fori_loop(0, 2 * pairs, attend, 0)
    att_out = pltpu.make_async_copy(att, o_att, out_sem.at[3])
    att_out.start()
    lse_out = pltpu.make_async_copy(lse, o_lse, out_sem.at[4])
    lse_out.start()
    loads[1].wait()
    branch = dot_nn(att[...], wo[...]).astype(bf16)
    brm[...] = dot_nn(perm[1], branch).astype(bf16).reshape(16, across, width)
    ret_away = remote(
        brm.at[pl.ds(7 * (1 - c), 9)], o_ret.at[:, c], ex_send.at[1], ex_recv.at[1], core
    )
    ret_away.start()
    ret_own = pltpu.make_async_copy(brm.at[pl.ds(7 * c, 9)], o_ret.at[:, c], own_sem.at[1])
    ret_own.start()
    for out in (x_out, tok_out, proj_out, att_out, lse_out, bias_out, ret_own):
        out.wait()
    ret_away.wait()
    spread_out(x_in, xf, x_send, x_recv, True)
    spread_out(cot_in, o_cot, c_send, c_recv, True)
    arrived(o_cot, c_recv)


def front(inputs, cotangent, names, moments, segments, kern, classes, times, wmod, wqkv, wo):
    across, width = inputs.shape[2], inputs.shape[3]
    tokens = 16 * across
    any_space = pl.BlockSpec(memory_space=pl.ANY)
    vmem = pl.BlockSpec(memory_space=pltpu.VMEM)
    smem = pl.BlockSpec(memory_space=pltpu.SMEM)
    shape = jax.ShapeDtypeStruct
    dma = pltpu.SemaphoreType.DMA
    return pl.pallas_call(
        front_kernel,
        out_shape=(
            shape((18, across, width), bf16),
            shape((18, across, width), bf16),
            shape((9, 2, across, width), bf16),
            shape((tokens, width), bf16),
            shape((tokens, 3 * width), bf16),
            shape((tokens, width), bf16),
            shape((2, tokens // 2, LANES), f32),
            shape((2, tokens // 2, tokens // 2), f32),
            shape((8, width), f32),
        ),
        in_specs=[any_space] * 2 + [smem] * 2 + [vmem] * 2 + [any_space] * 5,
        out_specs=[any_space] * 8 + [vmem],
        scratch_shapes=[
            pltpu.VMEM((18, across, width), bf16),
            pltpu.VMEM((2, *classes.shape), bf16),
            pltpu.VMEM(wmod.shape, bf16),
            pltpu.VMEM(wqkv.shape, bf16),
            pltpu.VMEM(wo.shape, bf16),
            pltpu.VMEM((3, 18, across, width), f32),
            pltpu.VMEM((8, 2, across, width), bf16),
            pltpu.VMEM((16, across, width), bf16),
            pltpu.VMEM((2, tokens, tokens), bf16),
            pltpu.VMEM((2, tokens // 2, tokens // 2), f32),
            pltpu.VMEM((tokens, width), bf16),
            pltpu.VMEM((tokens, 3 * width), bf16),
            pltpu.VMEM((tokens, width), bf16),
            pltpu.VMEM((2, tokens // 2, LANES), f32),
            pltpu.VMEM((16, across, width), bf16),
            dma((5,)), dma((3,)), dma((3,)), dma((3,)), dma((3,)), dma((2,)), dma((2,)),
            dma((2,)), dma((6,)),
        ],
        compiler_params=pltpu.CompilerParams(
            collective_id=1, has_side_effects=True, vmem_limit_bytes=60 << 20
        ),
        name="front",
    )(inputs, cotangent, names, moments, segments, kern, classes, times, wmod, wqkv, wo)


def gelu_parts(x):
    size = jnp.abs(x)
    t = 1.0 / (1.0 + (0.3275911 * 0.7071067811865476) * size)
    bell = jnp.exp(-0.5 * x * x)
    series = t * (
        0.254829592
        + t * (-0.284496736 + t * (1.421413741 + t * (-1.453152027 + t * 1.061405429)))
    )
    tail = 0.5 * series * bell
    mass = jnp.where(x >= 0, 1.0 - tail, tail)
    return x * mass, mass + x * bell * 0.3989422804014327


def feed_kernel(
    x_in, ret_in, cot_in, mod, up, kern, down,
    o_up, o_down, o_up_last, o_down_last, o_kern, o_res, o_mid, o_rg, o_small,
    feed_in, feed_t, btg, out_acc, back_acc, hid, hs, gs, act, slope, hg, wu, wd, ru, rd, xu, xd,
    u1_send, u1_recv, d1_send, d1_recv, u2_send, u2_recv, d2_send, d2_recv, u_out, d_out, l_out,
):
    j = pl.program_id(0)
    tiles = pl.num_programs(0)
    b = lax.axis_index("batch")
    g = lax.axis_index("group")
    c, p = lax.rem(g, 2), g // 2
    core, side = (b, g + 1 - 2 * c), (b, g + 2 - 4 * p)
    parts, grain = wd.shape[3], wd.shape[4]

    def up_1(t):
        return remote(wu.at[t, 1 - c], ru.at[t], u1_send.at[t], u1_recv.at[t], core)

    def down_1(t):
        return remote(wd.at[t, 1 - c], rd.at[t], d1_send.at[t], d1_recv.at[t], core)

    def up_2(t):
        return remote(wu.at[t, c, 1 - p], xu.at[t], u2_send.at[t], u2_recv.at[t], side)

    def down_2(t):
        return remote(wd.at[t, c, 1 - p], xd.at[t], d2_send.at[t], d2_recv.at[t], side)

    def up_store(t):
        spot = pl.ds(pl.multiple_of(t * LANES, LANES), LANES)
        return pltpu.make_async_copy(wu.at[t, c, p], o_up.at[:, spot], u_out.at[t])

    def down_store(t):
        return pltpu.make_async_copy(
            wd.at[t, c, p], o_down.at[pl.ds(t * parts, parts)], d_out.at[t]
        )

    def add_core(t):
        down_1(t).wait_recv()
        up_1(t).wait_recv()

        def step(i, carry):
            x, n = i // 8, lax.rem(i, 8)
            spot = pl.ds(pl.multiple_of(n * 96, 32), 96)
            wu[t, c, x, spot] = wu[t, c, x, spot] + ru[t, x, spot]
            for k in range(parts // 8):
                wd[t, c, x, n * (parts // 8) + k] = (
                    wd[t, c, x, n * (parts // 8) + k] + rd[t, x, n * (parts // 8) + k]
                )
            return carry

        lax.fori_loop(0, 16, step, 0)

    def add_side(t):
        down_2(t).wait_recv()
        up_2(t).wait_recv()

        def step(n, carry):
            spot = pl.ds(pl.multiple_of(n * 96, 32), 96)
            wu[t, c, p, spot] = wu[t, c, p, spot] + xu[t, spot]
            for k in range(parts // 8):
                wd[t, c, p, n * (parts // 8) + k] = (
                    wd[t, c, p, n * (parts // 8) + k] + xd[t, n * (parts // 8) + k]
                )
            return carry

        lax.fori_loop(0, 8, step, 0)
        up_store(t).start()
        down_store(t).start()
    across = 32
    width = feed_in.shape[1]
    tile = up.shape[1]
    frame_rows = feed_in.shape[0] // across
    own = pl.ds(pl.multiple_of(2 * c * across, 64), 16 * across)

    def middle_of(row):
        place = pl.ds(pl.multiple_of(row * across, across), across)
        returned = ret_in[place, :].astype(f32)
        return x_in[place, :].astype(f32) + mod[2:3, :] * returned, returned

    @pl.when(j == 0)
    def _():
        meet([core, side])

        def prepare(row, carry):
            place = pl.ds(pl.multiple_of(row * across, across), across)
            normal, _ = normalize(middle_of(row)[0])
            feed_in[place, :] = (normal * (1.0 + mod[4:5, :]) + mod[3:4, :]).astype(bf16)
            btg[place, :] = (mod[5:6, :] * cot_in[place, :].astype(f32)).astype(bf16)
            return carry

        lax.fori_loop(0, frame_rows, prepare, 0)
        feed_t[...] = feed_in[own, :].T
        out_acc[...] = jnp.zeros(out_acc.shape, f32)
        back_acc[...] = jnp.zeros(back_acc.shape, f32)
        for s in range(3):
            hs[s, 18 * c] = jnp.zeros((across, tile), f32)
            gs[s, 17 * c] = jnp.zeros((across, tile), f32)

    hid[...] = dot_nn(feed_in[...], up[...]).astype(bf16)

    def lay_hidden(row, carry):
        value = hid[pl.ds(pl.multiple_of(row * across, across), across), :].astype(f32)
        before, after = column_shifts(value)
        hs[0, 1 - c + row] = before
        hs[1, 1 - c + row] = value
        hs[2, 1 - c + row] = after
        return carry

    lax.fori_loop(0, frame_rows, lay_hidden, 0)

    for lane in range(0, tile, LANES):
        cut = slice(lane, lane + LANES)
        taps = [kern[n : n + 1, cut].astype(f32) for n in range(9)]

        def forward(row, carry):
            total = jnp.zeros((across, LANES), f32)
            for r in range(3):
                for s in range(3):
                    total = total + taps[3 * r + s] * hs[s, row + r, :, cut]
            place = pl.ds(pl.multiple_of(row * across, across), across)
            value, steep = gelu_parts(total)
            act[place, cut] = value.astype(bf16)
            slope[place, cut] = steep
            return carry

        lax.fori_loop(0, 17, forward, 0)

    @pl.when(j >= 1)
    def _():
        add_core(j - 1)
        up_2(j - 1).start()
        down_2(j - 1).start()

    inside = pl.ds(pl.multiple_of(c * across, across), 16 * across)
    around = pl.ds(pl.multiple_of(c * across, across), 17 * across)
    own_act = act[inside, :]
    out_acc[...] += dot_nn(own_act, down[...])
    grad_down = dot_tn(own_act, btg[own, :]).reshape(parts, 4, grain, width)
    for q in range(4):
        wd[j, q % 2, q // 2] = grad_down[:, q].astype(bf16)
    down_1(j).start()
    slope[...] = slope[...] * dot_nt(btg[around, :], down[...])

    def lay_grad(row, carry):
        value = slope[pl.ds(pl.multiple_of(row * across, across), across), :]
        value = value.astype(bf16).astype(f32)
        before, after = column_shifts(value)
        gs[0, 1 - c + row] = after
        gs[1, 1 - c + row] = value
        gs[2, 1 - c + row] = before
        return carry

    lax.fori_loop(0, 17, lay_grad, 0)

    for lane in range(0, tile, LANES):
        cut = slice(lane, lane + LANES)
        taps = [kern[n : n + 1, cut].astype(f32) for n in range(9)]

        def backward(row, sums):
            total = jnp.zeros((across, LANES), f32)
            value = hs[1, row + c + 1, :, cut]
            later = []
            for r in range(3):
                for s in range(3):
                    grad = gs[s, row + 2 - r, :, cut]
                    total = total + taps[3 * r + s] * grad
                    later.append(sums[3 * r + s] + fold(value * grad))
            hg[pl.ds(pl.multiple_of(row * across, across), across), cut] = total.astype(bf16)
            return tuple(later)

        sums = lax.fori_loop(
            0, 16, backward, tuple(jnp.zeros((8, LANES), f32) for _ in range(9))
        )
        for n in range(9):
            o_kern[n : n + 1, cut] = jnp.sum(sums[n], axis=0, keepdims=True)

    o_kern[9:16, :] = jnp.zeros((7, tile), f32)
    grad_up = dot_nn(feed_t[...], hg[...]).astype(bf16)
    for q in range(4):
        wu[j, q % 2, q // 2] = grad_up[:, q * LANES : (q + 1) * LANES]
    up_1(j).start()
    back_acc[...] += dot_nt(hg[...], up[...])

    @pl.when(j >= 1)
    def _():
        add_side(j - 1)

    @pl.when(j == tiles - 1)
    def _():
        def finish(row, sums):
            frame = row + 2 * c
            place = pl.ds(pl.multiple_of(row * across, across), across)
            at = pl.ds(pl.multiple_of(frame * across, across), across)
            middle, returned = middle_of(frame)
            cot = cot_in[at, :].astype(f32)
            branch = out_acc[place, :]
            o_res[place, :] = (middle + mod[5:6, :] * branch).astype(bf16)
            normal, scale = normalize(middle)
            grad = back_acc[place, :]
            mid = cot + normalize_back(grad * (1.0 + mod[4:5, :]), normal, scale)
            o_mid[place, :] = mid
            o_rg[place, :] = (mod[2:3, :] * mid).astype(bf16)
            terms = (mid * returned, grad, grad * normal, cot * branch)
            return tuple(total + fold(term) for total, term in zip(sums, terms))

        sums = lax.fori_loop(
            0, 16, finish, tuple(jnp.zeros((8, width), f32) for _ in range(4))
        )
        o_small[...] = jnp.zeros((8, width), f32)
        for n in range(4):
            o_small[n + 2 : n + 3, :] = jnp.sum(sums[n], axis=0, keepdims=True)
        add_core(j)
        last = (
            pltpu.make_async_copy(wu.at[j, c], o_up_last, l_out.at[0]),
            pltpu.make_async_copy(wd.at[j, c], o_down_last, l_out.at[1]),
        )
        for move in last:
            move.start()

        def settle(t, carry):
            up_2(t).wait_send()
            down_2(t).wait_send()
            up_1(t).wait_send()
            down_1(t).wait_send()
            up_store(t).wait()
            down_store(t).wait()
            return carry

        lax.fori_loop(0, tiles - 1, settle, 0)
        up_1(j).wait_send()
        down_1(j).wait_send()
        for move in last:
            move.wait()


def feed(x_frame, returned, cot_frame, mod, up, kern, down, grain):
    width, units = up.shape
    frame = x_frame.shape[0]
    across = frame // 18
    tokens = 16 * across
    shape = jax.ShapeDtypeStruct
    dma = pltpu.SemaphoreType.DMA
    any_space = pl.BlockSpec(memory_space=pl.ANY)
    tile = 4 * LANES
    tiles = units // tile
    parts = tile // (4 * grain)

    def still(*size):
        return pl.BlockSpec(size, lambda j: (0, 0), pipeline_mode=pl.Buffered(1))

    columns = pl.BlockSpec((width, tile), lambda j: (0, j))
    rows = pl.BlockSpec((tile, width), lambda j: (j, 0))
    work = 6 * 2 * tokens * width * units
    return pl.pallas_call(
        feed_kernel,
        grid=(units // tile,),
        out_shape=(
            shape((width, units // 4), bf16),
            shape((tiles * parts, grain, width), bf16),
            shape((2, width, LANES), bf16),
            shape((2, parts, grain, width), bf16),
            shape((16, units), f32),
            shape((tokens, width), bf16),
            shape((tokens, width), f32),
            shape((tokens, width), bf16),
            shape((8, width), f32),
        ),
        in_specs=[
            still(frame, width), still(frame, width), still(frame, width), still(8, width),
            columns, pl.BlockSpec((9, tile), lambda j: (0, j)), rows,
        ],
        out_specs=[
            *[any_space] * 4, pl.BlockSpec((16, tile), lambda j: (0, j)),
            still(tokens, width), still(tokens, width), still(tokens, width), still(8, width),
        ],
        scratch_shapes=[
            pltpu.VMEM((frame, width), bf16),
            pltpu.VMEM((width, tokens), bf16),
            pltpu.VMEM((frame, width), bf16),
            pltpu.VMEM((tokens, width), f32),
            pltpu.VMEM((tokens, width), f32),
            pltpu.VMEM((frame, tile), bf16),
            pltpu.VMEM((3, 19, across, tile), f32),
            pltpu.VMEM((3, 18, across, tile), f32),
            pltpu.VMEM((17 * across, tile), bf16),
            pltpu.VMEM((17 * across, tile), f32),
            pltpu.VMEM((tokens, tile), bf16),
            pltpu.VMEM((tiles, 2, 2, width, LANES), bf16),
            pltpu.VMEM((tiles, 2, 2, parts, grain, width), bf16),
            pltpu.VMEM((tiles, 2, width, LANES), bf16),
            pltpu.VMEM((tiles, 2, parts, grain, width), bf16),
            pltpu.VMEM((tiles, width, LANES), bf16),
            pltpu.VMEM((tiles, parts, grain, width), bf16),
            *[dma((tiles,)) for _ in range(10)],
            dma((2,)),
        ],
        compiler_params=pltpu.CompilerParams(
            dimension_semantics=("arbitrary",), collective_id=3, has_side_effects=True,
            vmem_limit_bytes=62 << 20,
        ),
        cost_estimate=pl.CostEstimate(
            flops=work, bytes_accessed=8 * width * units, transcendentals=tokens * units
        ),
        name="feed",
    )(x_frame, returned, cot_frame, mod, up, kern, down)


def back_kernel(
    mid_in, rg_in, tok_in, proj_in, att_in, lse, bias, x_in, mod, small, kern, wqkv_in, wo_in,
    res_in, uq_in, dq_in, ul_in, dl_in, kern_two,
    o_fu, o_fd, o_fp, o_res, o_ig, o_one, o_two, o_mg,
    mid, tok, tok_t, proj, att, xf, wqkv, wo, rows_m, perm, grad, datt, dproj,
    brm, frame, gs, value, agrad, ig,
    wp, p_r1, p_r2x, p_r2y, p_r3, p_r4, fin_p,
    fu, fd, fy_u, fy_d, fz_u, fz_d, fin_u, fin_d, lu, ld, lx_u, lx_d,
    mg_own, mg_r1, mg_all, kk_1, kr_1, kz_1, kk_2, kr_2, kz_2,
    load_sem, r_send, r_recv, i_send, i_recv, ex_send, ex_recv, own_sem, send_sem, recv_sem, out_sem,
):
    b = lax.axis_index("batch")
    g = lax.axis_index("group")
    nz = fu.shape[0]
    c, p = lax.rem(g, 2), g // 2
    yb, zb = lax.rem(b, 2), b // 2
    core, side, corner = (b, g + 1 - 2 * c), (b, g + 2 - 4 * p), (b, 3 - g)
    beside = (b + 1 - 2 * yb, g)
    others = [lax.rem(zb + d, nz) for d in range(nz)]
    far = [(2 * z + yb, g) for z in others]
    inner = jnp.logical_or(g == 1, g == 2)
    across, width = xf.shape[1], xf.shape[2]
    rows_own = fu.shape[2]
    pairs = width // LANES
    tokens = tok.shape[0]
    size = tokens // 2
    chunks = wp.shape[0]
    chunk = wp.shape[-1]
    lead = width - LANES
    per, parts = fd.shape[2], ld.shape[0]
    places = {}

    def link(name, src, dst, target):
        n = places.setdefault(name, len(places))
        return remote(src, dst, send_sem.at[n], recv_sem.at[n], target)

    def send_home(src, dst, send, recv, waiting):
        moves = [
            remote(
                src.at[pl.ds(8 * n, 8)], dst.at[p], send.at[n], recv.at[p], (b, 2 * c + n)
            )
            for n in range(2)
        ]
        away = remote(
            src.at[pl.ds(8 * (1 - c), 8)], dst.at[p], send.at[0], recv.at[p], core
        )
        stay = pltpu.make_async_copy(src.at[pl.ds(8 * c, 8)], dst.at[p], recv.at[p])

        @pl.when(inner)
        def _():
            for move in moves:
                if waiting:
                    move.wait_send()
                else:
                    move.start()

        @pl.when(jnp.logical_not(inner))
        def _():
            if waiting:
                away.wait_send()
            else:
                away.start()
                stay.start()

    def home(dst, recv):
        for n in range(2):
            pltpu.make_async_copy(dst.at[n], dst.at[n], recv.at[n]).wait()

    head, rest = pl.ds(0, lead), pl.ds(lead, LANES)

    def last_x():
        return [
            link("lu", ul_in.at[1 - p], lx_u, side),
            link("ld", dl_in.at[1 - p], lx_d, side),
        ]

    def fa_y():
        return [link("fay", fu.at[:, 1 - yb, :, head], fy_u.at[:, :, head], beside)]

    def fb_y():
        return [
            link("fby", fu.at[:, 1 - yb, :, rest], fy_u.at[:, :, rest], beside),
            link("fdy", fd.at[:, 1 - yb], fy_d, beside),
        ]

    def fa_z(d):
        return [link(f"faz{d}", fu.at[others[d], yb, :, head], fz_u.at[d - 1, :, head], far[d])]

    def fb_z(d):
        return [
            link(f"fbz{d}", fu.at[others[d], yb, :, rest], fz_u.at[d - 1, :, rest], far[d]),
            link(f"fdz{d}", fd.at[others[d], yb], fz_d.at[d - 1], far[d]),
        ]

    def f_side(mine):
        x = p if mine else 1 - p
        return [
            link("gux", fin_u.at[c, x], fin_u.at[c, x], side),
            link("gdx", fin_d.at[c, x], fin_d.at[c, x], side),
        ]

    def f_core(mine):
        x = c if mine else 1 - c
        return [
            link("guc", fin_u.at[x], fin_u.at[x], core),
            link("gdc", fin_d.at[x], fin_d.at[x], core),
        ]

    def start(moves):
        for move in moves:
            move.start()

    def come(moves):
        for move in moves:
            move.wait_recv()

    def gone(moves):
        for move in moves:
            move.wait_send()

    def place_last():
        for load in late:
            load.wait()
        come(last_x())

        def step(n, carry):
            z, y = n // 2, lax.rem(n, 2)
            fu[z, y, :, lead:] = lu[z, y] + lx_u[z, y]
            return carry

        lax.fori_loop(0, 2 * nz, step, 0)
        for t in range(parts):
            spot = 2 * nz * per - parts + t
            owner = spot // per
            fd[owner // 2, owner % 2, spot % per] = ld[t] + lx_d[t]
        start(fb_y())

    def fa_y_add():
        come(fa_y())

        def step(z, carry):
            fu[z, yb, :, :lead] = fu[z, yb, :, :lead] + fy_u[z, :, :lead]
            return carry

        lax.fori_loop(0, nz, step, 0)
        for d in range(1, nz):
            start(fa_z(d))

    def fb_y_add():
        come(fb_y())

        def step(z, carry):
            fu[z, yb, :, lead:] = fu[z, yb, :, lead:] + fy_u[z, :, lead:]
            fd[z, yb] = fd[z, yb] + fy_d[z]
            return carry

        lax.fori_loop(0, nz, step, 0)
        for d in range(1, nz):
            start(fb_z(d))

    def f_sum():
        total_u = fu[zb, yb].astype(f32)
        total_d = fd[zb, yb].astype(f32)
        for d in range(1, nz):
            come(fa_z(d))
            come(fb_z(d))
            total_u = total_u + fz_u[d - 1].astype(f32)
            total_d = total_d + fz_d[d - 1].astype(f32)
        fin_u[c, p] = total_u.astype(bf16)
        fin_d[c, p] = total_d.astype(bf16)
        start(f_side(True))

    def f_side_done():
        come(f_side(False))
        start(f_core(True))

    def f_core_done():
        come(f_core(False))
        start(f_out)

    f_out = [
        pltpu.make_async_copy(fin_u, o_fu, out_sem.at[0]),
        pltpu.make_async_copy(fin_d, o_fd, out_sem.at[1]),
    ]
    p_out = pltpu.make_async_copy(fin_p, o_fp, out_sem.at[2])
    mg_out = pltpu.make_async_copy(mg_all, o_mg, out_sem.at[3])

    def side_first(k):
        return k == 0

    def p1(k):
        return link(f"p1{k}", wp.at[k, 1 - c], p_r1.at[k], core)

    def p2(k):
        if side_first(k):
            return link(f"p2{k}", wp.at[k, c, 1 - p], p_r2x.at[k], side)
        return link(f"p2{k}", wp.at[k, c, :, :, 1 - yb], p_r2y.at[k], beside)

    def p3(k):
        if side_first(k):
            return link(f"p3{k}", wp.at[k, c, p, :, 1 - yb], p_r3.at[k], beside)
        return link(f"p3{k}", wp.at[k, c, 1 - p, :, yb], p_r3.at[k], side)

    def p4(k, d):
        return link(
            f"p4{k}{d}", wp.at[k, c, p, others[d], yb], p_r4.at[k, d - 1], far[d]
        )

    def p_side(k, mine):
        x = p if mine else 1 - p
        return link(f"p5{k}", fin_p.at[k, c, x], fin_p.at[k, c, x], side)

    def p_core(k, mine):
        x = c if mine else 1 - c
        return link(f"p6{k}", fin_p.at[k, x], fin_p.at[k, x], core)

    def p_add_1(k):
        p1(k).wait_recv()

        def step(i, carry):
            x, z, y = i // (2 * nz), lax.rem(i // 2, nz), lax.rem(i, 2)
            wp[k, c, x, z, y] = wp[k, c, x, z, y] + p_r1[k, x, z, y]
            return carry

        lax.fori_loop(0, 4 * nz, step, 0)
        p2(k).start()

    def p_add_2(k):
        p2(k).wait_recv()

        def step(i, carry):
            if side_first(k):
                z, y = i // 2, lax.rem(i, 2)
                wp[k, c, p, z, y] = wp[k, c, p, z, y] + p_r2x[k, z, y]
            else:
                x, z = i // nz, lax.rem(i, nz)
                wp[k, c, x, z, yb] = wp[k, c, x, z, yb] + p_r2y[k, x, z]
            return carry

        lax.fori_loop(0, 2 * nz, step, 0)
        p3(k).start()

    def p_add_3(k):
        p3(k).wait_recv()

        def step(z, carry):
            wp[k, c, p, z, yb] = wp[k, c, p, z, yb] + p_r3[k, z]
            return carry

        lax.fori_loop(0, nz, step, 0)
        for d in range(1, nz):
            p4(k, d).start()

    def p_add_4(k):
        total = wp[k, c, p, zb, yb].astype(f32)
        for d in range(1, nz):
            p4(k, d).wait_recv()
            total = total + p_r4[k, d - 1].astype(f32)
        fin_p[k, c, p] = total.astype(bf16)
        p_side(k, True).start()

    def p_pass(k):
        p_side(k, False).wait_recv()
        p_core(k, True).start()

    peers = [core, side, beside]

    def kern_copy(name, kk, kr, stage):
        return link(f"{name}{stage}", kk.at[stage], kr.at[stage], peers[stage])

    def kern_far(name, kk, kz, d):
        return link(f"{name}z{d}", kk.at[3], kz.at[d - 1], far[d])

    def kern_step(name, kk, kr, kz, stage):
        kern_copy(name, kk, kr, stage).wait_recv()
        kk[stage + 1] = (kk[stage].astype(f32) + kr[stage].astype(f32)).astype(bf16)
        if stage < 2:
            kern_copy(name, kk, kr, stage + 1).start()
        else:
            for d in range(1, nz):
                kern_far(name, kk, kz, d).start()

    def kern_sum(name, kk, kz, out):
        total = kk[3].astype(f32)
        for d in range(1, nz):
            kern_far(name, kk, kz, d).wait_recv()
            total = total + kz[d - 1].astype(f32)
        out[...] = total

    one = ("one", kk_1, kr_1, kz_1)
    two = ("two", kk_2, kr_2, kz_2)

    def mg_copy(stage, mine=True):
        if stage == 0:
            return link("mg0", mg_own, mg_r1, core)
        x = p if mine else 1 - p
        y = yb if mine else 1 - yb
        place = mg_all.at[zb, yb, x] if stage == 1 else mg_all.at[zb, y]
        return link(f"mg{stage}", place, place, peers[stage])

    def mg_far(d, z):
        return link(f"mgz{d}", mg_all.at[z], mg_all.at[z], far[d])

    pieces = [
        (wo_in, wo), (att_in, att), (tok_in, tok), (proj_in, proj), (wqkv_in, wqkv), (x_in, xf),
        (mid_in, mid),
    ]
    loads = [
        pltpu.make_async_copy(src, dst, load_sem.at[n]) for n, (src, dst) in enumerate(pieces)
    ]
    full = dq_in.shape[0] - parts
    early = [pltpu.make_async_copy(uq_in.at[:, :, :, head], fu.at[:, :, :, head], load_sem.at[7])]
    late = [
        pltpu.make_async_copy(ul_in.at[p], lu, load_sem.at[8]),
        pltpu.make_async_copy(dl_in.at[p], ld, load_sem.at[9]),
    ]
    for owner in range(2 * nz):
        count = min(per, full - owner * per)
        if count > 0:
            late.append(
                pltpu.make_async_copy(
                    dq_in.at[pl.ds(owner * per, count)],
                    fd.at[owner // 2, owner % 2, pl.ds(0, count)],
                    load_sem.at[10 + owner],
                )
            )
    for load in (*early, *loads, *late):
        load.start()
    kk_2[0] = kern_two[...].astype(bf16)
    meet([core, side, corner, beside, *far[1:]])
    grad_away = remote(
        rg_in.at[:, 1 - c], rows_m.at[pl.ds(8 * c, 8)], ex_send.at[0], ex_recv.at[0], core
    )
    grad_away.start()
    grad_own = pltpu.make_async_copy(rg_in.at[:, c], rows_m.at[pl.ds(8 * c, 8)], own_sem.at[0])
    grad_own.start()
    start(last_x())
    early[0].wait()
    start(fa_y())
    kern_copy("two", kk_2, kr_2, 0).start()
    perm[0] = permutation(False)
    perm[1] = permutation(True)
    grad_own.wait()
    grad_away.wait()
    grad[...] = dot_nn(perm[0], rows_m[...].reshape(tokens, width)).astype(bf16)
    loads[0].wait()
    loads[1].wait()
    datt[...] = dot_nt(grad[...], wo[...]).astype(bf16)
    out_grad = dot_tn(att[...], grad[...])
    for k in range(chunks):
        cut = slice(k * chunk, (k + 1) * chunk)
        wp[k, 1, 1] = out_grad[:, cut].reshape(nz, 2, rows_own, chunk).astype(bf16)
    loads[2].wait()
    tok_t[...] = tok[...].T
    loads[3].wait()
    place_last()
    send_home(res_in, o_res, r_send, r_recv, False)
    kern_step(*two, 0)

    low_lane = lax.broadcasted_iota(jnp.int32, (size, LANES), 1) < LANES // 2
    lane_id = lax.broadcasted_iota(jnp.int32, (size, LANES), 1)
    zero = jnp.zeros((), bf16)

    def attend(index, carry):
        pair, half = index // 2, lax.rem(index, 2)
        rows = pl.ds(pl.multiple_of(half * size, size), size)

        def cut(n):
            return pl.ds(pl.multiple_of(n * width + pair * LANES, LANES), LANES)

        q = proj[rows, cut(0)] * jnp.asarray(0.125, bf16)
        k, v, up = proj[rows, cut(1)], proj[rows, cut(2)], datt[rows, cut(0)]
        sums = lse[half]
        dq = jnp.zeros((size, LANES), f32)
        dk = jnp.zeros((size, LANES), f32)
        dv = jnp.zeros((size, LANES), f32)
        for h in range(2):
            mine = low_lane if h == 0 else jnp.logical_not(low_lane)
            key = jnp.where(mine, k, zero)
            scores = dot_nt(q, key) + bias[half]
            mass = jnp.sum(
                jnp.where(lane_id == 2 * pair + h, sums, 0.0), axis=-1, keepdims=True
            )
            weights = jnp.exp(scores - mass)
            pull = dot_nt(up, jnp.where(mine, v, zero))
            mean = jnp.sum(weights * pull, axis=-1, keepdims=True)
            spare = (weights * (pull - mean)).astype(bf16)
            dq = dq + dot_nn(spare, key)
            dk = dk + dot_tn(spare, jnp.where(mine, q, zero))
            dv = dv + dot_tn(weights.astype(bf16), jnp.where(mine, up, zero))
        dproj[rows, cut(0)] = (dq * 0.125).astype(bf16)
        dproj[rows, cut(1)] = dk.astype(bf16)
        dproj[rows, cut(2)] = dv.astype(bf16)
        return carry

    def weigh(k):
        for q in range(3):
            span = slice(q * width + k * chunk, q * width + (k + 1) * chunk)
            part = dot_nn(tok_t[...], dproj[:, span])
            wp[k, q % 2, q // 2] = part.reshape(nz, 2, rows_own, chunk).astype(bf16)
        p1(k).start()

    lax.fori_loop(0, 2, attend, 0)
    fa_y_add()
    kern_step(*two, 1)
    lax.fori_loop(2, 4, attend, 0)
    weigh(0)
    fb_y_add()
    kern_step(*two, 2)
    lax.fori_loop(4, 6, attend, 0)
    p_add_1(0)
    lax.fori_loop(6, 8, attend, 0)
    weigh(1)
    f_sum()
    kern_sum("two", kk_2, kz_2, o_two)
    lax.fori_loop(8, 10, attend, 0)
    p_add_1(1)
    p_add_2(0)
    f_side_done()
    lax.fori_loop(10, 12, attend, 0)
    weigh(2)
    loads[4].wait()
    back = dot_nt(dproj[...], wqkv[...]).astype(bf16)
    brm[...] = dot_nn(perm[1], back).astype(bf16).reshape(16, across, width)
    mixed_away = remote(
        brm.at[pl.ds(7 * (1 - c), 9)], frame.at[:, c], ex_send.at[1], ex_recv.at[1], core
    )
    mixed_away.start()
    mixed_own = pltpu.make_async_copy(brm.at[pl.ds(7 * c, 9)], frame.at[:, c], own_sem.at[1])
    mixed_own.start()
    p_add_1(2)
    p_add_3(0)
    p_add_2(1)
    f_core_done()
    loads[5].wait()
    loads[6].wait()

    shift = mod[0:1, :]
    scale_in = 1.0 + mod[1:2, :]

    def again(row, carry):
        normal, _ = normalize(xf[2 * c + row].astype(f32))
        value[row] = (normal * scale_in + shift).astype(bf16).astype(f32)
        return carry

    lax.fori_loop(0, 16, again, 0)
    mixed_own.wait()
    mixed_away.wait()

    def lay(row, carry):
        at = c + row
        line = frame[at // 2, lax.rem(at, 2)].astype(f32)
        before, after = column_shifts(line)
        gs[0, 1 - c + row] = after
        gs[1, 1 - c + row] = line
        gs[2, 1 - c + row] = before
        return carry

    lax.fori_loop(0, 17, lay, 0)
    for s in range(3):
        gs[s, 17 * c] = jnp.zeros((across, width), f32)

    kk_1[0] = jnp.zeros((16, width), bf16)

    def conv_back(lane):
        span = slice(lane, lane + LANES)
        taps = [kern[n : n + 1, span].astype(f32) for n in range(9)]

        def backward(row, sums):
            total = jnp.zeros((across, LANES), f32)
            own = value[row, :, span]
            later = []
            for r in range(3):
                for s in range(3):
                    line = gs[s, row + 2 - r, :, span]
                    total = total + taps[3 * r + s] * line
                    later.append(sums[3 * r + s] + fold(own * line))
            agrad[row, :, span] = total
            return tuple(later)

        sums = lax.fori_loop(
            0, 16, backward, tuple(jnp.zeros((8, LANES), f32) for _ in range(9))
        )
        rows9 = [jnp.sum(sums[n], axis=0, keepdims=True) for n in range(9)]
        kk_1[0, :, span] = jnp.concatenate(rows9 + [jnp.zeros((7, LANES), f32)]).astype(bf16)

    for lane in range(0, width // 2, LANES):
        conv_back(lane)
    p_add_4(0)
    p_add_3(1)
    p_add_2(2)
    for lane in range(width // 2, width, LANES):
        conv_back(lane)
    kern_copy("one", kk_1, kr_1, 0).start()

    def finish(row, sums):
        normal, scale = normalize(xf[2 * c + row].astype(f32))
        line = agrad[row]
        place = pl.ds(pl.multiple_of(row * across, across), across)
        total = mid[place, :] + normalize_back(line * scale_in, normal, scale)
        ig[row] = total.astype(bf16)
        return (sums[0] + fold(line), sums[1] + fold(line * normal))

    sums = lax.fori_loop(0, 16, finish, tuple(jnp.zeros((8, width), f32) for _ in range(2)))
    send_home(ig, o_ig, i_send, i_recv, False)
    mg_own[...] = small[...]
    for n in range(2):
        mg_own[n : n + 1, :] = jnp.sum(sums[n], axis=0, keepdims=True)
    mg_own[6:8, :] = mod[6:8, :]
    mg_copy(0).start()
    kern_step(*one, 0)
    p_pass(0)
    p_add_4(1)
    mg_copy(0).wait_recv()
    mg_all[zb, yb, p] = mg_own[...] + mg_r1[...]
    mg_copy(1).start()
    p_add_3(2)
    kern_step(*one, 1)
    mg_copy(1, False).wait_recv()
    mg_copy(2).start()
    p_pass(1)
    kern_step(*one, 2)
    mg_copy(2, False).wait_recv()
    for d in range(1, nz):
        mg_far(d, zb).start()
    p_add_4(2)
    p_core(0, False).wait_recv()
    p_core(1, False).wait_recv()
    p_pass(2)
    kern_sum("one", kk_1, kz_1, o_one)
    for d in range(1, nz):
        mg_far(d, lax.rem(zb + nz - d, nz)).wait_recv()
    mg_out.start()
    p_core(2, False).wait_recv()
    p_out.start()
    gone([*last_x(), *fa_y(), *fb_y(), *f_side(True), *f_core(True)])
    for d in range(1, nz):
        gone([*fa_z(d), *fb_z(d), mg_far(d, zb)])
        gone([kern_far("one", kk_1, kz_1, d), kern_far("two", kk_2, kz_2, d)])
    for k in range(chunks):
        gone([p1(k), p2(k), p3(k), p_side(k, True), p_core(k, True)])
        gone([p4(k, d) for d in range(1, nz)])
    for stage in range(3):
        gone([mg_copy(stage)])
        gone([kern_copy("one", kk_1, kr_1, stage), kern_copy("two", kk_2, kr_2, stage)])
    send_home(res_in, o_res, r_send, r_recv, True)
    send_home(ig, o_ig, i_send, i_recv, True)
    home(o_res, r_recv)
    home(o_ig, i_recv)
    for out in (*f_out, p_out, mg_out):
        out.wait()


def back(
    mid, rg, tok, proj, att, lse, bias, x_frame, mod, small, kern, wqkv, wo, res,
    uq, dq, ul, dl, kern_two,
):
    nb = lax.axis_size("batch")
    nz = nb // 2
    across, width = x_frame.shape[1], x_frame.shape[2]
    tokens = 16 * across
    rows = width // nb
    grain = dq.shape[1]
    parts = dl.shape[1]
    per = dq.shape[0] // nb
    chunks, chunk = 3, 2 * LANES
    many = max(nz - 1, 1)
    any_space = pl.BlockSpec(memory_space=pl.ANY)
    vmem = pl.BlockSpec(memory_space=pltpu.VMEM)
    shape = jax.ShapeDtypeStruct
    dma = pltpu.SemaphoreType.DMA
    wide = kern_two.shape[1]
    links = 80 + 12 * many

    def low(*dims):
        return pltpu.VMEM(dims, bf16)

    def high(*dims):
        return pltpu.VMEM(dims, f32)

    return pl.pallas_call(
        back_kernel,
        out_shape=(
            shape((2, 2, rows, width), bf16),
            shape((2, 2, per, grain, width), bf16),
            shape((chunks, 2, 2, rows, chunk), bf16),
            shape((2, 8, across, width), bf16),
            shape((2, 8, across, width), bf16),
            shape((16, width), f32),
            shape((16, wide), f32),
            shape((nz, 2, 2, 8, width), f32),
        ),
        in_specs=[any_space] * 5 + [vmem, vmem, any_space, vmem, vmem, vmem] + [any_space] * 7
        + [vmem],
        out_specs=[any_space] * 5 + [vmem, vmem, any_space],
        scratch_shapes=[
            high(tokens, width), low(tokens, width), low(width, tokens), low(tokens, 3 * width),
            low(tokens, width), low(18, across, width), low(*wqkv.shape), low(*wo.shape),
            low(16, across, width), low(2, tokens, tokens), low(tokens, width),
            low(tokens, width), low(tokens, 3 * width),
            low(16, across, width), low(9, 2, across, width), high(3, 18, across, width),
            high(16, across, width), high(16, across, width), low(16, across, width),
            low(chunks, 2, 2, nz, 2, rows, chunk), low(chunks, 2, nz, 2, rows, chunk),
            low(chunks, nz, 2, rows, chunk), low(chunks, 2, nz, rows, chunk),
            low(chunks, nz, rows, chunk), low(chunks, many, rows, chunk),
            low(chunks, 2, 2, rows, chunk),
            low(nz, 2, rows, width), low(nz, 2, per, grain, width),
            low(nz, rows, width), low(nz, per, grain, width),
            low(many, rows, width), low(many, per, grain, width),
            low(2, 2, rows, width), low(2, 2, per, grain, width),
            low(nz, 2, rows, LANES), low(parts, grain, width),
            low(nz, 2, rows, LANES), low(parts, grain, width),
            high(8, width), high(8, width), high(nz, 2, 2, 8, width),
            low(4, 16, width), low(3, 16, width), low(many, 16, width),
            low(4, 16, wide), low(3, 16, wide), low(many, 16, wide),
            dma((10 + nb,)), dma((2,)), dma((2,)), dma((2,)), dma((2,)), dma((2,)), dma((2,)),
            dma((2,)), dma((links,)), dma((links,)), dma((4,)),
        ],
        compiler_params=pltpu.CompilerParams(
            collective_id=2, has_side_effects=True, vmem_limit_bytes=63 << 20
        ),
        name="back",
    )(
        mid, rg, tok, proj, att, lse, bias, x_frame, mod, small, kern, wqkv, wo, res,
        uq, dq, ul, dl, kern_two,
    )


def tail_kernel(
    fu, fd, fp, mg, one, two, wm_in,
    o_class, o_time, o_mod, o_proj, o_out, o_one, o_up, o_two, o_down,
    wm, load_sem,
):
    b = lax.axis_index("batch")
    width = mg.shape[2]
    canvases = mg.shape[0]
    own = o_mod.shape[0]
    whole = wm_in.shape[0] == own
    source = wm_in if whole else wm_in.at[pl.ds(pl.multiple_of(b * own, 16), own)]
    load = pltpu.make_async_copy(source, wm, load_sem)
    load.start()
    chunks, chunk = fp.shape[0], fp.shape[4]
    per, grain = fd.shape[2], fd.shape[3]
    for q in range(4):
        for j in range(width // LANES):
            at = (4 * j + q) * LANES
            o_up[:, at : at + LANES] = fu[q % 2, q // 2, :, j * LANES : (j + 1) * LANES].astype(f32)
        for i in range(per):
            at = (4 * i + q) * grain
            o_down[at : at + grain, :] = fd[q % 2, q // 2, i].astype(f32)
        for k in range(chunks):
            part = fp[k, q % 2, q // 2].astype(f32)
            if q < 3:
                o_proj[:, q * width + k * chunk : q * width + (k + 1) * chunk] = part
            else:
                o_out[:, k * chunk : (k + 1) * chunk] = part

    def window(values, n):
        size = values.shape[1]
        return pltpu.roll(values, lax.rem(size - b * n, size), 1)[:, :n]

    o_one[...] = window(one[...], own)[0:9]
    o_two[...] = window(two[...], o_two.shape[1])[0:9]
    every = mg[...]
    cond = window(every[:, 7, :] * 0.5, own)
    sigma = 1.0 / (1.0 + jnp.exp(-cond))
    low = (cond * sigma).astype(bf16).astype(f32)
    steep = sigma * (1.0 + cond * (1.0 - sigma))
    act_grad = jnp.zeros((canvases, own), f32)
    load.wait()
    for part in range(6):
        span = slice(part * width, (part + 1) * width)
        line = every[:, part, :]
        o_mod[:, span] = lax.dot_general(
            low, line, (((0,), (0,)), ((), ())), precision=highest, preferred_element_type=f32
        )
        act_grad = act_grad + lax.dot_general(
            line, wm[:, span].astype(f32), (((1,), (1,)), ((), ())), precision=highest,
            preferred_element_type=f32,
        )
    cond_grad = act_grad * steep
    names = every[:, 6, :] * 0.5
    kinds = o_class.shape[0]
    spot = lax.broadcasted_iota(jnp.int32, (canvases, kinds), 1).astype(f32)
    for n, out in enumerate((o_class, o_time)):
        hot = jnp.where(spot == names[:, n : n + 1], 1.0, 0.0)
        out[...] = lax.dot_general(
            hot, cond_grad, (((0,), (0,)), ((), ())), precision=highest,
            preferred_element_type=f32,
        )


def tail(fu, fd, fp, mg, one, two, wmod, classes, times):
    nb = lax.axis_size("batch")
    width = mg.shape[2]
    own = width // nb
    wide = two.shape[1] // nb
    if own % 16:
        wmod = lax.dynamic_slice_in_dim(wmod, lax.axis_index("batch") * own, own, axis=0)
    any_space = pl.BlockSpec(memory_space=pl.ANY)
    vmem = pl.BlockSpec(memory_space=pltpu.VMEM)
    shape = jax.ShapeDtypeStruct
    return pl.pallas_call(
        tail_kernel,
        out_shape=(
            shape((classes, own), f32),
            shape((times, own), f32),
            shape((own, 6 * width), f32),
            shape((own, 3 * width), f32),
            shape((own, width), f32),
            shape((9, own), f32),
            shape((own, 4 * width), f32),
            shape((9, wide), f32),
            shape((4 * fd.shape[2] * fd.shape[3], width), f32),
        ),
        in_specs=[vmem] * 6 + [any_space],
        out_specs=[vmem] * 9,
        scratch_shapes=[pltpu.VMEM((own, 6 * width), bf16), pltpu.SemaphoreType.DMA],
        compiler_params=pltpu.CompilerParams(vmem_limit_bytes=60 << 20),
        name="tail",
    )(fu, fd, fp, mg, one, two, wmod)


def body(
    inputs,
    segments,
    class_labels,
    time_steps,
    class_table,
    time_table,
    modulation_weight,
    project_weight,
    output_weight,
    kernel_attention,
    up_weight,
    kernel_feed,
    down_weight,
    cotangent,
):
    across, width = inputs.shape[2], inputs.shape[3]
    nb = lax.axis_size("batch")
    nz = nb // 2
    rows = width // nb
    units = up_weight.shape[1]
    grain = 16 if (units // nb) % 64 == 0 else 8
    x_frame, cot_frame, returned, tok, proj, att, lse, bias, mod = front(
        inputs, cotangent, class_labels, time_steps, segments, kernel_attention, class_table,
        time_table, modulation_weight, project_weight, output_weight,
    )
    flat = (18 * across, width)
    uq, dq, ul, dl, kern_two, res, mid, rg, small = feed(
        x_frame.reshape(flat), returned.reshape(flat), cot_frame.reshape(flat), mod, up_weight,
        kernel_feed, down_weight, grain,
    )
    fu, fd, fp, result, inputs_gradient, one, two, gathered = back(
        mid, rg.reshape(8, 2, across, width), tok, proj, att, lse, bias, x_frame, mod, small,
        kernel_attention, project_weight, output_weight, res.reshape(16, across, width),
        uq.reshape(nz, 2, rows, width), dq, ul.reshape(2, nz, 2, rows, LANES), dl, kern_two,
    )
    (
        class_total, time_total, modulation_total, project_total, output_total,
        attention_kernel_total, up_total, feed_kernel_total, down_total,
    ) = tail(
        fu, fd, fp, gathered.reshape(2 * nb, 8, width), one, two, modulation_weight,
        class_table.shape[0], time_table.shape[0],
    )
    return (
        result,
        inputs_gradient,
        class_total,
        time_total,
        modulation_total,
        project_total,
        output_total,
        attention_kernel_total,
        up_total,
        feed_kernel_total,
        down_total,
    )


def solution(mesh):
    in_specs = (
        P("batch", "group", None, None),
        P("batch", None),
        P("batch"),
        P("batch"),
        P(),
        P(),
        P(),
        P(),
        P(),
        P(),
        P(),
        P(),
        P(),
        P("batch", "group", None, None),
    )
    out_specs = (
        P("batch", "group", None, None),
        P("batch", "group", None, None),
        P(None, "batch"),
        P(None, "batch"),
        P("batch", None),
        P("batch", None),
        P("batch", None),
        P(None, "batch"),
        P("batch", None),
        P(None, "batch"),
        P("batch", None),
    )
    return jax.shard_map(body, mesh=mesh, in_specs=in_specs, out_specs=out_specs, check_vma=False)
```

```python
from functools import partial

import jax
import jax.numpy as jnp
from jax import lax
from jax.experimental import pallas as pl
from jax.experimental.pallas import tpu as pltpu
from jax.sharding import PartitionSpec as P

HEADS = 12
MESH = pl.DeviceIdType.MESH
LANES = 128
f32 = jnp.float32
bf16 = jnp.bfloat16
highest = lax.Precision.HIGHEST


def dot_nn(a, b):
    return lax.dot_general(a, b, (((1,), (0,)), ((), ())), preferred_element_type=f32)


def dot_nt(a, b):
    return lax.dot_general(a, b, (((1,), (1,)), ((), ())), preferred_element_type=f32)


def dot_tn(a, b):
    return lax.dot_general(a, b, (((0,), (0,)), ((), ())), preferred_element_type=f32)


def remote(src, dst, send, recv, target):
    return pltpu.make_async_remote_copy(
        src_ref=src, dst_ref=dst, send_sem=send, recv_sem=recv, device_id=target,
        device_id_type=MESH,
    )


def meet(partners):
    barrier = pltpu.get_barrier_semaphore()
    for partner in partners:
        pl.semaphore_signal(barrier, inc=1, device_id=partner, device_id_type=MESH)
    pl.semaphore_wait(barrier, len(partners))


def normalize(values):
    center = values - jnp.mean(values, axis=-1, keepdims=True)
    second = jnp.mean(center * center, axis=-1, keepdims=True)
    scale = lax.rsqrt(second + 1e-06)
    return center * scale, scale


def normalize_back(grad, normal, scale):
    return scale * (
        grad
        - jnp.mean(grad, axis=-1, keepdims=True)
        - normal * jnp.mean(grad * normal, axis=-1, keepdims=True)
    )


def column_shifts(row):
    across = row.shape[0]
    column = lax.broadcasted_iota(jnp.int32, row.shape, 0)
    before = jnp.where(column == 0, 0.0, pltpu.roll(row, 1, 0))
    after = jnp.where(column == across - 1, 0.0, pltpu.roll(row, across - 1, 0))
    return before, after


def fold(values):
    rows, width = values.shape
    return jnp.sum(values.reshape(rows // 8, 8, width), axis=0)


def permutation(inverse):
    n = 512
    to = lax.broadcasted_iota(jnp.int32, (n, n), 1 if inverse else 0)
    source = lax.broadcasted_iota(jnp.int32, (n, n), 0 if inverse else 1)
    wanted = lax.shift_left(lax.shift_right_logical(to & 255, 4), 5) + 2 * (to & 15) + (
        lax.shift_right_logical(to, 8)
    )
    return jnp.where(source == wanted, 1.0, 0.0).astype(bf16)


def front_kernel(
    x_in, cot_in, names, moments, segments, kern, class_in, time_in, wmod_in, wqkv_in, wo_in,
    o_x, o_cot, o_ret, o_tok, o_proj, o_att, o_lse, o_bias, mod,
    xf, table, wmod, wqkv, wo, shifts, mixed, rows_m, perm, bias, tok, proj, att, lse, brm,
    load_sem, x_send, x_recv, c_send, c_recv, ex_send, ex_recv, own_sem, out_sem,
):
    b = lax.axis_index("batch")
    g = lax.axis_index("group")
    c, p = lax.rem(g, 2), g // 2
    core, side, corner = (b, g + 1 - 2 * c), (b, g + 2 - 4 * p), (b, 3 - g)
    inner = jnp.logical_or(g == 1, g == 2)
    width = xf.shape[-1]
    across = xf.shape[1]

    def spread_out(src, dst, send, recv, waiting):
        main = c * 8 + p * 2
        other_main = remote(
            src.at[1 - p], dst.at[pl.ds(main, 8)], send.at[0], recv.at[c], (b, 2 - p)
        )
        edge = 6 * (2 - g)
        edge_to = 16 * (g - 1)
        other_edge = remote(
            src.at[1 - p, pl.ds(edge, 2)], dst.at[pl.ds(edge_to, 2)], send.at[1], recv.at[2], side
        )
        own_main = remote(src.at[p], dst.at[pl.ds(main, 8)], send.at[2], recv.at[c], core)
        own_edge = pltpu.make_async_copy(
            src.at[p, pl.ds(edge, 2)], dst.at[pl.ds(edge_to, 2)], recv.at[2]
        )
        stay_main = pltpu.make_async_copy(src.at[p], dst.at[pl.ds(main, 8)], recv.at[c])
        if waiting:
            other_main.wait_send()

            @pl.when(inner)
            def _():
                other_edge.wait_send()
                own_main.wait_send()

        else:
            other_main.start()

            @pl.when(inner)
            def _():
                other_edge.start()
                own_main.start()
                own_edge.start()

            @pl.when(jnp.logical_not(inner))
            def _():
                stay_main.start()

    def arrived(dst, recv):
        for j in range(2):
            place = dst.at[pl.ds(8 * j + 2 * c, 8)]
            pltpu.make_async_copy(place, place, recv.at[j]).wait()
        place = dst.at[pl.ds(16 * (1 - c), 2)]
        pltpu.make_async_copy(place, place, recv.at[2]).wait()

    pieces = [
        (wqkv_in, wqkv), (wo_in, wo), (class_in, table.at[0]), (time_in, table.at[1]),
        (wmod_in, wmod),
    ]
    loads = [
        pltpu.make_async_copy(src, dst, load_sem.at[n]) for n, (src, dst) in enumerate(pieces)
    ]
    for n in (2, 3, 4, 0, 1):
        loads[n].start()
    meet([core, side, corner])
    spread_out(x_in, xf, x_send, x_recv, False)
    perm[0] = permutation(False)
    perm[1] = permutation(True)
    n = tok.shape[0]
    wide = segments.shape[1]
    to = lax.broadcasted_iota(jnp.int32, (n, wide), 0)
    source = lax.broadcasted_iota(jnp.int32, (n, wide), 1)
    wanted = lax.shift_left(2 * lax.shift_right_logical(to & 255, 4) + c, 5) + 2 * (to & 15) + (
        lax.shift_right_logical(to, 8)
    )
    chosen = source == wanted
    one_line = jnp.where(p == 0, segments[0:1, :], segments[1:2, :]).astype(f32)
    lines = jnp.broadcast_to(one_line, (8, wide)).astype(bf16)
    lab_row = dot_nt(lines, jnp.where(chosen, 1.0, 0.0).astype(bf16))
    lab_col = jnp.sum(jnp.where(chosen, one_line, 0.0), axis=-1, keepdims=True)
    for half in range(2):
        cut = slice(half * (n // 2), (half + 1) * (n // 2))
        bias[half] = jnp.where(lab_row[0:1, cut] == lab_col[cut], 0.0, -1e30)
    bias_out = pltpu.make_async_copy(bias, o_bias, out_sem.at[5])
    bias_out.start()
    name = jnp.where(p == 0, names[0], names[1])
    moment = jnp.where(p == 0, moments[0], moments[1])
    loads[2].wait()
    loads[3].wait()
    rows_all = lax.broadcasted_iota(jnp.int32, (8, table.shape[1]), 1)
    cond = dot_nn(jnp.where(rows_all == name, 1.0, 0.0).astype(bf16), table[0]) + dot_nn(
        jnp.where(rows_all == moment, 1.0, 0.0).astype(bf16), table[1]
    )
    cond_low = (cond / (1.0 + jnp.exp(-cond))).astype(bf16)
    loads[4].wait()
    for part in range(6):
        cut = slice(part * width, (part + 1) * width)
        mod[part : part + 1, :] = dot_nn(cond_low, wmod[:, cut])[0:1, :]
    lane_of = lax.broadcasted_iota(jnp.int32, (1, width), 1)
    mod[6:7, :] = jnp.where(
        lane_of == 0, name.astype(f32), jnp.where(lane_of == 1, moment.astype(f32), 0.0)
    )
    mod[7:8, :] = cond[0:1, :]
    arrived(xf, x_recv)
    spread_out(cot_in, o_cot, c_send, c_recv, False)
    x_out = pltpu.make_async_copy(xf, o_x, out_sem.at[0])
    x_out.start()

    shift = mod[0:1, :]
    scale = 1.0 + mod[1:2, :]

    def first(i, carry):
        normal, _ = normalize(xf[c + i].astype(f32))
        value = (normal * scale + shift).astype(bf16).astype(f32)
        before, after = column_shifts(value)
        shifts[0, 1 - c + i] = before
        shifts[1, 1 - c + i] = value
        shifts[2, 1 - c + i] = after
        return carry

    lax.fori_loop(0, 17, first, 0)
    for s in range(3):
        shifts[s, 17 * c] = jnp.zeros((across, width), f32)

    def conv(step, parity):
        o = 2 * step + parity
        for lane in range(0, width, LANES):
            cut = slice(lane, lane + LANES)
            total = jnp.zeros((across, LANES), f32)
            for r in range(3):
                for s in range(3):
                    tap = kern[3 * r + s : 3 * r + s + 1, cut].astype(f32)
                    total = total + tap * shifts[s, o + r, :, cut]
            mixed[step, parity, :, cut] = total.astype(bf16)

    def conv_away(step, carry):
        conv(step, 1 - c)
        return carry

    def conv_own(step, carry):
        conv(step, c)
        return carry

    lax.fori_loop(0, 8, conv_away, 0)
    mixed_away = remote(
        mixed.at[:, 1 - c], rows_m.at[pl.ds(8 * c, 8)], ex_send.at[0], ex_recv.at[0], core
    )
    mixed_away.start()
    lax.fori_loop(0, 8, conv_own, 0)
    mixed_own = pltpu.make_async_copy(mixed.at[:, c], rows_m.at[pl.ds(8 * c, 8)], own_sem.at[0])
    mixed_own.start()
    mixed_own.wait()
    mixed_away.wait()
    flat = rows_m[...].reshape(16 * across, width)
    tok[...] = dot_nn(perm[0], flat).astype(bf16)
    tok_out = pltpu.make_async_copy(tok, o_tok, out_sem.at[1])
    tok_out.start()
    loads[0].wait()
    for part in range(3):
        cut = slice(part * width, (part + 1) * width)
        proj[:, cut] = dot_nn(tok[...], wqkv[:, cut]).astype(bf16)
    proj_out = pltpu.make_async_copy(proj, o_proj, out_sem.at[2])
    proj_out.start()

    pairs = width // LANES
    size = tok.shape[0] // 2
    low_lane = lax.broadcasted_iota(jnp.int32, (size, LANES), 1) < LANES // 2
    lane_id = lax.broadcasted_iota(jnp.int32, (size, LANES), 1)
    zero = jnp.zeros((), bf16)

    def attend(index, carry):
        half, pair = index // pairs, lax.rem(index, pairs)
        rows = pl.ds(pl.multiple_of(half * size, size), size)

        def part(n):
            return proj[rows, pl.ds(pl.multiple_of(n * width + pair * LANES, LANES), LANES)]

        q, k, v = part(0) * jnp.asarray(0.125, bf16), part(1), part(2)
        total = jnp.zeros((size, LANES), f32)
        sums = lse[half]
        for h in range(2):
            mine = low_lane if h == 0 else jnp.logical_not(low_lane)
            scores = dot_nt(q, jnp.where(mine, k, zero)) + bias[half]
            top = jnp.max(scores, axis=-1, keepdims=True)
            powers = jnp.exp(scores - top)
            mass = jnp.sum(powers, axis=-1, keepdims=True)
            weights = (powers * (1.0 / mass)).astype(bf16)
            total = total + dot_nn(weights, jnp.where(mine, v, zero))
            sums = jnp.where(lane_id == 2 * pair + h, top + jnp.log(mass), sums)
        lse[half] = sums
        att[rows, pl.ds(pl.multiple_of(pair * LANES, LANES), LANES)] = total.astype(bf16)
        return carry

    lse[...] = jnp.zeros(lse.shape, f32)
    lax.fori_loop(0, 2 * pairs, attend, 0)
    att_out = pltpu.make_async_copy(att, o_att, out_sem.at[3])
    att_out.start()
    lse_out = pltpu.make_async_copy(lse, o_lse, out_sem.at[4])
    lse_out.start()
    loads[1].wait()
    branch = dot_nn(att[...], wo[...]).astype(bf16)
    brm[...] = dot_nn(perm[1], branch).astype(bf16).reshape(16, across, width)
    ret_away = remote(
        brm.at[pl.ds(7 * (1 - c), 9)], o_ret.at[:, c], ex_send.at[1], ex_recv.at[1], core
    )
    ret_away.start()
    ret_own = pltpu.make_async_copy(brm.at[pl.ds(7 * c, 9)], o_ret.at[:, c], own_sem.at[1])
    ret_own.start()
    for out in (x_out, tok_out, proj_out, att_out, lse_out, bias_out, ret_own):
        out.wait()
    ret_away.wait()
    spread_out(x_in, xf, x_send, x_recv, True)
    spread_out(cot_in, o_cot, c_send, c_recv, True)
    arrived(o_cot, c_recv)


def front(inputs, cotangent, names, moments, segments, kern, classes, times, wmod, wqkv, wo):
    across, width = inputs.shape[2], inputs.shape[3]
    tokens = 16 * across
    any_space = pl.BlockSpec(memory_space=pl.ANY)
    vmem = pl.BlockSpec(memory_space=pltpu.VMEM)
    smem = pl.BlockSpec(memory_space=pltpu.SMEM)
    shape = jax.ShapeDtypeStruct
    dma = pltpu.SemaphoreType.DMA
    return pl.pallas_call(
        front_kernel,
        out_shape=(
            shape((18, across, width), bf16),
            shape((18, across, width), bf16),
            shape((9, 2, across, width), bf16),
            shape((tokens, width), bf16),
            shape((tokens, 3 * width), bf16),
            shape((tokens, width), bf16),
            shape((2, tokens // 2, LANES), f32),
            shape((2, tokens // 2, tokens // 2), f32),
            shape((8, width), f32),
        ),
        in_specs=[any_space] * 2 + [smem] * 2 + [vmem] * 2 + [any_space] * 5,
        out_specs=[any_space] * 8 + [vmem],
        scratch_shapes=[
            pltpu.VMEM((18, across, width), bf16),
            pltpu.VMEM((2, *classes.shape), bf16),
            pltpu.VMEM(wmod.shape, bf16),
            pltpu.VMEM(wqkv.shape, bf16),
            pltpu.VMEM(wo.shape, bf16),
            pltpu.VMEM((3, 18, across, width), f32),
            pltpu.VMEM((8, 2, across, width), bf16),
            pltpu.VMEM((16, across, width), bf16),
            pltpu.VMEM((2, tokens, tokens), bf16),
            pltpu.VMEM((2, tokens // 2, tokens // 2), f32),
            pltpu.VMEM((tokens, width), bf16),
            pltpu.VMEM((tokens, 3 * width), bf16),
            pltpu.VMEM((tokens, width), bf16),
            pltpu.VMEM((2, tokens // 2, LANES), f32),
            pltpu.VMEM((16, across, width), bf16),
            dma((5,)), dma((3,)), dma((3,)), dma((3,)), dma((3,)), dma((2,)), dma((2,)),
            dma((2,)), dma((6,)),
        ],
        compiler_params=pltpu.CompilerParams(
            collective_id=1, has_side_effects=True, vmem_limit_bytes=60 << 20
        ),
        name="front",
    )(inputs, cotangent, names, moments, segments, kern, classes, times, wmod, wqkv, wo)


def gelu_parts(x):
    size = jnp.abs(x)
    t = 1.0 / (1.0 + (0.3275911 * 0.7071067811865476) * size)
    bell = jnp.exp(-0.5 * x * x)
    series = t * (
        0.254829592
        + t * (-0.284496736 + t * (1.421413741 + t * (-1.453152027 + t * 1.061405429)))
    )
    tail = 0.5 * series * bell
    mass = jnp.where(x >= 0, 1.0 - tail, tail)
    return x * mass, mass + x * bell * 0.3989422804014327


def feed_kernel(
    x_in, ret_in, cot_in, mod, up, kern, down,
    o_up, o_down, o_up_half, o_up_last, o_down_last, o_kern, o_res, o_mid, o_rg, o_small,
    feed_in, feed_t, btg, out_acc, back_acc, hid, hs, gs, act, slope, hg,
    wu, wd, ru, rd, yu, xu, zu, fin, xd,
    u1_send, u1_recv, u2_send, u2_recv, u3_send, u3_recv, d1_send, d1_recv, d2_send, d2_recv,
    u4_send, u4_recv, u_out, d_out, l_out,
):
    j = pl.program_id(0)
    tiles = pl.num_programs(0)
    b = lax.axis_index("batch")
    g = lax.axis_index("group")
    c, p = lax.rem(g, 2), g // 2
    nz = wu.shape[3]
    yb, zb = lax.rem(b, 2), b // 2
    core, side, beside = (b, g + 1 - 2 * c), (b, g + 2 - 4 * p), (b + 1 - 2 * yb, g)
    others = [lax.rem(zb + d, nz) for d in range(nz)]
    far = [(2 * z + yb, g) for z in others]
    parts = wd.shape[3]

    def up_1(t):
        return remote(wu.at[t, 1 - c], ru.at[t], u1_send.at[t], u1_recv.at[t], core)

    def down_1(t):
        return remote(wd.at[t, 1 - c], rd.at[t], d1_send.at[t], d1_recv.at[t], core)

    def up_2(t):
        return remote(wu.at[t, c, :, :, 1 - yb], yu.at[t], u2_send.at[t], u2_recv.at[t], beside)

    def down_2(t):
        return remote(wd.at[t, c, 1 - p], xd.at[t], d2_send.at[t], d2_recv.at[t], side)

    def up_3(t):
        return remote(wu.at[t, c, 1 - p, :, yb], xu.at[t], u3_send.at[t], u3_recv.at[t], side)

    def up_4(t, d):
        return remote(
            wu.at[t, c, p, others[d], yb], zu.at[t, d - 1], u4_send.at[t, d - 1],
            u4_recv.at[t, d - 1], far[d],
        )

    def up_store(t):
        spot = pl.ds(pl.multiple_of(t * LANES, LANES), LANES)
        return pltpu.make_async_copy(fin.at[t], o_up.at[:, spot], u_out.at[t])

    def down_store(t):
        return pltpu.make_async_copy(
            wd.at[t, c, p], o_down.at[pl.ds(t * parts, parts)], d_out.at[t]
        )

    def add_core(t):
        down_1(t).wait_recv()
        up_1(t).wait_recv()

        def step(i, carry):
            x, z, y = i // (2 * nz), lax.rem(i // 2, nz), lax.rem(i, 2)
            wu[t, c, x, z, y] = wu[t, c, x, z, y] + ru[t, x, z, y]
            return carry

        lax.fori_loop(0, 4 * nz, step, 0)

        def step_down(i, carry):
            x, n = i // 8, lax.rem(i, 8)
            for k in range(parts // 8):
                wd[t, c, x, n * (parts // 8) + k] = (
                    wd[t, c, x, n * (parts // 8) + k] + rd[t, x, n * (parts // 8) + k]
                )
            return carry

        lax.fori_loop(0, 16, step_down, 0)

    def add_beside(t):
        up_2(t).wait_recv()

        def step(i, carry):
            x, z = i // nz, lax.rem(i, nz)
            wu[t, c, x, z, yb] = wu[t, c, x, z, yb] + yu[t, x, z]
            return carry

        lax.fori_loop(0, 2 * nz, step, 0)

    def add_side(t):
        up_3(t).wait_recv()

        def step(z, carry):
            wu[t, c, p, z, yb] = wu[t, c, p, z, yb] + xu[t, z]
            return carry

        lax.fori_loop(0, nz, step, 0)
        for d in range(1, nz):
            up_4(t, d).start()

    def add_far(t):
        total = wu[t, c, p, zb, yb].astype(f32)
        for d in range(1, nz):
            up_4(t, d).wait_recv()
            total = total + zu[t, d - 1].astype(f32)
        fin[t] = total.astype(bf16)
        up_store(t).start()

    def add_side_down(t):
        down_2(t).wait_recv()

        def step(n, carry):
            for k in range(parts // 8):
                wd[t, c, p, n * (parts // 8) + k] = (
                    wd[t, c, p, n * (parts // 8) + k] + xd[t, n * (parts // 8) + k]
                )
            return carry

        lax.fori_loop(0, 8, step, 0)
        down_store(t).start()

    across = 32
    width = feed_in.shape[1]
    tile = up.shape[1]
    frame_rows = feed_in.shape[0] // across
    own = pl.ds(pl.multiple_of(2 * c * across, 64), 16 * across)

    def middle_of(row):
        place = pl.ds(pl.multiple_of(row * across, across), across)
        returned = ret_in[place, :].astype(f32)
        return x_in[place, :].astype(f32) + mod[2:3, :] * returned, returned

    @pl.when(j == 0)
    def _():
        meet([core, side, beside, *far[1:]])

        def prepare(row, carry):
            place = pl.ds(pl.multiple_of(row * across, across), across)
            normal, _ = normalize(middle_of(row)[0])
            feed_in[place, :] = (normal * (1.0 + mod[4:5, :]) + mod[3:4, :]).astype(bf16)
            btg[place, :] = (mod[5:6, :] * cot_in[place, :].astype(f32)).astype(bf16)
            return carry

        lax.fori_loop(0, frame_rows, prepare, 0)
        feed_t[...] = feed_in[own, :].T
        out_acc[...] = jnp.zeros(out_acc.shape, f32)
        back_acc[...] = jnp.zeros(back_acc.shape, f32)
        for s in range(3):
            hs[s, 18 * c] = jnp.zeros((across, tile), f32)
            gs[s, 17 * c] = jnp.zeros((across, tile), f32)

    hid[...] = dot_nn(feed_in[...], up[...]).astype(bf16)

    def lay_hidden(row, carry):
        value = hid[pl.ds(pl.multiple_of(row * across, across), across), :].astype(f32)
        before, after = column_shifts(value)
        hs[0, 1 - c + row] = before
        hs[1, 1 - c + row] = value
        hs[2, 1 - c + row] = after
        return carry

    lax.fori_loop(0, frame_rows, lay_hidden, 0)

    for lane in range(0, tile, LANES):
        cut = slice(lane, lane + LANES)
        taps = [kern[n : n + 1, cut].astype(f32) for n in range(9)]

        def forward(row, carry):
            total = jnp.zeros((across, LANES), f32)
            for r in range(3):
                for s in range(3):
                    total = total + taps[3 * r + s] * hs[s, row + r, :, cut]
            place = pl.ds(pl.multiple_of(row * across, across), across)
            value, steep = gelu_parts(total)
            act[place, cut] = value.astype(bf16)
            slope[place, cut] = steep
            return carry

        lax.fori_loop(0, 17, forward, 0)

    @pl.when(j >= 2)
    def _():
        add_side(j - 2)
        add_side_down(j - 2)

    @pl.when(j >= 1)
    def _():
        add_core(j - 1)
        up_2(j - 1).start()
        down_2(j - 1).start()

    @pl.when(j >= 3)
    def _():
        add_far(j - 3)

    inside = pl.ds(pl.multiple_of(c * across, across), 16 * across)
    around = pl.ds(pl.multiple_of(c * across, across), 17 * across)
    own_act = act[inside, :]
    out_acc[...] += dot_nn(own_act, down[...])
    grad_down = dot_tn(own_act, btg[own, :]).reshape(parts, 4, wd.shape[4], width)
    for q in range(4):
        wd[j, q % 2, q // 2] = grad_down[:, q].astype(bf16)
    down_1(j).start()
    slope[...] = slope[...] * dot_nt(btg[around, :], down[...])

    def lay_grad(row, carry):
        value = slope[pl.ds(pl.multiple_of(row * across, across), across), :]
        value = value.astype(bf16).astype(f32)
        before, after = column_shifts(value)
        gs[0, 1 - c + row] = after
        gs[1, 1 - c + row] = value
        gs[2, 1 - c + row] = before
        return carry

    lax.fori_loop(0, 17, lay_grad, 0)

    for lane in range(0, tile, LANES):
        cut = slice(lane, lane + LANES)
        taps = [kern[n : n + 1, cut].astype(f32) for n in range(9)]

        def backward(row, sums):
            total = jnp.zeros((across, LANES), f32)
            value = hs[1, row + c + 1, :, cut]
            later = []
            for r in range(3):
                for s in range(3):
                    grad = gs[s, row + 2 - r, :, cut]
                    total = total + taps[3 * r + s] * grad
                    later.append(sums[3 * r + s] + fold(value * grad))
            hg[pl.ds(pl.multiple_of(row * across, across), across), cut] = total.astype(bf16)
            return tuple(later)

        sums = lax.fori_loop(
            0, 16, backward, tuple(jnp.zeros((8, LANES), f32) for _ in range(9))
        )
        for n in range(9):
            o_kern[n : n + 1, cut] = jnp.sum(sums[n], axis=0, keepdims=True)

    o_kern[9:16, :] = jnp.zeros((7, tile), f32)
    grad_up = dot_nn(feed_t[...], hg[...])
    for q in range(4):
        part = grad_up[:, q * LANES : (q + 1) * LANES]
        wu[j, q % 2, q // 2] = part.reshape(nz, 2, wu.shape[5], LANES).astype(bf16)
    up_1(j).start()
    back_acc[...] += dot_nt(hg[...], up[...])

    @pl.when(jnp.logical_and(j >= 1, j < tiles - 1))
    def _():
        add_beside(j - 1)
        up_3(j - 1).start()

    @pl.when(j == tiles - 1)
    def _():
        def finish(row, sums):
            frame = row + 2 * c
            place = pl.ds(pl.multiple_of(row * across, across), across)
            at = pl.ds(pl.multiple_of(frame * across, across), across)
            middle, returned = middle_of(frame)
            cot = cot_in[at, :].astype(f32)
            branch = out_acc[place, :]
            o_res[place, :] = (middle + mod[5:6, :] * branch).astype(bf16)
            normal, scale = normalize(middle)
            grad = back_acc[place, :]
            mid = cot + normalize_back(grad * (1.0 + mod[4:5, :]), normal, scale)
            o_mid[place, :] = mid
            o_rg[place, :] = (mod[2:3, :] * mid).astype(bf16)
            terms = (mid * returned, grad, grad * normal, cot * branch)
            return tuple(total + fold(term) for total, term in zip(sums, terms))

        sums = lax.fori_loop(
            0, 16, finish, tuple(jnp.zeros((8, width), f32) for _ in range(4))
        )
        o_small[...] = jnp.zeros((8, width), f32)
        for n in range(4):
            o_small[n + 2 : n + 3, :] = jnp.sum(sums[n], axis=0, keepdims=True)
        add_far(j - 2)
        add_beside(j - 1)
        half = pltpu.make_async_copy(wu.at[j - 1, c, :, :, yb], o_up_half, l_out.at[2])
        half.start()
        add_side_down(j - 1)
        add_core(j)
        last = (
            half,
            pltpu.make_async_copy(wu.at[j, c], o_up_last, l_out.at[0]),
            pltpu.make_async_copy(wd.at[j, c], o_down_last, l_out.at[1]),
        )
        for move in last[1:]:
            move.start()

        def settle(t, carry):
            up_3(t).wait_send()
            for d in range(1, nz):
                up_4(t, d).wait_send()
            up_store(t).wait()
            return carry

        def settle_more(t, carry):
            up_2(t).wait_send()
            down_2(t).wait_send()
            up_1(t).wait_send()
            down_1(t).wait_send()
            down_store(t).wait()
            return carry

        lax.fori_loop(0, tiles - 2, settle, 0)
        lax.fori_loop(0, tiles - 1, settle_more, 0)
        up_1(j).wait_send()
        down_1(j).wait_send()
        for move in last:
            move.wait()


def feed(x_frame, returned, cot_frame, mod, up, kern, down, grain):
    width, units = up.shape
    frame = x_frame.shape[0]
    across = frame // 18
    tokens = 16 * across
    shape = jax.ShapeDtypeStruct
    dma = pltpu.SemaphoreType.DMA
    any_space = pl.BlockSpec(memory_space=pl.ANY)
    tile = 4 * LANES
    tiles = units // tile
    parts = tile // (4 * grain)
    nb = lax.axis_size("batch")
    nz = nb // 2
    own = width // nb
    many = max(nz - 1, 1)

    def still(*size):
        return pl.BlockSpec(size, lambda j: (0, 0), pipeline_mode=pl.Buffered(1))

    columns = pl.BlockSpec((width, tile), lambda j: (0, j))
    rows = pl.BlockSpec((tile, width), lambda j: (j, 0))
    work = 6 * 2 * tokens * width * units
    return pl.pallas_call(
        feed_kernel,
        grid=(units // tile,),
        out_shape=(
            shape((own, (tiles - 2) * LANES), bf16),
            shape((tiles * parts, grain, width), bf16),
            shape((2, nz, own, LANES), bf16),
            shape((2, nz, 2, own, LANES), bf16),
            shape((2, parts, grain, width), bf16),
            shape((16, units), f32),
            shape((tokens, width), bf16),
            shape((tokens, width), f32),
            shape((tokens, width), bf16),
            shape((8, width), f32),
        ),
        in_specs=[
            still(frame, width), still(frame, width), still(frame, width), still(8, width),
            columns, pl.BlockSpec((9, tile), lambda j: (0, j)), rows,
        ],
        out_specs=[
            *[any_space] * 5, pl.BlockSpec((16, tile), lambda j: (0, j)),
            still(tokens, width), still(tokens, width), still(tokens, width), still(8, width),
        ],
        scratch_shapes=[
            pltpu.VMEM((frame, width), bf16),
            pltpu.VMEM((width, tokens), bf16),
            pltpu.VMEM((frame, width), bf16),
            pltpu.VMEM((tokens, width), f32),
            pltpu.VMEM((tokens, width), f32),
            pltpu.VMEM((frame, tile), bf16),
            pltpu.VMEM((3, 19, across, tile), f32),
            pltpu.VMEM((3, 18, across, tile), f32),
            pltpu.VMEM((17 * across, tile), bf16),
            pltpu.VMEM((17 * across, tile), f32),
            pltpu.VMEM((tokens, tile), bf16),
            pltpu.VMEM((tiles, 2, 2, nz, 2, own, LANES), bf16),
            pltpu.VMEM((tiles, 2, 2, parts, grain, width), bf16),
            pltpu.VMEM((tiles, 2, nz, 2, own, LANES), bf16),
            pltpu.VMEM((tiles, 2, parts, grain, width), bf16),
            pltpu.VMEM((tiles, 2, nz, own, LANES), bf16),
            pltpu.VMEM((tiles, nz, own, LANES), bf16),
            pltpu.VMEM((tiles, many, own, LANES), bf16),
            pltpu.VMEM((tiles, own, LANES), bf16),
            pltpu.VMEM((tiles, parts, grain, width), bf16),
            *[dma((tiles,)) for _ in range(10)],
            dma((tiles, many)), dma((tiles, many)), dma((tiles,)), dma((tiles,)), dma((3,)),
        ],
        compiler_params=pltpu.CompilerParams(
            dimension_semantics=("arbitrary",), collective_id=3, has_side_effects=True,
            vmem_limit_bytes=62 << 20,
        ),
        cost_estimate=pl.CostEstimate(
            flops=work, bytes_accessed=8 * width * units, transcendentals=tokens * units
        ),
        name="feed",
    )(x_frame, returned, cot_frame, mod, up, kern, down)


def back_kernel(
    mid_in, rg_in, tok_in, proj_in, att_in, lse, bias, x_in, mod, small, kern, wqkv_in, wo_in,
    res_in, ud_in, dq_in, uh_in, ul_in, dl_in, kern_two,
    o_fu, o_fd, o_fp, o_res, o_ig, o_one, o_two, o_mg, o_ml,
    mid, tok, tok_t, proj, att, xf, wqkv, wo, rows_m, perm, grad, datt, dproj,
    brm, frame, gs, value, agrad, ig,
    wp, p_r1, p_r2x, p_r2y, p_r3, p_r4, fin_p,
    fu, fd, fz_u, fy_d, fz_d, fin_u, fin_d, ld, lx_d, hx, ly, ly_r, lx,
    mg_own, mg_r1, mg_all, ml_own, ml_r1, ml_all, taps_sum, kk_1, kr_1, kz_1, kk_2, kr_2, kz_2,
    load_sem, r_send, r_recv, i_send, i_recv, ex_send, ex_recv, own_sem, send_sem, recv_sem, out_sem,
):
    b = lax.axis_index("batch")
    g = lax.axis_index("group")
    nz = fu.shape[0]
    c, p = lax.rem(g, 2), g // 2
    yb, zb = lax.rem(b, 2), b // 2
    core, side, corner = (b, g + 1 - 2 * c), (b, g + 2 - 4 * p), (b, 3 - g)
    beside = (b + 1 - 2 * yb, g)
    others = [lax.rem(zb + d, nz) for d in range(nz)]
    far = [(2 * z + yb, g) for z in others]
    inner = jnp.logical_or(g == 1, g == 2)
    across, width = xf.shape[1], xf.shape[2]
    rows_own = fu.shape[1]
    pairs = width // LANES
    tokens = tok.shape[0]
    size = tokens // 2
    chunks = wp.shape[0]
    chunk = wp.shape[-1]
    lead = width - 2 * LANES
    per, parts = fd.shape[2], ld.shape[0]
    places = {}

    def link(name, src, dst, target):
        n = places.setdefault(name, len(places))
        return remote(src, dst, send_sem.at[n], recv_sem.at[n], target)

    def send_home(n, src, dst, send, recv, waiting):
        move = remote(src.at[pl.ds(8 * n, 8)], dst.at[p], send.at[n], recv.at[p], (b, 2 * c + n))
        away = remote(src.at[pl.ds(8 * n, 8)], dst.at[p], send.at[n], recv.at[p], core)
        stay = pltpu.make_async_copy(src.at[pl.ds(8 * n, 8)], dst.at[p], recv.at[p])

        @pl.when(inner)
        def _():
            if waiting:
                move.wait_send()
            else:
                move.start()

        @pl.when(jnp.logical_and(jnp.logical_not(inner), c != n))
        def _():
            if waiting:
                away.wait_send()
            else:
                away.start()

        if not waiting:

            @pl.when(jnp.logical_and(jnp.logical_not(inner), c == n))
            def _():
                stay.start()

    def home(dst, recv):
        for n in range(2):
            pltpu.make_async_copy(dst.at[n], dst.at[n], recv.at[n]).wait()

    def gone(moves):
        for move in moves:
            move.wait_send()

    def half_x():
        return link("hx", uh_in.at[1 - p], hx, side)

    def last_y():
        return link("ly", ul_in.at[:, :, 1 - yb], ly_r, beside)

    def last_x():
        return link("lx", ly.at[1 - p], lx, side)

    def last_d():
        return link("ld", dl_in.at[1 - p], lx_d, side)

    def down_y():
        return link("fdy", fd.at[:, 1 - yb], fy_d, beside)

    def up_z(d):
        return link(f"fuz{d}", fu.at[others[d]], fz_u.at[d - 1], far[d])

    def down_z(d):
        return link(f"fdz{d}", fd.at[others[d], yb], fz_d.at[d - 1], far[d])

    def to_side(name, fin, mine):
        x = p if mine else 1 - p
        return link(f"{name}x", fin.at[c, x], fin.at[c, x], side)

    def to_core(name, fin, mine):
        x = c if mine else 1 - c
        return link(f"{name}c", fin.at[x], fin.at[x], core)

    def half_add():
        early[0].wait()
        half_x().wait_recv()

        def step(z, carry):
            fu[z, :, :LANES] = fu[z, :, :LANES] + hx[z]
            return carry

        lax.fori_loop(0, nz, step, 0)

    def last_y_add():
        early[1].wait()
        last_y().wait_recv()

        def step(i, carry):
            x, z = i // nz, lax.rem(i, nz)
            ly[x, z] = ly[x, z] + ly_r[x, z]
            return carry

        lax.fori_loop(0, 2 * nz, step, 0)
        last_x().start()

    def last_x_add():
        last_x().wait_recv()

        def step(z, carry):
            fu[z, :, LANES:] = ly[p, z] + lx[z]
            return carry

        lax.fori_loop(0, nz, step, 0)
        for d in range(1, nz):
            up_z(d).start()

    def up_sum():
        early[2].wait()
        total = fu[zb].astype(f32)
        for d in range(1, nz):
            up_z(d).wait_recv()
            total = total + fz_u[d - 1].astype(f32)
        fin_u[c, p, :, lead:] = total.astype(bf16)
        to_side("gu", fin_u, True).start()

    def place_last():
        for load in late:
            load.wait()
        last_d().wait_recv()
        for t in range(parts):
            spot = 2 * nz * per - parts + t
            owner = spot // per
            fd[owner // 2, owner % 2, spot % per] = ld[t] + lx_d[t]
        down_y().start()

    def down_y_add():
        down_y().wait_recv()

        def step(z, carry):
            fd[z, yb] = fd[z, yb] + fy_d[z]
            return carry

        lax.fori_loop(0, nz, step, 0)
        for d in range(1, nz):
            down_z(d).start()

    def down_sum():
        total = fd[zb, yb].astype(f32)
        for d in range(1, nz):
            down_z(d).wait_recv()
            total = total + fz_d[d - 1].astype(f32)
        fin_d[c, p] = total.astype(bf16)
        to_side("gd", fin_d, True).start()

    def pass_on(name, fin):
        to_side(name, fin, False).wait_recv()
        to_core(name, fin, True).start()

    u_out = pltpu.make_async_copy(fin_u, o_fu, out_sem.at[0])
    d_out = pltpu.make_async_copy(fin_d, o_fd, out_sem.at[1])
    p_out = pltpu.make_async_copy(fin_p, o_fp, out_sem.at[2])
    mg_out = pltpu.make_async_copy(mg_all, o_mg, out_sem.at[3])
    ml_out = pltpu.make_async_copy(ml_all, o_ml, out_sem.at[4])

    def side_first(k):
        return k % 2 == 0

    def p1(k):
        return link(f"p1{k}", wp.at[k, 1 - c], p_r1.at[k], core)

    def p2(k):
        if side_first(k):
            return link(f"p2{k}", wp.at[k, c, 1 - p], p_r2x.at[k], side)
        return link(f"p2{k}", wp.at[k, c, :, :, 1 - yb], p_r2y.at[k], beside)

    def p3(k):
        if side_first(k):
            return link(f"p3{k}", wp.at[k, c, p, :, 1 - yb], p_r3.at[k], beside)
        return link(f"p3{k}", wp.at[k, c, 1 - p, :, yb], p_r3.at[k], side)

    def p4(k, d):
        return link(
            f"p4{k}{d}", wp.at[k, c, p, others[d], yb], p_r4.at[k, d - 1], far[d]
        )

    def p_side(k, mine):
        x = p if mine else 1 - p
        return link(f"p5{k}", fin_p.at[k, c, x], fin_p.at[k, c, x], side)

    def p_core(k, mine):
        x = c if mine else 1 - c
        return link(f"p6{k}", fin_p.at[k, x], fin_p.at[k, x], core)

    def p_add_1(k):
        p1(k).wait_recv()

        def step(i, carry):
            x, z, y = i // (2 * nz), lax.rem(i // 2, nz), lax.rem(i, 2)
            wp[k, c, x, z, y] = wp[k, c, x, z, y] + p_r1[k, x, z, y]
            return carry

        lax.fori_loop(0, 4 * nz, step, 0)
        p2(k).start()

    def p_add_2(k):
        p2(k).wait_recv()

        def step(i, carry):
            if side_first(k):
                z, y = i // 2, lax.rem(i, 2)
                wp[k, c, p, z, y] = wp[k, c, p, z, y] + p_r2x[k, z, y]
            else:
                x, z = i // nz, lax.rem(i, nz)
                wp[k, c, x, z, yb] = wp[k, c, x, z, yb] + p_r2y[k, x, z]
            return carry

        lax.fori_loop(0, 2 * nz, step, 0)
        p3(k).start()

    def p_add_3(k):
        p3(k).wait_recv()

        def step(z, carry):
            wp[k, c, p, z, yb] = wp[k, c, p, z, yb] + p_r3[k, z]
            return carry

        lax.fori_loop(0, nz, step, 0)
        for d in range(1, nz):
            p4(k, d).start()

    def p_add_4(k):
        total = wp[k, c, p, zb, yb].astype(f32)
        for d in range(1, nz):
            p4(k, d).wait_recv()
            total = total + p_r4[k, d - 1].astype(f32)
        fin_p[k, c, p] = total.astype(bf16)
        p_side(k, True).start()

    def p_pass(k):
        p_side(k, False).wait_recv()
        p_core(k, True).start()

    peers = [core, side, beside]

    def kern_copy(name, kk, kr, stage):
        return link(f"{name}{stage}", kk.at[stage], kr.at[stage], peers[stage])

    def kern_far(name, kk, kz, d):
        return link(f"{name}z{d}", kk.at[3], kz.at[d - 1], far[d])

    def kern_step(name, kk, kr, kz, stage):
        kern_copy(name, kk, kr, stage).wait_recv()
        kk[stage + 1] = (kk[stage].astype(f32) + kr[stage].astype(f32)).astype(bf16)
        if stage < 2:
            kern_copy(name, kk, kr, stage + 1).start()
        else:
            for d in range(1, nz):
                kern_far(name, kk, kz, d).start()

    def kern_sum(name, kk, kz, out):
        total = kk[3].astype(f32)
        for d in range(1, nz):
            kern_far(name, kk, kz, d).wait_recv()
            total = total + kz[d - 1].astype(f32)
        out[...] = total

    one = ("one", kk_1, kr_1, kz_1)
    two = ("two", kk_2, kr_2, kz_2)

    def mg_copy(part, stage, mine=True):
        name, own, first, every = part
        if stage == 0:
            return link(f"{name}0", own, first, core)
        x = p if mine else 1 - p
        y = yb if mine else 1 - yb
        place = every.at[zb, yb, x] if stage == 1 else every.at[zb, y]
        return link(f"{name}{stage}", place, place, peers[stage])

    def mg_far(part, d, z):
        return link(f"{part[0]}z{d}", part[3].at[z], part[3].at[z], far[d])

    def mg_step(part, stage):
        name, own, first, every = part
        mg_copy(part, stage, False).wait_recv()
        if stage == 0:
            every[zb, yb, p] = own[...] + first[...]
        if stage < 2:
            mg_copy(part, stage + 1).start()
        else:
            for d in range(1, nz):
                mg_far(part, d, zb).start()

    def mg_end(part):
        for d in range(1, nz):
            mg_far(part, d, lax.rem(zb + nz - d, nz)).wait_recv()

    soon = ("mg", mg_own, mg_r1, mg_all)
    final = ("ml", ml_own, ml_r1, ml_all)

    pieces = [
        (wo_in, wo), (att_in, att), (tok_in, tok), (proj_in, proj), (wqkv_in, wqkv), (x_in, xf),
        (mid_in, mid),
    ]
    loads = [
        pltpu.make_async_copy(src, dst, load_sem.at[n]) for n, (src, dst) in enumerate(pieces)
    ]
    full = dq_in.shape[0] - parts
    early = [
        pltpu.make_async_copy(uh_in.at[p], fu.at[:, :, pl.ds(0, LANES)], load_sem.at[7]),
        pltpu.make_async_copy(ul_in.at[:, :, yb], ly, load_sem.at[8]),
        pltpu.make_async_copy(ud_in, fin_u.at[c, p, :, pl.ds(0, lead)], load_sem.at[9]),
    ]
    late = [pltpu.make_async_copy(dl_in.at[p], ld, load_sem.at[10])]
    for owner in range(2 * nz):
        count = min(per, full - owner * per)
        if count > 0:
            late.append(
                pltpu.make_async_copy(
                    dq_in.at[pl.ds(owner * per, count)],
                    fd.at[owner // 2, owner % 2, pl.ds(0, count)],
                    load_sem.at[11 + owner],
                )
            )
    for load in (*loads[:4], *late, *early, *loads[4:]):
        load.start()
    kk_2[0] = kern_two[...].astype(bf16)
    mg_own[...] = small[...]
    mg_own[6:8, :] = mod[6:8, :]
    meet([core, side, corner, beside, *far[1:]])
    grad_away = remote(
        rg_in.at[:, 1 - c], rows_m.at[pl.ds(8 * c, 8)], ex_send.at[0], ex_recv.at[0], core
    )
    grad_away.start()
    grad_own = pltpu.make_async_copy(rg_in.at[:, c], rows_m.at[pl.ds(8 * c, 8)], own_sem.at[0])
    grad_own.start()
    last_d().start()
    last_y().start()
    half_x().start()
    kern_copy("two", kk_2, kr_2, 0).start()
    mg_copy(soon, 0).start()
    perm[0] = permutation(False)
    perm[1] = permutation(True)
    grad_own.wait()
    grad_away.wait()
    grad[...] = dot_nn(perm[0], rows_m[...].reshape(tokens, width)).astype(bf16)
    loads[0].wait()
    loads[1].wait()
    datt[...] = dot_nt(grad[...], wo[...]).astype(bf16)
    out_grad = dot_tn(att[...], grad[...])
    for k in range(chunks):
        cut = slice(k * chunk, (k + 1) * chunk)
        wp[k, 1, 1] = out_grad[:, cut].reshape(nz, 2, rows_own, chunk).astype(bf16)
    loads[2].wait()
    tok_t[...] = tok[...].T
    loads[3].wait()
    place_last()
    for n in range(2):
        send_home(n, res_in, o_res, r_send, r_recv, False)
    kern_step(*two, 0)
    mg_step(soon, 0)

    low_lane = lax.broadcasted_iota(jnp.int32, (size, LANES), 1) < LANES // 2
    lane_id = lax.broadcasted_iota(jnp.int32, (size, LANES), 1)
    zero = jnp.zeros((), bf16)

    def attend(index, carry):
        pair, half = index // 2, lax.rem(index, 2)
        rows = pl.ds(pl.multiple_of(half * size, size), size)

        def cut(n):
            return pl.ds(pl.multiple_of(n * width + pair * LANES, LANES), LANES)

        q = proj[rows, cut(0)] * jnp.asarray(0.125, bf16)
        k, v, up = proj[rows, cut(1)], proj[rows, cut(2)], datt[rows, cut(0)]
        sums = lse[half]
        dq = jnp.zeros((size, LANES), f32)
        dk = jnp.zeros((size, LANES), f32)
        dv = jnp.zeros((size, LANES), f32)
        for h in range(2):
            mine = low_lane if h == 0 else jnp.logical_not(low_lane)
            key = jnp.where(mine, k, zero)
            scores = dot_nt(q, key) + bias[half]
            mass = jnp.sum(
                jnp.where(lane_id == 2 * pair + h, sums, 0.0), axis=-1, keepdims=True
            )
            weights = jnp.exp(scores - mass)
            pull = dot_nt(up, jnp.where(mine, v, zero))
            mean = jnp.sum(weights * pull, axis=-1, keepdims=True)
            spare = (weights * (pull - mean)).astype(bf16)
            dq = dq + dot_nn(spare, key)
            dk = dk + dot_tn(spare, jnp.where(mine, q, zero))
            dv = dv + dot_tn(weights.astype(bf16), jnp.where(mine, up, zero))
        dproj[rows, cut(0)] = (dq * 0.125).astype(bf16)
        dproj[rows, cut(1)] = dk.astype(bf16)
        dproj[rows, cut(2)] = dv.astype(bf16)
        return carry

    def weigh(k):
        span = slice(2 * k * chunk, 2 * (k + 1) * chunk)
        for q in range(3):
            part = dot_nn(tok_t[...], dproj[:, q * width + span.start : q * width + span.stop])
            part = part.reshape(nz, 2, rows_own, 2 * chunk).astype(bf16)
            for n in range(2):
                wp[2 * k + n, q % 2, q // 2] = part[..., n * chunk : (n + 1) * chunk]
        p1(2 * k).start()
        p1(2 * k + 1).start()

    lax.fori_loop(0, 2, attend, 0)
    half_add()
    kern_step(*two, 1)
    lax.fori_loop(2, 4, attend, 0)
    weigh(0)
    last_y_add()
    mg_step(soon, 1)
    lax.fori_loop(4, 6, attend, 0)
    p_add_1(0)
    p_add_1(1)
    kern_step(*two, 2)
    lax.fori_loop(6, 8, attend, 0)
    weigh(1)
    last_x_add()
    mg_step(soon, 2)
    lax.fori_loop(8, 10, attend, 0)
    p_add_1(2)
    p_add_1(3)
    p_add_2(0)
    p_add_2(1)
    kern_sum("two", kk_2, kz_2, o_two)
    lax.fori_loop(10, 12, attend, 0)
    weigh(2)
    down_y_add()
    loads[4].wait()
    back = dot_nt(dproj[...], wqkv[...]).astype(bf16)
    brm[...] = dot_nn(perm[1], back).astype(bf16).reshape(16, across, width)
    mixed_away = remote(
        brm.at[pl.ds(7 * (1 - c), 9)], frame.at[:, c], ex_send.at[1], ex_recv.at[1], core
    )
    mixed_away.start()
    mixed_own = pltpu.make_async_copy(brm.at[pl.ds(7 * c, 9)], frame.at[:, c], own_sem.at[1])
    mixed_own.start()
    p_add_1(4)
    p_add_1(5)
    p_add_3(0)
    p_add_3(1)
    p_add_2(2)
    p_add_2(3)
    loads[5].wait()
    loads[6].wait()

    shift = mod[0:1, :]
    scale_in = 1.0 + mod[1:2, :]

    def again(row, carry):
        normal, _ = normalize(xf[2 * c + row].astype(f32))
        value[row] = (normal * scale_in + shift).astype(bf16).astype(f32)
        return carry

    lax.fori_loop(0, 16, again, 0)
    mixed_own.wait()
    mixed_away.wait()

    def lay(row, carry):
        at = c + row
        line = frame[at // 2, lax.rem(at, 2)].astype(f32)
        before, after = column_shifts(line)
        gs[0, 1 - c + row] = after
        gs[1, 1 - c + row] = line
        gs[2, 1 - c + row] = before
        return carry

    lax.fori_loop(0, 17, lay, 0)
    for s in range(3):
        gs[s, 17 * c] = jnp.zeros((across, width), f32)

    def conv_back(lane, half):
        span = slice(lane, lane + LANES)
        taps = [kern[n : n + 1, span].astype(f32) for n in range(9)]

        def backward(row, sums):
            total = jnp.zeros((across, LANES), f32)
            own = value[row, :, span]
            later = []
            for r in range(3):
                for s in range(3):
                    line = gs[s, row + 2 - r, :, span]
                    total = total + taps[3 * r + s] * line
                    later.append(sums[3 * r + s] + fold(own * line))
            agrad[row, :, span] = total
            return tuple(later)

        sums = lax.fori_loop(
            8 * half, 8 * half + 8, backward,
            tuple(jnp.zeros((8, LANES), f32) for _ in range(9)),
        )
        rows9 = [jnp.sum(sums[n], axis=0, keepdims=True) for n in range(9)]
        lines = jnp.concatenate(rows9 + [jnp.zeros((7, LANES), f32)])
        if half == 0:
            taps_sum[:, span] = lines
        else:
            kk_1[0, :, span] = (taps_sum[:, span] + lines).astype(bf16)

    def finish(row, sums):
        normal, scale = normalize(xf[2 * c + row].astype(f32))
        line = agrad[row]
        place = pl.ds(pl.multiple_of(row * across, across), across)
        total = mid[place, :] + normalize_back(line * scale_in, normal, scale)
        ig[row] = total.astype(bf16)
        return (sums[0] + fold(line), sums[1] + fold(line * normal))

    sums = tuple(jnp.zeros((8, width), f32) for _ in range(2))
    up_sum()
    for lane in range(0, width, LANES):
        conv_back(lane, 0)
    p_add_2(4)
    p_add_2(5)
    p_add_3(2)
    p_add_3(3)
    sums = lax.fori_loop(0, 8, finish, sums)
    send_home(0, ig, o_ig, i_send, i_recv, False)
    p_add_4(0)
    p_add_4(1)
    mg_end(soon)
    mg_out.start()
    for lane in range(0, width, LANES):
        conv_back(lane, 1)
    kern_copy("one", kk_1, kr_1, 0).start()
    p_add_3(4)
    p_add_3(5)
    down_sum()
    pass_on("gu", fin_u)
    sums = lax.fori_loop(8, 16, finish, sums)
    for n in range(2):
        ml_own[n : n + 1, :] = jnp.sum(sums[n], axis=0, keepdims=True)
    mg_copy(final, 0).start()
    send_home(1, ig, o_ig, i_send, i_recv, False)
    kern_step(*one, 0)
    p_pass(0)
    p_pass(1)
    mg_step(final, 0)
    p_add_4(2)
    p_add_4(3)
    kern_step(*one, 1)
    mg_step(final, 1)
    to_core("gu", fin_u, False).wait_recv()
    u_out.start()
    pass_on("gd", fin_d)
    kern_step(*one, 2)
    mg_step(final, 2)
    p_add_4(4)
    p_add_4(5)
    p_pass(2)
    p_pass(3)
    to_core("gd", fin_d, False).wait_recv()
    d_out.start()
    kern_sum("one", kk_1, kz_1, o_one)
    mg_end(final)
    ml_out.start()
    p_pass(4)
    p_pass(5)
    for k in range(chunks):
        p_core(k, False).wait_recv()
    p_out.start()
    gone([half_x(), last_y(), last_x(), last_d(), down_y()])
    for name, fin in (("gu", fin_u), ("gd", fin_d)):
        gone([to_side(name, fin, True), to_core(name, fin, True)])
    for d in range(1, nz):
        gone([up_z(d), down_z(d), mg_far(soon, d, zb), mg_far(final, d, zb)])
        gone([kern_far("one", kk_1, kz_1, d), kern_far("two", kk_2, kz_2, d)])
    for k in range(chunks):
        gone([p1(k), p2(k), p3(k), p_side(k, True), p_core(k, True)])
        gone([p4(k, d) for d in range(1, nz)])
    for stage in range(3):
        gone([mg_copy(soon, stage), mg_copy(final, stage)])
        gone([kern_copy("one", kk_1, kr_1, stage), kern_copy("two", kk_2, kr_2, stage)])
    for n in range(2):
        send_home(n, res_in, o_res, r_send, r_recv, True)
        send_home(n, ig, o_ig, i_send, i_recv, True)
    home(o_res, r_recv)
    home(o_ig, i_recv)
    for out in (u_out, d_out, p_out, mg_out, ml_out):
        out.wait()


def back(
    mid, rg, tok, proj, att, lse, bias, x_frame, mod, small, kern, wqkv, wo, res,
    ud, dq, uh, ul, dl, kern_two,
):
    nb = lax.axis_size("batch")
    nz = nb // 2
    across, width = x_frame.shape[1], x_frame.shape[2]
    tokens = 16 * across
    rows = width // nb
    grain = dq.shape[1]
    parts = dl.shape[1]
    per = dq.shape[0] // nb
    chunks, chunk = width // LANES, LANES
    many = max(nz - 1, 1)
    any_space = pl.BlockSpec(memory_space=pl.ANY)
    vmem = pl.BlockSpec(memory_space=pltpu.VMEM)
    shape = jax.ShapeDtypeStruct
    dma = pltpu.SemaphoreType.DMA
    wide = kern_two.shape[1]
    links = 100 + 20 * many

    def low(*dims):
        return pltpu.VMEM(dims, bf16)

    def high(*dims):
        return pltpu.VMEM(dims, f32)

    return pl.pallas_call(
        back_kernel,
        out_shape=(
            shape((2, 2, rows, width), bf16),
            shape((2, 2, per, grain, width), bf16),
            shape((chunks, 2, 2, rows, chunk), bf16),
            shape((2, 8, across, width), bf16),
            shape((2, 8, across, width), bf16),
            shape((16, width), f32),
            shape((16, wide), f32),
            shape((nz, 2, 2, 8, width), f32),
            shape((nz, 2, 2, 2, width), f32),
        ),
        in_specs=[any_space] * 5 + [vmem, vmem, any_space, vmem, vmem, vmem] + [any_space] * 8
        + [vmem],
        out_specs=[any_space] * 5 + [vmem, vmem, any_space, any_space],
        scratch_shapes=[
            high(tokens, width), low(tokens, width), low(width, tokens), low(tokens, 3 * width),
            low(tokens, width), low(18, across, width), low(*wqkv.shape), low(*wo.shape),
            low(16, across, width), low(2, tokens, tokens), low(tokens, width),
            low(tokens, width), low(tokens, 3 * width),
            low(16, across, width), low(9, 2, across, width), high(3, 18, across, width),
            high(16, across, width), high(16, across, width), low(16, across, width),
            low(chunks, 2, 2, nz, 2, rows, chunk), low(chunks, 2, nz, 2, rows, chunk),
            low(chunks, nz, 2, rows, chunk), low(chunks, 2, nz, rows, chunk),
            low(chunks, nz, rows, chunk), low(chunks, many, rows, chunk),
            low(chunks, 2, 2, rows, chunk),
            low(nz, rows, 2 * LANES), low(nz, 2, per, grain, width),
            low(many, rows, 2 * LANES), low(nz, per, grain, width), low(many, per, grain, width),
            low(2, 2, rows, width), low(2, 2, per, grain, width),
            low(parts, grain, width), low(parts, grain, width),
            low(nz, rows, LANES), low(2, nz, rows, LANES), low(2, nz, rows, LANES),
            low(nz, rows, LANES),
            high(8, width), high(8, width), high(nz, 2, 2, 8, width),
            high(2, width), high(2, width), high(nz, 2, 2, 2, width), high(16, width),
            low(4, 16, width), low(3, 16, width), low(many, 16, width),
            low(4, 16, wide), low(3, 16, wide), low(many, 16, wide),
            dma((11 + nb,)), dma((2,)), dma((2,)), dma((2,)), dma((2,)), dma((2,)), dma((2,)),
            dma((2,)), dma((links,)), dma((links,)), dma((5,)),
        ],
        compiler_params=pltpu.CompilerParams(
            collective_id=2, has_side_effects=True, vmem_limit_bytes=63 << 20
        ),
        name="back",
    )(
        mid, rg, tok, proj, att, lse, bias, x_frame, mod, small, kern, wqkv, wo, res,
        ud, dq, uh, ul, dl, kern_two,
    )


def parts_of(values):
    first = values.astype(bf16)
    rest = values - first.astype(f32)
    second = rest.astype(bf16)
    third = (rest - second.astype(f32)).astype(bf16)
    return jnp.concatenate([first, second, third], axis=0)


def thrice(values):
    return jnp.concatenate([values] * 3, axis=0).astype(bf16)


def tail_kernel(
    fu, fd, fp, mg, late, one, two, wm_in, res_in, ig_in,
    o_class, o_time, o_mod, o_proj, o_out, o_one, o_up, o_two, o_down, o_res, o_ig,
    wm, moved, load_sem, in_sem, out_sem,
):
    b = lax.axis_index("batch")
    width = mg.shape[2]
    canvases = mg.shape[0]
    own = o_mod.shape[0]
    whole = wm_in.shape[0] == own
    source = wm_in if whole else wm_in.at[pl.ds(pl.multiple_of(b * own, 16), own)]
    load = pltpu.make_async_copy(source, wm, load_sem)
    load.start()
    takes = [
        pltpu.make_async_copy(src, moved.at[n], in_sem.at[n]) for n, src in enumerate((res_in, ig_in))
    ]
    gives = [
        pltpu.make_async_copy(moved.at[n], dst, out_sem.at[n]) for n, dst in enumerate((o_res, o_ig))
    ]
    for take in takes:
        take.start()
    chunks, chunk = fp.shape[0], fp.shape[4]
    per, grain = fd.shape[2], fd.shape[3]
    for q in range(4):
        for j in range(width // LANES):
            at = (4 * j + q) * LANES
            o_up[:, at : at + LANES] = fu[q % 2, q // 2, :, j * LANES : (j + 1) * LANES].astype(f32)
        for i in range(per):
            at = (4 * i + q) * grain
            o_down[at : at + grain, :] = fd[q % 2, q // 2, i].astype(f32)
        for k in range(chunks):
            part = fp[k, q % 2, q // 2].astype(f32)
            if q < 3:
                o_proj[:, q * width + k * chunk : q * width + (k + 1) * chunk] = part
            else:
                o_out[:, k * chunk : (k + 1) * chunk] = part
    for take, give in zip(takes, gives):
        take.wait()
        give.start()

    def window(values, n):
        size = values.shape[1]
        return pltpu.roll(values, lax.rem(size - b * n, size), 1)[:, :n]

    o_one[...] = window(one[...], own)[0:9]
    o_two[...] = window(two[...], o_two.shape[1])[0:9]
    every = mg[...]
    begin = late[...]
    cond = window(every[:, 7, :] * 0.5, own)
    sigma = 1.0 / (1.0 + jnp.exp(-cond))
    low = thrice(cond * sigma)
    steep = sigma * (1.0 + cond * (1.0 - sigma))
    act_grad = jnp.zeros((3 * canvases, own), f32)
    load.wait()
    for part in range(6):
        span = slice(part * width, (part + 1) * width)
        line = parts_of(begin[:, part, :] if part < 2 else every[:, part, :])
        o_mod[:, span] = dot_tn(low, line)
        act_grad = act_grad + dot_nt(line, wm[:, span])
    act_grad = (
        act_grad[2 * canvases :] + act_grad[canvases : 2 * canvases] + act_grad[:canvases]
    )
    cond_grad = parts_of(act_grad * steep)
    names = every[:, 6, :] * 0.5
    kinds = o_class.shape[1]
    spot = lax.broadcasted_iota(jnp.int32, (canvases, kinds), 1).astype(f32)
    for n, out in enumerate((o_class, o_time)):
        hot = thrice(jnp.where(spot == names[:, n : n + 1], 1.0, 0.0))
        out[...] = dot_tn(cond_grad, hot)
    for give in gives:
        give.wait()


def tail(fu, fd, fp, mg, late, one, two, wmod, res, ig, classes, times):
    nb = lax.axis_size("batch")
    width = mg.shape[2]
    own = width // nb
    wide = two.shape[1] // nb
    if own % 16:
        wmod = lax.dynamic_slice_in_dim(wmod, lax.axis_index("batch") * own, own, axis=0)
    any_space = pl.BlockSpec(memory_space=pl.ANY)
    vmem = pl.BlockSpec(memory_space=pltpu.VMEM)
    shape = jax.ShapeDtypeStruct
    dma = pltpu.SemaphoreType.DMA
    return pl.pallas_call(
        tail_kernel,
        out_shape=(
            shape((own, classes), f32),
            shape((own, times), f32),
            shape((own, 6 * width), f32),
            shape((own, 3 * width), f32),
            shape((own, width), f32),
            shape((9, own), f32),
            shape((own, 4 * width), f32),
            shape((9, wide), f32),
            shape((4 * fd.shape[2] * fd.shape[3], width), f32),
            shape(res.shape, bf16),
            shape(ig.shape, bf16),
        ),
        in_specs=[vmem] * 7 + [any_space] * 3,
        out_specs=[vmem] * 9 + [any_space] * 2,
        scratch_shapes=[
            pltpu.VMEM((own, 6 * width), bf16), pltpu.VMEM((2, *res.shape), bf16),
            dma, dma((2,)), dma((2,)),
        ],
        compiler_params=pltpu.CompilerParams(vmem_limit_bytes=60 << 20),
        name="tail",
    )(fu, fd, fp, mg, late, one, two, wmod, res, ig)


def body(
    inputs,
    segments,
    class_labels,
    time_steps,
    class_table,
    time_table,
    modulation_weight,
    project_weight,
    output_weight,
    kernel_attention,
    up_weight,
    kernel_feed,
    down_weight,
    cotangent,
):
    across, width = inputs.shape[2], inputs.shape[3]
    nb = lax.axis_size("batch")
    units = up_weight.shape[1]
    grain = 16 if (units // nb) % 64 == 0 else 8
    x_frame, cot_frame, returned, tok, proj, att, lse, bias, mod = front(
        inputs, cotangent, class_labels, time_steps, segments, kernel_attention, class_table,
        time_table, modulation_weight, project_weight, output_weight,
    )
    flat = (18 * across, width)
    ud, dq, uh, ul, dl, kern_two, res, mid, rg, small = feed(
        x_frame.reshape(flat), returned.reshape(flat), cot_frame.reshape(flat), mod, up_weight,
        kernel_feed, down_weight, grain,
    )
    fu, fd, fp, result, inputs_gradient, one, two, gathered, late = back(
        mid, rg.reshape(8, 2, across, width), tok, proj, att, lse, bias, x_frame, mod, small,
        kernel_attention, project_weight, output_weight, res.reshape(16, across, width),
        ud, dq, uh, ul, dl, kern_two,
    )
    (
        class_total, time_total, modulation_total, project_total, output_total,
        attention_kernel_total, up_total, feed_kernel_total, down_total, result, inputs_gradient,
    ) = tail(
        fu, fd, fp, gathered.reshape(2 * nb, 8, width), late.reshape(2 * nb, 2, width), one, two,
        modulation_weight, result, inputs_gradient, class_table.shape[0], time_table.shape[0],
    )
    return (
        result,
        inputs_gradient,
        class_total.T,
        time_total.T,
        modulation_total,
        project_total,
        output_total,
        attention_kernel_total,
        up_total,
        feed_kernel_total,
        down_total,
    )


def solution(mesh):
    in_specs = (
        P("batch", "group", None, None),
        P("batch", None),
        P("batch"),
        P("batch"),
        P(),
        P(),
        P(),
        P(),
        P(),
        P(),
        P(),
        P(),
        P(),
        P("batch", "group", None, None),
    )
    out_specs = (
        P("batch", "group", None, None),
        P("batch", "group", None, None),
        P(None, "batch"),
        P(None, "batch"),
        P("batch", None),
        P("batch", None),
        P("batch", None),
        P(None, "batch"),
        P("batch", None),
        P(None, "batch"),
        P("batch", None),
    )
    return jax.shard_map(body, mesh=mesh, in_specs=in_specs, out_specs=out_specs, check_vma=False)
```

```python
from functools import partial

import jax
import jax.numpy as jnp
from jax import lax
from jax.experimental import pallas as pl
from jax.experimental.pallas import tpu as pltpu
from jax.sharding import PartitionSpec as P

HEADS = 12
MESH = pl.DeviceIdType.MESH
LANES = 128
f32 = jnp.float32
bf16 = jnp.bfloat16
highest = lax.Precision.HIGHEST


def dot_nn(a, b):
    return lax.dot_general(a, b, (((1,), (0,)), ((), ())), preferred_element_type=f32)


def dot_nt(a, b):
    return lax.dot_general(a, b, (((1,), (1,)), ((), ())), preferred_element_type=f32)


def dot_tn(a, b):
    return lax.dot_general(a, b, (((0,), (0,)), ((), ())), preferred_element_type=f32)


def remote(src, dst, send, recv, target):
    return pltpu.make_async_remote_copy(
        src_ref=src, dst_ref=dst, send_sem=send, recv_sem=recv, device_id=target,
        device_id_type=MESH,
    )


def meet(partners):
    barrier = pltpu.get_barrier_semaphore()
    for partner in partners:
        pl.semaphore_signal(barrier, inc=1, device_id=partner, device_id_type=MESH)
    pl.semaphore_wait(barrier, len(partners))


def normalize(values):
    center = values - jnp.mean(values, axis=-1, keepdims=True)
    second = jnp.mean(center * center, axis=-1, keepdims=True)
    scale = lax.rsqrt(second + 1e-06)
    return center * scale, scale


def normalize_back(grad, normal, scale):
    return scale * (
        grad
        - jnp.mean(grad, axis=-1, keepdims=True)
        - normal * jnp.mean(grad * normal, axis=-1, keepdims=True)
    )


def column_shifts(row):
    across = row.shape[0]
    column = lax.broadcasted_iota(jnp.int32, row.shape, 0)
    before = jnp.where(column == 0, 0.0, pltpu.roll(row, 1, 0))
    after = jnp.where(column == across - 1, 0.0, pltpu.roll(row, across - 1, 0))
    return before, after


def fold(values):
    rows, width = values.shape
    return jnp.sum(values.reshape(rows // 8, 8, width), axis=0)


def permutation(inverse):
    n = 512
    to = lax.broadcasted_iota(jnp.int32, (n, n), 1 if inverse else 0)
    source = lax.broadcasted_iota(jnp.int32, (n, n), 0 if inverse else 1)
    wanted = lax.shift_left(lax.shift_right_logical(to & 255, 4), 5) + 2 * (to & 15) + (
        lax.shift_right_logical(to, 8)
    )
    return jnp.where(source == wanted, 1.0, 0.0).astype(bf16)


def front_kernel(
    x_in, cot_in, names, moments, segments, kern, class_in, time_in, wmod_in, wqkv_in, wo_in,
    o_x, o_cot, o_ret, o_tok, o_proj, o_att, o_lse, o_bias, mod,
    xf, table, wmod, wqkv, wo, shifts, mixed, rows_m, perm, bias, tok, proj, att, lse, brm,
    load_sem, x_send, x_recv, c_send, c_recv, ex_send, ex_recv, own_sem, out_sem,
):
    b = lax.axis_index("batch")
    g = lax.axis_index("group")
    c, p = lax.rem(g, 2), g // 2
    core, side, corner = (b, g + 1 - 2 * c), (b, g + 2 - 4 * p), (b, 3 - g)
    inner = jnp.logical_or(g == 1, g == 2)
    width = xf.shape[-1]
    across = xf.shape[1]

    def spread_out(src, dst, send, recv, waiting):
        main = c * 8 + p * 2
        other_main = remote(
            src.at[1 - p], dst.at[pl.ds(main, 8)], send.at[0], recv.at[c], (b, 2 - p)
        )
        edge = 6 * (2 - g)
        edge_to = 16 * (g - 1)
        other_edge = remote(
            src.at[1 - p, pl.ds(edge, 2)], dst.at[pl.ds(edge_to, 2)], send.at[1], recv.at[2], side
        )
        own_main = remote(src.at[p], dst.at[pl.ds(main, 8)], send.at[2], recv.at[c], core)
        own_edge = pltpu.make_async_copy(
            src.at[p, pl.ds(edge, 2)], dst.at[pl.ds(edge_to, 2)], recv.at[2]
        )
        stay_main = pltpu.make_async_copy(src.at[p], dst.at[pl.ds(main, 8)], recv.at[c])
        if waiting:
            other_main.wait_send()

            @pl.when(inner)
            def _():
                other_edge.wait_send()
                own_main.wait_send()

        else:
            other_main.start()

            @pl.when(inner)
            def _():
                other_edge.start()
                own_main.start()
                own_edge.start()

            @pl.when(jnp.logical_not(inner))
            def _():
                stay_main.start()

    def arrived(dst, recv):
        for j in range(2):
            place = dst.at[pl.ds(8 * j + 2 * c, 8)]
            pltpu.make_async_copy(place, place, recv.at[j]).wait()
        place = dst.at[pl.ds(16 * (1 - c), 2)]
        pltpu.make_async_copy(place, place, recv.at[2]).wait()

    pieces = [
        (wqkv_in, wqkv), (wo_in, wo), (class_in, table.at[0]), (time_in, table.at[1]),
        (wmod_in, wmod),
    ]
    loads = [
        pltpu.make_async_copy(src, dst, load_sem.at[n]) for n, (src, dst) in enumerate(pieces)
    ]
    for n in (2, 3, 4, 0, 1):
        loads[n].start()
    meet([core, side, corner])
    spread_out(x_in, xf, x_send, x_recv, False)
    perm[0] = permutation(False)
    perm[1] = permutation(True)
    n = tok.shape[0]
    wide = segments.shape[1]
    to = lax.broadcasted_iota(jnp.int32, (n, wide), 0)
    source = lax.broadcasted_iota(jnp.int32, (n, wide), 1)
    wanted = lax.shift_left(2 * lax.shift_right_logical(to & 255, 4) + c, 5) + 2 * (to & 15) + (
        lax.shift_right_logical(to, 8)
    )
    chosen = source == wanted
    one_line = jnp.where(p == 0, segments[0:1, :], segments[1:2, :]).astype(f32)
    lines = jnp.broadcast_to(one_line, (8, wide)).astype(bf16)
    lab_row = dot_nt(lines, jnp.where(chosen, 1.0, 0.0).astype(bf16))
    lab_col = jnp.sum(jnp.where(chosen, one_line, 0.0), axis=-1, keepdims=True)
    for half in range(2):
        cut = slice(half * (n // 2), (half + 1) * (n // 2))
        bias[half] = jnp.where(lab_row[0:1, cut] == lab_col[cut], 0.0, -1e30)
    bias_out = pltpu.make_async_copy(bias, o_bias, out_sem.at[5])
    bias_out.start()
    name = jnp.where(p == 0, names[0], names[1])
    moment = jnp.where(p == 0, moments[0], moments[1])
    loads[2].wait()
    loads[3].wait()
    rows_all = lax.broadcasted_iota(jnp.int32, (8, table.shape[1]), 1)
    cond = dot_nn(jnp.where(rows_all == name, 1.0, 0.0).astype(bf16), table[0]) + dot_nn(
        jnp.where(rows_all == moment, 1.0, 0.0).astype(bf16), table[1]
    )
    cond_low = (cond / (1.0 + jnp.exp(-cond))).astype(bf16)
    loads[4].wait()
    for part in range(6):
        cut = slice(part * width, (part + 1) * width)
        mod[part : part + 1, :] = dot_nn(cond_low, wmod[:, cut])[0:1, :]
    lane_of = lax.broadcasted_iota(jnp.int32, (1, width), 1)
    mod[6:7, :] = jnp.where(
        lane_of == 0, name.astype(f32), jnp.where(lane_of == 1, moment.astype(f32), 0.0)
    )
    mod[7:8, :] = cond[0:1, :]
    arrived(xf, x_recv)
    spread_out(cot_in, o_cot, c_send, c_recv, False)
    x_out = pltpu.make_async_copy(xf, o_x, out_sem.at[0])
    x_out.start()

    shift = mod[0:1, :]
    scale = 1.0 + mod[1:2, :]

    def first(i, carry):
        normal, _ = normalize(xf[c + i].astype(f32))
        value = (normal * scale + shift).astype(bf16).astype(f32)
        before, after = column_shifts(value)
        shifts[0, 1 - c + i] = before
        shifts[1, 1 - c + i] = value
        shifts[2, 1 - c + i] = after
        return carry

    lax.fori_loop(0, 17, first, 0)
    for s in range(3):
        shifts[s, 17 * c] = jnp.zeros((across, width), f32)

    def conv(step, parity):
        o = 2 * step + parity
        for lane in range(0, width, LANES):
            cut = slice(lane, lane + LANES)
            total = jnp.zeros((across, LANES), f32)
            for r in range(3):
                for s in range(3):
                    tap = kern[3 * r + s : 3 * r + s + 1, cut].astype(f32)
                    total = total + tap * shifts[s, o + r, :, cut]
            mixed[step, parity, :, cut] = total.astype(bf16)

    def conv_away(step, carry):
        conv(step, 1 - c)
        return carry

    def conv_own(step, carry):
        conv(step, c)
        return carry

    lax.fori_loop(0, 8, conv_away, 0)
    mixed_away = remote(
        mixed.at[:, 1 - c], rows_m.at[pl.ds(8 * c, 8)], ex_send.at[0], ex_recv.at[0], core
    )
    mixed_away.start()
    lax.fori_loop(0, 8, conv_own, 0)
    mixed_own = pltpu.make_async_copy(mixed.at[:, c], rows_m.at[pl.ds(8 * c, 8)], own_sem.at[0])
    mixed_own.start()
    mixed_own.wait()
    mixed_away.wait()
    flat = rows_m[...].reshape(16 * across, width)
    tok[...] = dot_nn(perm[0], flat).astype(bf16)
    tok_out = pltpu.make_async_copy(tok, o_tok, out_sem.at[1])
    tok_out.start()
    loads[0].wait()
    for part in range(3):
        cut = slice(part * width, (part + 1) * width)
        proj[:, cut] = dot_nn(tok[...], wqkv[:, cut]).astype(bf16)
    proj_out = pltpu.make_async_copy(proj, o_proj, out_sem.at[2])
    proj_out.start()

    pairs = width // LANES
    size = tok.shape[0] // 2
    low_lane = lax.broadcasted_iota(jnp.int32, (size, LANES), 1) < LANES // 2
    lane_id = lax.broadcasted_iota(jnp.int32, (size, LANES), 1)
    zero = jnp.zeros((), bf16)

    def attend(index, carry):
        half, pair = index // pairs, lax.rem(index, pairs)
        rows = pl.ds(pl.multiple_of(half * size, size), size)

        def part(n):
            return proj[rows, pl.ds(pl.multiple_of(n * width + pair * LANES, LANES), LANES)]

        q, k, v = part(0) * jnp.asarray(0.125, bf16), part(1), part(2)
        total = jnp.zeros((size, LANES), f32)
        sums = lse[half]
        for h in range(2):
            mine = low_lane if h == 0 else jnp.logical_not(low_lane)
            scores = dot_nt(q, jnp.where(mine, k, zero)) + bias[half]
            top = jnp.max(scores, axis=-1, keepdims=True)
            powers = jnp.exp(scores - top)
            mass = jnp.sum(powers, axis=-1, keepdims=True)
            weights = (powers * (1.0 / mass)).astype(bf16)
            total = total + dot_nn(weights, jnp.where(mine, v, zero))
            sums = jnp.where(lane_id == 2 * pair + h, top + jnp.log(mass), sums)
        lse[half] = sums
        att[rows, pl.ds(pl.multiple_of(pair * LANES, LANES), LANES)] = total.astype(bf16)
        return carry

    lse[...] = jnp.zeros(lse.shape, f32)
    lax.fori_loop(0, 2 * pairs, attend, 0)
    att_out = pltpu.make_async_copy(att, o_att, out_sem.at[3])
    att_out.start()
    lse_out = pltpu.make_async_copy(lse, o_lse, out_sem.at[4])
    lse_out.start()
    loads[1].wait()
    branch = dot_nn(att[...], wo[...]).astype(bf16)
    brm[...] = dot_nn(perm[1], branch).astype(bf16).reshape(16, across, width)
    ret_away = remote(
        brm.at[pl.ds(7 * (1 - c), 9)], o_ret.at[:, c], ex_send.at[1], ex_recv.at[1], core
    )
    ret_away.start()
    ret_own = pltpu.make_async_copy(brm.at[pl.ds(7 * c, 9)], o_ret.at[:, c], own_sem.at[1])
    ret_own.start()
    for out in (x_out, tok_out, proj_out, att_out, lse_out, bias_out, ret_own):
        out.wait()
    ret_away.wait()
    spread_out(x_in, xf, x_send, x_recv, True)
    spread_out(cot_in, o_cot, c_send, c_recv, True)
    arrived(o_cot, c_recv)


def front(inputs, cotangent, names, moments, segments, kern, classes, times, wmod, wqkv, wo):
    across, width = inputs.shape[2], inputs.shape[3]
    tokens = 16 * across
    any_space = pl.BlockSpec(memory_space=pl.ANY)
    vmem = pl.BlockSpec(memory_space=pltpu.VMEM)
    smem = pl.BlockSpec(memory_space=pltpu.SMEM)
    shape = jax.ShapeDtypeStruct
    dma = pltpu.SemaphoreType.DMA
    return pl.pallas_call(
        front_kernel,
        out_shape=(
            shape((18, across, width), bf16),
            shape((18, across, width), bf16),
            shape((9, 2, across, width), bf16),
            shape((tokens, width), bf16),
            shape((tokens, 3 * width), bf16),
            shape((tokens, width), bf16),
            shape((2, tokens // 2, LANES), f32),
            shape((2, tokens // 2, tokens // 2), f32),
            shape((8, width), f32),
        ),
        in_specs=[any_space] * 2 + [smem] * 2 + [vmem] * 2 + [any_space] * 5,
        out_specs=[any_space] * 8 + [vmem],
        scratch_shapes=[
            pltpu.VMEM((18, across, width), bf16),
            pltpu.VMEM((2, *classes.shape), bf16),
            pltpu.VMEM(wmod.shape, bf16),
            pltpu.VMEM(wqkv.shape, bf16),
            pltpu.VMEM(wo.shape, bf16),
            pltpu.VMEM((3, 18, across, width), f32),
            pltpu.VMEM((8, 2, across, width), bf16),
            pltpu.VMEM((16, across, width), bf16),
            pltpu.VMEM((2, tokens, tokens), bf16),
            pltpu.VMEM((2, tokens // 2, tokens // 2), f32),
            pltpu.VMEM((tokens, width), bf16),
            pltpu.VMEM((tokens, 3 * width), bf16),
            pltpu.VMEM((tokens, width), bf16),
            pltpu.VMEM((2, tokens // 2, LANES), f32),
            pltpu.VMEM((16, across, width), bf16),
            dma((5,)), dma((3,)), dma((3,)), dma((3,)), dma((3,)), dma((2,)), dma((2,)),
            dma((2,)), dma((6,)),
        ],
        compiler_params=pltpu.CompilerParams(
            collective_id=1, has_side_effects=True, vmem_limit_bytes=60 << 20
        ),
        name="front",
    )(inputs, cotangent, names, moments, segments, kern, classes, times, wmod, wqkv, wo)


def gelu_parts(x):
    size = jnp.abs(x)
    t = 1.0 / (1.0 + (0.3275911 * 0.7071067811865476) * size)
    bell = jnp.exp(-0.5 * x * x)
    series = t * (
        0.254829592
        + t * (-0.284496736 + t * (1.421413741 + t * (-1.453152027 + t * 1.061405429)))
    )
    tail = 0.5 * series * bell
    mass = jnp.where(x >= 0, 1.0 - tail, tail)
    return x * mass, mass + x * bell * 0.3989422804014327


def feed_kernel(
    x_in, ret_in, cot_in, mod, up, kern, down,
    o_up, o_down, o_up_half, o_up_last, o_down_last, o_kern, o_res, o_mid, o_rg, o_small,
    feed_in, feed_t, btg, out_acc, back_acc, hid, hs, gs, act, slope, hg,
    wu, wd, ru, rd, yu, xu, zu, fin, xd,
    u1_send, u1_recv, u2_send, u2_recv, u3_send, u3_recv, d1_send, d1_recv, d2_send, d2_recv,
    u4_send, u4_recv, u_out, d_out, l_out,
):
    j = pl.program_id(0)
    tiles = pl.num_programs(0)
    b = lax.axis_index("batch")
    g = lax.axis_index("group")
    c, p = lax.rem(g, 2), g // 2
    nz = wu.shape[3]
    yb, zb = lax.rem(b, 2), b // 2
    core, side, beside = (b, g + 1 - 2 * c), (b, g + 2 - 4 * p), (b + 1 - 2 * yb, g)
    others = [lax.rem(zb + d, nz) for d in range(nz)]
    far = [(2 * z + yb, g) for z in others]
    parts = wd.shape[3]

    def up_1(t):
        return remote(wu.at[t, 1 - c], ru.at[t], u1_send.at[t], u1_recv.at[t], core)

    def down_1(t):
        return remote(wd.at[t, 1 - c], rd.at[t], d1_send.at[t], d1_recv.at[t], core)

    def up_2(t):
        return remote(wu.at[t, c, :, :, 1 - yb], yu.at[t], u2_send.at[t], u2_recv.at[t], beside)

    def down_2(t):
        return remote(wd.at[t, c, 1 - p], xd.at[t], d2_send.at[t], d2_recv.at[t], side)

    def up_3(t):
        return remote(wu.at[t, c, 1 - p, :, yb], xu.at[t], u3_send.at[t], u3_recv.at[t], side)

    def up_4(t, d):
        return remote(
            wu.at[t, c, p, others[d], yb], zu.at[t, d - 1], u4_send.at[t, d - 1],
            u4_recv.at[t, d - 1], far[d],
        )

    def up_store(t):
        spot = pl.ds(pl.multiple_of(t * LANES, LANES), LANES)
        return pltpu.make_async_copy(fin.at[t], o_up.at[:, spot], u_out.at[t])

    def down_store(t):
        return pltpu.make_async_copy(
            wd.at[t, c, p], o_down.at[pl.ds(t * parts, parts)], d_out.at[t]
        )

    def add_core(t):
        down_1(t).wait_recv()
        up_1(t).wait_recv()

        def step(i, carry):
            x, z, y = i // (2 * nz), lax.rem(i // 2, nz), lax.rem(i, 2)
            wu[t, c, x, z, y] = wu[t, c, x, z, y] + ru[t, x, z, y]
            return carry

        lax.fori_loop(0, 4 * nz, step, 0)

        def step_down(i, carry):
            x, n = i // 8, lax.rem(i, 8)
            for k in range(parts // 8):
                wd[t, c, x, n * (parts // 8) + k] = (
                    wd[t, c, x, n * (parts // 8) + k] + rd[t, x, n * (parts // 8) + k]
                )
            return carry

        lax.fori_loop(0, 16, step_down, 0)

    def add_beside(t):
        up_2(t).wait_recv()

        def step(i, carry):
            x, z = i // nz, lax.rem(i, nz)
            wu[t, c, x, z, yb] = wu[t, c, x, z, yb] + yu[t, x, z]
            return carry

        lax.fori_loop(0, 2 * nz, step, 0)

    def add_side(t):
        up_3(t).wait_recv()

        def step(z, carry):
            wu[t, c, p, z, yb] = wu[t, c, p, z, yb] + xu[t, z]
            return carry

        lax.fori_loop(0, nz, step, 0)
        for d in range(1, nz):
            up_4(t, d).start()

    def add_far(t):
        total = wu[t, c, p, zb, yb].astype(f32)
        for d in range(1, nz):
            up_4(t, d).wait_recv()
            total = total + zu[t, d - 1].astype(f32)
        fin[t] = total.astype(bf16)
        up_store(t).start()

    def add_side_down(t):
        down_2(t).wait_recv()

        def step(n, carry):
            for k in range(parts // 8):
                wd[t, c, p, n * (parts // 8) + k] = (
                    wd[t, c, p, n * (parts // 8) + k] + xd[t, n * (parts // 8) + k]
                )
            return carry

        lax.fori_loop(0, 8, step, 0)
        down_store(t).start()

    across = 32
    width = feed_in.shape[1]
    tile = up.shape[1]
    frame_rows = feed_in.shape[0] // across
    own = pl.ds(pl.multiple_of(2 * c * across, 64), 16 * across)

    def middle_of(row):
        place = pl.ds(pl.multiple_of(row * across, across), across)
        returned = ret_in[place, :].astype(f32)
        return x_in[place, :].astype(f32) + mod[2:3, :] * returned, returned

    @pl.when(j == 0)
    def _():
        meet([core, side, beside, *far[1:]])

        def prepare(row, carry):
            place = pl.ds(pl.multiple_of(row * across, across), across)
            normal, _ = normalize(middle_of(row)[0])
            feed_in[place, :] = (normal * (1.0 + mod[4:5, :]) + mod[3:4, :]).astype(bf16)
            btg[place, :] = (mod[5:6, :] * cot_in[place, :].astype(f32)).astype(bf16)
            return carry

        lax.fori_loop(0, frame_rows, prepare, 0)
        feed_t[...] = feed_in[own, :].T
        out_acc[...] = jnp.zeros(out_acc.shape, f32)
        back_acc[...] = jnp.zeros(back_acc.shape, f32)
        for s in range(3):
            hs[s, 18 * c] = jnp.zeros((across, tile), f32)
            gs[s, 17 * c] = jnp.zeros((across, tile), f32)

    hid[...] = dot_nn(feed_in[...], up[...]).astype(bf16)

    def lay_hidden(row, carry):
        value = hid[pl.ds(pl.multiple_of(row * across, across), across), :].astype(f32)
        before, after = column_shifts(value)
        hs[0, 1 - c + row] = before
        hs[1, 1 - c + row] = value
        hs[2, 1 - c + row] = after
        return carry

    lax.fori_loop(0, frame_rows, lay_hidden, 0)

    for lane in range(0, tile, LANES):
        cut = slice(lane, lane + LANES)
        taps = [kern[n : n + 1, cut].astype(f32) for n in range(9)]

        def forward(row, carry):
            total = jnp.zeros((across, LANES), f32)
            for r in range(3):
                for s in range(3):
                    total = total + taps[3 * r + s] * hs[s, row + r, :, cut]
            place = pl.ds(pl.multiple_of(row * across, across), across)
            value, steep = gelu_parts(total)
            act[place, cut] = value.astype(bf16)
            slope[place, cut] = steep
            return carry

        lax.fori_loop(0, 17, forward, 0)

    @pl.when(j >= 2)
    def _():
        add_side(j - 2)
        add_side_down(j - 2)

    @pl.when(j >= 1)
    def _():
        add_core(j - 1)
        up_2(j - 1).start()
        down_2(j - 1).start()

    @pl.when(j >= 3)
    def _():
        add_far(j - 3)

    inside = pl.ds(pl.multiple_of(c * across, across), 16 * across)
    around = pl.ds(pl.multiple_of(c * across, across), 17 * across)
    own_act = act[inside, :]
    out_acc[...] += dot_nn(own_act, down[...])
    grad_down = dot_tn(own_act, btg[own, :]).reshape(parts, 4, wd.shape[4], width)
    for q in range(4):
        wd[j, q % 2, q // 2] = grad_down[:, q].astype(bf16)
    down_1(j).start()
    slope[...] = slope[...] * dot_nt(btg[around, :], down[...])

    def lay_grad(row, carry):
        value = slope[pl.ds(pl.multiple_of(row * across, across), across), :]
        value = value.astype(bf16).astype(f32)
        before, after = column_shifts(value)
        gs[0, 1 - c + row] = after
        gs[1, 1 - c + row] = value
        gs[2, 1 - c + row] = before
        return carry

    lax.fori_loop(0, 17, lay_grad, 0)

    for lane in range(0, tile, LANES):
        cut = slice(lane, lane + LANES)
        taps = [kern[n : n + 1, cut].astype(f32) for n in range(9)]

        def backward(row, sums):
            total = jnp.zeros((across, LANES), f32)
            value = hs[1, row + c + 1, :, cut]
            later = []
            for r in range(3):
                for s in range(3):
                    grad = gs[s, row + 2 - r, :, cut]
                    total = total + taps[3 * r + s] * grad
                    later.append(sums[3 * r + s] + fold(value * grad))
            hg[pl.ds(pl.multiple_of(row * across, across), across), cut] = total.astype(bf16)
            return tuple(later)

        sums = lax.fori_loop(
            0, 16, backward, tuple(jnp.zeros((8, LANES), f32) for _ in range(9))
        )
        for n in range(9):
            o_kern[n : n + 1, cut] = jnp.sum(sums[n], axis=0, keepdims=True)

    o_kern[9:16, :] = jnp.zeros((7, tile), f32)
    grad_up = dot_nn(feed_t[...], hg[...])
    for q in range(4):
        part = grad_up[:, q * LANES : (q + 1) * LANES]
        wu[j, q % 2, q // 2] = part.reshape(nz, 2, wu.shape[5], LANES).astype(bf16)
    up_1(j).start()
    back_acc[...] += dot_nt(hg[...], up[...])

    @pl.when(jnp.logical_and(j >= 1, j < tiles - 1))
    def _():
        add_beside(j - 1)
        up_3(j - 1).start()

    @pl.when(j == tiles - 1)
    def _():
        def finish(row, sums):
            frame = row + 2 * c
            place = pl.ds(pl.multiple_of(row * across, across), across)
            at = pl.ds(pl.multiple_of(frame * across, across), across)
            middle, returned = middle_of(frame)
            cot = cot_in[at, :].astype(f32)
            branch = out_acc[place, :]
            o_res[place, :] = (middle + mod[5:6, :] * branch).astype(bf16)
            normal, scale = normalize(middle)
            grad = back_acc[place, :]
            mid = cot + normalize_back(grad * (1.0 + mod[4:5, :]), normal, scale)
            o_mid[place, :] = mid
            o_rg[place, :] = (mod[2:3, :] * mid).astype(bf16)
            terms = (mid * returned, grad, grad * normal, cot * branch)
            return tuple(total + fold(term) for total, term in zip(sums, terms))

        sums = lax.fori_loop(
            0, 16, finish, tuple(jnp.zeros((8, width), f32) for _ in range(4))
        )
        o_small[...] = jnp.zeros((8, width), f32)
        for n in range(4):
            o_small[n + 2 : n + 3, :] = jnp.sum(sums[n], axis=0, keepdims=True)
        add_far(j - 2)
        add_beside(j - 1)
        half = pltpu.make_async_copy(wu.at[j - 1, c, :, :, yb], o_up_half, l_out.at[2])
        half.start()
        add_side_down(j - 1)
        add_core(j)
        last = (
            half,
            pltpu.make_async_copy(wu.at[j, c], o_up_last, l_out.at[0]),
            pltpu.make_async_copy(wd.at[j, c], o_down_last, l_out.at[1]),
        )
        for move in last[1:]:
            move.start()

        def settle(t, carry):
            up_3(t).wait_send()
            for d in range(1, nz):
                up_4(t, d).wait_send()
            up_store(t).wait()
            return carry

        def settle_more(t, carry):
            up_2(t).wait_send()
            down_2(t).wait_send()
            up_1(t).wait_send()
            down_1(t).wait_send()
            down_store(t).wait()
            return carry

        lax.fori_loop(0, tiles - 2, settle, 0)
        lax.fori_loop(0, tiles - 1, settle_more, 0)
        up_1(j).wait_send()
        down_1(j).wait_send()
        for move in last:
            move.wait()


def feed(x_frame, returned, cot_frame, mod, up, kern, down, grain):
    width, units = up.shape
    frame = x_frame.shape[0]
    across = frame // 18
    tokens = 16 * across
    shape = jax.ShapeDtypeStruct
    dma = pltpu.SemaphoreType.DMA
    any_space = pl.BlockSpec(memory_space=pl.ANY)
    tile = 4 * LANES
    tiles = units // tile
    parts = tile // (4 * grain)
    nb = lax.axis_size("batch")
    nz = nb // 2
    own = width // nb
    many = max(nz - 1, 1)

    def still(*size):
        return pl.BlockSpec(size, lambda j: (0, 0), pipeline_mode=pl.Buffered(1))

    columns = pl.BlockSpec((width, tile), lambda j: (0, j))
    rows = pl.BlockSpec((tile, width), lambda j: (j, 0))
    work = 6 * 2 * tokens * width * units
    return pl.pallas_call(
        feed_kernel,
        grid=(units // tile,),
        out_shape=(
            shape((own, (tiles - 2) * LANES), bf16),
            shape((tiles * parts, grain, width), bf16),
            shape((2, nz, own, LANES), bf16),
            shape((2, nz, 2, own, LANES), bf16),
            shape((2, parts, grain, width), bf16),
            shape((16, units), f32),
            shape((tokens, width), bf16),
            shape((tokens, width), f32),
            shape((tokens, width), bf16),
            shape((8, width), f32),
        ),
        in_specs=[
            still(frame, width), still(frame, width), still(frame, width), still(8, width),
            columns, pl.BlockSpec((9, tile), lambda j: (0, j)), rows,
        ],
        out_specs=[
            *[any_space] * 5, pl.BlockSpec((16, tile), lambda j: (0, j)),
            still(tokens, width), still(tokens, width), still(tokens, width), still(8, width),
        ],
        scratch_shapes=[
            pltpu.VMEM((frame, width), bf16),
            pltpu.VMEM((width, tokens), bf16),
            pltpu.VMEM((frame, width), bf16),
            pltpu.VMEM((tokens, width), f32),
            pltpu.VMEM((tokens, width), f32),
            pltpu.VMEM((frame, tile), bf16),
            pltpu.VMEM((3, 19, across, tile), f32),
            pltpu.VMEM((3, 18, across, tile), f32),
            pltpu.VMEM((17 * across, tile), bf16),
            pltpu.VMEM((17 * across, tile), f32),
            pltpu.VMEM((tokens, tile), bf16),
            pltpu.VMEM((tiles, 2, 2, nz, 2, own, LANES), bf16),
            pltpu.VMEM((tiles, 2, 2, parts, grain, width), bf16),
            pltpu.VMEM((tiles, 2, nz, 2, own, LANES), bf16),
            pltpu.VMEM((tiles, 2, parts, grain, width), bf16),
            pltpu.VMEM((tiles, 2, nz, own, LANES), bf16),
            pltpu.VMEM((tiles, nz, own, LANES), bf16),
            pltpu.VMEM((tiles, many, own, LANES), bf16),
            pltpu.VMEM((tiles, own, LANES), bf16),
            pltpu.VMEM((tiles, parts, grain, width), bf16),
            *[dma((tiles,)) for _ in range(10)],
            dma((tiles, many)), dma((tiles, many)), dma((tiles,)), dma((tiles,)), dma((3,)),
        ],
        compiler_params=pltpu.CompilerParams(
            dimension_semantics=("arbitrary",), collective_id=3, has_side_effects=True,
            vmem_limit_bytes=62 << 20,
        ),
        cost_estimate=pl.CostEstimate(
            flops=work, bytes_accessed=8 * width * units, transcendentals=tokens * units
        ),
        name="feed",
    )(x_frame, returned, cot_frame, mod, up, kern, down)


def back_kernel(
    mid_in, rg_in, tok_in, proj_in, att_in, lse, bias, x_in, mod, small, kern, wqkv_in, wo_in,
    res_in, ud_in, dq_in, uh_in, ul_in, dl_in, kern_two,
    o_fu, o_fd, o_fp, o_res, o_ig, o_one, o_two, o_mg, o_ml,
    mid, tok, tok_t, proj, att, xf, wqkv, wo, rows_m, perm, grad, datt, dproj,
    brm, frame, gs, value, agrad, ig,
    wp, p_r1, p_r2x, p_r2y, p_r3, p_r4, fin_p,
    fu, fd, fz_u, fy_d, fz_d, fin_u, fin_d, ld, lx_d, hx, ly, ly_r, lx,
    mg_own, mg_r1, mg_all, ml_own, ml_r1, ml_all, taps_sum, kk_1, kr_1, kz_1,
    kt, kt_core, kt_side, kt_y, kt_sum, kt_z, fin_k,
    load_sem, r_send, r_recv, i_send, i_recv, ex_send, ex_recv, own_sem, send_sem, recv_sem, out_sem,
):
    b = lax.axis_index("batch")
    g = lax.axis_index("group")
    nz = fu.shape[0]
    c, p = lax.rem(g, 2), g // 2
    yb, zb = lax.rem(b, 2), b // 2
    core, side, corner = (b, g + 1 - 2 * c), (b, g + 2 - 4 * p), (b, 3 - g)
    beside = (b + 1 - 2 * yb, g)
    others = [lax.rem(zb + d, nz) for d in range(nz)]
    far = [(2 * z + yb, g) for z in others]
    inner = jnp.logical_or(g == 1, g == 2)
    across, width = xf.shape[1], xf.shape[2]
    rows_own = fu.shape[1]
    pairs = width // LANES
    tokens = tok.shape[0]
    size = tokens // 2
    chunks = wp.shape[0]
    chunk = wp.shape[-1]
    lead = width - 2 * LANES
    per, parts = fd.shape[2], ld.shape[0]
    places = {}

    def link(name, src, dst, target):
        n = places.setdefault(name, len(places))
        return remote(src, dst, send_sem.at[n], recv_sem.at[n], target)

    def send_home(n, src, dst, send, recv, waiting):
        move = remote(src.at[pl.ds(8 * n, 8)], dst.at[p], send.at[n], recv.at[p], (b, 2 * c + n))
        away = remote(src.at[pl.ds(8 * n, 8)], dst.at[p], send.at[n], recv.at[p], core)
        stay = pltpu.make_async_copy(src.at[pl.ds(8 * n, 8)], dst.at[p], recv.at[p])

        @pl.when(inner)
        def _():
            if waiting:
                move.wait_send()
            else:
                move.start()

        @pl.when(jnp.logical_and(jnp.logical_not(inner), c != n))
        def _():
            if waiting:
                away.wait_send()
            else:
                away.start()

        if not waiting:

            @pl.when(jnp.logical_and(jnp.logical_not(inner), c == n))
            def _():
                stay.start()

    def home(dst, recv):
        for n in range(2):
            pltpu.make_async_copy(dst.at[n], dst.at[n], recv.at[n]).wait()

    def gone(moves):
        for move in moves:
            move.wait_send()

    def half_x():
        return link("hx", uh_in.at[1 - p], hx, side)

    def last_y():
        return link("ly", ul_in.at[:, :, 1 - yb], ly_r, beside)

    def last_x():
        return link("lx", ly.at[1 - p], lx, side)

    def last_d():
        return link("ld", dl_in.at[1 - p], lx_d, side)

    def down_y():
        return link("fdy", fd.at[:, 1 - yb], fy_d, beside)

    def up_z(d):
        return link(f"fuz{d}", fu.at[others[d]], fz_u.at[d - 1], far[d])

    def down_z(d):
        return link(f"fdz{d}", fd.at[others[d], yb], fz_d.at[d - 1], far[d])

    def to_side(name, fin, mine):
        x = p if mine else 1 - p
        return link(f"{name}x", fin.at[c, x], fin.at[c, x], side)

    def to_core(name, fin, mine):
        x = c if mine else 1 - c
        return link(f"{name}c", fin.at[x], fin.at[x], core)

    def half_add():
        early[0].wait()
        half_x().wait_recv()

        def step(z, carry):
            fu[z, :, :LANES] = fu[z, :, :LANES] + hx[z]
            return carry

        lax.fori_loop(0, nz, step, 0)

    def last_y_add():
        early[1].wait()
        last_y().wait_recv()

        def step(i, carry):
            x, z = i // nz, lax.rem(i, nz)
            ly[x, z] = ly[x, z] + ly_r[x, z]
            return carry

        lax.fori_loop(0, 2 * nz, step, 0)
        last_x().start()

    def last_x_add():
        last_x().wait_recv()

        def step(z, carry):
            fu[z, :, LANES:] = ly[p, z] + lx[z]
            return carry

        lax.fori_loop(0, nz, step, 0)
        for d in range(1, nz):
            up_z(d).start()

    def up_sum():
        early[2].wait()
        total = fu[zb].astype(f32)
        for d in range(1, nz):
            up_z(d).wait_recv()
            total = total + fz_u[d - 1].astype(f32)
        fin_u[c, p, :, lead:] = total.astype(bf16)
        to_side("gu", fin_u, True).start()

    def place_last():
        for load in late:
            load.wait()
        last_d().wait_recv()
        for t in range(parts):
            spot = 2 * nz * per - parts + t
            owner = spot // per
            fd[owner // 2, owner % 2, spot % per] = ld[t] + lx_d[t]
        down_y().start()

    def down_y_add():
        down_y().wait_recv()

        def step(z, carry):
            fd[z, yb] = fd[z, yb] + fy_d[z]
            return carry

        lax.fori_loop(0, nz, step, 0)
        for d in range(1, nz):
            down_z(d).start()

    def down_sum():
        total = fd[zb, yb].astype(f32)
        for d in range(1, nz):
            down_z(d).wait_recv()
            total = total + fz_d[d - 1].astype(f32)
        fin_d[c, p] = total.astype(bf16)
        to_side("gd", fin_d, True).start()

    def pass_on(name, fin):
        to_side(name, fin, False).wait_recv()
        to_core(name, fin, True).start()

    u_out = pltpu.make_async_copy(fin_u, o_fu, out_sem.at[0])
    d_out = pltpu.make_async_copy(fin_d, o_fd, out_sem.at[1])
    p_out = pltpu.make_async_copy(fin_p, o_fp, out_sem.at[2])
    mg_out = pltpu.make_async_copy(mg_all, o_mg, out_sem.at[3])
    ml_out = pltpu.make_async_copy(ml_all, o_ml, out_sem.at[4])

    def side_first(k):
        return k % 2 == 0

    def p1(k):
        return link(f"p1{k}", wp.at[k, 1 - c], p_r1.at[k], core)

    def p2(k):
        if side_first(k):
            return link(f"p2{k}", wp.at[k, c, 1 - p], p_r2x.at[k], side)
        return link(f"p2{k}", wp.at[k, c, :, :, 1 - yb], p_r2y.at[k], beside)

    def p3(k):
        if side_first(k):
            return link(f"p3{k}", wp.at[k, c, p, :, 1 - yb], p_r3.at[k], beside)
        return link(f"p3{k}", wp.at[k, c, 1 - p, :, yb], p_r3.at[k], side)

    def p4(k, d):
        return link(
            f"p4{k}{d}", wp.at[k, c, p, others[d], yb], p_r4.at[k, d - 1], far[d]
        )

    def p_side(k, mine):
        x = p if mine else 1 - p
        return link(f"p5{k}", fin_p.at[k, c, x], fin_p.at[k, c, x], side)

    def p_core(k, mine):
        x = c if mine else 1 - c
        return link(f"p6{k}", fin_p.at[k, x], fin_p.at[k, x], core)

    def p_add_1(k):
        p1(k).wait_recv()

        def step(i, carry):
            x, z, y = i // (2 * nz), lax.rem(i // 2, nz), lax.rem(i, 2)
            wp[k, c, x, z, y] = wp[k, c, x, z, y] + p_r1[k, x, z, y]
            return carry

        lax.fori_loop(0, 4 * nz, step, 0)
        p2(k).start()

    def p_add_2(k):
        p2(k).wait_recv()

        def step(i, carry):
            if side_first(k):
                z, y = i // 2, lax.rem(i, 2)
                wp[k, c, p, z, y] = wp[k, c, p, z, y] + p_r2x[k, z, y]
            else:
                x, z = i // nz, lax.rem(i, nz)
                wp[k, c, x, z, yb] = wp[k, c, x, z, yb] + p_r2y[k, x, z]
            return carry

        lax.fori_loop(0, 2 * nz, step, 0)
        p3(k).start()

    def p_add_3(k):
        p3(k).wait_recv()

        def step(z, carry):
            wp[k, c, p, z, yb] = wp[k, c, p, z, yb] + p_r3[k, z]
            return carry

        lax.fori_loop(0, nz, step, 0)
        for d in range(1, nz):
            p4(k, d).start()

    def p_add_4(k):
        total = wp[k, c, p, zb, yb].astype(f32)
        for d in range(1, nz):
            p4(k, d).wait_recv()
            total = total + p_r4[k, d - 1].astype(f32)
        fin_p[k, c, p] = total.astype(bf16)
        p_side(k, True).start()

    def p_pass(k):
        p_side(k, False).wait_recv()
        p_core(k, True).start()

    peers = [core, side, beside]

    def kern_copy(name, kk, kr, stage):
        return link(f"{name}{stage}", kk.at[stage], kr.at[stage], peers[stage])

    def kern_far(name, kk, kz, d):
        return link(f"{name}z{d}", kk.at[3], kz.at[d - 1], far[d])

    def kern_step(name, kk, kr, kz, stage):
        kern_copy(name, kk, kr, stage).wait_recv()
        kk[stage + 1] = (kk[stage].astype(f32) + kr[stage].astype(f32)).astype(bf16)
        if stage < 2:
            kern_copy(name, kk, kr, stage + 1).start()
        else:
            for d in range(1, nz):
                kern_far(name, kk, kz, d).start()

    def kern_sum(name, kk, kz, out):
        total = kk[3].astype(f32)
        for d in range(1, nz):
            kern_far(name, kk, kz, d).wait_recv()
            total = total + kz[d - 1].astype(f32)
        out[...] = total

    one = ("one", kk_1, kr_1, kz_1)

    def taps_core():
        return link("kt0", kt.at[1 - c], kt_core, core)

    def taps_side():
        return link("kt1", kt.at[c, 1 - p], kt_side, side)

    def taps_y():
        return link("kt2", kt.at[c, p], kt_y, beside)

    def taps_z(d):
        return link(f"kt3{d}", kt_sum, kt_z.at[d - 1], far[d])

    def taps_core_add():
        taps_core().wait_recv()
        for x in range(2):
            kt[c, x] = kt[c, x] + kt_core[x]
        taps_side().start()

    def taps_side_add():
        taps_side().wait_recv()
        kt[c, p] = kt[c, p] + kt_side[...]
        taps_y().start()

    def taps_y_add():
        taps_y().wait_recv()
        kt_sum[...] = kt[c, p] + kt_y[...]
        for d in range(1, nz):
            taps_z(d).start()

    def taps_total():
        total = kt_sum[...].astype(f32)
        for d in range(1, nz):
            taps_z(d).wait_recv()
            total = total + kt_z[d - 1].astype(f32)
        fin_k[c, p] = total.astype(bf16)
        to_side("gk", fin_k, True).start()

    def mg_swap(mine=True):
        x = c if mine else 1 - c
        return link("mgc", mg_all.at[x], mg_all.at[x], core)

    def mg_copy(part, stage, mine=True):
        name, own, first, every = part
        if stage == 0:
            return link(f"{name}0", own.at[1 - c] if name == "mg" else own, first, core)
        every = every.at[c] if name == "mg" else every
        x = p if mine else 1 - p
        y = yb if mine else 1 - yb
        place = every.at[zb, yb, x] if stage == 1 else every.at[zb, y]
        return link(f"{name}{stage}", place, place, peers[stage])

    def mg_far(part, d, z):
        place = part[3].at[c, z] if part[0] == "mg" else part[3].at[z]
        return link(f"{part[0]}z{d}", place, place, far[d])

    def mg_step(part, stage):
        name, own, first, every = part
        mg_copy(part, stage, False).wait_recv()
        if stage == 0 and name == "mg":
            every[c, zb, yb, p] = own[c] + first[...]
        elif stage == 0:
            every[zb, yb, p] = own[...] + first[...]
        if stage < 2:
            mg_copy(part, stage + 1).start()
        else:
            for d in range(1, nz):
                mg_far(part, d, zb).start()

    def mg_end(part):
        for d in range(1, nz):
            mg_far(part, d, lax.rem(zb + nz - d, nz)).wait_recv()

    soon = ("mg", mg_own, mg_r1, mg_all)
    final = ("ml", ml_own, ml_r1, ml_all)

    pieces = [
        (wo_in, wo), (att_in, att), (tok_in, tok), (proj_in, proj), (wqkv_in, wqkv), (x_in, xf),
        (mid_in, mid),
    ]
    loads = [
        pltpu.make_async_copy(src, dst, load_sem.at[n]) for n, (src, dst) in enumerate(pieces)
    ]
    full = dq_in.shape[0] - parts
    early = [
        pltpu.make_async_copy(uh_in.at[p], fu.at[:, :, pl.ds(0, LANES)], load_sem.at[7]),
        pltpu.make_async_copy(ul_in.at[:, :, yb], ly, load_sem.at[8]),
        pltpu.make_async_copy(ud_in, fin_u.at[c, p, :, pl.ds(0, lead)], load_sem.at[9]),
    ]
    late = [pltpu.make_async_copy(dl_in.at[p], ld, load_sem.at[10])]
    for owner in range(2 * nz):
        count = min(per, full - owner * per)
        if count > 0:
            late.append(
                pltpu.make_async_copy(
                    dq_in.at[pl.ds(owner * per, count)],
                    fd.at[owner // 2, owner % 2, pl.ds(0, count)],
                    load_sem.at[11 + owner],
                )
            )
    for load in (*loads[:4], *late, *early, *loads[4:]):
        load.start()
    half_width, quarter = width // 2, kt.shape[3]
    for x in range(2):
        span = slice(x * half_width, (x + 1) * half_width)
        mg_own[x] = small[:, span]
        mg_own[x, 6:8, :] = mod[6:8, span]
        for q in range(2):
            at = (2 * x + q) * quarter
            kt[x, q] = kern_two[:, at : at + quarter].astype(bf16)
    meet([core, side, corner, beside, *far[1:]])
    grad_away = remote(
        rg_in.at[:, 1 - c], rows_m.at[pl.ds(8 * c, 8)], ex_send.at[0], ex_recv.at[0], core
    )
    grad_away.start()
    grad_own = pltpu.make_async_copy(rg_in.at[:, c], rows_m.at[pl.ds(8 * c, 8)], own_sem.at[0])
    grad_own.start()
    last_d().start()
    last_y().start()
    half_x().start()
    mg_copy(soon, 0).start()
    taps_core().start()
    perm[0] = permutation(False)
    perm[1] = permutation(True)
    grad_own.wait()
    grad_away.wait()
    grad[...] = dot_nn(perm[0], rows_m[...].reshape(tokens, width)).astype(bf16)
    loads[0].wait()
    loads[1].wait()
    datt[...] = dot_nt(grad[...], wo[...]).astype(bf16)
    out_grad = dot_tn(att[...], grad[...])
    for k in range(chunks):
        cut = slice(k * chunk, (k + 1) * chunk)
        wp[k, 1, 1] = out_grad[:, cut].reshape(nz, 2, rows_own, chunk).astype(bf16)
    loads[2].wait()
    tok_t[...] = tok[...].T
    loads[3].wait()
    for n in range(2):
        send_home(n, res_in, o_res, r_send, r_recv, False)

    low_lane = lax.broadcasted_iota(jnp.int32, (size, LANES), 1) < LANES // 2
    lane_id = lax.broadcasted_iota(jnp.int32, (size, LANES), 1)
    zero = jnp.zeros((), bf16)

    def attend(index, carry):
        pair, half = index // 2, lax.rem(index, 2)
        rows = pl.ds(pl.multiple_of(half * size, size), size)

        def cut(n):
            return pl.ds(pl.multiple_of(n * width + pair * LANES, LANES), LANES)

        q = proj[rows, cut(0)] * jnp.asarray(0.125, bf16)
        k, v, up = proj[rows, cut(1)], proj[rows, cut(2)], datt[rows, cut(0)]
        sums = lse[half]
        dq = jnp.zeros((size, LANES), f32)
        dk = jnp.zeros((size, LANES), f32)
        dv = jnp.zeros((size, LANES), f32)
        for h in range(2):
            mine = low_lane if h == 0 else jnp.logical_not(low_lane)
            key = jnp.where(mine, k, zero)
            scores = dot_nt(q, key) + bias[half]
            mass = jnp.sum(
                jnp.where(lane_id == 2 * pair + h, sums, 0.0), axis=-1, keepdims=True
            )
            weights = jnp.exp(scores - mass)
            pull = dot_nt(up, jnp.where(mine, v, zero))
            mean = jnp.sum(weights * pull, axis=-1, keepdims=True)
            spare = (weights * (pull - mean)).astype(bf16)
            dq = dq + dot_nn(spare, key)
            dk = dk + dot_tn(spare, jnp.where(mine, q, zero))
            dv = dv + dot_tn(weights.astype(bf16), jnp.where(mine, up, zero))
        dproj[rows, cut(0)] = (dq * 0.125).astype(bf16)
        dproj[rows, cut(1)] = dk.astype(bf16)
        dproj[rows, cut(2)] = dv.astype(bf16)
        return carry

    def weigh(k):
        span = slice(2 * k * chunk, 2 * (k + 1) * chunk)
        for q in range(3):
            part = dot_nn(tok_t[...], dproj[:, q * width + span.start : q * width + span.stop])
            part = part.reshape(nz, 2, rows_own, 2 * chunk).astype(bf16)
            for n in range(2):
                wp[2 * k + n, q % 2, q // 2] = part[..., n * chunk : (n + 1) * chunk]
        p1(2 * k).start()
        p1(2 * k + 1).start()

    hooks = {
        0: [lambda: mg_step(soon, 0), taps_core_add],
        1: [half_add],
        2: [place_last],
        3: [lambda: weigh(0), last_y_add],
        5: [lambda: mg_step(soon, 1), taps_side_add],
        7: [lambda: weigh(1), lambda: p_add_1(0), lambda: p_add_1(1)],
        9: [last_x_add],
        10: [lambda: mg_step(soon, 2), taps_y_add],
        11: [lambda: weigh(2)],
    }

    def attend_and_pass(index, carry):
        attend(index, carry)
        for at, steps in hooks.items():

            @pl.when(index == at)
            def _(steps=steps):
                for step in steps:
                    step()

        return carry

    lax.fori_loop(0, 2 * pairs, attend_and_pass, 0)
    loads[4].wait()
    back = dot_nt(dproj[...], wqkv[...]).astype(bf16)
    brm[...] = dot_nn(perm[1], back).astype(bf16).reshape(16, across, width)
    mixed_away = remote(
        brm.at[pl.ds(7 * (1 - c), 9)], frame.at[:, c], ex_send.at[1], ex_recv.at[1], core
    )
    mixed_away.start()
    mixed_own = pltpu.make_async_copy(brm.at[pl.ds(7 * c, 9)], frame.at[:, c], own_sem.at[1])
    mixed_own.start()
    p_add_2(0)
    p_add_2(1)
    p_add_1(2)
    p_add_1(3)
    loads[5].wait()
    loads[6].wait()

    shift = mod[0:1, :]
    scale_in = 1.0 + mod[1:2, :]

    def again(row, carry):
        normal, _ = normalize(xf[2 * c + row].astype(f32))
        value[row] = (normal * scale_in + shift).astype(bf16).astype(f32)
        return carry

    lax.fori_loop(0, 16, again, 0)
    p_add_1(4)
    p_add_1(5)
    mixed_own.wait()
    mixed_away.wait()

    def lay(row, carry):
        at = c + row
        line = frame[at // 2, lax.rem(at, 2)].astype(f32)
        before, after = column_shifts(line)
        gs[0, 1 - c + row] = after
        gs[1, 1 - c + row] = line
        gs[2, 1 - c + row] = before
        return carry

    lax.fori_loop(0, 17, lay, 0)
    for s in range(3):
        gs[s, 17 * c] = jnp.zeros((across, width), f32)

    def conv_back(lane, half):
        span = slice(lane, lane + LANES)
        taps = [kern[n : n + 1, span].astype(f32) for n in range(9)]

        def backward(row, sums):
            total = jnp.zeros((across, LANES), f32)
            own = value[row, :, span]
            later = []
            for r in range(3):
                for s in range(3):
                    line = gs[s, row + 2 - r, :, span]
                    total = total + taps[3 * r + s] * line
                    later.append(sums[3 * r + s] + fold(own * line))
            agrad[row, :, span] = total
            return tuple(later)

        sums = lax.fori_loop(
            8 * half, 8 * half + 8, backward,
            tuple(jnp.zeros((8, LANES), f32) for _ in range(9)),
        )
        rows9 = [jnp.sum(sums[n], axis=0, keepdims=True) for n in range(9)]
        lines = jnp.concatenate(rows9 + [jnp.zeros((7, LANES), f32)])
        if half == 0:
            taps_sum[:, span] = lines
        else:
            kk_1[0, :, span] = (taps_sum[:, span] + lines).astype(bf16)

    def finish(row, sums):
        normal, scale = normalize(xf[2 * c + row].astype(f32))
        line = agrad[row]
        place = pl.ds(pl.multiple_of(row * across, across), across)
        total = mid[place, :] + normalize_back(line * scale_in, normal, scale)
        ig[row] = total.astype(bf16)
        return (sums[0] + fold(line), sums[1] + fold(line * normal))

    sums = tuple(jnp.zeros((8, width), f32) for _ in range(2))
    down_y_add()
    p_add_3(0)
    p_add_3(1)
    for lane in range(0, width, LANES):
        conv_back(lane, 0)
        if lane == 2 * LANES:
            p_add_2(2)
            p_add_2(3)
    sums = lax.fori_loop(0, 8, finish, sums)
    send_home(0, ig, o_ig, i_send, i_recv, False)
    p_add_2(4)
    p_add_2(5)
    for lane in range(0, width, LANES):
        conv_back(lane, 1)
        if lane == 2 * LANES:
            p_add_3(2)
            p_add_3(3)
    kern_copy("one", kk_1, kr_1, 0).start()
    sums = lax.fori_loop(8, 16, finish, sums)
    for n in range(2):
        ml_own[n : n + 1, :] = jnp.sum(sums[n], axis=0, keepdims=True)
    mg_copy(final, 0).start()
    send_home(1, ig, o_ig, i_send, i_recv, False)
    up_sum()
    p_add_3(4)
    p_add_3(5)
    p_add_4(0)
    p_add_4(1)
    taps_total()
    mg_end(soon)
    mg_swap().start()
    kern_step(*one, 0)
    mg_step(final, 0)
    down_sum()
    pass_on("gu", fin_u)
    p_pass(0)
    p_pass(1)
    pass_on("gk", fin_k)
    kern_step(*one, 1)
    mg_step(final, 1)
    p_add_4(2)
    p_add_4(3)
    mg_swap(False).wait_recv()
    mg_out.start()
    to_core("gu", fin_u, False).wait_recv()
    u_out.start()
    kern_step(*one, 2)
    mg_step(final, 2)
    pass_on("gd", fin_d)
    p_add_4(4)
    p_add_4(5)
    p_pass(2)
    p_pass(3)
    to_core("gd", fin_d, False).wait_recv()
    d_out.start()
    kern_sum("one", kk_1, kz_1, o_one)
    mg_end(final)
    ml_out.start()
    p_pass(4)
    p_pass(5)
    for k in range(chunks):
        p_core(k, False).wait_recv()
    p_out.start()
    to_core("gk", fin_k, False).wait_recv()
    for x in range(4):
        o_two[:, x * quarter : (x + 1) * quarter] = fin_k[x // 2, x % 2].astype(f32)
    gone([half_x(), last_y(), last_x(), last_d(), down_y()])
    gone([taps_core(), taps_side(), taps_y(), mg_swap()])
    for name, fin in (("gu", fin_u), ("gd", fin_d), ("gk", fin_k)):
        gone([to_side(name, fin, True), to_core(name, fin, True)])
    for d in range(1, nz):
        gone([up_z(d), down_z(d), mg_far(soon, d, zb), mg_far(final, d, zb)])
        gone([kern_far("one", kk_1, kz_1, d), taps_z(d)])
    for k in range(chunks):
        gone([p1(k), p2(k), p3(k), p_side(k, True), p_core(k, True)])
        gone([p4(k, d) for d in range(1, nz)])
    for stage in range(3):
        gone([mg_copy(soon, stage), mg_copy(final, stage)])
        gone([kern_copy("one", kk_1, kr_1, stage)])
    for n in range(2):
        send_home(n, res_in, o_res, r_send, r_recv, True)
        send_home(n, ig, o_ig, i_send, i_recv, True)
    home(o_res, r_recv)
    home(o_ig, i_recv)
    for out in (u_out, d_out, p_out, mg_out, ml_out):
        out.wait()


def back(
    mid, rg, tok, proj, att, lse, bias, x_frame, mod, small, kern, wqkv, wo, res,
    ud, dq, uh, ul, dl, kern_two,
):
    nb = lax.axis_size("batch")
    nz = nb // 2
    across, width = x_frame.shape[1], x_frame.shape[2]
    tokens = 16 * across
    rows = width // nb
    grain = dq.shape[1]
    parts = dl.shape[1]
    per = dq.shape[0] // nb
    chunks, chunk = width // LANES, LANES
    many = max(nz - 1, 1)
    any_space = pl.BlockSpec(memory_space=pl.ANY)
    vmem = pl.BlockSpec(memory_space=pltpu.VMEM)
    shape = jax.ShapeDtypeStruct
    dma = pltpu.SemaphoreType.DMA
    wide = kern_two.shape[1]
    links = 100 + 20 * many

    def low(*dims):
        return pltpu.VMEM(dims, bf16)

    def high(*dims):
        return pltpu.VMEM(dims, f32)

    return pl.pallas_call(
        back_kernel,
        out_shape=(
            shape((2, 2, rows, width), bf16),
            shape((2, 2, per, grain, width), bf16),
            shape((chunks, 2, 2, rows, chunk), bf16),
            shape((2, 8, across, width), bf16),
            shape((2, 8, across, width), bf16),
            shape((16, width), f32),
            shape((16, wide), f32),
            shape((2, nz, 2, 2, 8, width // 2), f32),
            shape((nz, 2, 2, 2, width), f32),
        ),
        in_specs=[any_space] * 5 + [vmem, vmem, any_space, vmem, vmem, vmem] + [any_space] * 8
        + [vmem],
        out_specs=[any_space] * 5 + [vmem, vmem, any_space, any_space],
        scratch_shapes=[
            high(tokens, width), low(tokens, width), low(width, tokens), low(tokens, 3 * width),
            low(tokens, width), low(18, across, width), low(*wqkv.shape), low(*wo.shape),
            low(16, across, width), low(2, tokens, tokens), low(tokens, width),
            low(tokens, width), low(tokens, 3 * width),
            low(16, across, width), low(9, 2, across, width), high(3, 18, across, width),
            high(16, across, width), high(16, across, width), low(16, across, width),
            low(chunks, 2, 2, nz, 2, rows, chunk), low(chunks, 2, nz, 2, rows, chunk),
            low(chunks, nz, 2, rows, chunk), low(chunks, 2, nz, rows, chunk),
            low(chunks, nz, rows, chunk), low(chunks, many, rows, chunk),
            low(chunks, 2, 2, rows, chunk),
            low(nz, rows, 2 * LANES), low(nz, 2, per, grain, width),
            low(many, rows, 2 * LANES), low(nz, per, grain, width), low(many, per, grain, width),
            low(2, 2, rows, width), low(2, 2, per, grain, width),
            low(parts, grain, width), low(parts, grain, width),
            low(nz, rows, LANES), low(2, nz, rows, LANES), low(2, nz, rows, LANES),
            low(nz, rows, LANES),
            high(2, 8, width // 2), high(8, width // 2), high(2, nz, 2, 2, 8, width // 2),
            high(2, width), high(2, width), high(nz, 2, 2, 2, width), high(16, width),
            low(4, 16, width), low(3, 16, width), low(many, 16, width),
            low(2, 2, 16, wide // 4), low(2, 16, wide // 4), low(16, wide // 4), low(16, wide // 4),
            low(16, wide // 4), low(many, 16, wide // 4), low(2, 2, 16, wide // 4),
            dma((11 + nb,)), dma((2,)), dma((2,)), dma((2,)), dma((2,)), dma((2,)), dma((2,)),
            dma((2,)), dma((links,)), dma((links,)), dma((5,)),
        ],
        compiler_params=pltpu.CompilerParams(
            collective_id=2, has_side_effects=True, vmem_limit_bytes=63 << 20
        ),
        name="back",
    )(
        mid, rg, tok, proj, att, lse, bias, x_frame, mod, small, kern, wqkv, wo, res,
        ud, dq, uh, ul, dl, kern_two,
    )


def parts_of(values):
    first = values.astype(bf16)
    rest = values - first.astype(f32)
    second = rest.astype(bf16)
    third = (rest - second.astype(f32)).astype(bf16)
    return jnp.concatenate([first, second, third], axis=0)


def thrice(values):
    return jnp.concatenate([values] * 3, axis=0).astype(bf16)


def tail_kernel(
    fu, fd, fp, mg, late, one, two, wm_in, res_in, ig_in,
    o_class, o_time, o_mod, o_proj, o_out, o_one, o_up, o_two, o_down, o_res, o_ig,
    wm, moved, load_sem, in_sem, out_sem,
):
    b = lax.axis_index("batch")
    width = 2 * mg.shape[3]
    canvases = mg.shape[1]
    own = o_mod.shape[0]
    whole = wm_in.shape[0] == own
    source = wm_in if whole else wm_in.at[pl.ds(pl.multiple_of(b * own, 16), own)]
    load = pltpu.make_async_copy(source, wm, load_sem)
    load.start()
    takes = [
        pltpu.make_async_copy(src, moved.at[n], in_sem.at[n]) for n, src in enumerate((res_in, ig_in))
    ]
    gives = [
        pltpu.make_async_copy(moved.at[n], dst, out_sem.at[n]) for n, dst in enumerate((o_res, o_ig))
    ]
    for take in takes:
        take.start()
    chunks, chunk = fp.shape[0], fp.shape[4]
    per, grain = fd.shape[2], fd.shape[3]
    for q in range(4):
        for j in range(width // LANES):
            at = (4 * j + q) * LANES
            o_up[:, at : at + LANES] = fu[q % 2, q // 2, :, j * LANES : (j + 1) * LANES].astype(f32)
        for i in range(per):
            at = (4 * i + q) * grain
            o_down[at : at + grain, :] = fd[q % 2, q // 2, i].astype(f32)
        for k in range(chunks):
            part = fp[k, q % 2, q // 2].astype(f32)
            if q < 3:
                o_proj[:, q * width + k * chunk : q * width + (k + 1) * chunk] = part
            else:
                o_out[:, k * chunk : (k + 1) * chunk] = part
    for take, give in zip(takes, gives):
        take.wait()
        give.start()

    def window(values, n):
        size = values.shape[1]
        return pltpu.roll(values, lax.rem(size - b * n, size), 1)[:, :n]

    o_one[...] = window(one[...], own)[0:9]
    o_two[...] = window(two[...], o_two.shape[1])[0:9]
    every = jnp.concatenate([mg[0], mg[1]], axis=2)
    begin = late[...]
    cond = window(every[:, 7, :] * 0.5, own)
    sigma = 1.0 / (1.0 + jnp.exp(-cond))
    low = thrice(cond * sigma)
    steep = sigma * (1.0 + cond * (1.0 - sigma))
    act_grad = jnp.zeros((3 * canvases, own), f32)
    load.wait()
    for part in range(6):
        span = slice(part * width, (part + 1) * width)
        line = parts_of(begin[:, part, :] if part < 2 else every[:, part, :])
        o_mod[:, span] = dot_tn(low, line)
        act_grad = act_grad + dot_nt(line, wm[:, span])
    act_grad = (
        act_grad[2 * canvases :] + act_grad[canvases : 2 * canvases] + act_grad[:canvases]
    )
    cond_grad = parts_of(act_grad * steep)
    names = every[:, 6, :] * 0.5
    kinds = o_class.shape[1]
    spot = lax.broadcasted_iota(jnp.int32, (canvases, kinds), 1).astype(f32)
    for n, out in enumerate((o_class, o_time)):
        hot = thrice(jnp.where(spot == names[:, n : n + 1], 1.0, 0.0))
        out[...] = dot_tn(cond_grad, hot)
    for give in gives:
        give.wait()


def tail(fu, fd, fp, mg, late, one, two, wmod, res, ig, classes, times):
    nb = lax.axis_size("batch")
    width = 2 * mg.shape[3]
    own = width // nb
    wide = two.shape[1] // nb
    if own % 16:
        wmod = lax.dynamic_slice_in_dim(wmod, lax.axis_index("batch") * own, own, axis=0)
    any_space = pl.BlockSpec(memory_space=pl.ANY)
    vmem = pl.BlockSpec(memory_space=pltpu.VMEM)
    shape = jax.ShapeDtypeStruct
    dma = pltpu.SemaphoreType.DMA
    return pl.pallas_call(
        tail_kernel,
        out_shape=(
            shape((own, classes), f32),
            shape((own, times), f32),
            shape((own, 6 * width), f32),
            shape((own, 3 * width), f32),
            shape((own, width), f32),
            shape((9, own), f32),
            shape((own, 4 * width), f32),
            shape((9, wide), f32),
            shape((4 * fd.shape[2] * fd.shape[3], width), f32),
            shape(res.shape, bf16),
            shape(ig.shape, bf16),
        ),
        in_specs=[vmem] * 7 + [any_space] * 3,
        out_specs=[vmem] * 9 + [any_space] * 2,
        scratch_shapes=[
            pltpu.VMEM((own, 6 * width), bf16), pltpu.VMEM((2, *res.shape), bf16),
            dma, dma((2,)), dma((2,)),
        ],
        compiler_params=pltpu.CompilerParams(vmem_limit_bytes=60 << 20),
        name="tail",
    )(fu, fd, fp, mg, late, one, two, wmod, res, ig)


def body(
    inputs,
    segments,
    class_labels,
    time_steps,
    class_table,
    time_table,
    modulation_weight,
    project_weight,
    output_weight,
    kernel_attention,
    up_weight,
    kernel_feed,
    down_weight,
    cotangent,
):
    across, width = inputs.shape[2], inputs.shape[3]
    nb = lax.axis_size("batch")
    units = up_weight.shape[1]
    grain = 16 if (units // nb) % 64 == 0 else 8
    x_frame, cot_frame, returned, tok, proj, att, lse, bias, mod = front(
        inputs, cotangent, class_labels, time_steps, segments, kernel_attention, class_table,
        time_table, modulation_weight, project_weight, output_weight,
    )
    flat = (18 * across, width)
    ud, dq, uh, ul, dl, kern_two, res, mid, rg, small = feed(
        x_frame.reshape(flat), returned.reshape(flat), cot_frame.reshape(flat), mod, up_weight,
        kernel_feed, down_weight, grain,
    )
    fu, fd, fp, result, inputs_gradient, one, two, gathered, late = back(
        mid, rg.reshape(8, 2, across, width), tok, proj, att, lse, bias, x_frame, mod, small,
        kernel_attention, project_weight, output_weight, res.reshape(16, across, width),
        ud, dq, uh, ul, dl, kern_two,
    )
    (
        class_total, time_total, modulation_total, project_total, output_total,
        attention_kernel_total, up_total, feed_kernel_total, down_total, result, inputs_gradient,
    ) = tail(
        fu, fd, fp, gathered.reshape(2, 2 * nb, 8, width // 2), late.reshape(2 * nb, 2, width), one, two,
        modulation_weight, result, inputs_gradient, class_table.shape[0], time_table.shape[0],
    )
    return (
        result,
        inputs_gradient,
        class_total.T,
        time_total.T,
        modulation_total,
        project_total,
        output_total,
        attention_kernel_total,
        up_total,
        feed_kernel_total,
        down_total,
    )


def solution(mesh):
    in_specs = (
        P("batch", "group", None, None),
        P("batch", None),
        P("batch"),
        P("batch"),
        P(),
        P(),
        P(),
        P(),
        P(),
        P(),
        P(),
        P(),
        P(),
        P("batch", "group", None, None),
    )
    out_specs = (
        P("batch", "group", None, None),
        P("batch", "group", None, None),
        P(None, "batch"),
        P(None, "batch"),
        P("batch", None),
        P("batch", None),
        P("batch", None),
        P(None, "batch"),
        P("batch", None),
        P(None, "batch"),
        P("batch", None),
    )
    return jax.shard_map(body, mesh=mesh, in_specs=in_specs, out_specs=out_specs, check_vma=False)
```

```python
from functools import partial

import jax
import jax.numpy as jnp
from jax import lax
from jax.experimental import pallas as pl
from jax.experimental.pallas import tpu as pltpu
from jax.sharding import PartitionSpec as P

HEADS = 12
MESH = pl.DeviceIdType.MESH
LANES = 128
f32 = jnp.float32
bf16 = jnp.bfloat16
highest = lax.Precision.HIGHEST


def dot_nn(a, b):
    return lax.dot_general(a, b, (((1,), (0,)), ((), ())), preferred_element_type=f32)


def dot_nt(a, b):
    return lax.dot_general(a, b, (((1,), (1,)), ((), ())), preferred_element_type=f32)


def dot_tn(a, b):
    return lax.dot_general(a, b, (((0,), (0,)), ((), ())), preferred_element_type=f32)


def remote(src, dst, send, recv, target):
    return pltpu.make_async_remote_copy(
        src_ref=src, dst_ref=dst, send_sem=send, recv_sem=recv, device_id=target,
        device_id_type=MESH,
    )


def meet(partners):
    barrier = pltpu.get_barrier_semaphore()
    for partner in partners:
        pl.semaphore_signal(barrier, inc=1, device_id=partner, device_id_type=MESH)
    pl.semaphore_wait(barrier, len(partners))


def normalize(values):
    center = values - jnp.mean(values, axis=-1, keepdims=True)
    second = jnp.mean(center * center, axis=-1, keepdims=True)
    scale = lax.rsqrt(second + 1e-06)
    return center * scale, scale


def normalize_back(grad, normal, scale):
    return scale * (
        grad
        - jnp.mean(grad, axis=-1, keepdims=True)
        - normal * jnp.mean(grad * normal, axis=-1, keepdims=True)
    )


def column_shifts(row):
    across = row.shape[0]
    column = lax.broadcasted_iota(jnp.int32, row.shape, 0)
    before = jnp.where(column == 0, 0.0, pltpu.roll(row, 1, 0))
    after = jnp.where(column == across - 1, 0.0, pltpu.roll(row, across - 1, 0))
    return before, after


def fold(values):
    rows, width = values.shape
    return jnp.sum(values.reshape(rows // 8, 8, width), axis=0)


def grouped(count, body, carry, size=4, begin=0):
    def several(i, carry):
        for n in range(size):
            carry = body(begin + size * i + n, carry)
        return carry

    whole = count // size
    carry = lax.fori_loop(0, whole, several, carry)
    for n in range(whole * size, count):
        carry = body(begin + n, carry)
    return carry


def permutation(inverse):
    n = 512
    to = lax.broadcasted_iota(jnp.int32, (n, n), 1 if inverse else 0)
    source = lax.broadcasted_iota(jnp.int32, (n, n), 0 if inverse else 1)
    wanted = lax.shift_left(lax.shift_right_logical(to & 255, 4), 5) + 2 * (to & 15) + (
        lax.shift_right_logical(to, 8)
    )
    return jnp.where(source == wanted, 1.0, 0.0).astype(bf16)


def front_kernel(
    x_in, cot_in, names, moments, segments, kern, class_in, time_in, wmod_in, wqkv_in, wo_in,
    o_x, o_cot, o_ret, o_tok, o_proj, o_att, o_lse, o_bias, mod,
    xf, table, wmod, wqkv, wo, shifts, mixed, rows_m, perm, bias, tok, proj, att, lse, brm,
    load_sem, x_send, x_recv, c_send, c_recv, ex_send, ex_recv, own_sem, out_sem,
):
    b = lax.axis_index("batch")
    g = lax.axis_index("group")
    c, p = lax.rem(g, 2), g // 2
    core, side, corner = (b, g + 1 - 2 * c), (b, g + 2 - 4 * p), (b, 3 - g)
    inner = jnp.logical_or(g == 1, g == 2)
    width = xf.shape[-1]
    across = xf.shape[1]

    def spread_out(src, dst, send, recv, waiting):
        main = c * 8 + p * 2
        other_main = remote(
            src.at[1 - p], dst.at[pl.ds(main, 8)], send.at[0], recv.at[c], (b, 2 - p)
        )
        edge = 6 * (2 - g)
        edge_to = 16 * (g - 1)
        other_edge = remote(
            src.at[1 - p, pl.ds(edge, 2)], dst.at[pl.ds(edge_to, 2)], send.at[1], recv.at[2], side
        )
        own_main = remote(src.at[p], dst.at[pl.ds(main, 8)], send.at[2], recv.at[c], core)
        own_edge = pltpu.make_async_copy(
            src.at[p, pl.ds(edge, 2)], dst.at[pl.ds(edge_to, 2)], recv.at[2]
        )
        stay_main = pltpu.make_async_copy(src.at[p], dst.at[pl.ds(main, 8)], recv.at[c])
        if waiting:
            other_main.wait_send()

            @pl.when(inner)
            def _():
                other_edge.wait_send()
                own_main.wait_send()

        else:
            other_main.start()

            @pl.when(inner)
            def _():
                other_edge.start()
                own_main.start()
                own_edge.start()

            @pl.when(jnp.logical_not(inner))
            def _():
                stay_main.start()

    def arrived(dst, recv):
        for j in range(2):
            place = dst.at[pl.ds(8 * j + 2 * c, 8)]
            pltpu.make_async_copy(place, place, recv.at[j]).wait()
        place = dst.at[pl.ds(16 * (1 - c), 2)]
        pltpu.make_async_copy(place, place, recv.at[2]).wait()

    pieces = [
        (wqkv_in, wqkv), (wo_in, wo), (class_in, table.at[0]), (time_in, table.at[1]),
        (wmod_in, wmod),
    ]
    loads = [
        pltpu.make_async_copy(src, dst, load_sem.at[n]) for n, (src, dst) in enumerate(pieces)
    ]
    for n in (2, 3, 4, 0, 1):
        loads[n].start()
    meet([core, side, corner])
    spread_out(x_in, xf, x_send, x_recv, False)
    perm[0] = permutation(False)
    perm[1] = permutation(True)
    n = tok.shape[0]
    wide = segments.shape[1]
    to = lax.broadcasted_iota(jnp.int32, (n, wide), 0)
    source = lax.broadcasted_iota(jnp.int32, (n, wide), 1)
    wanted = lax.shift_left(2 * lax.shift_right_logical(to & 255, 4) + c, 5) + 2 * (to & 15) + (
        lax.shift_right_logical(to, 8)
    )
    chosen = source == wanted
    one_line = jnp.where(p == 0, segments[0:1, :], segments[1:2, :]).astype(f32)
    lines = jnp.broadcast_to(one_line, (8, wide)).astype(bf16)
    lab_row = dot_nt(lines, jnp.where(chosen, 1.0, 0.0).astype(bf16))
    lab_col = jnp.sum(jnp.where(chosen, one_line, 0.0), axis=-1, keepdims=True)
    for half in range(2):
        cut = slice(half * (n // 2), (half + 1) * (n // 2))
        bias[half] = jnp.where(lab_row[0:1, cut] == lab_col[cut], 0.0, -1e30)
    bias_out = pltpu.make_async_copy(bias, o_bias, out_sem.at[5])
    bias_out.start()
    name = jnp.where(p == 0, names[0], names[1])
    moment = jnp.where(p == 0, moments[0], moments[1])
    loads[2].wait()
    loads[3].wait()
    rows_all = lax.broadcasted_iota(jnp.int32, (8, table.shape[1]), 1)
    cond = dot_nn(jnp.where(rows_all == name, 1.0, 0.0).astype(bf16), table[0]) + dot_nn(
        jnp.where(rows_all == moment, 1.0, 0.0).astype(bf16), table[1]
    )
    cond_low = (cond / (1.0 + jnp.exp(-cond))).astype(bf16)
    loads[4].wait()
    for part in range(6):
        cut = slice(part * width, (part + 1) * width)
        mod[part : part + 1, :] = dot_nn(cond_low, wmod[:, cut])[0:1, :]
    lane_of = lax.broadcasted_iota(jnp.int32, (1, width), 1)
    mod[6:7, :] = jnp.where(
        lane_of == 0, name.astype(f32), jnp.where(lane_of == 1, moment.astype(f32), 0.0)
    )
    mod[7:8, :] = cond[0:1, :]
    arrived(xf, x_recv)
    spread_out(cot_in, o_cot, c_send, c_recv, False)
    x_out = pltpu.make_async_copy(xf, o_x, out_sem.at[0])
    x_out.start()

    shift = mod[0:1, :]
    scale = 1.0 + mod[1:2, :]

    def first(i, carry):
        normal, _ = normalize(xf[c + i].astype(f32))
        value = (normal * scale + shift).astype(bf16).astype(f32)
        before, after = column_shifts(value)
        shifts[0, 1 - c + i] = before
        shifts[1, 1 - c + i] = value
        shifts[2, 1 - c + i] = after
        return carry

    grouped(17, first, 0)
    for s in range(3):
        shifts[s, 17 * c] = jnp.zeros((across, width), f32)

    def conv(step, parity):
        o = 2 * step + parity
        for lane in range(0, width, LANES):
            cut = slice(lane, lane + LANES)
            total = jnp.zeros((across, LANES), f32)
            for r in range(3):
                for s in range(3):
                    tap = kern[3 * r + s : 3 * r + s + 1, cut].astype(f32)
                    total = total + tap * shifts[s, o + r, :, cut]
            mixed[step, parity, :, cut] = total.astype(bf16)

    def conv_away(step, carry):
        conv(step, 1 - c)
        return carry

    def conv_own(step, carry):
        conv(step, c)
        return carry

    lax.fori_loop(0, 8, conv_away, 0)
    mixed_away = remote(
        mixed.at[:, 1 - c], rows_m.at[pl.ds(8 * c, 8)], ex_send.at[0], ex_recv.at[0], core
    )
    mixed_away.start()
    lax.fori_loop(0, 8, conv_own, 0)
    mixed_own = pltpu.make_async_copy(mixed.at[:, c], rows_m.at[pl.ds(8 * c, 8)], own_sem.at[0])
    mixed_own.start()
    mixed_own.wait()
    mixed_away.wait()
    flat = rows_m[...].reshape(16 * across, width)
    tok[...] = dot_nn(perm[0], flat).astype(bf16)
    tok_out = pltpu.make_async_copy(tok, o_tok, out_sem.at[1])
    tok_out.start()
    loads[0].wait()
    for part in range(3):
        cut = slice(part * width, (part + 1) * width)
        proj[:, cut] = dot_nn(tok[...], wqkv[:, cut]).astype(bf16)
    proj_out = pltpu.make_async_copy(proj, o_proj, out_sem.at[2])
    proj_out.start()

    pairs = width // LANES
    size = tok.shape[0] // 2
    low_lane = lax.broadcasted_iota(jnp.int32, (size, LANES), 1) < LANES // 2
    lane_id = lax.broadcasted_iota(jnp.int32, (size, LANES), 1)
    zero = jnp.zeros((), bf16)

    def attend(index, carry):
        half, pair = index // pairs, lax.rem(index, pairs)
        rows = pl.ds(pl.multiple_of(half * size, size), size)

        def part(n):
            return proj[rows, pl.ds(pl.multiple_of(n * width + pair * LANES, LANES), LANES)]

        q, k, v = part(0) * jnp.asarray(0.125, bf16), part(1), part(2)
        total = jnp.zeros((size, LANES), f32)
        sums = lse[half]
        for h in range(2):
            mine = low_lane if h == 0 else jnp.logical_not(low_lane)
            scores = dot_nt(q, jnp.where(mine, k, zero)) + bias[half]
            top = jnp.max(scores, axis=-1, keepdims=True)
            powers = jnp.exp(scores - top)
            mass = jnp.sum(powers, axis=-1, keepdims=True)
            weights = (powers * (1.0 / mass)).astype(bf16)
            total = total + dot_nn(weights, jnp.where(mine, v, zero))
            sums = jnp.where(lane_id == 2 * pair + h, top + jnp.log(mass), sums)
        lse[half] = sums
        att[rows, pl.ds(pl.multiple_of(pair * LANES, LANES), LANES)] = total.astype(bf16)
        return carry

    lse[...] = jnp.zeros(lse.shape, f32)
    grouped(2 * pairs, attend, 0)
    att_out = pltpu.make_async_copy(att, o_att, out_sem.at[3])
    att_out.start()
    lse_out = pltpu.make_async_copy(lse, o_lse, out_sem.at[4])
    lse_out.start()
    loads[1].wait()
    branch = dot_nn(att[...], wo[...]).astype(bf16)
    brm[...] = dot_nn(perm[1], branch).astype(bf16).reshape(16, across, width)
    ret_away = remote(
        brm.at[pl.ds(7 * (1 - c), 9)], o_ret.at[:, c], ex_send.at[1], ex_recv.at[1], core
    )
    ret_away.start()
    ret_own = pltpu.make_async_copy(brm.at[pl.ds(7 * c, 9)], o_ret.at[:, c], own_sem.at[1])
    ret_own.start()
    for out in (x_out, tok_out, proj_out, att_out, lse_out, bias_out, ret_own):
        out.wait()
    ret_away.wait()
    spread_out(x_in, xf, x_send, x_recv, True)
    spread_out(cot_in, o_cot, c_send, c_recv, True)
    arrived(o_cot, c_recv)


def front(inputs, cotangent, names, moments, segments, kern, classes, times, wmod, wqkv, wo):
    across, width = inputs.shape[2], inputs.shape[3]
    tokens = 16 * across
    any_space = pl.BlockSpec(memory_space=pl.ANY)
    vmem = pl.BlockSpec(memory_space=pltpu.VMEM)
    smem = pl.BlockSpec(memory_space=pltpu.SMEM)
    shape = jax.ShapeDtypeStruct
    dma = pltpu.SemaphoreType.DMA
    return pl.pallas_call(
        front_kernel,
        out_shape=(
            shape((18, across, width), bf16),
            shape((18, across, width), bf16),
            shape((9, 2, across, width), bf16),
            shape((tokens, width), bf16),
            shape((tokens, 3 * width), bf16),
            shape((tokens, width), bf16),
            shape((2, tokens // 2, LANES), f32),
            shape((2, tokens // 2, tokens // 2), f32),
            shape((8, width), f32),
        ),
        in_specs=[any_space] * 2 + [smem] * 2 + [vmem] * 2 + [any_space] * 5,
        out_specs=[any_space] * 8 + [vmem],
        scratch_shapes=[
            pltpu.VMEM((18, across, width), bf16),
            pltpu.VMEM((2, *classes.shape), bf16),
            pltpu.VMEM(wmod.shape, bf16),
            pltpu.VMEM(wqkv.shape, bf16),
            pltpu.VMEM(wo.shape, bf16),
            pltpu.VMEM((3, 18, across, width), f32),
            pltpu.VMEM((8, 2, across, width), bf16),
            pltpu.VMEM((16, across, width), bf16),
            pltpu.VMEM((2, tokens, tokens), bf16),
            pltpu.VMEM((2, tokens // 2, tokens // 2), f32),
            pltpu.VMEM((tokens, width), bf16),
            pltpu.VMEM((tokens, 3 * width), bf16),
            pltpu.VMEM((tokens, width), bf16),
            pltpu.VMEM((2, tokens // 2, LANES), f32),
            pltpu.VMEM((16, across, width), bf16),
            dma((5,)), dma((3,)), dma((3,)), dma((3,)), dma((3,)), dma((2,)), dma((2,)),
            dma((2,)), dma((6,)),
        ],
        compiler_params=pltpu.CompilerParams(
            collective_id=1, has_side_effects=True, vmem_limit_bytes=60 << 20
        ),
        name="front",
    )(inputs, cotangent, names, moments, segments, kern, classes, times, wmod, wqkv, wo)


def gelu_parts(x):
    size = jnp.abs(x)
    t = 1.0 / (1.0 + (0.3275911 * 0.7071067811865476) * size)
    bell = jnp.exp(-0.5 * x * x)
    series = t * (
        0.254829592
        + t * (-0.284496736 + t * (1.421413741 + t * (-1.453152027 + t * 1.061405429)))
    )
    tail = 0.5 * series * bell
    mass = jnp.where(x >= 0, 1.0 - tail, tail)
    return x * mass, mass + x * bell * 0.3989422804014327


def tile_of(step, tiles):
    return jnp.where(lax.rem(step, 2) == 0, step // 2, tiles - 1 - step // 2)


def feed_kernel(
    x_in, ret_in, cot_in, mod, up, kern, down,
    o_up, o_down, o_up_half, o_down_half, o_up_last, o_down_last, o_kern, o_res, o_mid, o_rg, o_small,
    feed_in, feed_t, btg, out_acc, back_acc, hid, hs, gs, act, slope, hg,
    wu, wd, ru, rd, yu, xu, zu, fin, xd, yd, zd, fin_d,
    u1_send, u1_recv, u2_send, u2_recv, u3_send, u3_recv, d1_send, d1_recv, d2_send, d2_recv,
    u4_send, u4_recv, d3_send, d3_recv, d4_send, d4_recv, u_out, d_out, l_out,
):
    j = pl.program_id(0)
    tiles = pl.num_programs(0)
    b = lax.axis_index("batch")
    g = lax.axis_index("group")
    c, p = lax.rem(g, 2), g // 2
    nz = wu.shape[3]
    yb, zb = lax.rem(b, 2), b // 2
    core, side, beside = (b, g + 1 - 2 * c), (b, g + 2 - 4 * p), (b + 1 - 2 * yb, g)
    others = [lax.rem(zb + d, nz) for d in range(nz)]
    far = [(2 * z + yb, g) for z in others]
    parts = wd.shape[3]

    def up_1(t):
        return remote(wu.at[t, 1 - c], ru.at[t], u1_send.at[t], u1_recv.at[t], core)

    def down_1(t):
        return remote(wd.at[t, 1 - c], rd.at[t], d1_send.at[t], d1_recv.at[t], core)

    def up_2(t):
        return remote(wu.at[t, c, :, :, 1 - yb], yu.at[t], u2_send.at[t], u2_recv.at[t], beside)

    def down_2(t):
        return remote(wd.at[t, c, 1 - p], xd.at[t], d2_send.at[t], d2_recv.at[t], side)

    def up_3(t):
        return remote(wu.at[t, c, 1 - p, :, yb], xu.at[t], u3_send.at[t], u3_recv.at[t], side)

    def up_4(t, d):
        return remote(
            wu.at[t, c, p, others[d], yb], zu.at[t, d - 1], u4_send.at[t, d - 1],
            u4_recv.at[t, d - 1], far[d],
        )

    def up_store(t):
        spot = pl.ds(pl.multiple_of(tile_of(t, tiles) * LANES, LANES), LANES)
        return pltpu.make_async_copy(fin.at[t], o_up.at[:, spot], u_out.at[t])

    per = fin_d.shape[0]

    def owner_of(t, k):
        place = parts * tile_of(t, tiles) + k
        return place // per, lax.rem(place, per)

    def down_3(t, k):
        return remote(
            wd.at[t, c, p, k], yd.at[t, k], d3_send.at[t, k], d3_recv.at[t, k], beside
        )

    def down_4(t, k):
        owner, spot = owner_of(t, k)
        slot = lax.rem(zb - owner // 2 + nz, nz) - 1
        return remote(
            wd.at[t, c, p, k], zd.at[spot, slot], d4_send.at[t, k], d4_recv.at[spot, slot],
            (2 * (owner // 2) + yb, g),
        )

    def each_part(t, away, here):
        def step(k, carry):
            owner, spot = owner_of(t, k)
            mine = lax.rem(owner, 2) == yb

            @pl.when(jnp.logical_not(mine))
            def _():
                away(k)

            @pl.when(mine)
            def _():
                here(k, owner, spot)

            return carry

        lax.fori_loop(0, parts, step, 0)

    def nothing(*_):
        pass

    def down_store(spot):
        return pltpu.make_async_copy(fin_d.at[spot], o_down.at[spot], d_out.at[spot])

    def add_core(t):
        down_1(t).wait_recv()
        up_1(t).wait_recv()

        def step(i, carry):
            x, z, y = i // (2 * nz), lax.rem(i // 2, nz), lax.rem(i, 2)
            wu[t, c, x, z, y] = wu[t, c, x, z, y] + ru[t, x, z, y]
            return carry

        grouped(4 * nz, step, 0)

        def step_down(i, carry):
            x, k = i // parts, lax.rem(i, parts)
            wd[t, c, x, k] = wd[t, c, x, k] + rd[t, x, k]
            return carry

        grouped(2 * parts, step_down, 0)

    def add_beside(t):
        up_2(t).wait_recv()

        def step(i, carry):
            x, z = i // nz, lax.rem(i, nz)
            wu[t, c, x, z, yb] = wu[t, c, x, z, yb] + yu[t, x, z]
            return carry

        grouped(2 * nz, step, 0)

    def add_side(t):
        up_3(t).wait_recv()

        def step(z, carry):
            wu[t, c, p, z, yb] = wu[t, c, p, z, yb] + xu[t, z]
            return carry

        grouped(nz, step, 0)
        for d in range(1, nz):
            up_4(t, d).start()

    def add_far(t):
        total = wu[t, c, p, zb, yb].astype(f32)
        for d in range(1, nz):
            up_4(t, d).wait_recv()
            total = total + zu[t, d - 1].astype(f32)
        fin[t] = total.astype(bf16)
        up_store(t).start()

    def add_side_down(t):
        down_2(t).wait_recv()

        def step(k, carry):
            wd[t, c, p, k] = wd[t, c, p, k] + xd[t, k]
            return carry

        grouped(parts, step, 0)

    def send_beside_down(t):
        each_part(t, lambda k: down_3(t, k).start(), nothing)

    def add_beside_down(t):
        def here(k, owner, spot):
            down_3(t, k).wait_recv()
            wd[t, c, p, k] = wd[t, c, p, k] + yd[t, k]

            @pl.when(owner // 2 != zb)
            def _():
                down_4(t, k).start()

        each_part(t, nothing, here)

    def add_far_down(t):
        def here(k, owner, spot):
            @pl.when(owner // 2 == zb)
            def _():
                total = wd[t, c, p, k].astype(f32)
                for d in range(1, nz):
                    place = zd.at[spot, d - 1]
                    pltpu.make_async_copy(place, place, d4_recv.at[spot, d - 1]).wait()
                    total = total + zd[spot, d - 1].astype(f32)
                fin_d[spot] = total.astype(bf16)
                down_store(spot).start()

        each_part(t, nothing, here)

    def settle_down(t):
        def here(k, owner, spot):
            @pl.when(owner // 2 != zb)
            def _():
                down_4(t, k).wait_send()

            @pl.when(owner // 2 == zb)
            def _():
                down_store(spot).wait()

        each_part(t, lambda k: down_3(t, k).wait_send(), here)

    across = 32
    width = feed_in.shape[1]
    tile = up.shape[1]
    frame_rows = feed_in.shape[0] // across
    own = pl.ds(pl.multiple_of(2 * c * across, 64), 16 * across)

    def middle_of(row):
        place = pl.ds(pl.multiple_of(row * across, across), across)
        returned = ret_in[place, :].astype(f32)
        return x_in[place, :].astype(f32) + mod[2:3, :] * returned, returned

    @pl.when(j == 0)
    def _():
        meet([core, side, beside, *far[1:]])

        def prepare(row, carry):
            place = pl.ds(pl.multiple_of(row * across, across), across)
            normal, _ = normalize(middle_of(row)[0])
            feed_in[place, :] = (normal * (1.0 + mod[4:5, :]) + mod[3:4, :]).astype(bf16)
            btg[place, :] = (mod[5:6, :] * cot_in[place, :].astype(f32)).astype(bf16)
            return carry

        grouped(frame_rows, prepare, 0)
        feed_t[...] = feed_in[own, :].T
        out_acc[...] = jnp.zeros(out_acc.shape, f32)
        back_acc[...] = jnp.zeros(back_acc.shape, f32)
        for s in range(3):
            hs[s, 18 * c] = jnp.zeros((across, tile), f32)
            gs[s, 17 * c] = jnp.zeros((across, tile), f32)

    hid[...] = dot_nn(feed_in[...], up[...]).astype(bf16)

    def lay_hidden(row, carry):
        value = hid[pl.ds(pl.multiple_of(row * across, across), across), :].astype(f32)
        before, after = column_shifts(value)
        hs[0, 1 - c + row] = before
        hs[1, 1 - c + row] = value
        hs[2, 1 - c + row] = after
        return carry

    grouped(frame_rows, lay_hidden, 0)

    for lane in range(0, tile, LANES):
        cut = slice(lane, lane + LANES)
        taps = [kern[n : n + 1, cut].astype(f32) for n in range(9)]

        def forward(row, carry):
            total = jnp.zeros((across, LANES), f32)
            for r in range(3):
                for s in range(3):
                    total = total + taps[3 * r + s] * hs[s, row + r, :, cut]
            place = pl.ds(pl.multiple_of(row * across, across), across)
            value, steep = gelu_parts(total)
            act[place, cut] = value.astype(bf16)
            slope[place, cut] = steep
            return carry

        grouped(17, forward, 0)

    @pl.when(j >= 2)
    def _():
        add_side(j - 2)
        add_beside_down(j - 2)

    @pl.when(j >= 1)
    def _():
        add_core(j - 1)
        up_2(j - 1).start()
        down_2(j - 1).start()

    @pl.when(j >= 3)
    def _():
        add_far(j - 3)
        add_far_down(j - 3)

    inside = pl.ds(pl.multiple_of(c * across, across), 16 * across)
    around = pl.ds(pl.multiple_of(c * across, across), 17 * across)
    own_act = act[inside, :]
    out_acc[...] += dot_nn(own_act, down[...])
    grad_down = dot_tn(own_act, btg[own, :]).reshape(parts, 4, wd.shape[4], width)
    for q in range(4):
        wd[j, q % 2, q // 2] = grad_down[:, q].astype(bf16)
    down_1(j).start()
    slope[...] = slope[...] * dot_nt(btg[around, :], down[...])

    def lay_grad(row, carry):
        value = slope[pl.ds(pl.multiple_of(row * across, across), across), :]
        value = value.astype(bf16).astype(f32)
        before, after = column_shifts(value)
        gs[0, 1 - c + row] = after
        gs[1, 1 - c + row] = value
        gs[2, 1 - c + row] = before
        return carry

    grouped(17, lay_grad, 0)

    for lane in range(0, tile, LANES):
        cut = slice(lane, lane + LANES)
        taps = [kern[n : n + 1, cut].astype(f32) for n in range(9)]

        def backward(row, sums):
            total = jnp.zeros((across, LANES), f32)
            value = hs[1, row + c + 1, :, cut]
            later = []
            for r in range(3):
                for s in range(3):
                    grad = gs[s, row + 2 - r, :, cut]
                    total = total + taps[3 * r + s] * grad
                    later.append(sums[3 * r + s] + fold(value * grad))
            hg[pl.ds(pl.multiple_of(row * across, across), across), cut] = total.astype(bf16)
            return tuple(later)

        sums = grouped(16, backward, tuple(jnp.zeros((8, LANES), f32) for _ in range(9)))
        for n in range(9):
            o_kern[n : n + 1, cut] = jnp.sum(sums[n], axis=0, keepdims=True)

    o_kern[9:16, :] = jnp.zeros((7, tile), f32)
    grad_up = dot_nn(feed_t[...], hg[...])
    for q in range(4):
        part = grad_up[:, q * LANES : (q + 1) * LANES]
        wu[j, q % 2, q // 2] = part.reshape(nz, 2, wu.shape[5], LANES).astype(bf16)
    up_1(j).start()
    back_acc[...] += dot_nt(hg[...], up[...])

    @pl.when(jnp.logical_and(j >= 1, j < tiles - 1))
    def _():
        add_beside(j - 1)
        up_3(j - 1).start()
        add_side_down(j - 1)
        send_beside_down(j - 1)

    @pl.when(j == tiles - 1)
    def _():
        def finish(row, sums):
            frame = row + 2 * c
            place = pl.ds(pl.multiple_of(row * across, across), across)
            at = pl.ds(pl.multiple_of(frame * across, across), across)
            middle, returned = middle_of(frame)
            cot = cot_in[at, :].astype(f32)
            branch = out_acc[place, :]
            o_res[place, :] = (middle + mod[5:6, :] * branch).astype(bf16)
            normal, scale = normalize(middle)
            grad = back_acc[place, :]
            mid = cot + normalize_back(grad * (1.0 + mod[4:5, :]), normal, scale)
            o_mid[place, :] = mid
            o_rg[place, :] = (mod[2:3, :] * mid).astype(bf16)
            terms = (mid * returned, grad, grad * normal, cot * branch)
            return tuple(total + fold(term) for total, term in zip(sums, terms))

        sums = grouped(16, finish, tuple(jnp.zeros((8, width), f32) for _ in range(4)))
        o_small[...] = jnp.zeros((8, width), f32)
        for n in range(4):
            o_small[n + 2 : n + 3, :] = jnp.sum(sums[n], axis=0, keepdims=True)
        add_beside(j - 1)
        half = pltpu.make_async_copy(wu.at[j - 1, c, :, :, yb], o_up_half, l_out.at[2])
        half.start()
        add_side_down(j - 1)
        half_down = pltpu.make_async_copy(wd.at[j - 1, c, p], o_down_half, l_out.at[3])
        half_down.start()
        add_core(j)
        last = (
            half,
            half_down,
            pltpu.make_async_copy(wu.at[j, c], o_up_last, l_out.at[0]),
            pltpu.make_async_copy(wd.at[j, c], o_down_last, l_out.at[1]),
        )
        for move in last[2:]:
            move.start()
        add_far(j - 2)
        add_far_down(j - 2)

        def settle(t, carry):
            up_3(t).wait_send()
            for d in range(1, nz):
                up_4(t, d).wait_send()
            up_store(t).wait()
            settle_down(t)
            return carry

        def settle_more(t, carry):
            up_2(t).wait_send()
            down_2(t).wait_send()
            up_1(t).wait_send()
            down_1(t).wait_send()
            return carry

        lax.fori_loop(0, tiles - 2, settle, 0)
        lax.fori_loop(0, tiles - 1, settle_more, 0)
        up_1(j).wait_send()
        down_1(j).wait_send()
        for move in last:
            move.wait()


def feed(x_frame, returned, cot_frame, mod, up, kern, down, grain):
    width, units = up.shape
    frame = x_frame.shape[0]
    across = frame // 18
    tokens = 16 * across
    shape = jax.ShapeDtypeStruct
    dma = pltpu.SemaphoreType.DMA
    any_space = pl.BlockSpec(memory_space=pl.ANY)
    tile = 4 * LANES
    tiles = units // tile
    parts = tile // (4 * grain)
    nb = lax.axis_size("batch")
    nz = nb // 2
    own = width // nb
    many = max(nz - 1, 1)

    def still(*size):
        return pl.BlockSpec(size, lambda j: (0, 0), pipeline_mode=pl.Buffered(1))

    columns = pl.BlockSpec((width, tile), lambda j: (0, tile_of(j, tiles)))
    rows = pl.BlockSpec((tile, width), lambda j: (tile_of(j, tiles), 0))
    per = tiles * parts // nb
    work = 6 * 2 * tokens * width * units
    return pl.pallas_call(
        feed_kernel,
        grid=(units // tile,),
        out_shape=(
            shape((own, tiles * LANES), bf16),
            shape((per, grain, width), bf16),
            shape((2, nz, own, LANES), bf16),
            shape((parts, grain, width), bf16),
            shape((2, nz, 2, own, LANES), bf16),
            shape((2, parts, grain, width), bf16),
            shape((16, units), f32),
            shape((tokens, width), bf16),
            shape((tokens, width), f32),
            shape((tokens, width), bf16),
            shape((8, width), f32),
        ),
        in_specs=[
            still(frame, width), still(frame, width), still(frame, width), still(8, width),
            columns, pl.BlockSpec((9, tile), lambda j: (0, tile_of(j, tiles))), rows,
        ],
        out_specs=[
            *[any_space] * 6, pl.BlockSpec((16, tile), lambda j: (0, tile_of(j, tiles))),
            still(tokens, width), still(tokens, width), still(tokens, width), still(8, width),
        ],
        scratch_shapes=[
            pltpu.VMEM((frame, width), bf16),
            pltpu.VMEM((width, tokens), bf16),
            pltpu.VMEM((frame, width), bf16),
            pltpu.VMEM((tokens, width), f32),
            pltpu.VMEM((tokens, width), f32),
            pltpu.VMEM((frame, tile), bf16),
            pltpu.VMEM((3, 19, across, tile), f32),
            pltpu.VMEM((3, 18, across, tile), f32),
            pltpu.VMEM((17 * across, tile), bf16),
            pltpu.VMEM((17 * across, tile), f32),
            pltpu.VMEM((tokens, tile), bf16),
            pltpu.VMEM((tiles, 2, 2, nz, 2, own, LANES), bf16),
            pltpu.VMEM((tiles, 2, 2, parts, grain, width), bf16),
            pltpu.VMEM((tiles, 2, nz, 2, own, LANES), bf16),
            pltpu.VMEM((tiles, 2, parts, grain, width), bf16),
            pltpu.VMEM((tiles, 2, nz, own, LANES), bf16),
            pltpu.VMEM((tiles, nz, own, LANES), bf16),
            pltpu.VMEM((tiles, many, own, LANES), bf16),
            pltpu.VMEM((tiles, own, LANES), bf16),
            pltpu.VMEM((tiles, parts, grain, width), bf16),
            pltpu.VMEM((tiles, parts, grain, width), bf16),
            pltpu.VMEM((per, many, grain, width), bf16),
            pltpu.VMEM((per, grain, width), bf16),
            *[dma((tiles,)) for _ in range(10)],
            dma((tiles, many)), dma((tiles, many)), dma((tiles, parts)), dma((tiles, parts)),
            dma((tiles, parts)), dma((per, many)), dma((tiles,)), dma((per,)), dma((4,)),
        ],
        compiler_params=pltpu.CompilerParams(
            dimension_semantics=("arbitrary",), collective_id=3, has_side_effects=True,
            vmem_limit_bytes=62 << 20,
        ),
        cost_estimate=pl.CostEstimate(
            flops=work, bytes_accessed=8 * width * units, transcendentals=tokens * units
        ),
        name="feed",
    )(x_frame, returned, cot_frame, mod, up, kern, down)


def back_kernel(
    mid_in, rg_in, tok_in, proj_in, att_in, lse, bias, x_in, mod, small, kern, wqkv_in, wo_in,
    res_in, ud_in, dd_in, uh_in, dh_in, ul_in, dl_in, kern_two,
    o_fu, o_fd, o_fp, o_res, o_ig, o_one, o_two, o_mg, o_ml,
    mid, tok, tok_t, proj, att, xf, wqkv, wo, rows_m, perm, grad, datt, dproj,
    brm, frame, gs, value, agrad, ig,
    wp, p_r1, p_r2x, p_r2y, p_r3, p_r4, fin_p,
    fu, fd, fz_u, fy_d, fz_d, fin_u, fin_d, lx_d, hx, ly, ly_r, lx,
    mg_own, mg_r1, mg_all, ml_own, ml_r1, ml_all, taps_sum, kk_1, kr_1, kz_1,
    kt, kt_core, kt_side, kt_y, kt_sum, kt_z, fin_k,
    dy_send, dy_recv, dz_send, dz_recv, load_sem, r_send, r_recv, i_send, i_recv, ex_send, ex_recv, own_sem, send_sem, recv_sem, out_sem,
):
    b = lax.axis_index("batch")
    g = lax.axis_index("group")
    nz = fu.shape[0]
    c, p = lax.rem(g, 2), g // 2
    yb, zb = lax.rem(b, 2), b // 2
    core, side, corner = (b, g + 1 - 2 * c), (b, g + 2 - 4 * p), (b, 3 - g)
    beside = (b + 1 - 2 * yb, g)
    others = [lax.rem(zb + d, nz) for d in range(nz)]
    far = [(2 * z + yb, g) for z in others]
    inner = jnp.logical_or(g == 1, g == 2)
    across, width = xf.shape[1], xf.shape[2]
    rows_own = fu.shape[1]
    pairs = width // LANES
    tokens = tok.shape[0]
    size = tokens // 2
    chunks = wp.shape[0]
    chunk = wp.shape[-1]
    tiles = width // LANES
    lead = (tiles // 2 - 1) * LANES
    per, parts = fin_d.shape[2], lx_d.shape[0]
    places = {}

    def link(name, src, dst, target):
        n = places.setdefault(name, len(places))
        return remote(src, dst, send_sem.at[n], recv_sem.at[n], target)

    def send_home(n, src, dst, send, recv, waiting, first=0, count=8):
        from_rows = src.at[pl.ds(8 * n + first, count)]
        to_rows = dst.at[p, pl.ds(first, count)]
        move = remote(from_rows, to_rows, send.at[n], recv.at[p], (b, 2 * c + n))
        away = remote(from_rows, to_rows, send.at[n], recv.at[p], core)
        stay = pltpu.make_async_copy(from_rows, to_rows, recv.at[p])

        @pl.when(inner)
        def _():
            if waiting:
                move.wait_send()
            else:
                move.start()

        @pl.when(jnp.logical_and(jnp.logical_not(inner), c != n))
        def _():
            if waiting:
                away.wait_send()
            else:
                away.start()

        if not waiting:

            @pl.when(jnp.logical_and(jnp.logical_not(inner), c == n))
            def _():
                stay.start()

    def home(dst, recv):
        for n in range(2):
            pltpu.make_async_copy(dst.at[n], dst.at[n], recv.at[n]).wait()

    def gone(moves):
        for move in moves:
            move.wait_send()

    def half_x():
        return link("hx", uh_in.at[1 - p], hx, side)

    def last_y():
        return link("ly", ul_in.at[:, :, 1 - yb], ly_r, beside)

    def last_x():
        return link("lx", ly.at[1 - p], lx, side)

    def last_d():
        return link("ld", dl_in.at[1 - p], lx_d, side)

    def owner_of(k):
        place = parts * (tiles // 2 - 1) + k
        return place // per, lax.rem(place, per)

    def down_y(k):
        return remote(fd.at[k], fy_d.at[k], dy_send.at[k], dy_recv.at[k], beside)

    def down_z(k):
        owner, spot = owner_of(k)
        slot = lax.rem(zb - owner // 2 + nz, nz) - 1
        return remote(
            fd.at[k], fz_d.at[spot, slot], dz_send.at[k], dz_recv.at[spot, slot],
            (2 * (owner // 2) + yb, g),
        )

    def each_part(begin, away, here):
        def step(k, carry):
            owner, spot = owner_of(k)
            mine = lax.rem(owner, 2) == yb

            @pl.when(jnp.logical_not(mine))
            def _():
                away(k)

            @pl.when(mine)
            def _():
                here(k, owner, spot)

            return carry

        lax.fori_loop(begin, begin + parts, step, 0)

    def nothing(*_):
        pass

    def up_z(d):
        return link(f"fuz{d}", fu.at[others[d]], fz_u.at[d - 1], far[d])

    def to_side(name, fin, mine):
        x = p if mine else 1 - p
        return link(f"{name}x", fin.at[c, x], fin.at[c, x], side)

    def to_core(name, fin, mine):
        x = c if mine else 1 - c
        return link(f"{name}c", fin.at[x], fin.at[x], core)

    def half_add():
        early[0].wait()
        half_x().wait_recv()

        def step(z, carry):
            fu[z, :, :LANES] = fu[z, :, :LANES] + hx[z]
            return carry

        grouped(nz, step, 0)

    def last_y_add():
        early[1].wait()
        last_y().wait_recv()

        def step(i, carry):
            x, z = i // nz, lax.rem(i, nz)
            ly[x, z] = ly[x, z] + ly_r[x, z]
            return carry

        grouped(2 * nz, step, 0)
        last_x().start()

    def last_x_add():
        last_x().wait_recv()

        def step(z, carry):
            fu[z, :, LANES:] = ly[p, z] + lx[z]
            return carry

        grouped(nz, step, 0)
        for d in range(1, nz):
            up_z(d).start()

    def up_sum():
        early[2].wait()
        early[3].wait()
        total = fu[zb].astype(f32)
        for d in range(1, nz):
            up_z(d).wait_recv()
            total = total + fz_u[d - 1].astype(f32)
        fin_u[c, p, :, lead : lead + 2 * LANES] = total.astype(bf16)
        to_side("gu", fin_u, True).start()

    def place_half():
        late[0].wait()
        each_part(0, lambda k: down_y(k).start(), nothing)

    def place_last():
        late[1].wait()
        last_d().wait_recv()

        def step(k, carry):
            fd[parts + k] = fd[parts + k] + lx_d[k]
            return carry

        grouped(parts, step, 0)
        each_part(parts, lambda k: down_y(k).start(), nothing)

    def down_y_add(begin):
        def here(k, owner, spot):
            down_y(k).wait_recv()
            fd[k] = fd[k] + fy_d[k]

            @pl.when(owner // 2 != zb)
            def _():
                down_z(k).start()

        each_part(begin, nothing, here)

    def down_sum():
        early[4].wait()

        def here(k, owner, spot):
            @pl.when(owner // 2 == zb)
            def _():
                total = fd[k].astype(f32)
                for d in range(1, nz):
                    place = fz_d.at[spot, d - 1]
                    pltpu.make_async_copy(place, place, dz_recv.at[spot, d - 1]).wait()
                    total = total + fz_d[spot, d - 1].astype(f32)
                fin_d[c, p, spot] = total.astype(bf16)

        for begin in (0, parts):
            each_part(begin, nothing, here)
        to_side("gd", fin_d, True).start()

    def down_gone():
        def here(k, owner, spot):
            @pl.when(owner // 2 != zb)
            def _():
                down_z(k).wait_send()

        for begin in (0, parts):
            each_part(begin, lambda k: down_y(k).wait_send(), here)

    def pass_on(name, fin):
        to_side(name, fin, False).wait_recv()
        to_core(name, fin, True).start()

    u_out = pltpu.make_async_copy(fin_u, o_fu, out_sem.at[0])
    d_out = pltpu.make_async_copy(fin_d, o_fd, out_sem.at[1])
    p_out = pltpu.make_async_copy(fin_p, o_fp, out_sem.at[2])
    mg_out = pltpu.make_async_copy(mg_all, o_mg, out_sem.at[3])
    ml_out = pltpu.make_async_copy(ml_all, o_ml, out_sem.at[4])

    def side_first(k):
        return k % 2 == 0

    def p1(k):
        return link(f"p1{k}", wp.at[k, 1 - c], p_r1.at[k], core)

    def p2(k):
        if side_first(k):
            return link(f"p2{k}", wp.at[k, c, 1 - p], p_r2x.at[k], side)
        return link(f"p2{k}", wp.at[k, c, :, :, 1 - yb], p_r2y.at[k], beside)

    def p3(k):
        if side_first(k):
            return link(f"p3{k}", wp.at[k, c, p, :, 1 - yb], p_r3.at[k], beside)
        return link(f"p3{k}", wp.at[k, c, 1 - p, :, yb], p_r3.at[k], side)

    def p4(k, d):
        return link(
            f"p4{k}{d}", wp.at[k, c, p, others[d], yb], p_r4.at[k, d - 1], far[d]
        )

    def p_side(k, mine):
        x = p if mine else 1 - p
        return link(f"p5{k}", fin_p.at[k, c, x], fin_p.at[k, c, x], side)

    def p_core(k, mine):
        x = c if mine else 1 - c
        return link(f"p6{k}", fin_p.at[k, x], fin_p.at[k, x], core)

    def p_add_1(k):
        p1(k).wait_recv()

        def step(i, carry):
            x, z, y = i // (2 * nz), lax.rem(i // 2, nz), lax.rem(i, 2)
            wp[k, c, x, z, y] = wp[k, c, x, z, y] + p_r1[k, x, z, y]
            return carry

        grouped(4 * nz, step, 0)
        p2(k).start()

    def p_add_2(k):
        p2(k).wait_recv()

        def step(i, carry):
            if side_first(k):
                z, y = i // 2, lax.rem(i, 2)
                wp[k, c, p, z, y] = wp[k, c, p, z, y] + p_r2x[k, z, y]
            else:
                x, z = i // nz, lax.rem(i, nz)
                wp[k, c, x, z, yb] = wp[k, c, x, z, yb] + p_r2y[k, x, z]
            return carry

        grouped(2 * nz, step, 0)
        p3(k).start()

    def p_add_3(k):
        p3(k).wait_recv()

        def step(z, carry):
            wp[k, c, p, z, yb] = wp[k, c, p, z, yb] + p_r3[k, z]
            return carry

        grouped(nz, step, 0)
        for d in range(1, nz):
            p4(k, d).start()

    def p_add_4(k):
        total = wp[k, c, p, zb, yb].astype(f32)
        for d in range(1, nz):
            p4(k, d).wait_recv()
            total = total + p_r4[k, d - 1].astype(f32)
        fin_p[k, c, p] = total.astype(bf16)
        p_side(k, True).start()

    def p_pass(k):
        p_side(k, False).wait_recv()
        p_core(k, True).start()

    peers = [core, side, beside]
    order = [core, beside, side]

    def kern_copy(name, kk, kr, stage):
        return link(f"{name}{stage}", kk.at[stage], kr.at[stage], order[stage])

    def kern_far(name, kk, kz, d):
        return link(f"{name}z{d}", kk.at[3], kz.at[d - 1], far[d])

    def kern_step(name, kk, kr, kz, stage):
        kern_copy(name, kk, kr, stage).wait_recv()
        kk[stage + 1] = (kk[stage].astype(f32) + kr[stage].astype(f32)).astype(bf16)
        if stage < 2:
            kern_copy(name, kk, kr, stage + 1).start()
        else:
            for d in range(1, nz):
                kern_far(name, kk, kz, d).start()

    def kern_sum(name, kk, kz, out):
        total = kk[3].astype(f32)
        for d in range(1, nz):
            kern_far(name, kk, kz, d).wait_recv()
            total = total + kz[d - 1].astype(f32)
        out[...] = total

    one = ("one", kk_1, kr_1, kz_1)

    def taps_core():
        return link("kt0", kt.at[1 - c], kt_core, core)

    def taps_side():
        return link("kt1", kt.at[c, 1 - p], kt_side, side)

    def taps_y():
        return link("kt2", kt.at[c, p], kt_y, beside)

    def taps_z(d):
        return link(f"kt3{d}", kt_sum, kt_z.at[d - 1], far[d])

    def taps_core_add():
        taps_core().wait_recv()
        for x in range(2):
            kt[c, x] = kt[c, x] + kt_core[x]
        taps_side().start()

    def taps_side_add():
        taps_side().wait_recv()
        kt[c, p] = kt[c, p] + kt_side[...]
        taps_y().start()

    def taps_y_add():
        taps_y().wait_recv()
        kt_sum[...] = kt[c, p] + kt_y[...]
        for d in range(1, nz):
            taps_z(d).start()

    def taps_total():
        total = kt_sum[...].astype(f32)
        for d in range(1, nz):
            taps_z(d).wait_recv()
            total = total + kt_z[d - 1].astype(f32)
        fin_k[c, p] = total.astype(bf16)
        to_side("gk", fin_k, True).start()

    def mg_swap(mine=True):
        x = c if mine else 1 - c
        return link("mgc", mg_all.at[x], mg_all.at[x], core)

    def mg_copy(part, stage, mine=True):
        name, own, first, every = part
        if stage == 0:
            return link(f"{name}0", own.at[1 - c] if name == "mg" else own, first, core)
        every = every.at[c] if name == "mg" else every
        x = p if mine else 1 - p
        y = yb if mine else 1 - yb
        place = every.at[zb, yb, x] if stage == 1 else every.at[zb, y]
        return link(f"{name}{stage}", place, place, peers[stage])

    def mg_far(part, d, z):
        place = part[3].at[c, z] if part[0] == "mg" else part[3].at[z]
        return link(f"{part[0]}z{d}", place, place, far[d])

    def mg_step(part, stage):
        name, own, first, every = part
        mg_copy(part, stage, False).wait_recv()
        if stage == 0 and name == "mg":
            every[c, zb, yb, p] = own[c] + first[...]
        elif stage == 0:
            every[zb, yb, p] = own[...] + first[...]
        if stage < 2:
            mg_copy(part, stage + 1).start()
        else:
            for d in range(1, nz):
                mg_far(part, d, zb).start()

    def mg_end(part):
        for d in range(1, nz):
            mg_far(part, d, lax.rem(zb + nz - d, nz)).wait_recv()

    soon = ("mg", mg_own, mg_r1, mg_all)

    def ml_copy(stage, mine=True):
        if stage == 0:
            return link("ml0", ml_own, ml_r1, core)
        if stage == 1:
            place = ml_all.at[zb, yb if mine else 1 - yb, p]
            return link("ml1", place, place, beside)
        place = ml_all.at[:, :, p if mine else 1 - p]
        return link("ml2", place, place, side)

    def ml_far(d, z):
        return link(f"mlz{d}", ml_all.at[z, :, p], ml_all.at[z, :, p], far[d])

    def ml_step(stage):
        if stage == 0:
            ml_copy(0).wait_recv()
            ml_all[zb, yb, p] = ml_own[...] + ml_r1[...]
            ml_copy(1).start()
        elif stage == 1:
            ml_copy(1, False).wait_recv()
            for d in range(1, nz):
                ml_far(d, zb).start()
        elif stage == 2:
            for d in range(1, nz):
                ml_far(d, lax.rem(zb + nz - d, nz)).wait_recv()
            ml_copy(2).start()
        else:
            ml_copy(2, False).wait_recv()

    pieces = [
        (wo_in, wo), (att_in, att), (tok_in, tok), (proj_in, proj), (wqkv_in, wqkv), (x_in, xf),
        (mid_in, mid),
    ]
    loads = [
        pltpu.make_async_copy(src, dst, load_sem.at[n]) for n, (src, dst) in enumerate(pieces)
    ]
    early = [
        pltpu.make_async_copy(uh_in.at[p], fu.at[:, :, pl.ds(0, LANES)], load_sem.at[7]),
        pltpu.make_async_copy(ul_in.at[:, :, yb], ly, load_sem.at[8]),
        *[
            pltpu.make_async_copy(
                ud_in.at[:, pl.ds(at, lead)], fin_u.at[c, p, :, pl.ds(at, lead)], load_sem.at[n]
            )
            for n, at in ((9, 0), (10, lead + 2 * LANES))
        ],
        pltpu.make_async_copy(dd_in, fin_d.at[c, p], load_sem.at[11]),
    ]
    late = [
        pltpu.make_async_copy(dh_in, fd.at[pl.ds(0, parts)], load_sem.at[12]),
        pltpu.make_async_copy(dl_in.at[p], fd.at[pl.ds(parts, parts)], load_sem.at[13]),
    ]
    for load in (*loads[:4], *late, *early, *loads[4:]):
        load.start()
    half_width, quarter = width // 2, kt.shape[3]
    for x in range(2):
        span = slice(x * half_width, (x + 1) * half_width)
        mg_own[x] = small[:, span]
        mg_own[x, 6:8, :] = mod[6:8, span]
        for q in range(2):
            at = (2 * x + q) * quarter
            kt[x, q] = kern_two[:, at : at + quarter].astype(bf16)
    meet([core, side, corner, beside, *far[1:]])
    grad_away = remote(
        rg_in.at[:, 1 - c], rows_m.at[pl.ds(8 * c, 8)], ex_send.at[0], ex_recv.at[0], core
    )
    grad_away.start()
    grad_own = pltpu.make_async_copy(rg_in.at[:, c], rows_m.at[pl.ds(8 * c, 8)], own_sem.at[0])
    grad_own.start()
    last_d().start()
    last_y().start()
    half_x().start()
    mg_copy(soon, 0).start()
    taps_core().start()
    perm[0] = permutation(False)
    perm[1] = permutation(True)
    grad_own.wait()
    grad_away.wait()
    grad[...] = dot_nn(perm[0], rows_m[...].reshape(tokens, width)).astype(bf16)
    loads[0].wait()
    loads[1].wait()
    datt[...] = dot_nt(grad[...], wo[...]).astype(bf16)
    out_grad = dot_tn(att[...], grad[...])
    for k in range(chunks):
        cut = slice(k * chunk, (k + 1) * chunk)
        wp[k, 1, 1] = out_grad[:, cut].reshape(nz, 2, rows_own, chunk).astype(bf16)
    loads[2].wait()
    tok_t[...] = tok[...].T
    loads[3].wait()
    low_lane = lax.broadcasted_iota(jnp.int32, (size, LANES), 1) < LANES // 2
    lane_id = lax.broadcasted_iota(jnp.int32, (size, LANES), 1)
    zero = jnp.zeros((), bf16)

    def attend(index, carry):
        pair, half = index // 2, lax.rem(index, 2)
        rows = pl.ds(pl.multiple_of(half * size, size), size)

        def cut(n):
            return pl.ds(pl.multiple_of(n * width + pair * LANES, LANES), LANES)

        q = proj[rows, cut(0)] * jnp.asarray(0.125, bf16)
        k, v, up = proj[rows, cut(1)], proj[rows, cut(2)], datt[rows, cut(0)]
        sums = lse[half]
        dq = jnp.zeros((size, LANES), f32)
        dk = jnp.zeros((size, LANES), f32)
        dv = jnp.zeros((size, LANES), f32)
        for h in range(2):
            mine = low_lane if h == 0 else jnp.logical_not(low_lane)
            key = jnp.where(mine, k, zero)
            scores = dot_nt(q, key) + bias[half]
            mass = jnp.sum(
                jnp.where(lane_id == 2 * pair + h, sums, 0.0), axis=-1, keepdims=True
            )
            weights = jnp.exp(scores - mass)
            pull = dot_nt(up, jnp.where(mine, v, zero))
            mean = jnp.sum(weights * pull, axis=-1, keepdims=True)
            spare = (weights * (pull - mean)).astype(bf16)
            dq = dq + dot_nn(spare, key)
            dk = dk + dot_tn(spare, jnp.where(mine, q, zero))
            dv = dv + dot_tn(weights.astype(bf16), jnp.where(mine, up, zero))
        dproj[rows, cut(0)] = (dq * 0.125).astype(bf16)
        dproj[rows, cut(1)] = dk.astype(bf16)
        dproj[rows, cut(2)] = dv.astype(bf16)
        return carry

    def weigh(k):
        span = slice(2 * k * chunk, 2 * (k + 1) * chunk)
        for q in range(3):
            part = dot_nn(tok_t[...], dproj[:, q * width + span.start : q * width + span.stop])
            part = part.reshape(nz, 2, rows_own, 2 * chunk).astype(bf16)
            for n in range(2):
                wp[2 * k + n, q % 2, q // 2] = part[..., n * chunk : (n + 1) * chunk]
        p1(2 * k).start()
        p1(2 * k + 1).start()

    def res_home(n, i):
        return lambda: send_home(n, res_in, o_res, r_send, r_recv, False, 2 * i, 2)

    def ig_home(n, i):
        send_home(n, ig, o_ig, i_send, i_recv, False, 2 * i, 2)

    hooks = {
        0: [lambda: mg_step(soon, 0), taps_core_add],
        1: [half_add, place_half],
        2: [place_last, res_home(0, 0)],
        3: [lambda: weigh(0), last_y_add, res_home(0, 1)],
        4: [res_home(0, 2)],
        5: [lambda: mg_step(soon, 1), taps_side_add],
        6: [lambda: down_y_add(0), res_home(0, 3)],
        7: [lambda: weigh(1), lambda: p_add_1(0), lambda: p_add_1(1)],
        8: [last_x_add, res_home(1, 0)],
        9: [lambda: down_y_add(parts), res_home(1, 1)],
        10: [lambda: mg_step(soon, 2), taps_y_add],
        11: [lambda: weigh(2)],
    }

    def attend_and_pass(index, carry):
        attend(index, carry)
        for at, steps in hooks.items():

            @pl.when(index == at)
            def _(steps=steps):
                for step in steps:
                    step()

        return carry

    lax.fori_loop(0, 2 * pairs, attend_and_pass, 0)
    loads[4].wait()
    back = dot_nt(dproj[...], wqkv[...]).astype(bf16)
    brm[...] = dot_nn(perm[1], back).astype(bf16).reshape(16, across, width)
    mixed_away = remote(
        brm.at[pl.ds(7 * (1 - c), 9)], frame.at[:, c], ex_send.at[1], ex_recv.at[1], core
    )
    mixed_away.start()
    mixed_own = pltpu.make_async_copy(brm.at[pl.ds(7 * c, 9)], frame.at[:, c], own_sem.at[1])
    mixed_own.start()
    p_add_2(0)
    p_add_2(1)
    p_add_1(2)
    p_add_1(3)
    res_home(1, 2)()
    loads[5].wait()
    loads[6].wait()

    shift = mod[0:1, :]
    scale_in = 1.0 + mod[1:2, :]

    def again(row, carry):
        normal, _ = normalize(xf[2 * c + row].astype(f32))
        value[row] = (normal * scale_in + shift).astype(bf16).astype(f32)
        return carry

    grouped(16, again, 0)
    p_add_1(4)
    p_add_1(5)
    res_home(1, 3)()
    up_sum()
    mixed_own.wait()
    mixed_away.wait()

    def lay(row, carry):
        at = c + row
        line = frame[at // 2, lax.rem(at, 2)].astype(f32)
        before, after = column_shifts(line)
        gs[0, 1 - c + row] = after
        gs[1, 1 - c + row] = line
        gs[2, 1 - c + row] = before
        return carry

    grouped(17, lay, 0)
    for s in range(3):
        gs[s, 17 * c] = jnp.zeros((across, width), f32)

    def conv_back(lane, half):
        span = slice(lane, lane + LANES)
        taps = [kern[n : n + 1, span].astype(f32) for n in range(9)]

        def backward(row, sums):
            total = jnp.zeros((across, LANES), f32)
            own = value[row, :, span]
            later = []
            for r in range(3):
                for s in range(3):
                    line = gs[s, row + 2 - r, :, span]
                    total = total + taps[3 * r + s] * line
                    later.append(sums[3 * r + s] + fold(own * line))
            agrad[row, :, span] = total
            return tuple(later)

        sums = lax.fori_loop(
            8 * half, 8 * half + 8, backward,
            tuple(jnp.zeros((8, LANES), f32) for _ in range(9)),
        )
        rows9 = [jnp.sum(sums[n], axis=0, keepdims=True) for n in range(9)]
        lines = jnp.concatenate(rows9 + [jnp.zeros((7, LANES), f32)])
        if half == 0:
            taps_sum[:, span] = lines
        else:
            kk_1[0, :, span] = (taps_sum[:, span] + lines).astype(bf16)

    def finish(row, sums):
        normal, scale = normalize(xf[2 * c + row].astype(f32))
        line = agrad[row]
        place = pl.ds(pl.multiple_of(row * across, across), across)
        total = mid[place, :] + normalize_back(line * scale_in, normal, scale)
        ig[row] = total.astype(bf16)
        return (sums[0] + fold(line), sums[1] + fold(line * normal))

    sums = tuple(jnp.zeros((8, width), f32) for _ in range(2))
    p_add_3(0)
    p_add_3(1)
    down_sum()
    for lane in range(0, width, LANES):
        conv_back(lane, 0)
        if lane == 2 * LANES:
            p_add_2(2)
            p_add_2(3)
    sums = lax.fori_loop(0, 8, finish, sums)
    ig_home(0, 0)
    p_add_2(4)
    ig_home(0, 1)
    p_add_2(5)
    ig_home(0, 2)
    ig_home(0, 3)
    pass_on("gu", fin_u)
    taps_total()
    for lane in range(0, width, LANES):
        conv_back(lane, 1)
        if lane == 2 * LANES:
            p_add_3(2)
            p_add_3(3)
            pass_on("gd", fin_d)
            p_add_4(0)
            p_add_4(1)
    kern_copy("one", kk_1, kr_1, 0).start()
    sums = lax.fori_loop(8, 16, finish, sums)
    for n in range(2):
        ml_own[n : n + 1, :] = jnp.sum(sums[n], axis=0, keepdims=True)
    ml_copy(0).start()
    ig_home(1, 0)
    p_add_3(4)
    p_add_3(5)
    ig_home(1, 1)
    mg_end(soon)
    mg_swap().start()
    kern_step(*one, 0)
    ml_step(0)
    ig_home(1, 2)
    p_pass(0)
    p_pass(1)
    pass_on("gk", fin_k)
    p_add_4(2)
    p_add_4(3)
    ig_home(1, 3)
    kern_step(*one, 1)
    ml_step(1)
    mg_swap(False).wait_recv()
    mg_out.start()
    to_core("gu", fin_u, False).wait_recv()
    u_out.start()
    to_core("gd", fin_d, False).wait_recv()
    d_out.start()
    p_add_4(4)
    p_add_4(5)
    kern_step(*one, 2)
    ml_step(2)
    p_pass(2)
    p_pass(3)
    p_pass(4)
    p_pass(5)
    ml_step(3)
    ml_out.start()
    kern_sum("one", kk_1, kz_1, o_one)
    for k in range(chunks):
        p_core(k, False).wait_recv()
    p_out.start()
    to_core("gk", fin_k, False).wait_recv()
    for x in range(4):
        o_two[:, x * quarter : (x + 1) * quarter] = fin_k[x // 2, x % 2].astype(f32)
    gone([half_x(), last_y(), last_x(), last_d()])
    down_gone()
    gone([taps_core(), taps_side(), taps_y(), mg_swap()])
    for name, fin in (("gu", fin_u), ("gd", fin_d), ("gk", fin_k)):
        gone([to_side(name, fin, True), to_core(name, fin, True)])
    for d in range(1, nz):
        gone([up_z(d), mg_far(soon, d, zb), ml_far(d, zb)])
        gone([kern_far("one", kk_1, kz_1, d), taps_z(d)])
    for k in range(chunks):
        gone([p1(k), p2(k), p3(k), p_side(k, True), p_core(k, True)])
        gone([p4(k, d) for d in range(1, nz)])
    for stage in range(3):
        gone([mg_copy(soon, stage), ml_copy(stage)])
        gone([kern_copy("one", kk_1, kr_1, stage)])
    for n in range(2):
        send_home(n, res_in, o_res, r_send, r_recv, True)
        send_home(n, ig, o_ig, i_send, i_recv, True)
    home(o_res, r_recv)
    home(o_ig, i_recv)
    for out in (u_out, d_out, p_out, mg_out, ml_out):
        out.wait()


def back(
    mid, rg, tok, proj, att, lse, bias, x_frame, mod, small, kern, wqkv, wo, res,
    ud, dd, uh, dh, ul, dl, kern_two,
):
    nb = lax.axis_size("batch")
    nz = nb // 2
    across, width = x_frame.shape[1], x_frame.shape[2]
    tokens = 16 * across
    rows = width // nb
    grain = dd.shape[1]
    parts = dl.shape[1]
    per = dd.shape[0]
    chunks, chunk = width // LANES, LANES
    many = max(nz - 1, 1)
    any_space = pl.BlockSpec(memory_space=pl.ANY)
    vmem = pl.BlockSpec(memory_space=pltpu.VMEM)
    shape = jax.ShapeDtypeStruct
    dma = pltpu.SemaphoreType.DMA
    wide = kern_two.shape[1]
    links = 100 + 20 * many

    def low(*dims):
        return pltpu.VMEM(dims, bf16)

    def high(*dims):
        return pltpu.VMEM(dims, f32)

    return pl.pallas_call(
        back_kernel,
        out_shape=(
            shape((2, 2, rows, width), bf16),
            shape((2, 2, per, grain, width), bf16),
            shape((chunks, 2, 2, rows, chunk), bf16),
            shape((2, 8, across, width), bf16),
            shape((2, 8, across, width), bf16),
            shape((16, width), f32),
            shape((16, wide), f32),
            shape((2, nz, 2, 2, 8, width // 2), f32),
            shape((nz, 2, 2, 2, width), f32),
        ),
        in_specs=[any_space] * 5 + [vmem, vmem, any_space, vmem, vmem, vmem] + [any_space] * 9
        + [vmem],
        out_specs=[any_space] * 5 + [vmem, vmem, any_space, any_space],
        scratch_shapes=[
            high(tokens, width), low(tokens, width), low(width, tokens), low(tokens, 3 * width),
            low(tokens, width), low(18, across, width), low(*wqkv.shape), low(*wo.shape),
            low(16, across, width), low(2, tokens, tokens), low(tokens, width),
            low(tokens, width), low(tokens, 3 * width),
            low(16, across, width), low(9, 2, across, width), high(3, 18, across, width),
            high(16, across, width), high(16, across, width), low(16, across, width),
            low(chunks, 2, 2, nz, 2, rows, chunk), low(chunks, 2, nz, 2, rows, chunk),
            low(chunks, nz, 2, rows, chunk), low(chunks, 2, nz, rows, chunk),
            low(chunks, nz, rows, chunk), low(chunks, many, rows, chunk),
            low(chunks, 2, 2, rows, chunk),
            low(nz, rows, 2 * LANES), low(2 * parts, grain, width),
            low(many, rows, 2 * LANES), low(2 * parts, grain, width), low(per, many, grain, width),
            low(2, 2, rows, width), low(2, 2, per, grain, width), low(parts, grain, width),
            low(nz, rows, LANES), low(2, nz, rows, LANES), low(2, nz, rows, LANES),
            low(nz, rows, LANES),
            high(2, 8, width // 2), high(8, width // 2), high(2, nz, 2, 2, 8, width // 2),
            high(2, width), high(2, width), high(nz, 2, 2, 2, width), high(16, width),
            low(4, 16, width), low(3, 16, width), low(many, 16, width),
            low(2, 2, 16, wide // 4), low(2, 16, wide // 4), low(16, wide // 4), low(16, wide // 4),
            low(16, wide // 4), low(many, 16, wide // 4), low(2, 2, 16, wide // 4),
            dma((2 * parts,)), dma((2 * parts,)), dma((2 * parts,)), dma((per, many)), dma((14,)), dma((2,)), dma((2,)), dma((2,)), dma((2,)), dma((2,)), dma((2,)),
            dma((2,)), dma((links,)), dma((links,)), dma((5,)),
        ],
        compiler_params=pltpu.CompilerParams(
            collective_id=2, has_side_effects=True, vmem_limit_bytes=63 << 20
        ),
        name="back",
    )(
        mid, rg, tok, proj, att, lse, bias, x_frame, mod, small, kern, wqkv, wo, res,
        ud, dd, uh, dh, ul, dl, kern_two,
    )


def parts_of(values):
    first = values.astype(bf16)
    rest = values - first.astype(f32)
    second = rest.astype(bf16)
    third = (rest - second.astype(f32)).astype(bf16)
    return jnp.concatenate([first, second, third], axis=0)


def thrice(values):
    return jnp.concatenate([values] * 3, axis=0).astype(bf16)


def tail_kernel(
    fu, fd, fp, mg, late, one, two, wm_in, res_in, ig_in,
    o_class, o_time, o_mod, o_proj, o_out, o_one, o_up, o_two, o_down, o_res, o_ig,
    wm, moved, load_sem, in_sem, out_sem,
):
    b = lax.axis_index("batch")
    width = 2 * mg.shape[3]
    canvases = mg.shape[1]
    own = o_mod.shape[0]
    whole = wm_in.shape[0] == own
    source = wm_in if whole else wm_in.at[pl.ds(pl.multiple_of(b * own, 16), own)]
    load = pltpu.make_async_copy(source, wm, load_sem)
    load.start()
    takes = [
        pltpu.make_async_copy(src, moved.at[n], in_sem.at[n]) for n, src in enumerate((res_in, ig_in))
    ]
    gives = [
        pltpu.make_async_copy(moved.at[n], dst, out_sem.at[n]) for n, dst in enumerate((o_res, o_ig))
    ]
    for take in takes:
        take.start()
    chunks, chunk = fp.shape[0], fp.shape[4]
    per, grain = fd.shape[2], fd.shape[3]
    for q in range(4):
        for j in range(width // LANES):
            at = (4 * j + q) * LANES
            o_up[:, at : at + LANES] = fu[q % 2, q // 2, :, j * LANES : (j + 1) * LANES].astype(f32)
        for i in range(per):
            at = (4 * i + q) * grain
            o_down[at : at + grain, :] = fd[q % 2, q // 2, i].astype(f32)
        for k in range(chunks):
            part = fp[k, q % 2, q // 2].astype(f32)
            if q < 3:
                o_proj[:, q * width + k * chunk : q * width + (k + 1) * chunk] = part
            else:
                o_out[:, k * chunk : (k + 1) * chunk] = part
    for take, give in zip(takes, gives):
        take.wait()
        give.start()

    def window(values, n):
        size = values.shape[1]
        return pltpu.roll(values, lax.rem(size - b * n, size), 1)[:, :n]

    o_one[...] = window(one[...], own)[0:9]
    o_two[...] = window(two[...], o_two.shape[1])[0:9]
    every = jnp.concatenate([mg[0], mg[1]], axis=2)
    begin = late[...]
    cond = window(every[:, 7, :] * 0.5, own)
    sigma = 1.0 / (1.0 + jnp.exp(-cond))
    low = thrice(cond * sigma)
    steep = sigma * (1.0 + cond * (1.0 - sigma))
    act_grad = jnp.zeros((3 * canvases, own), f32)
    load.wait()
    for part in range(6):
        span = slice(part * width, (part + 1) * width)
        line = parts_of(begin[:, part, :] if part < 2 else every[:, part, :])
        o_mod[:, span] = dot_tn(low, line)
        act_grad = act_grad + dot_nt(line, wm[:, span])
    act_grad = (
        act_grad[2 * canvases :] + act_grad[canvases : 2 * canvases] + act_grad[:canvases]
    )
    cond_grad = parts_of(act_grad * steep)
    names = every[:, 6, :] * 0.5
    kinds = o_class.shape[1]
    spot = lax.broadcasted_iota(jnp.int32, (canvases, kinds), 1).astype(f32)
    for n, out in enumerate((o_class, o_time)):
        hot = thrice(jnp.where(spot == names[:, n : n + 1], 1.0, 0.0))
        out[...] = dot_tn(cond_grad, hot)
    for give in gives:
        give.wait()


def tail(fu, fd, fp, mg, late, one, two, wmod, res, ig, classes, times):
    nb = lax.axis_size("batch")
    width = 2 * mg.shape[3]
    own = width // nb
    wide = two.shape[1] // nb
    if own % 16:
        wmod = lax.dynamic_slice_in_dim(wmod, lax.axis_index("batch") * own, own, axis=0)
    any_space = pl.BlockSpec(memory_space=pl.ANY)
    vmem = pl.BlockSpec(memory_space=pltpu.VMEM)
    shape = jax.ShapeDtypeStruct
    dma = pltpu.SemaphoreType.DMA
    return pl.pallas_call(
        tail_kernel,
        out_shape=(
            shape((own, classes), f32),
            shape((own, times), f32),
            shape((own, 6 * width), f32),
            shape((own, 3 * width), f32),
            shape((own, width), f32),
            shape((9, own), f32),
            shape((own, 4 * width), f32),
            shape((9, wide), f32),
            shape((4 * fd.shape[2] * fd.shape[3], width), f32),
            shape(res.shape, bf16),
            shape(ig.shape, bf16),
        ),
        in_specs=[vmem] * 7 + [any_space] * 3,
        out_specs=[vmem] * 9 + [any_space] * 2,
        scratch_shapes=[
            pltpu.VMEM((own, 6 * width), bf16), pltpu.VMEM((2, *res.shape), bf16),
            dma, dma((2,)), dma((2,)),
        ],
        compiler_params=pltpu.CompilerParams(vmem_limit_bytes=60 << 20),
        name="tail",
    )(fu, fd, fp, mg, late, one, two, wmod, res, ig)


def body(
    inputs,
    segments,
    class_labels,
    time_steps,
    class_table,
    time_table,
    modulation_weight,
    project_weight,
    output_weight,
    kernel_attention,
    up_weight,
    kernel_feed,
    down_weight,
    cotangent,
):
    across, width = inputs.shape[2], inputs.shape[3]
    nb = lax.axis_size("batch")
    units = up_weight.shape[1]
    share = units // nb
    grain = 32 if share % 128 == 0 else 16 if share % 64 == 0 else 8
    x_frame, cot_frame, returned, tok, proj, att, lse, bias, mod = front(
        inputs, cotangent, class_labels, time_steps, segments, kernel_attention, class_table,
        time_table, modulation_weight, project_weight, output_weight,
    )
    flat = (18 * across, width)
    ud, dd, uh, dh, ul, dl, kern_two, res, mid, rg, small = feed(
        x_frame.reshape(flat), returned.reshape(flat), cot_frame.reshape(flat), mod, up_weight,
        kernel_feed, down_weight, grain,
    )
    fu, fd, fp, result, inputs_gradient, one, two, gathered, late = back(
        mid, rg.reshape(8, 2, across, width), tok, proj, att, lse, bias, x_frame, mod, small,
        kernel_attention, project_weight, output_weight, res.reshape(16, across, width),
        ud, dd, uh, dh, ul, dl, kern_two,
    )
    (
        class_total, time_total, modulation_total, project_total, output_total,
        attention_kernel_total, up_total, feed_kernel_total, down_total, result, inputs_gradient,
    ) = tail(
        fu, fd, fp, gathered.reshape(2, 2 * nb, 8, width // 2), late.reshape(2 * nb, 2, width), one, two,
        modulation_weight, result, inputs_gradient, class_table.shape[0], time_table.shape[0],
    )
    return (
        result,
        inputs_gradient,
        class_total.T,
        time_total.T,
        modulation_total,
        project_total,
        output_total,
        attention_kernel_total,
        up_total,
        feed_kernel_total,
        down_total,
    )


def solution(mesh):
    in_specs = (
        P("batch", "group", None, None),
        P("batch", None),
        P("batch"),
        P("batch"),
        P(),
        P(),
        P(),
        P(),
        P(),
        P(),
        P(),
        P(),
        P(),
        P("batch", "group", None, None),
    )
    out_specs = (
        P("batch", "group", None, None),
        P("batch", "group", None, None),
        P(None, "batch"),
        P(None, "batch"),
        P("batch", None),
        P("batch", None),
        P("batch", None),
        P(None, "batch"),
        P("batch", None),
        P(None, "batch"),
        P("batch", None),
    )
    return jax.shard_map(body, mesh=mesh, in_specs=in_specs, out_specs=out_specs, check_vma=False)
```

```python
from functools import partial

import jax
import jax.numpy as jnp
from jax import lax
from jax.experimental import pallas as pl
from jax.experimental.pallas import tpu as pltpu
from jax.sharding import PartitionSpec as P

HEADS = 12
MESH = pl.DeviceIdType.MESH
LANES = 128
f32 = jnp.float32
bf16 = jnp.bfloat16
highest = lax.Precision.HIGHEST


def dot_nn(a, b):
    return lax.dot_general(a, b, (((1,), (0,)), ((), ())), preferred_element_type=f32)


def dot_nt(a, b):
    return lax.dot_general(a, b, (((1,), (1,)), ((), ())), preferred_element_type=f32)


def dot_tn(a, b):
    return lax.dot_general(a, b, (((0,), (0,)), ((), ())), preferred_element_type=f32)


def remote(src, dst, send, recv, target):
    return pltpu.make_async_remote_copy(
        src_ref=src, dst_ref=dst, send_sem=send, recv_sem=recv, device_id=target,
        device_id_type=MESH,
    )


def meet(partners):
    barrier = pltpu.get_barrier_semaphore()
    for partner in partners:
        pl.semaphore_signal(barrier, inc=1, device_id=partner, device_id_type=MESH)
    pl.semaphore_wait(barrier, len(partners))


def normalize(values):
    center = values - jnp.mean(values, axis=-1, keepdims=True)
    second = jnp.mean(center * center, axis=-1, keepdims=True)
    scale = lax.rsqrt(second + 1e-06)
    return center * scale, scale


def normalize_back(grad, normal, scale):
    return scale * (
        grad
        - jnp.mean(grad, axis=-1, keepdims=True)
        - normal * jnp.mean(grad * normal, axis=-1, keepdims=True)
    )


def column_shifts(row):
    across = row.shape[0]
    column = lax.broadcasted_iota(jnp.int32, row.shape, 0)
    before = jnp.where(column == 0, 0.0, pltpu.roll(row, 1, 0))
    after = jnp.where(column == across - 1, 0.0, pltpu.roll(row, across - 1, 0))
    return before, after


def fold(values):
    rows, width = values.shape
    return jnp.sum(values.reshape(rows // 8, 8, width), axis=0)


def grouped(count, body, carry, size=4, begin=0):
    def several(i, carry):
        for n in range(size):
            carry = body(begin + size * i + n, carry)
        return carry

    whole = count // size
    carry = lax.fori_loop(0, whole, several, carry)
    for n in range(whole * size, count):
        carry = body(begin + n, carry)
    return carry


def permutation(inverse):
    n = 512
    to = lax.broadcasted_iota(jnp.int32, (n, n), 1 if inverse else 0)
    source = lax.broadcasted_iota(jnp.int32, (n, n), 0 if inverse else 1)
    wanted = lax.shift_left(lax.shift_right_logical(to & 255, 4), 5) + 2 * (to & 15) + (
        lax.shift_right_logical(to, 8)
    )
    return jnp.where(source == wanted, 1.0, 0.0).astype(bf16)


def front_kernel(
    x_in, cot_in, names, moments, segments, kern, class_in, time_in, wmod_in, wqkv_in, wo_in,
    o_x, o_cot, o_ret, o_tok, o_proj, o_att, o_lse, o_bias, mod,
    xf, table, wmod, wqkv, wo, shifts, mixed, rows_m, perm, bias, tok, proj, att, lse, brm,
    load_sem, x_send, x_recv, c_send, c_recv, ex_send, ex_recv, own_sem, out_sem,
):
    b = lax.axis_index("batch")
    g = lax.axis_index("group")
    c, p = lax.rem(g, 2), g // 2
    core, side, corner = (b, g + 1 - 2 * c), (b, g + 2 - 4 * p), (b, 3 - g)
    inner = jnp.logical_or(g == 1, g == 2)
    width = xf.shape[-1]
    across = xf.shape[1]

    def spread_out(src, dst, send, recv, waiting):
        main = c * 8 + p * 2
        other_main = remote(
            src.at[1 - p], dst.at[pl.ds(main, 8)], send.at[0], recv.at[c], (b, 2 - p)
        )
        edge = 6 * (2 - g)
        edge_to = 16 * (g - 1)
        other_edge = remote(
            src.at[1 - p, pl.ds(edge, 2)], dst.at[pl.ds(edge_to, 2)], send.at[1], recv.at[2], side
        )
        own_main = remote(src.at[p], dst.at[pl.ds(main, 8)], send.at[2], recv.at[c], core)
        own_edge = pltpu.make_async_copy(
            src.at[p, pl.ds(edge, 2)], dst.at[pl.ds(edge_to, 2)], recv.at[2]
        )
        stay_main = pltpu.make_async_copy(src.at[p], dst.at[pl.ds(main, 8)], recv.at[c])
        if waiting:
            other_main.wait_send()

            @pl.when(inner)
            def _():
                other_edge.wait_send()
                own_main.wait_send()

        else:
            other_main.start()

            @pl.when(inner)
            def _():
                other_edge.start()
                own_main.start()
                own_edge.start()

            @pl.when(jnp.logical_not(inner))
            def _():
                stay_main.start()

    def arrived(dst, recv):
        for j in range(2):
            place = dst.at[pl.ds(8 * j + 2 * c, 8)]
            pltpu.make_async_copy(place, place, recv.at[j]).wait()
        place = dst.at[pl.ds(16 * (1 - c), 2)]
        pltpu.make_async_copy(place, place, recv.at[2]).wait()

    pieces = [
        (wqkv_in, wqkv), (wo_in, wo), (class_in, table.at[0]), (time_in, table.at[1]),
        (wmod_in, wmod),
    ]
    loads = [
        pltpu.make_async_copy(src, dst, load_sem.at[n]) for n, (src, dst) in enumerate(pieces)
    ]
    for n in (2, 3, 4, 0, 1):
        loads[n].start()
    meet([core, side, corner])
    spread_out(x_in, xf, x_send, x_recv, False)
    perm[0] = permutation(False)
    perm[1] = permutation(True)
    n = tok.shape[0]
    wide = segments.shape[1]
    to = lax.broadcasted_iota(jnp.int32, (n, wide), 0)
    source = lax.broadcasted_iota(jnp.int32, (n, wide), 1)
    wanted = lax.shift_left(2 * lax.shift_right_logical(to & 255, 4) + c, 5) + 2 * (to & 15) + (
        lax.shift_right_logical(to, 8)
    )
    chosen = source == wanted
    one_line = jnp.where(p == 0, segments[0:1, :], segments[1:2, :]).astype(f32)
    lines = jnp.broadcast_to(one_line, (8, wide)).astype(bf16)
    lab_row = dot_nt(lines, jnp.where(chosen, 1.0, 0.0).astype(bf16))
    lab_col = jnp.sum(jnp.where(chosen, one_line, 0.0), axis=-1, keepdims=True)
    for half in range(2):
        cut = slice(half * (n // 2), (half + 1) * (n // 2))
        bias[half] = jnp.where(lab_row[0:1, cut] == lab_col[cut], 0.0, -1e30)
    bias_out = pltpu.make_async_copy(bias, o_bias, out_sem.at[5])
    bias_out.start()
    name = jnp.where(p == 0, names[0], names[1])
    moment = jnp.where(p == 0, moments[0], moments[1])
    loads[2].wait()
    loads[3].wait()
    rows_all = lax.broadcasted_iota(jnp.int32, (8, table.shape[1]), 1)
    cond = dot_nn(jnp.where(rows_all == name, 1.0, 0.0).astype(bf16), table[0]) + dot_nn(
        jnp.where(rows_all == moment, 1.0, 0.0).astype(bf16), table[1]
    )
    cond_low = (cond / (1.0 + jnp.exp(-cond))).astype(bf16)
    loads[4].wait()
    for part in range(6):
        cut = slice(part * width, (part + 1) * width)
        mod[part : part + 1, :] = dot_nn(cond_low, wmod[:, cut])[0:1, :]
    lane_of = lax.broadcasted_iota(jnp.int32, (1, width), 1)
    mod[6:7, :] = jnp.where(
        lane_of == 0, name.astype(f32), jnp.where(lane_of == 1, moment.astype(f32), 0.0)
    )
    mod[7:8, :] = cond[0:1, :]
    arrived(xf, x_recv)
    spread_out(cot_in, o_cot, c_send, c_recv, False)
    x_out = pltpu.make_async_copy(xf, o_x, out_sem.at[0])
    x_out.start()

    shift = mod[0:1, :]
    scale = 1.0 + mod[1:2, :]

    def first(i, carry):
        normal, _ = normalize(xf[c + i].astype(f32))
        value = (normal * scale + shift).astype(bf16).astype(f32)
        before, after = column_shifts(value)
        shifts[0, 1 - c + i] = before
        shifts[1, 1 - c + i] = value
        shifts[2, 1 - c + i] = after
        return carry

    grouped(17, first, 0)
    for s in range(3):
        shifts[s, 17 * c] = jnp.zeros((across, width), f32)

    def conv(step, parity):
        o = 2 * step + parity
        for lane in range(0, width, LANES):
            cut = slice(lane, lane + LANES)
            total = jnp.zeros((across, LANES), f32)
            for r in range(3):
                for s in range(3):
                    tap = kern[3 * r + s : 3 * r + s + 1, cut].astype(f32)
                    total = total + tap * shifts[s, o + r, :, cut]
            mixed[step, parity, :, cut] = total.astype(bf16)

    def conv_away(step, carry):
        conv(step, 1 - c)
        return carry

    def conv_own(step, carry):
        conv(step, c)
        return carry

    lax.fori_loop(0, 8, conv_away, 0)
    mixed_away = remote(
        mixed.at[:, 1 - c], rows_m.at[pl.ds(8 * c, 8)], ex_send.at[0], ex_recv.at[0], core
    )
    mixed_away.start()
    lax.fori_loop(0, 8, conv_own, 0)
    mixed_own = pltpu.make_async_copy(mixed.at[:, c], rows_m.at[pl.ds(8 * c, 8)], own_sem.at[0])
    mixed_own.start()
    mixed_own.wait()
    mixed_away.wait()
    flat = rows_m[...].reshape(16 * across, width)
    tok[...] = dot_nn(perm[0], flat).astype(bf16)
    tok_out = pltpu.make_async_copy(tok, o_tok, out_sem.at[1])
    tok_out.start()
    loads[0].wait()
    for part in range(3):
        cut = slice(part * width, (part + 1) * width)
        proj[:, cut] = dot_nn(tok[...], wqkv[:, cut]).astype(bf16)
    proj_out = pltpu.make_async_copy(proj, o_proj, out_sem.at[2])
    proj_out.start()

    pairs = width // LANES
    size = tok.shape[0] // 2
    low_lane = lax.broadcasted_iota(jnp.int32, (size, LANES), 1) < LANES // 2
    lane_id = lax.broadcasted_iota(jnp.int32, (size, LANES), 1)
    zero = jnp.zeros((), bf16)

    def attend(index, carry):
        half, pair = index // pairs, lax.rem(index, pairs)
        rows = pl.ds(pl.multiple_of(half * size, size), size)

        def part(n):
            return proj[rows, pl.ds(pl.multiple_of(n * width + pair * LANES, LANES), LANES)]

        q, k, v = part(0) * jnp.asarray(0.125, bf16), part(1), part(2)
        total = jnp.zeros((size, LANES), f32)
        sums = lse[half]
        for h in range(2):
            mine = low_lane if h == 0 else jnp.logical_not(low_lane)
            scores = dot_nt(q, jnp.where(mine, k, zero)) + bias[half]
            top = jnp.max(scores, axis=-1, keepdims=True)
            powers = jnp.exp(scores - top)
            mass = jnp.sum(powers, axis=-1, keepdims=True)
            weights = (powers * (1.0 / mass)).astype(bf16)
            total = total + dot_nn(weights, jnp.where(mine, v, zero))
            sums = jnp.where(lane_id == 2 * pair + h, top + jnp.log(mass), sums)
        lse[half] = sums
        att[rows, pl.ds(pl.multiple_of(pair * LANES, LANES), LANES)] = total.astype(bf16)
        return carry

    lse[...] = jnp.zeros(lse.shape, f32)
    grouped(2 * pairs, attend, 0)
    att_out = pltpu.make_async_copy(att, o_att, out_sem.at[3])
    att_out.start()
    lse_out = pltpu.make_async_copy(lse, o_lse, out_sem.at[4])
    lse_out.start()
    loads[1].wait()
    branch = dot_nn(att[...], wo[...]).astype(bf16)
    brm[...] = dot_nn(perm[1], branch).astype(bf16).reshape(16, across, width)
    ret_away = remote(
        brm.at[pl.ds(7 * (1 - c), 9)], o_ret.at[:, c], ex_send.at[1], ex_recv.at[1], core
    )
    ret_away.start()
    ret_own = pltpu.make_async_copy(brm.at[pl.ds(7 * c, 9)], o_ret.at[:, c], own_sem.at[1])
    ret_own.start()
    for out in (x_out, tok_out, proj_out, att_out, lse_out, bias_out, ret_own):
        out.wait()
    ret_away.wait()
    spread_out(x_in, xf, x_send, x_recv, True)
    spread_out(cot_in, o_cot, c_send, c_recv, True)
    arrived(o_cot, c_recv)


def front(inputs, cotangent, names, moments, segments, kern, classes, times, wmod, wqkv, wo):
    across, width = inputs.shape[2], inputs.shape[3]
    tokens = 16 * across
    any_space = pl.BlockSpec(memory_space=pl.ANY)
    vmem = pl.BlockSpec(memory_space=pltpu.VMEM)
    smem = pl.BlockSpec(memory_space=pltpu.SMEM)
    shape = jax.ShapeDtypeStruct
    dma = pltpu.SemaphoreType.DMA
    return pl.pallas_call(
        front_kernel,
        out_shape=(
            shape((18, across, width), bf16),
            shape((18, across, width), bf16),
            shape((9, 2, across, width), bf16),
            shape((tokens, width), bf16),
            shape((tokens, 3 * width), bf16),
            shape((tokens, width), bf16),
            shape((2, tokens // 2, LANES), f32),
            shape((2, tokens // 2, tokens // 2), f32),
            shape((8, width), f32),
        ),
        in_specs=[any_space] * 2 + [smem] * 2 + [vmem] * 2 + [any_space] * 5,
        out_specs=[any_space] * 8 + [vmem],
        scratch_shapes=[
            pltpu.VMEM((18, across, width), bf16),
            pltpu.VMEM((2, *classes.shape), bf16),
            pltpu.VMEM(wmod.shape, bf16),
            pltpu.VMEM(wqkv.shape, bf16),
            pltpu.VMEM(wo.shape, bf16),
            pltpu.VMEM((3, 18, across, width), f32),
            pltpu.VMEM((8, 2, across, width), bf16),
            pltpu.VMEM((16, across, width), bf16),
            pltpu.VMEM((2, tokens, tokens), bf16),
            pltpu.VMEM((2, tokens // 2, tokens // 2), f32),
            pltpu.VMEM((tokens, width), bf16),
            pltpu.VMEM((tokens, 3 * width), bf16),
            pltpu.VMEM((tokens, width), bf16),
            pltpu.VMEM((2, tokens // 2, LANES), f32),
            pltpu.VMEM((16, across, width), bf16),
            dma((5,)), dma((3,)), dma((3,)), dma((3,)), dma((3,)), dma((2,)), dma((2,)),
            dma((2,)), dma((6,)),
        ],
        compiler_params=pltpu.CompilerParams(
            collective_id=1, has_side_effects=True, vmem_limit_bytes=60 << 20
        ),
        name="front",
    )(inputs, cotangent, names, moments, segments, kern, classes, times, wmod, wqkv, wo)


def gelu_parts(x):
    size = jnp.abs(x)
    t = 1.0 / (1.0 + (0.3275911 * 0.7071067811865476) * size)
    bell = jnp.exp(-0.5 * x * x)
    series = t * (
        0.254829592
        + t * (-0.284496736 + t * (1.421413741 + t * (-1.453152027 + t * 1.061405429)))
    )
    tail = 0.5 * series * bell
    mass = jnp.where(x >= 0, 1.0 - tail, tail)
    return x * mass, mass + x * bell * 0.3989422804014327


def tile_of(step, tiles):
    return jnp.where(lax.rem(step, 2) == 0, step // 2, tiles - 1 - step // 2)


def feed_kernel(
    x_in, ret_in, cot_in, mod, up, kern, down,
    o_up, o_down, o_up_half, o_down_half, o_up_last, o_down_last, o_kern, o_res, o_mid, o_rg, o_small,
    feed_in, feed_t, btg, out_acc, back_acc, hid, hs, gs, act, slope, hg,
    wu, wd, ru, rd, yu, xu, zu, fin, xd, yd, zd, fin_d,
    u1_send, u1_recv, u2_send, u2_recv, u3_send, u3_recv, d1_send, d1_recv, d2_send, d2_recv,
    u4_send, u4_recv, d3_send, d3_recv, d4_send, d4_recv, u_out, d_out, l_out,
):
    j = pl.program_id(0)
    tiles = pl.num_programs(0)
    b = lax.axis_index("batch")
    g = lax.axis_index("group")
    c, p = lax.rem(g, 2), g // 2
    nz = wu.shape[3]
    yb, zb = lax.rem(b, 2), b // 2
    core, side, beside = (b, g + 1 - 2 * c), (b, g + 2 - 4 * p), (b + 1 - 2 * yb, g)
    others = [lax.rem(zb + d, nz) for d in range(nz)]
    far = [(2 * z + yb, g) for z in others]
    parts = wd.shape[3]

    def up_1(t):
        return remote(wu.at[t, 1 - c], ru.at[t], u1_send.at[t], u1_recv.at[t], core)

    def down_1(t):
        return remote(wd.at[t, 1 - c], rd.at[t], d1_send.at[t], d1_recv.at[t], core)

    def up_2(t):
        return remote(wu.at[t, c, :, :, 1 - yb], yu.at[t], u2_send.at[t], u2_recv.at[t], beside)

    def down_2(t):
        return remote(wd.at[t, c, 1 - p], xd.at[t], d2_send.at[t], d2_recv.at[t], side)

    def up_3(t):
        return remote(wu.at[t, c, 1 - p, :, yb], xu.at[t], u3_send.at[t], u3_recv.at[t], side)

    def up_4(t, d):
        return remote(
            wu.at[t, c, p, others[d], yb], zu.at[t, d - 1], u4_send.at[t, d - 1],
            u4_recv.at[t, d - 1], far[d],
        )

    def up_store(t):
        spot = pl.ds(pl.multiple_of(tile_of(t, tiles) * LANES, LANES), LANES)
        return pltpu.make_async_copy(fin.at[t], o_up.at[:, spot], u_out.at[t])

    per = fin_d.shape[0]

    def owner_of(t, k):
        place = parts * tile_of(t, tiles) + k
        return place // per, lax.rem(place, per)

    def down_3(t, k):
        return remote(
            wd.at[t, c, p, k], yd.at[t, k], d3_send.at[t, k], d3_recv.at[t, k], beside
        )

    def down_4(t, k):
        owner, spot = owner_of(t, k)
        slot = lax.rem(zb - owner // 2 + nz, nz) - 1
        return remote(
            wd.at[t, c, p, k], zd.at[spot, slot], d4_send.at[t, k], d4_recv.at[spot, slot],
            (2 * (owner // 2) + yb, g),
        )

    def each_part(t, away, here):
        def step(k, carry):
            owner, spot = owner_of(t, k)
            mine = lax.rem(owner, 2) == yb

            @pl.when(jnp.logical_not(mine))
            def _():
                away(k)

            @pl.when(mine)
            def _():
                here(k, owner, spot)

            return carry

        lax.fori_loop(0, parts, step, 0)

    def nothing(*_):
        pass

    def down_store(spot):
        return pltpu.make_async_copy(fin_d.at[spot], o_down.at[spot], d_out.at[spot])

    def add_core(t):
        down_1(t).wait_recv()
        up_1(t).wait_recv()

        def step(i, carry):
            x, z, y = i // (2 * nz), lax.rem(i // 2, nz), lax.rem(i, 2)
            wu[t, c, x, z, y] = wu[t, c, x, z, y] + ru[t, x, z, y]
            return carry

        grouped(4 * nz, step, 0)

        def step_down(i, carry):
            x, k = i // parts, lax.rem(i, parts)
            wd[t, c, x, k] = wd[t, c, x, k] + rd[t, x, k]
            return carry

        grouped(2 * parts, step_down, 0)

    def add_beside(t):
        up_2(t).wait_recv()

        def step(i, carry):
            x, z = i // nz, lax.rem(i, nz)
            wu[t, c, x, z, yb] = wu[t, c, x, z, yb] + yu[t, x, z]
            return carry

        grouped(2 * nz, step, 0)

    def add_side(t):
        up_3(t).wait_recv()

        def step(z, carry):
            wu[t, c, p, z, yb] = wu[t, c, p, z, yb] + xu[t, z]
            return carry

        grouped(nz, step, 0)
        for d in range(1, nz):
            up_4(t, d).start()

    def add_far(t):
        total = wu[t, c, p, zb, yb].astype(f32)
        for d in range(1, nz):
            up_4(t, d).wait_recv()
            total = total + zu[t, d - 1].astype(f32)
        fin[t] = total.astype(bf16)
        up_store(t).start()

    def add_side_down(t):
        down_2(t).wait_recv()

        def step(k, carry):
            wd[t, c, p, k] = wd[t, c, p, k] + xd[t, k]
            return carry

        grouped(parts, step, 0)

    def send_beside_down(t):
        each_part(t, lambda k: down_3(t, k).start(), nothing)

    def add_beside_down(t):
        def here(k, owner, spot):
            down_3(t, k).wait_recv()
            wd[t, c, p, k] = wd[t, c, p, k] + yd[t, k]

            @pl.when(owner // 2 != zb)
            def _():
                down_4(t, k).start()

        each_part(t, nothing, here)

    def add_far_down(t):
        def here(k, owner, spot):
            @pl.when(owner // 2 == zb)
            def _():
                total = wd[t, c, p, k].astype(f32)
                for d in range(1, nz):
                    place = zd.at[spot, d - 1]
                    pltpu.make_async_copy(place, place, d4_recv.at[spot, d - 1]).wait()
                    total = total + zd[spot, d - 1].astype(f32)
                fin_d[spot] = total.astype(bf16)
                down_store(spot).start()

        each_part(t, nothing, here)

    def settle_down(t):
        def here(k, owner, spot):
            @pl.when(owner // 2 != zb)
            def _():
                down_4(t, k).wait_send()

            @pl.when(owner // 2 == zb)
            def _():
                down_store(spot).wait()

        each_part(t, lambda k: down_3(t, k).wait_send(), here)

    across = 32
    width = feed_in.shape[1]
    tile = up.shape[1]
    frame_rows = feed_in.shape[0] // across
    own = pl.ds(pl.multiple_of(2 * c * across, 64), 16 * across)

    def middle_of(row):
        place = pl.ds(pl.multiple_of(row * across, across), across)
        returned = ret_in[place, :].astype(f32)
        return x_in[place, :].astype(f32) + mod[2:3, :] * returned, returned

    @pl.when(j == 0)
    def _():
        meet([core, side, beside, *far[1:]])

        def prepare(row, carry):
            place = pl.ds(pl.multiple_of(row * across, across), across)
            normal, _ = normalize(middle_of(row)[0])
            feed_in[place, :] = (normal * (1.0 + mod[4:5, :]) + mod[3:4, :]).astype(bf16)
            btg[place, :] = (mod[5:6, :] * cot_in[place, :].astype(f32)).astype(bf16)
            return carry

        grouped(frame_rows, prepare, 0)
        feed_t[...] = feed_in[own, :].T
        out_acc[...] = jnp.zeros(out_acc.shape, f32)
        back_acc[...] = jnp.zeros(back_acc.shape, f32)
        for s in range(3):
            hs[s, 18 * c] = jnp.zeros((across, tile), f32)
            gs[s, 17 * c] = jnp.zeros((across, tile), f32)

    hid[...] = dot_nn(feed_in[...], up[...]).astype(bf16)

    def lay_hidden(row, carry):
        value = hid[pl.ds(pl.multiple_of(row * across, across), across), :].astype(f32)
        before, after = column_shifts(value)
        hs[0, 1 - c + row] = before
        hs[1, 1 - c + row] = value
        hs[2, 1 - c + row] = after
        return carry

    grouped(frame_rows, lay_hidden, 0)

    for lane in range(0, tile, LANES):
        cut = slice(lane, lane + LANES)
        taps = [kern[n : n + 1, cut].astype(f32) for n in range(9)]

        def forward(row, carry):
            total = jnp.zeros((across, LANES), f32)
            for r in range(3):
                for s in range(3):
                    total = total + taps[3 * r + s] * hs[s, row + r, :, cut]
            place = pl.ds(pl.multiple_of(row * across, across), across)
            value, steep = gelu_parts(total)
            act[place, cut] = value.astype(bf16)
            slope[place, cut] = steep
            return carry

        grouped(17, forward, 0)

    @pl.when(j >= 2)
    def _():
        add_side(j - 2)
        add_beside_down(j - 2)

    @pl.when(j >= 1)
    def _():
        add_core(j - 1)
        up_2(j - 1).start()
        down_2(j - 1).start()

    @pl.when(j >= 3)
    def _():
        add_far(j - 3)
        add_far_down(j - 3)

    inside = pl.ds(pl.multiple_of(c * across, across), 16 * across)
    around = pl.ds(pl.multiple_of(c * across, across), 17 * across)
    own_act = act[inside, :]
    out_acc[...] += dot_nn(own_act, down[...])
    grad_down = dot_tn(own_act, btg[own, :]).reshape(parts, 4, wd.shape[4], width)
    for q in range(4):
        wd[j, q % 2, q // 2] = grad_down[:, q].astype(bf16)
    down_1(j).start()
    slope[...] = slope[...] * dot_nt(btg[around, :], down[...])

    def lay_grad(row, carry):
        value = slope[pl.ds(pl.multiple_of(row * across, across), across), :]
        value = value.astype(bf16).astype(f32)
        before, after = column_shifts(value)
        gs[0, 1 - c + row] = after
        gs[1, 1 - c + row] = value
        gs[2, 1 - c + row] = before
        return carry

    grouped(17, lay_grad, 0)

    for lane in range(0, tile, LANES):
        cut = slice(lane, lane + LANES)
        taps = [kern[n : n + 1, cut].astype(f32) for n in range(9)]

        def backward(row, sums):
            total = jnp.zeros((across, LANES), f32)
            value = hs[1, row + c + 1, :, cut]
            later = []
            for r in range(3):
                for s in range(3):
                    grad = gs[s, row + 2 - r, :, cut]
                    total = total + taps[3 * r + s] * grad
                    later.append(sums[3 * r + s] + fold(value * grad))
            hg[pl.ds(pl.multiple_of(row * across, across), across), cut] = total.astype(bf16)
            return tuple(later)

        sums = grouped(16, backward, tuple(jnp.zeros((8, LANES), f32) for _ in range(9)))
        for n in range(9):
            o_kern[n : n + 1, cut] = jnp.sum(sums[n], axis=0, keepdims=True)

    o_kern[9:16, :] = jnp.zeros((7, tile), f32)
    grad_up = dot_nn(feed_t[...], hg[...])
    for q in range(4):
        part = grad_up[:, q * LANES : (q + 1) * LANES]
        wu[j, q % 2, q // 2] = part.reshape(nz, 2, wu.shape[5], LANES).astype(bf16)
    up_1(j).start()
    back_acc[...] += dot_nt(hg[...], up[...])

    @pl.when(jnp.logical_and(j >= 1, j < tiles - 1))
    def _():
        add_beside(j - 1)
        up_3(j - 1).start()
        add_side_down(j - 1)
        send_beside_down(j - 1)

    @pl.when(j == tiles - 1)
    def _():
        def finish(row, sums):
            frame = row + 2 * c
            place = pl.ds(pl.multiple_of(row * across, across), across)
            at = pl.ds(pl.multiple_of(frame * across, across), across)
            middle, returned = middle_of(frame)
            cot = cot_in[at, :].astype(f32)
            branch = out_acc[place, :]
            o_res[place, :] = (middle + mod[5:6, :] * branch).astype(bf16)
            normal, scale = normalize(middle)
            grad = back_acc[place, :]
            mid = cot + normalize_back(grad * (1.0 + mod[4:5, :]), normal, scale)
            o_mid[place, :] = mid
            o_rg[place, :] = (mod[2:3, :] * mid).astype(bf16)
            terms = (mid * returned, grad, grad * normal, cot * branch)
            return tuple(total + fold(term) for total, term in zip(sums, terms))

        sums = grouped(16, finish, tuple(jnp.zeros((8, width), f32) for _ in range(4)))
        o_small[...] = jnp.zeros((8, width), f32)
        for n in range(4):
            o_small[n + 2 : n + 3, :] = jnp.sum(sums[n], axis=0, keepdims=True)
        add_beside(j - 1)
        half = pltpu.make_async_copy(wu.at[j - 1, c, :, :, yb], o_up_half, l_out.at[2])
        half.start()
        add_side_down(j - 1)
        half_down = pltpu.make_async_copy(wd.at[j - 1, c, p], o_down_half, l_out.at[3])
        half_down.start()
        add_core(j)
        last = (
            half,
            half_down,
            pltpu.make_async_copy(wu.at[j, c], o_up_last, l_out.at[0]),
            pltpu.make_async_copy(wd.at[j, c], o_down_last, l_out.at[1]),
        )
        for move in last[2:]:
            move.start()
        add_far(j - 2)
        add_far_down(j - 2)

        def settle(t, carry):
            up_3(t).wait_send()
            for d in range(1, nz):
                up_4(t, d).wait_send()
            up_store(t).wait()
            settle_down(t)
            return carry

        def settle_more(t, carry):
            up_2(t).wait_send()
            down_2(t).wait_send()
            up_1(t).wait_send()
            down_1(t).wait_send()
            return carry

        lax.fori_loop(0, tiles - 2, settle, 0)
        lax.fori_loop(0, tiles - 1, settle_more, 0)
        up_1(j).wait_send()
        down_1(j).wait_send()
        for move in last:
            move.wait()


def feed(x_frame, returned, cot_frame, mod, up, kern, down, grain):
    width, units = up.shape
    frame = x_frame.shape[0]
    across = frame // 18
    tokens = 16 * across
    shape = jax.ShapeDtypeStruct
    dma = pltpu.SemaphoreType.DMA
    any_space = pl.BlockSpec(memory_space=pl.ANY)
    tile = 4 * LANES
    tiles = units // tile
    parts = tile // (4 * grain)
    nb = lax.axis_size("batch")
    nz = nb // 2
    own = width // nb
    many = max(nz - 1, 1)

    def still(*size):
        return pl.BlockSpec(size, lambda j: (0, 0), pipeline_mode=pl.Buffered(1))

    columns = pl.BlockSpec((width, tile), lambda j: (0, tile_of(j, tiles)))
    rows = pl.BlockSpec((tile, width), lambda j: (tile_of(j, tiles), 0))
    per = tiles * parts // nb
    work = 6 * 2 * tokens * width * units
    return pl.pallas_call(
        feed_kernel,
        grid=(units // tile,),
        out_shape=(
            shape((own, tiles * LANES), bf16),
            shape((per, grain, width), bf16),
            shape((2, nz, own, LANES), bf16),
            shape((parts, grain, width), bf16),
            shape((2, nz, 2, own, LANES), bf16),
            shape((2, parts, grain, width), bf16),
            shape((16, units), f32),
            shape((tokens, width), bf16),
            shape((tokens, width), f32),
            shape((tokens, width), bf16),
            shape((8, width), f32),
        ),
        in_specs=[
            still(frame, width), still(frame, width), still(frame, width), still(8, width),
            columns, pl.BlockSpec((9, tile), lambda j: (0, tile_of(j, tiles))), rows,
        ],
        out_specs=[
            *[any_space] * 6, pl.BlockSpec((16, tile), lambda j: (0, tile_of(j, tiles))),
            still(tokens, width), still(tokens, width), still(tokens, width), still(8, width),
        ],
        scratch_shapes=[
            pltpu.VMEM((frame, width), bf16),
            pltpu.VMEM((width, tokens), bf16),
            pltpu.VMEM((frame, width), bf16),
            pltpu.VMEM((tokens, width), f32),
            pltpu.VMEM((tokens, width), f32),
            pltpu.VMEM((frame, tile), bf16),
            pltpu.VMEM((3, 19, across, tile), f32),
            pltpu.VMEM((3, 18, across, tile), f32),
            pltpu.VMEM((17 * across, tile), bf16),
            pltpu.VMEM((17 * across, tile), f32),
            pltpu.VMEM((tokens, tile), bf16),
            pltpu.VMEM((tiles, 2, 2, nz, 2, own, LANES), bf16),
            pltpu.VMEM((tiles, 2, 2, parts, grain, width), bf16),
            pltpu.VMEM((tiles, 2, nz, 2, own, LANES), bf16),
            pltpu.VMEM((tiles, 2, parts, grain, width), bf16),
            pltpu.VMEM((tiles, 2, nz, own, LANES), bf16),
            pltpu.VMEM((tiles, nz, own, LANES), bf16),
            pltpu.VMEM((tiles, many, own, LANES), bf16),
            pltpu.VMEM((tiles, own, LANES), bf16),
            pltpu.VMEM((tiles, parts, grain, width), bf16),
            pltpu.VMEM((tiles, parts, grain, width), bf16),
            pltpu.VMEM((per, many, grain, width), bf16),
            pltpu.VMEM((per, grain, width), bf16),
            *[dma((tiles,)) for _ in range(10)],
            dma((tiles, many)), dma((tiles, many)), dma((tiles, parts)), dma((tiles, parts)),
            dma((tiles, parts)), dma((per, many)), dma((tiles,)), dma((per,)), dma((4,)),
        ],
        compiler_params=pltpu.CompilerParams(
            dimension_semantics=("arbitrary",), collective_id=3, has_side_effects=True,
            vmem_limit_bytes=62 << 20,
        ),
        cost_estimate=pl.CostEstimate(
            flops=work, bytes_accessed=8 * width * units, transcendentals=tokens * units
        ),
        name="feed",
    )(x_frame, returned, cot_frame, mod, up, kern, down)


def back_kernel(
    mid_in, rg_in, tok_in, proj_in, att_in, lse, bias, x_in, mod, small, kern, wqkv_in, wo_in,
    res_in, ud_in, dd_in, uh_in, dh_in, ul_in, dl_in, kern_two,
    o_fu, o_fd, o_fp, o_res, o_ig, o_one, o_two, o_mg, o_ml,
    mid, tok, tok_t, proj, att, xf, wqkv, wo, rows_m, perm, grad, datt, dproj,
    brm, frame, gs, value, agrad, ig,
    wp, p_r1, p_r2x, p_r2y, p_r3, p_r4, fin_p,
    fu, fd, fz_u, fy_d, fz_d, fin_u, fin_d, lx_d, hx, ly, ly_r, lx,
    mg_own, mg_r1, mg_all, ml_own, ml_r1, ml_all, taps_sum, kk_1, kr_1, kz_1,
    kt, kt_core, kt_side, kt_y, kt_sum, kt_z, fin_k,
    dy_send, dy_recv, dz_send, dz_recv, load_sem, r_send, r_recv, i_send, i_recv, ex_send, ex_recv, own_sem, send_sem, recv_sem, out_sem,
):
    b = lax.axis_index("batch")
    g = lax.axis_index("group")
    nz = fu.shape[0]
    c, p = lax.rem(g, 2), g // 2
    yb, zb = lax.rem(b, 2), b // 2
    core, side, corner = (b, g + 1 - 2 * c), (b, g + 2 - 4 * p), (b, 3 - g)
    beside = (b + 1 - 2 * yb, g)
    others = [lax.rem(zb + d, nz) for d in range(nz)]
    far = [(2 * z + yb, g) for z in others]
    inner = jnp.logical_or(g == 1, g == 2)
    across, width = xf.shape[1], xf.shape[2]
    rows_own = fu.shape[1]
    pairs = width // LANES
    tokens = tok.shape[0]
    size = tokens // 2
    chunks = wp.shape[0]
    chunk = wp.shape[-1]
    tiles = width // LANES
    lead = (tiles // 2 - 1) * LANES
    per, parts = fin_d.shape[2], lx_d.shape[0]
    places = {}

    def link(name, src, dst, target):
        n = places.setdefault(name, len(places))
        return remote(src, dst, send_sem.at[n], recv_sem.at[n], target)

    def send_home(n, src, dst, send, recv, waiting, first=0, count=8):
        from_rows = src.at[pl.ds(8 * n + first, count)]
        to_rows = dst.at[p, pl.ds(first, count)]
        move = remote(from_rows, to_rows, send.at[n], recv.at[p], (b, 2 * c + n))
        away = remote(from_rows, to_rows, send.at[n], recv.at[p], core)
        stay = pltpu.make_async_copy(from_rows, to_rows, recv.at[p])

        @pl.when(inner)
        def _():
            if waiting:
                move.wait_send()
            else:
                move.start()

        @pl.when(jnp.logical_and(jnp.logical_not(inner), c != n))
        def _():
            if waiting:
                away.wait_send()
            else:
                away.start()

        if not waiting:

            @pl.when(jnp.logical_and(jnp.logical_not(inner), c == n))
            def _():
                stay.start()

    def home(dst, recv):
        for n in range(2):
            pltpu.make_async_copy(dst.at[n], dst.at[n], recv.at[n]).wait()

    def gone(moves):
        for move in moves:
            move.wait_send()

    def half_x():
        return link("hx", uh_in.at[1 - p], hx, side)

    def last_y():
        return link("ly", ul_in.at[:, :, 1 - yb], ly_r, beside)

    def last_x():
        return link("lx", ly.at[1 - p], lx, side)

    def last_d():
        return link("ld", dl_in.at[1 - p], lx_d, side)

    def owner_of(k):
        place = parts * (tiles // 2 - 1) + k
        return place // per, lax.rem(place, per)

    def down_y(k):
        return remote(fd.at[k], fy_d.at[k], dy_send.at[k], dy_recv.at[k], beside)

    def down_z(k):
        owner, spot = owner_of(k)
        slot = lax.rem(zb - owner // 2 + nz, nz) - 1
        return remote(
            fd.at[k], fz_d.at[spot, slot], dz_send.at[k], dz_recv.at[spot, slot],
            (2 * (owner // 2) + yb, g),
        )

    def each_part(begin, away, here):
        def step(k, carry):
            owner, spot = owner_of(k)
            mine = lax.rem(owner, 2) == yb

            @pl.when(jnp.logical_not(mine))
            def _():
                away(k)

            @pl.when(mine)
            def _():
                here(k, owner, spot)

            return carry

        lax.fori_loop(begin, begin + parts, step, 0)

    def nothing(*_):
        pass

    def up_z(d):
        return link(f"fuz{d}", fu.at[others[d]], fz_u.at[d - 1], far[d])

    def to_side(name, fin, mine):
        x = p if mine else 1 - p
        return link(f"{name}x", fin.at[c, x], fin.at[c, x], side)

    def to_core(name, fin, mine):
        x = c if mine else 1 - c
        return link(f"{name}c", fin.at[x], fin.at[x], core)

    def half_add():
        early[0].wait()
        half_x().wait_recv()

        def step(z, carry):
            fu[z, :, :LANES] = fu[z, :, :LANES] + hx[z]
            return carry

        grouped(nz, step, 0)

    def last_y_add():
        early[1].wait()
        last_y().wait_recv()

        def step(i, carry):
            x, z = i // nz, lax.rem(i, nz)
            ly[x, z] = ly[x, z] + ly_r[x, z]
            return carry

        grouped(2 * nz, step, 0)
        last_x().start()

    def last_x_add():
        last_x().wait_recv()

        def step(z, carry):
            fu[z, :, LANES:] = ly[p, z] + lx[z]
            return carry

        grouped(nz, step, 0)
        for d in range(1, nz):
            up_z(d).start()

    def up_sum():
        early[2].wait()
        early[3].wait()
        total = fu[zb].astype(f32)
        for d in range(1, nz):
            up_z(d).wait_recv()
            total = total + fz_u[d - 1].astype(f32)
        fin_u[c, p, :, lead : lead + 2 * LANES] = total.astype(bf16)
        to_side("gu", fin_u, True).start()

    def place_half():
        late[0].wait()
        each_part(0, lambda k: down_y(k).start(), nothing)

    def place_last():
        late[1].wait()
        last_d().wait_recv()

        def step(k, carry):
            fd[parts + k] = fd[parts + k] + lx_d[k]
            return carry

        grouped(parts, step, 0)
        each_part(parts, lambda k: down_y(k).start(), nothing)

    def down_y_add(begin):
        def here(k, owner, spot):
            down_y(k).wait_recv()
            fd[k] = fd[k] + fy_d[k]

            @pl.when(owner // 2 != zb)
            def _():
                down_z(k).start()

        each_part(begin, nothing, here)

    def down_sum():
        early[4].wait()

        def here(k, owner, spot):
            @pl.when(owner // 2 == zb)
            def _():
                total = fd[k].astype(f32)
                for d in range(1, nz):
                    place = fz_d.at[spot, d - 1]
                    pltpu.make_async_copy(place, place, dz_recv.at[spot, d - 1]).wait()
                    total = total + fz_d[spot, d - 1].astype(f32)
                fin_d[c, p, spot] = total.astype(bf16)

        for begin in (0, parts):
            each_part(begin, nothing, here)
        to_side("gd", fin_d, True).start()

    def down_gone():
        def here(k, owner, spot):
            @pl.when(owner // 2 != zb)
            def _():
                down_z(k).wait_send()

        for begin in (0, parts):
            each_part(begin, lambda k: down_y(k).wait_send(), here)

    def pass_on(name, fin):
        to_side(name, fin, False).wait_recv()
        to_core(name, fin, True).start()

    u_out = pltpu.make_async_copy(fin_u, o_fu, out_sem.at[0])
    d_out = pltpu.make_async_copy(fin_d, o_fd, out_sem.at[1])
    p_out = pltpu.make_async_copy(fin_p, o_fp, out_sem.at[2])
    mg_out = pltpu.make_async_copy(mg_all, o_mg, out_sem.at[3])
    ml_out = pltpu.make_async_copy(ml_all, o_ml, out_sem.at[4])

    def side_first(k):
        return k % 2 == 0

    def p1(k):
        return link(f"p1{k}", wp.at[k, 1 - c], p_r1.at[k], core)

    def p2(k):
        if side_first(k):
            return link(f"p2{k}", wp.at[k, c, 1 - p], p_r2x.at[k], side)
        return link(f"p2{k}", wp.at[k, c, :, :, 1 - yb], p_r2y.at[k], beside)

    def p3(k):
        if side_first(k):
            return link(f"p3{k}", wp.at[k, c, p, :, 1 - yb], p_r3.at[k], beside)
        return link(f"p3{k}", wp.at[k, c, 1 - p, :, yb], p_r3.at[k], side)

    def p4(k, d):
        return link(
            f"p4{k}{d}", wp.at[k, c, p, others[d], yb], p_r4.at[k, d - 1], far[d]
        )

    def p_side(k, mine):
        x = p if mine else 1 - p
        return link(f"p5{k}", fin_p.at[k, c, x], fin_p.at[k, c, x], side)

    def p_core(k, mine):
        x = c if mine else 1 - c
        return link(f"p6{k}", fin_p.at[k, x], fin_p.at[k, x], core)

    def p_add_1(k):
        p1(k).wait_recv()

        def step(i, carry):
            x, z, y = i // (2 * nz), lax.rem(i // 2, nz), lax.rem(i, 2)
            wp[k, c, x, z, y] = wp[k, c, x, z, y] + p_r1[k, x, z, y]
            return carry

        grouped(4 * nz, step, 0)
        p2(k).start()

    def p_add_2(k):
        p2(k).wait_recv()

        def step(i, carry):
            if side_first(k):
                z, y = i // 2, lax.rem(i, 2)
                wp[k, c, p, z, y] = wp[k, c, p, z, y] + p_r2x[k, z, y]
            else:
                x, z = i // nz, lax.rem(i, nz)
                wp[k, c, x, z, yb] = wp[k, c, x, z, yb] + p_r2y[k, x, z]
            return carry

        grouped(2 * nz, step, 0)
        p3(k).start()

    def p_add_3(k):
        p3(k).wait_recv()

        def step(z, carry):
            wp[k, c, p, z, yb] = wp[k, c, p, z, yb] + p_r3[k, z]
            return carry

        grouped(nz, step, 0)
        for d in range(1, nz):
            p4(k, d).start()

    def p_add_4(k):
        total = wp[k, c, p, zb, yb].astype(f32)
        for d in range(1, nz):
            p4(k, d).wait_recv()
            total = total + p_r4[k, d - 1].astype(f32)
        fin_p[k, c, p] = total.astype(bf16)
        p_side(k, True).start()

    def p_pass(k):
        p_side(k, False).wait_recv()
        p_core(k, True).start()

    peers = [core, side, beside]
    order = [core, beside, side]

    def kern_copy(name, kk, kr, stage):
        return link(f"{name}{stage}", kk.at[stage], kr.at[stage], order[stage])

    def kern_far(name, kk, kz, d):
        return link(f"{name}z{d}", kk.at[3], kz.at[d - 1], far[d])

    def kern_step(name, kk, kr, kz, stage):
        kern_copy(name, kk, kr, stage).wait_recv()
        kk[stage + 1] = (kk[stage].astype(f32) + kr[stage].astype(f32)).astype(bf16)
        if stage < 2:
            kern_copy(name, kk, kr, stage + 1).start()
        else:
            for d in range(1, nz):
                kern_far(name, kk, kz, d).start()

    def kern_sum(name, kk, kz, out):
        total = kk[3].astype(f32)
        for d in range(1, nz):
            kern_far(name, kk, kz, d).wait_recv()
            total = total + kz[d - 1].astype(f32)
        out[...] = total

    one = ("one", kk_1, kr_1, kz_1)

    def taps_core():
        return link("kt0", kt.at[1 - c], kt_core, core)

    def taps_side():
        return link("kt1", kt.at[c, 1 - p], kt_side, side)

    def taps_y():
        return link("kt2", kt.at[c, p], kt_y, beside)

    def taps_z(d):
        return link(f"kt3{d}", kt_sum, kt_z.at[d - 1], far[d])

    def taps_core_add():
        taps_core().wait_recv()
        for x in range(2):
            kt[c, x] = kt[c, x] + kt_core[x]
        taps_side().start()

    def taps_side_add():
        taps_side().wait_recv()
        kt[c, p] = kt[c, p] + kt_side[...]
        taps_y().start()

    def taps_y_add():
        taps_y().wait_recv()
        kt_sum[...] = kt[c, p] + kt_y[...]
        for d in range(1, nz):
            taps_z(d).start()

    def taps_total():
        total = kt_sum[...].astype(f32)
        for d in range(1, nz):
            taps_z(d).wait_recv()
            total = total + kt_z[d - 1].astype(f32)
        fin_k[c, p] = total.astype(bf16)
        to_side("gk", fin_k, True).start()

    def mg_swap(mine=True):
        x = c if mine else 1 - c
        return link("mgc", mg_all.at[x], mg_all.at[x], core)

    def mg_copy(part, stage, mine=True):
        name, own, first, every = part
        if stage == 0:
            return link(f"{name}0", own.at[1 - c] if name == "mg" else own, first, core)
        every = every.at[c] if name == "mg" else every
        x = p if mine else 1 - p
        y = yb if mine else 1 - yb
        place = every.at[zb, yb, x] if stage == 1 else every.at[zb, y]
        return link(f"{name}{stage}", place, place, peers[stage])

    def mg_far(part, d, z):
        place = part[3].at[c, z] if part[0] == "mg" else part[3].at[z]
        return link(f"{part[0]}z{d}", place, place, far[d])

    def mg_step(part, stage):
        name, own, first, every = part
        mg_copy(part, stage, False).wait_recv()
        if stage == 0 and name == "mg":
            every[c, zb, yb, p] = own[c] + first[...]
        elif stage == 0:
            every[zb, yb, p] = own[...] + first[...]
        if stage < 2:
            mg_copy(part, stage + 1).start()
        else:
            for d in range(1, nz):
                mg_far(part, d, zb).start()

    def mg_end(part):
        for d in range(1, nz):
            mg_far(part, d, lax.rem(zb + nz - d, nz)).wait_recv()

    soon = ("mg", mg_own, mg_r1, mg_all)

    def ml_copy(stage, mine=True):
        if stage == 0:
            return link("ml0", ml_own, ml_r1, core)
        if stage == 1:
            place = ml_all.at[zb, yb if mine else 1 - yb, p]
            return link("ml1", place, place, beside)
        place = ml_all.at[:, :, p if mine else 1 - p]
        return link("ml2", place, place, side)

    def ml_far(d, z):
        return link(f"mlz{d}", ml_all.at[z, :, p], ml_all.at[z, :, p], far[d])

    def ml_step(stage):
        if stage == 0:
            ml_copy(0).wait_recv()
            ml_all[zb, yb, p] = ml_own[...] + ml_r1[...]
            ml_copy(1).start()
        elif stage == 1:
            ml_copy(1, False).wait_recv()
            for d in range(1, nz):
                ml_far(d, zb).start()
        elif stage == 2:
            for d in range(1, nz):
                ml_far(d, lax.rem(zb + nz - d, nz)).wait_recv()
            ml_copy(2).start()
        else:
            ml_copy(2, False).wait_recv()

    pieces = [
        (wo_in, wo), (att_in, att), (tok_in, tok), (proj_in, proj), (wqkv_in, wqkv), (x_in, xf),
        (mid_in, mid),
    ]
    loads = [
        pltpu.make_async_copy(src, dst, load_sem.at[n]) for n, (src, dst) in enumerate(pieces)
    ]
    early = [
        pltpu.make_async_copy(uh_in.at[p], fu.at[:, :, pl.ds(0, LANES)], load_sem.at[7]),
        pltpu.make_async_copy(ul_in.at[:, :, yb], ly, load_sem.at[8]),
        *[
            pltpu.make_async_copy(
                ud_in.at[:, pl.ds(at, lead)], fin_u.at[c, p, :, pl.ds(at, lead)], load_sem.at[n]
            )
            for n, at in ((9, 0), (10, lead + 2 * LANES))
        ],
        pltpu.make_async_copy(dd_in, fin_d.at[c, p], load_sem.at[11]),
    ]
    late = [
        pltpu.make_async_copy(dh_in, fd.at[pl.ds(0, parts)], load_sem.at[12]),
        pltpu.make_async_copy(dl_in.at[p], fd.at[pl.ds(parts, parts)], load_sem.at[13]),
    ]
    for load in (*loads[:4], *late, *early, *loads[4:]):
        load.start()
    half_width, quarter = width // 2, kt.shape[3]
    for x in range(2):
        span = slice(x * half_width, (x + 1) * half_width)
        mg_own[x] = small[:, span]
        mg_own[x, 6:8, :] = mod[6:8, span]
        for q in range(2):
            at = (2 * x + q) * quarter
            kt[x, q] = kern_two[:, at : at + quarter].astype(bf16)
    meet([core, side, corner, beside, *far[1:]])
    grad_away = remote(
        rg_in.at[:, 1 - c], rows_m.at[pl.ds(8 * c, 8)], ex_send.at[0], ex_recv.at[0], core
    )
    grad_away.start()
    grad_own = pltpu.make_async_copy(rg_in.at[:, c], rows_m.at[pl.ds(8 * c, 8)], own_sem.at[0])
    grad_own.start()
    last_d().start()
    last_y().start()
    half_x().start()
    mg_copy(soon, 0).start()
    taps_core().start()
    perm[0] = permutation(False)
    perm[1] = permutation(True)
    grad_own.wait()
    grad_away.wait()
    grad[...] = dot_nn(perm[0], rows_m[...].reshape(tokens, width)).astype(bf16)
    loads[0].wait()
    loads[1].wait()
    datt[...] = dot_nt(grad[...], wo[...]).astype(bf16)
    out_grad = dot_tn(att[...], grad[...])
    for k in range(chunks):
        cut = slice(k * chunk, (k + 1) * chunk)
        wp[k, 1, 1] = out_grad[:, cut].reshape(nz, 2, rows_own, chunk).astype(bf16)
    loads[2].wait()
    tok_t[...] = tok[...].T
    loads[3].wait()
    low_lane = lax.broadcasted_iota(jnp.int32, (size, LANES), 1) < LANES // 2
    lane_id = lax.broadcasted_iota(jnp.int32, (size, LANES), 1)
    zero = jnp.zeros((), bf16)

    def attend(index, carry):
        pair, half = index // 2, lax.rem(index, 2)
        rows = pl.ds(pl.multiple_of(half * size, size), size)

        def cut(n):
            return pl.ds(pl.multiple_of(n * width + pair * LANES, LANES), LANES)

        q = proj[rows, cut(0)] * jnp.asarray(0.125, bf16)
        k, v, up = proj[rows, cut(1)], proj[rows, cut(2)], datt[rows, cut(0)]
        sums = lse[half]
        dq = jnp.zeros((size, LANES), f32)
        dk = jnp.zeros((size, LANES), f32)
        dv = jnp.zeros((size, LANES), f32)
        for h in range(2):
            mine = low_lane if h == 0 else jnp.logical_not(low_lane)
            key = jnp.where(mine, k, zero)
            scores = dot_nt(q, key) + bias[half]
            mass = jnp.sum(
                jnp.where(lane_id == 2 * pair + h, sums, 0.0), axis=-1, keepdims=True
            )
            weights = jnp.exp(scores - mass)
            pull = dot_nt(up, jnp.where(mine, v, zero))
            mean = jnp.sum(weights * pull, axis=-1, keepdims=True)
            spare = (weights * (pull - mean)).astype(bf16)
            dq = dq + dot_nn(spare, key)
            dk = dk + dot_tn(spare, jnp.where(mine, q, zero))
            dv = dv + dot_tn(weights.astype(bf16), jnp.where(mine, up, zero))
        dproj[rows, cut(0)] = (dq * 0.125).astype(bf16)
        dproj[rows, cut(1)] = dk.astype(bf16)
        dproj[rows, cut(2)] = dv.astype(bf16)
        return carry

    def weigh(k):
        span = slice(2 * k * chunk, 2 * (k + 1) * chunk)
        for q in range(3):
            part = dot_nn(tok_t[...], dproj[:, q * width + span.start : q * width + span.stop])
            part = part.reshape(nz, 2, rows_own, 2 * chunk).astype(bf16)
            for n in range(2):
                wp[2 * k + n, q % 2, q // 2] = part[..., n * chunk : (n + 1) * chunk]
        p1(2 * k).start()
        p1(2 * k + 1).start()

    def res_home(n, i):
        return lambda: send_home(n, res_in, o_res, r_send, r_recv, False, 2 * i, 2)

    def ig_home(n, i):
        send_home(n, ig, o_ig, i_send, i_recv, False, 2 * i, 2)

    hooks = {
        0: [lambda: mg_step(soon, 0), taps_core_add],
        1: [half_add, place_half],
        2: [place_last, res_home(0, 0)],
        3: [lambda: weigh(0), last_y_add, res_home(0, 1)],
        4: [res_home(0, 2)],
        5: [lambda: mg_step(soon, 1), taps_side_add],
        6: [lambda: down_y_add(0), res_home(0, 3)],
        7: [lambda: weigh(1), lambda: p_add_1(0), lambda: p_add_1(1)],
        8: [last_x_add, res_home(1, 0)],
        9: [lambda: down_y_add(parts), res_home(1, 1)],
        10: [lambda: mg_step(soon, 2), taps_y_add],
        11: [lambda: weigh(2)],
    }

    def attend_and_pass(index, carry):
        attend(index, carry)
        for at, steps in hooks.items():

            @pl.when(index == at)
            def _(steps=steps):
                for step in steps:
                    step()

        return carry

    lax.fori_loop(0, 2 * pairs, attend_and_pass, 0)
    loads[4].wait()
    back = dot_nt(dproj[...], wqkv[...]).astype(bf16)
    brm[...] = dot_nn(perm[1], back).astype(bf16).reshape(16, across, width)
    mixed_away = remote(
        brm.at[pl.ds(7 * (1 - c), 9)], frame.at[:, c], ex_send.at[1], ex_recv.at[1], core
    )
    mixed_away.start()
    mixed_own = pltpu.make_async_copy(brm.at[pl.ds(7 * c, 9)], frame.at[:, c], own_sem.at[1])
    mixed_own.start()
    p_add_2(0)
    p_add_2(1)
    p_add_1(2)
    p_add_1(3)
    res_home(1, 2)()
    loads[5].wait()
    loads[6].wait()

    shift = mod[0:1, :]
    scale_in = 1.0 + mod[1:2, :]

    def again(row, carry):
        normal, _ = normalize(xf[2 * c + row].astype(f32))
        value[row] = (normal * scale_in + shift).astype(bf16).astype(f32)
        return carry

    grouped(16, again, 0)
    p_add_1(4)
    p_add_1(5)
    res_home(1, 3)()
    up_sum()
    mixed_own.wait()
    mixed_away.wait()

    def lay(row, carry):
        at = c + row
        line = frame[at // 2, lax.rem(at, 2)].astype(f32)
        before, after = column_shifts(line)
        gs[0, 1 - c + row] = after
        gs[1, 1 - c + row] = line
        gs[2, 1 - c + row] = before
        return carry

    grouped(17, lay, 0)
    for s in range(3):
        gs[s, 17 * c] = jnp.zeros((across, width), f32)

    def conv_back(lane, half):
        span = slice(lane, lane + LANES)
        taps = [kern[n : n + 1, span].astype(f32) for n in range(9)]

        def backward(row, sums):
            total = jnp.zeros((across, LANES), f32)
            own = value[row, :, span]
            later = []
            for r in range(3):
                for s in range(3):
                    line = gs[s, row + 2 - r, :, span]
                    total = total + taps[3 * r + s] * line
                    later.append(sums[3 * r + s] + fold(own * line))
            agrad[row, :, span] = total
            return tuple(later)

        sums = lax.fori_loop(
            8 * half, 8 * half + 8, backward,
            tuple(jnp.zeros((8, LANES), f32) for _ in range(9)),
        )
        rows9 = [jnp.sum(sums[n], axis=0, keepdims=True) for n in range(9)]
        lines = jnp.concatenate(rows9 + [jnp.zeros((7, LANES), f32)])
        if half == 0:
            taps_sum[:, span] = lines
        else:
            kk_1[0, :, span] = (taps_sum[:, span] + lines).astype(bf16)

    def finish(row, sums):
        normal, scale = normalize(xf[2 * c + row].astype(f32))
        line = agrad[row]
        place = pl.ds(pl.multiple_of(row * across, across), across)
        total = mid[place, :] + normalize_back(line * scale_in, normal, scale)
        ig[row] = total.astype(bf16)
        return (sums[0] + fold(line), sums[1] + fold(line * normal))

    sums = tuple(jnp.zeros((8, width), f32) for _ in range(2))
    p_add_3(0)
    p_add_3(1)
    down_sum()
    for lane in range(0, width, LANES):
        conv_back(lane, 0)
        if lane == 2 * LANES:
            p_add_2(2)
            p_add_2(3)
    sums = lax.fori_loop(0, 8, finish, sums)
    ig_home(0, 0)
    p_add_2(4)
    ig_home(0, 1)
    p_add_2(5)
    ig_home(0, 2)
    ig_home(0, 3)
    pass_on("gu", fin_u)
    taps_total()
    for lane in range(0, width, LANES):
        conv_back(lane, 1)
        if lane == 2 * LANES:
            p_add_3(2)
            p_add_3(3)
            pass_on("gd", fin_d)
            p_add_4(0)
            p_add_4(1)
    kern_copy("one", kk_1, kr_1, 0).start()
    sums = lax.fori_loop(8, 16, finish, sums)
    for n in range(2):
        ml_own[n : n + 1, :] = jnp.sum(sums[n], axis=0, keepdims=True)
    ml_copy(0).start()
    ig_home(1, 0)
    p_add_3(4)
    p_add_3(5)
    ig_home(1, 1)
    mg_end(soon)
    mg_swap().start()
    kern_step(*one, 0)
    ml_step(0)
    ig_home(1, 2)
    p_pass(0)
    p_pass(1)
    pass_on("gk", fin_k)
    p_add_4(2)
    p_add_4(3)
    ig_home(1, 3)
    kern_step(*one, 1)
    ml_step(1)
    mg_swap(False).wait_recv()
    mg_out.start()
    to_core("gu", fin_u, False).wait_recv()
    u_out.start()
    to_core("gd", fin_d, False).wait_recv()
    d_out.start()
    p_add_4(4)
    p_add_4(5)
    kern_step(*one, 2)
    ml_step(2)
    p_pass(2)
    p_pass(3)
    p_pass(4)
    p_pass(5)
    ml_step(3)
    ml_out.start()
    kern_sum("one", kk_1, kz_1, o_one)
    for k in range(chunks):
        p_core(k, False).wait_recv()
    p_out.start()
    to_core("gk", fin_k, False).wait_recv()
    for x in range(4):
        o_two[:, x * quarter : (x + 1) * quarter] = fin_k[x // 2, x % 2].astype(f32)
    gone([half_x(), last_y(), last_x(), last_d()])
    down_gone()
    gone([taps_core(), taps_side(), taps_y(), mg_swap()])
    for name, fin in (("gu", fin_u), ("gd", fin_d), ("gk", fin_k)):
        gone([to_side(name, fin, True), to_core(name, fin, True)])
    for d in range(1, nz):
        gone([up_z(d), mg_far(soon, d, zb), ml_far(d, zb)])
        gone([kern_far("one", kk_1, kz_1, d), taps_z(d)])
    for k in range(chunks):
        gone([p1(k), p2(k), p3(k), p_side(k, True), p_core(k, True)])
        gone([p4(k, d) for d in range(1, nz)])
    for stage in range(3):
        gone([mg_copy(soon, stage), ml_copy(stage)])
        gone([kern_copy("one", kk_1, kr_1, stage)])
    for n in range(2):
        send_home(n, res_in, o_res, r_send, r_recv, True)
        send_home(n, ig, o_ig, i_send, i_recv, True)
    home(o_res, r_recv)
    home(o_ig, i_recv)
    for out in (u_out, d_out, p_out, mg_out, ml_out):
        out.wait()


def back(
    mid, rg, tok, proj, att, lse, bias, x_frame, mod, small, kern, wqkv, wo, res,
    ud, dd, uh, dh, ul, dl, kern_two,
):
    nb = lax.axis_size("batch")
    nz = nb // 2
    across, width = x_frame.shape[1], x_frame.shape[2]
    tokens = 16 * across
    rows = width // nb
    grain = dd.shape[1]
    parts = dl.shape[1]
    per = dd.shape[0]
    chunks, chunk = width // LANES, LANES
    many = max(nz - 1, 1)
    any_space = pl.BlockSpec(memory_space=pl.ANY)
    vmem = pl.BlockSpec(memory_space=pltpu.VMEM)
    shape = jax.ShapeDtypeStruct
    dma = pltpu.SemaphoreType.DMA
    wide = kern_two.shape[1]
    links = 100 + 20 * many

    def low(*dims):
        return pltpu.VMEM(dims, bf16)

    def high(*dims):
        return pltpu.VMEM(dims, f32)

    return pl.pallas_call(
        back_kernel,
        out_shape=(
            shape((2, 2, rows, width), bf16),
            shape((2, 2, per, grain, width), bf16),
            shape((chunks, 2, 2, rows, chunk), bf16),
            shape((2, 8, across, width), bf16),
            shape((2, 8, across, width), bf16),
            shape((16, width), f32),
            shape((16, wide), f32),
            shape((2, nz, 2, 2, 8, width // 2), f32),
            shape((nz, 2, 2, 2, width), f32),
        ),
        in_specs=[any_space] * 5 + [vmem, vmem, any_space, vmem, vmem, vmem] + [any_space] * 9
        + [vmem],
        out_specs=[any_space] * 5 + [vmem, vmem, any_space, any_space],
        scratch_shapes=[
            high(tokens, width), low(tokens, width), low(width, tokens), low(tokens, 3 * width),
            low(tokens, width), low(18, across, width), low(*wqkv.shape), low(*wo.shape),
            low(16, across, width), low(2, tokens, tokens), low(tokens, width),
            low(tokens, width), low(tokens, 3 * width),
            low(16, across, width), low(9, 2, across, width), high(3, 18, across, width),
            high(16, across, width), high(16, across, width), low(16, across, width),
            low(chunks, 2, 2, nz, 2, rows, chunk), low(chunks, 2, nz, 2, rows, chunk),
            low(chunks, nz, 2, rows, chunk), low(chunks, 2, nz, rows, chunk),
            low(chunks, nz, rows, chunk), low(chunks, many, rows, chunk),
            low(chunks, 2, 2, rows, chunk),
            low(nz, rows, 2 * LANES), low(2 * parts, grain, width),
            low(many, rows, 2 * LANES), low(2 * parts, grain, width), low(per, many, grain, width),
            low(2, 2, rows, width), low(2, 2, per, grain, width), low(parts, grain, width),
            low(nz, rows, LANES), low(2, nz, rows, LANES), low(2, nz, rows, LANES),
            low(nz, rows, LANES),
            high(2, 8, width // 2), high(8, width // 2), high(2, nz, 2, 2, 8, width // 2),
            high(2, width), high(2, width), high(nz, 2, 2, 2, width), high(16, width),
            low(4, 16, width), low(3, 16, width), low(many, 16, width),
            low(2, 2, 16, wide // 4), low(2, 16, wide // 4), low(16, wide // 4), low(16, wide // 4),
            low(16, wide // 4), low(many, 16, wide // 4), low(2, 2, 16, wide // 4),
            dma((2 * parts,)), dma((2 * parts,)), dma((2 * parts,)), dma((per, many)), dma((14,)), dma((2,)), dma((2,)), dma((2,)), dma((2,)), dma((2,)), dma((2,)),
            dma((2,)), dma((links,)), dma((links,)), dma((5,)),
        ],
        compiler_params=pltpu.CompilerParams(
            collective_id=2, has_side_effects=True, vmem_limit_bytes=63 << 20
        ),
        name="back",
    )(
        mid, rg, tok, proj, att, lse, bias, x_frame, mod, small, kern, wqkv, wo, res,
        ud, dd, uh, dh, ul, dl, kern_two,
    )


def parts_of(values):
    first = values.astype(bf16)
    rest = values - first.astype(f32)
    second = rest.astype(bf16)
    third = (rest - second.astype(f32)).astype(bf16)
    return jnp.concatenate([first, second, third], axis=0)


def thrice(values):
    return jnp.concatenate([values] * 3, axis=0).astype(bf16)


def tail_kernel(
    fu, fd, fp, mg, late, one, two, wm_in, res_in, ig_in,
    o_class, o_time, mod_out, proj_out, o_out, o_one, up_out, o_two, down_out, o_res, o_ig,
    wm, moved, o_mod, o_proj, o_up, o_down, load_sem, in_sem, out_sem, big_sem,
):
    b = lax.axis_index("batch")
    width = 2 * mg.shape[3]
    canvases = mg.shape[1]
    own = o_mod.shape[0]
    whole = wm_in.shape[0] == own
    source = wm_in if whole else wm_in.at[pl.ds(pl.multiple_of(b * own, 16), own)]
    load = pltpu.make_async_copy(source, wm, load_sem)
    load.start()
    takes = [
        pltpu.make_async_copy(src, moved.at[n], in_sem.at[n]) for n, src in enumerate((res_in, ig_in))
    ]
    gives = [
        pltpu.make_async_copy(moved.at[n], dst, out_sem.at[n]) for n, dst in enumerate((o_res, o_ig))
    ]
    for take in takes:
        take.start()
    big = [
        pltpu.make_async_copy(src, dst, big_sem.at[n])
        for n, (src, dst) in enumerate(
            ((o_up, up_out), (o_down, down_out), (o_proj, proj_out), (o_mod, mod_out))
        )
    ]
    chunks, chunk = fp.shape[0], fp.shape[4]
    per, grain = fd.shape[2], fd.shape[3]
    for q in range(4):
        for j in range(width // LANES):
            at = (4 * j + q) * LANES
            o_up[:, at : at + LANES] = fu[q % 2, q // 2, :, j * LANES : (j + 1) * LANES].astype(f32)
        for i in range(per):
            at = (4 * i + q) * grain
            o_down[at : at + grain, :] = fd[q % 2, q // 2, i].astype(f32)
        for k in range(chunks):
            part = fp[k, q % 2, q // 2].astype(f32)
            if q < 3:
                o_proj[:, q * width + k * chunk : q * width + (k + 1) * chunk] = part
            else:
                o_out[:, k * chunk : (k + 1) * chunk] = part
    for move in big[:3]:
        move.start()
    for take, give in zip(takes, gives):
        take.wait()
        give.start()

    def window(values, n):
        size = values.shape[1]
        return pltpu.roll(values, lax.rem(size - b * n, size), 1)[:, :n]

    o_one[...] = window(one[...], own)[0:9]
    o_two[...] = window(two[...], o_two.shape[1])[0:9]
    every = jnp.concatenate([mg[0], mg[1]], axis=2)
    begin = late[...]
    cond = window(every[:, 7, :] * 0.5, own)
    sigma = 1.0 / (1.0 + jnp.exp(-cond))
    low = thrice(cond * sigma)
    steep = sigma * (1.0 + cond * (1.0 - sigma))
    act_grad = jnp.zeros((3 * canvases, own), f32)
    load.wait()
    for part in range(6):
        span = slice(part * width, (part + 1) * width)
        line = parts_of(begin[:, part, :] if part < 2 else every[:, part, :])
        o_mod[:, span] = dot_tn(low, line)
        act_grad = act_grad + dot_nt(line, wm[:, span])
    big[3].start()
    act_grad = (
        act_grad[2 * canvases :] + act_grad[canvases : 2 * canvases] + act_grad[:canvases]
    )
    cond_grad = parts_of(act_grad * steep)
    names = every[:, 6, :] * 0.5
    kinds = o_class.shape[1]
    spot = lax.broadcasted_iota(jnp.int32, (canvases, kinds), 1).astype(f32)
    for n, out in enumerate((o_class, o_time)):
        hot = thrice(jnp.where(spot == names[:, n : n + 1], 1.0, 0.0))
        out[...] = dot_tn(cond_grad, hot)
    for give in (*gives, *big):
        give.wait()


def tail(fu, fd, fp, mg, late, one, two, wmod, res, ig, classes, times):
    nb = lax.axis_size("batch")
    width = 2 * mg.shape[3]
    own = width // nb
    wide = two.shape[1] // nb
    if own % 16:
        wmod = lax.dynamic_slice_in_dim(wmod, lax.axis_index("batch") * own, own, axis=0)
    any_space = pl.BlockSpec(memory_space=pl.ANY)
    vmem = pl.BlockSpec(memory_space=pltpu.VMEM)
    shape = jax.ShapeDtypeStruct
    dma = pltpu.SemaphoreType.DMA
    return pl.pallas_call(
        tail_kernel,
        out_shape=(
            shape((own, classes), f32),
            shape((own, times), f32),
            shape((own, 6 * width), f32),
            shape((own, 3 * width), f32),
            shape((own, width), f32),
            shape((9, own), f32),
            shape((own, 4 * width), f32),
            shape((9, wide), f32),
            shape((4 * fd.shape[2] * fd.shape[3], width), f32),
            shape(res.shape, bf16),
            shape(ig.shape, bf16),
        ),
        in_specs=[vmem] * 7 + [any_space] * 3,
        out_specs=[
            vmem, vmem, any_space, any_space, vmem, vmem, any_space, vmem, any_space, any_space,
            any_space,
        ],
        scratch_shapes=[
            pltpu.VMEM((own, 6 * width), bf16), pltpu.VMEM((2, *res.shape), bf16),
            pltpu.VMEM((own, 6 * width), f32), pltpu.VMEM((own, 3 * width), f32),
            pltpu.VMEM((own, 4 * width), f32),
            pltpu.VMEM((4 * fd.shape[2] * fd.shape[3], width), f32),
            dma, dma((2,)), dma((2,)), dma((4,)),
        ],
        compiler_params=pltpu.CompilerParams(vmem_limit_bytes=60 << 20),
        name="tail",
    )(fu, fd, fp, mg, late, one, two, wmod, res, ig)


def body(
    inputs,
    segments,
    class_labels,
    time_steps,
    class_table,
    time_table,
    modulation_weight,
    project_weight,
    output_weight,
    kernel_attention,
    up_weight,
    kernel_feed,
    down_weight,
    cotangent,
):
    across, width = inputs.shape[2], inputs.shape[3]
    nb = lax.axis_size("batch")
    units = up_weight.shape[1]
    share = units // nb
    grain = 32 if share % 128 == 0 else 16 if share % 64 == 0 else 8
    x_frame, cot_frame, returned, tok, proj, att, lse, bias, mod = front(
        inputs, cotangent, class_labels, time_steps, segments, kernel_attention, class_table,
        time_table, modulation_weight, project_weight, output_weight,
    )
    flat = (18 * across, width)
    ud, dd, uh, dh, ul, dl, kern_two, res, mid, rg, small = feed(
        x_frame.reshape(flat), returned.reshape(flat), cot_frame.reshape(flat), mod, up_weight,
        kernel_feed, down_weight, grain,
    )
    fu, fd, fp, result, inputs_gradient, one, two, gathered, late = back(
        mid, rg.reshape(8, 2, across, width), tok, proj, att, lse, bias, x_frame, mod, small,
        kernel_attention, project_weight, output_weight, res.reshape(16, across, width),
        ud, dd, uh, dh, ul, dl, kern_two,
    )
    (
        class_total, time_total, modulation_total, project_total, output_total,
        attention_kernel_total, up_total, feed_kernel_total, down_total, result, inputs_gradient,
    ) = tail(
        fu, fd, fp, gathered.reshape(2, 2 * nb, 8, width // 2), late.reshape(2 * nb, 2, width), one, two,
        modulation_weight, result, inputs_gradient, class_table.shape[0], time_table.shape[0],
    )
    return (
        result,
        inputs_gradient,
        class_total.T,
        time_total.T,
        modulation_total,
        project_total,
        output_total,
        attention_kernel_total,
        up_total,
        feed_kernel_total,
        down_total,
    )


def solution(mesh):
    in_specs = (
        P("batch", "group", None, None),
        P("batch", None),
        P("batch"),
        P("batch"),
        P(),
        P(),
        P(),
        P(),
        P(),
        P(),
        P(),
        P(),
        P(),
        P("batch", "group", None, None),
    )
    out_specs = (
        P("batch", "group", None, None),
        P("batch", "group", None, None),
        P(None, "batch"),
        P(None, "batch"),
        P("batch", None),
        P("batch", None),
        P("batch", None),
        P(None, "batch"),
        P("batch", None),
        P(None, "batch"),
        P("batch", None),
    )
    return jax.shard_map(body, mesh=mesh, in_specs=in_specs, out_specs=out_specs, check_vma=False)
```
